32 devices in a mesh: dp: 16 (over z, y, core), tensor: 2 (over x).
Axes of the slice: x: 2, y: 2, z: 4, core: 2. Of those that a mesh axis runs over, the one named last changes fastest.
Arguments:
- hidden_in: bfloat16 [2048, 2048], P('dp'), may hold values from -6 to 6
- seq_lengths: int32 [64], replicated, may hold values from 1 to 128, as said below
- seq_device: int32 [64], replicated, may hold values from 0 to 15, as said below
- positions: int32 [2048], P('dp'), may hold values from 0 to 2047, as said below
- norm_gain: bfloat16 [2, 2048], P(None, 'dp'), may hold values from 0.5 to 1.5
- norm_bias: bfloat16 [2, 2048], P(None, 'dp'), may hold values from -2 to 2
- qkv_weight: bfloat16 [2, 2048, 3, 2048], P(None, 'dp', None, 'tensor'), may hold values from -0.125 to 0.125
- qkv_bias: bfloat16 [2, 3, 2048], P(None, None, ('tensor', 'dp')), may hold values from -3 to 3
- out_weight: bfloat16 [2, 2048, 2048], P(None, 'tensor', 'dp'), may hold values from -0.375 to 0.375
- fc1_weight: bfloat16 [2, 2048, 8192], P(None, 'dp', 'tensor'), may hold values from -0.125 to 0.125
- fc1_bias: bfloat16 [2, 8192], P(None, ('tensor', 'dp')), may hold values from -3 to 3
- fc2_weight: bfloat16 [2, 8192, 2048], P(None, 'tensor', 'dp'), may hold values from -0.0625 to 0.0625
- output_bias: bfloat16 [2, 2048], P(None, 'dp'), may hold values from -2 to 2
- out_cotangent: bfloat16 [2048, 2048], P('dp'), may hold values from -6 to 6
Outputs:
- hidden_out: bfloat16 [2048, 2048], P('dp')
- grad_hidden: float32 [2048, 2048], P('dp')
- grad_norm_gain: float32 [2, 2048], P(None, 'dp')
- grad_norm_bias: float32 [2, 2048], P(None, 'dp')
- grad_qkv_weight: float32 [2, 2048, 3, 2048], P(None, 'dp', None, 'tensor')
- grad_qkv_bias: float32 [2, 3, 2048], P(None, None, ('tensor', 'dp'))
- grad_out_weight: float32 [2, 2048, 2048], P(None, 'tensor', 'dp')
- grad_fc1_weight: float32 [2, 2048, 8192], P(None, 'dp', 'tensor')
- grad_fc1_bias: float32 [2, 8192], P(None, ('tensor', 'dp'))
- grad_fc2_weight: float32 [2, 8192, 2048], P(None, 'tensor', 'dp')
- grad_output_bias: float32 [2, 2048], P(None, 'dp')
The draws below stay inside these ranges and needn't reach their ends.
Inputs may be any that keep to these rules, and one draw needn't show every extreme that they name: `seq_lengths`: the sequences of one device hold 128 tokens or fewer together, and some device holds a single sequence of exactly 128 tokens. `seq_device`: every device of dp holds between 1 and 7 sequences; both ends occur in every draw. `positions`: the j-th row of a sequence has the sequence's starting position plus j; padding rows have position 0.
All inputs are finite; a program needn't handle non-finite values.
Results may differ from the reference program's by a relative error of at most 0.02.
Values may be sent and summed in bfloat16 or wider, within the bound.
No kernel may reach another device: no remote copies, remote signals or barrier semaphores. Data moves between devices by JAX's collectives and lax.ppermute only.
A program may use at most 384 MiB of HBM per device.

```python
import jax
import jax.numpy as jnp
from jax import lax

D = 2048
HEADS = 32
HEAD_DIM = 64
ROT = 32
FF = 8192
POS_LIMIT = 2048
LAYERS = 2
TOK_DEV = 128
SEQ_MEAN = 4
TOKENS = 2048
N_DP = 16


def sequence_plan(key):
    pairs = N_DP // 2
    swing = jax.random.randint(jax.random.fold_in(key, 101), (pairs,), 1 - SEQ_MEAN, SEQ_MEAN)
    swing = swing.at[0].set(1 - SEQ_MEAN)
    per_slot = jnp.stack([SEQ_MEAN + swing, SEQ_MEAN - swing], axis=1).reshape(N_DP).astype(jnp.int32)
    order = jax.random.permutation(jax.random.fold_in(key, 102), N_DP)
    loads = jnp.zeros((N_DP,), jnp.int32).at[order].set(per_slot)
    bounds = jnp.cumsum(loads)
    slots = jnp.arange(SEQ_MEAN * N_DP, dtype=jnp.int32)
    owner_slot = jnp.sum((bounds[None, :] <= slots[:, None]).astype(jnp.int32), axis=1)
    shuffle = jax.random.permutation(jax.random.fold_in(key, 103), SEQ_MEAN * N_DP)
    owners = owner_slot[shuffle]
    sharing = loads[owners]
    limit = TOK_DEV // sharing
    lengths = jax.random.randint(jax.random.fold_in(key, 104), (SEQ_MEAN * N_DP,), 1, limit + 1)
    lengths = jnp.where(sharing == 1, TOK_DEV, lengths)
    starts = jax.random.randint(jax.random.fold_in(key, 105), (SEQ_MEAN * N_DP,), 0, POS_LIMIT - TOK_DEV + 1)
    return (lengths.astype(jnp.int32), owners.astype(jnp.int32), starts.astype(jnp.int32))


def draw_seq_lengths(key, part):
    lengths, owners, starts = sequence_plan(key)
    return lengths


def draw_seq_device(key, part):
    lengths, owners, starts = sequence_plan(key)
    return owners


def draw_positions(key, part):
    lengths, owners, starts = sequence_plan(key)
    index = jnp.arange(SEQ_MEAN * N_DP, dtype=jnp.int32)
    devices = jnp.arange(N_DP, dtype=jnp.int32)
    owned = jnp.where(owners[None, :] == devices[:, None], lengths[None, :], 0)
    earlier = index[None, :] < index[:, None]
    offsets = jnp.sum(jnp.where(earlier[None, :, :], owned[:, None, :], 0), axis=2)
    places = jnp.arange(TOK_DEV, dtype=jnp.int32)
    inside = (places[None, :, None] >= offsets[:, None, :]) & (places[None, :, None] < (offsets + owned)[:, None, :])
    value_rows = starts[None, None, :] + places[None, :, None] - offsets[:, None, :]
    return jnp.sum(jnp.where(inside, value_rows, 0), axis=2).reshape(N_DP * TOK_DEV).astype(jnp.int32)


def strengthened(array, own_key, source, target, blocks, factor):
    def block_of(axis_at):
        return (jnp.arange(array.shape[axis_at]) // (array.shape[axis_at] // blocks)).reshape((-1,) + (1,) * (array.ndim - 1 - axis_at))

    first = jax.random.permutation(own_key, blocks)[block_of(target)]
    far = (block_of(target) + blocks // 2) % blocks
    return jnp.where((block_of(source) == first) | (block_of(source) == far), factor * array, array)


def shard_levels(stream_key, dims, cuts, least, top_value):
    factor_of = 1.0
    for dim, shards_of in cuts:
        draws = jax.random.uniform(jax.random.fold_in(jax.random.fold_in(stream_key, 6), dim), (shards_of,), jnp.float32, least / len(cuts), top_value / len(cuts))
        factor_of = factor_of * jnp.repeat(jnp.exp(draws), dims[dim] // shards_of).reshape((-1,) + (1,) * (len(dims) - 1 - dim))
    return factor_of


def scatter_about(own_key, extent, scale, bound, shards=(), held_as=jnp.bfloat16):
    level = shard_levels(own_key, extent, shards, -0.22, 0.18) if shards else 1.0
    values = jax.random.normal(own_key, extent, jnp.float32) * scale * level
    return jnp.minimum(jnp.maximum(values, -bound), bound).astype(held_as)


def bell_draw_with(stream_key, dims, width, most, cuts, heavy, kind=jnp.bfloat16):
    entries = width * jax.random.normal(stream_key, dims, jnp.float32)
    if cuts:
        entries = entries * shard_levels(stream_key, dims, cuts, -0.22, 0.18)
    return jnp.clip(strengthened(entries, jax.random.fold_in(stream_key, 3), *heavy), -most, most).astype(kind)


def setup_inputs(seed: int = 0) -> dict:
    key_list = jax.random.split(jax.random.key(seed), 15)
    return {
        "hidden_in": bell_draw_with(key_list[0], (TOKENS, D), 1.0, 6.0, ((0, 16),), (0, 1, 16, 2.0)),
        "seq_lengths": draw_seq_lengths(jax.random.fold_in(key_list[14], 71), 0),
        "seq_device": draw_seq_device(jax.random.fold_in(key_list[14], 71), 0),
        "positions": draw_positions(jax.random.fold_in(key_list[14], 71), 0),
        "norm_gain": jnp.clip(1.0 + 0.1 * jax.random.normal(key_list[4], (LAYERS, D), jnp.float32), 0.5, 1.5).astype(jnp.bfloat16),
        "norm_bias": scatter_about(key_list[5], (LAYERS, D), 0.3, 2.0, ((1, 16),)),
        "qkv_weight": scatter_about(key_list[6], (LAYERS, D, 3, D), D ** -0.5, 0.125, ((1, 16), (3, 2))),
        "qkv_bias": scatter_about(key_list[7], (LAYERS, 3, D), 0.5, 3.0, ((2, 32),)),
        "out_weight": scatter_about(key_list[8], (LAYERS, D, D), (D * 16 // TOK_DEV) ** -0.5, 0.375, ((1, 2), (2, 16))),
        "fc1_weight": scatter_about(key_list[9], (LAYERS, D, FF), D ** -0.5, 0.125, ((1, 16), (2, 2))),
        "fc1_bias": scatter_about(key_list[10], (LAYERS, FF), 0.5, 3.0, ((1, 32),)),
        "fc2_weight": scatter_about(key_list[11], (LAYERS, FF, D), FF ** -0.5, 0.0625, ((1, 2), (2, 16))),
        "output_bias": scatter_about(key_list[12], (LAYERS, D), 0.3, 2.0, ((1, 16),)),
        "out_cotangent": scatter_about(key_list[13], (TOKENS, D), 1.0, 6.0, ((0, 16),)),
    }


@jax.custom_vjp
def low(v):
    return lax.optimization_barrier(v.astype(jnp.bfloat16)).astype(jnp.float32)

@jax.custom_vjp
def low_back(v):
    return v

def low_keep(v):
    return (low(v), None)

def low_pass(kept, grad):
    return (grad,)

def back_keep(v):
    return (v, None)

def back_low(kept, grad):
    return (low(grad),)
low.defvjp(low_keep, low_pass)
low_back.defvjp(back_keep, back_low)
highest = lax.Precision.HIGHEST
norm_epsilon = 1e-05
masked_score = -1e+30

def sequence_labels(seq_lengths, seq_device, owner, count_rows):
    index = jnp.arange(seq_lengths.shape[0], dtype=jnp.int32)
    owned = jnp.where(seq_device == owner, seq_lengths, 0)
    earlier = index[None, :] < index[:, None]
    starts = lax.optimization_barrier(jnp.sum(jnp.where(earlier, owned[None, :], 0), axis=1))
    places = jnp.arange(count_rows, dtype=jnp.int32)
    inside = (places[:, None] >= starts[None, :]) & (places[:, None] < (starts + owned)[None, :])
    return lax.optimization_barrier(jnp.sum(jnp.where(inside, index[None, :] + 1, 0), axis=1))

def allowed_pairs(labels):
    places = jnp.arange(labels.shape[0], dtype=jnp.int32)
    same = (labels[:, None] == labels[None, :]) & (labels[:, None] > 0) & (places[None, :] <= places[:, None])
    return same | (places[:, None] == places[None, :])

def rotate(field, positions):
    half = ROT // 2
    frequency = 10000.0 ** (-2.0 * jnp.arange(half, dtype=jnp.float32) / ROT)
    angles = positions.astype(jnp.float32)[:, None] * frequency[None, :]
    layout = (field.shape[0],) + (1,) * (field.ndim - 2) + (half,)
    cosine = jnp.cos(angles).reshape(layout)
    sine = jnp.sin(angles).reshape(layout)
    first = field[..., :half]
    second = field[..., half:ROT]
    return jnp.concatenate([first * cosine - second * sine, second * cosine + first * sine, field[..., ROT:]], axis=-1)

def norm_piece(state, gain, shift):
    centre = lax.optimization_barrier(jnp.mean(state, axis=1, keepdims=True))
    centered = state - centre
    spread = lax.optimization_barrier(jnp.mean(centered * centered, axis=1, keepdims=True))
    return centered * lax.rsqrt(spread + norm_epsilon) * gain + shift

def layer_forward(state, allowed, place, layer_weights):
    gain, shift, qkv_full, qkv_shift, mix_weight, up_weight, up_shift, down_weight, after_bias = layer_weights
    count_rows = state.shape[0]
    normed = low(norm_piece(state, gain, shift))
    projected = low_back(jnp.einsum('td,dpe->tpe', normed, qkv_full, precision=highest) + qkv_shift)
    turned = rotate(projected[:, 0:2].reshape(count_rows, 2, HEADS, HEAD_DIM), place)
    queries = low(turned[:, 0])
    keys_all = low(turned[:, 1])
    values_all = low(projected[:, 2].reshape(count_rows, HEADS, HEAD_DIM))
    scores = low_back(jnp.einsum('qhe,khe->hqk', queries, keys_all, precision=highest) * HEAD_DIM ** (-0.5))
    masked = jnp.where(allowed[None], scores, masked_score)
    chances = low(jax.nn.softmax(masked, axis=-1))
    attended = low(low_back(jnp.einsum('hqk,khe->qhe', chances, values_all, precision=highest).reshape(count_rows, D)))
    hidden_pre = low_back(jnp.dot(normed, up_weight, precision=highest) + up_shift)
    active = low(jax.nn.gelu(hidden_pre, approximate=True))
    branch = low_back(jnp.dot(attended, mix_weight, precision=highest) + jnp.dot(active, down_weight, precision=highest))
    return state + branch + after_bias

def reference(hidden_in, seq_lengths, seq_device, positions, norm_gain, norm_bias, qkv_weight, qkv_bias, out_weight, fc1_weight, fc1_bias, fc2_weight, output_bias, out_cotangent):
    weights_all = tuple((member.astype(jnp.float32) for member in (norm_gain, norm_bias, qkv_weight, qkv_bias, out_weight, fc1_weight, fc1_bias, fc2_weight, output_bias)))
    states = hidden_in.astype(jnp.float32).reshape(N_DP, TOK_DEV, D)
    cotangents = out_cotangent.astype(jnp.float32).reshape(N_DP, TOK_DEV, D)
    places = positions.reshape(N_DP, TOK_DEV)
    owners = jnp.arange(N_DP, dtype=jnp.int32)

    def one_block(totals, member):
        state, cotangent, place, owner = member
        labels = sequence_labels(seq_lengths, seq_device, owner, TOK_DEV)
        allowed = allowed_pairs(labels)
        valid = (labels > 0).astype(jnp.float32)

        def forward(state, weights_all):
            for layer in range(LAYERS):
                state = layer_forward(state, allowed, place, tuple((entry[layer] for entry in weights_all)))
            return state
        result, pullback = jax.vjp(forward, state, weights_all)
        grad_state, grad_weights = pullback(cotangent * valid[:, None])
        totals = tuple((left + right for left, right in zip(totals, grad_weights)))
        return (totals, (result.astype(jnp.bfloat16), grad_state))
    zeros = tuple((jnp.zeros_like(member) for member in weights_all))
    totals, (outputs, grads_in) = lax.scan(one_block, zeros, (states, cotangents, places, owners))
    return (outputs.reshape(TOKENS, D), grads_in.reshape(TOKENS, D), totals[0], totals[1], totals[2], totals[3], totals[4], totals[5], totals[6], totals[7], totals[8])
```

```python
from functools import partial

import jax
import jax.numpy as jnp
from jax import lax
from jax.experimental import pallas as pl
from jax.experimental.pallas import tpu as pltpu
from jax.sharding import PartitionSpec as P

HEAD_DIM = 64
ROT = 32
LAYERS = 2
GROUP = 16

norm_epsilon = 1e-05
masked_score = -1e30
bf16 = jnp.bfloat16
f32 = jnp.float32

contract_last = (((1,), (1,)), ((), ()))
contract_first = (((0,), (0,)), ((), ()))


def dot(a, b, dims=(((1,), (0,)), ((), ()))):
    return lax.dot_general(a, b, dims, preferred_element_type=f32)


def turn(x, cosine, up, down):
    return x * cosine + pltpu.roll(x, x.shape[1] - ROT // 2, 1) * up + pltpu.roll(x, ROT // 2, 1) * down


def stacked_heads(x):
    lane = lax.broadcasted_iota(jnp.int32, x.shape, 1)
    zero = jnp.zeros_like(x)
    return jnp.concatenate(
        [jnp.where(lane < HEAD_DIM, x, zero), jnp.where(lane < HEAD_DIM, zero, x)], axis=0
    )


def merged_heads(x):
    rows = x.shape[0] // 2
    lane = lax.broadcasted_iota(jnp.int32, (rows, x.shape[1]), 1)
    return jnp.where(lane < HEAD_DIM, x[:rows], x[rows:])


def softmax_rows(queries, keys, allowed):
    scores = dot(stacked_heads(queries), keys, contract_last) * HEAD_DIM ** (-0.5)
    masked = jnp.where(jnp.concatenate([allowed, allowed], axis=0) > 0, scores, masked_score)
    weights = jnp.exp(masked - jnp.max(masked, axis=1, keepdims=True))
    return weights / jnp.sum(weights, axis=1, keepdims=True)


def attention_forward(proj_ref, cos_ref, up_ref, down_ref, allowed_ref, kept_ref, out_ref):
    wide = 2 * HEAD_DIM
    tables = (cos_ref[...], up_ref[...], down_ref[...])
    queries = turn(proj_ref[:, :wide], *tables).astype(bf16)
    keys = turn(proj_ref[:, wide : 2 * wide], *tables).astype(bf16)
    values = proj_ref[:, 2 * wide :].astype(bf16)
    kept_ref[:, :wide] = queries
    kept_ref[:, wide : 2 * wide] = keys
    kept_ref[:, 2 * wide :] = values
    chances = softmax_rows(queries, keys, allowed_ref[...]).astype(bf16)
    out_ref[...] = merged_heads(dot(chances, values)).astype(bf16)


def attention_backward(kept_ref, grad_ref, cos_ref, up_ref, down_ref, allowed_ref, out_ref):
    wide = 2 * HEAD_DIM
    queries = kept_ref[:, :wide]
    keys = kept_ref[:, wide : 2 * wide]
    values = kept_ref[:, 2 * wide :]
    chances = softmax_rows(queries, keys, allowed_ref[...])
    grads = stacked_heads(grad_ref[...])
    grad_chances = dot(grads, values, contract_last)
    grad_values = dot(chances.astype(bf16), grads, contract_first)
    centre = jnp.sum(grad_chances * chances, axis=1, keepdims=True)
    grad_scores = (chances * (grad_chances - centre)).astype(bf16)
    scale = HEAD_DIM ** (-0.5)
    grad_queries = merged_heads(dot(grad_scores, keys)) * scale
    grad_keys = dot(grad_scores, stacked_heads(queries), contract_first) * scale
    tables = (cos_ref[...], -up_ref[...], -down_ref[...])
    out_ref[:, :wide] = turn(grad_queries, *tables).astype(bf16)
    out_ref[:, wide : 2 * wide] = turn(grad_keys, *tables).astype(bf16)
    out_ref[:, 2 * wide :] = grad_values.astype(bf16)


def row_blocks(rows, width):
    return pl.BlockSpec((rows, width), lambda i: (i, 0))


def call_forward(proj, tables, allowed, block):
    wide = 2 * HEAD_DIM
    rows = proj.shape[0]
    return pl.pallas_call(
        attention_forward,
        grid=(rows // block,),
        in_specs=[row_blocks(block, 3 * wide)] + [row_blocks(block, wide)] * 3 + [row_blocks(block, block)],
        out_specs=[row_blocks(block, 3 * wide), row_blocks(block, wide)],
        out_shape=[
            jax.ShapeDtypeStruct((rows, 3 * wide), bf16),
            jax.ShapeDtypeStruct((rows, wide), bf16),
        ],
        cost_estimate=pl.CostEstimate(flops=rows * block * wide * 8, bytes_accessed=rows * 6000, transcendentals=rows * block * 2),
        name="attention_forward",
    )(proj, *tables, allowed)


def call_backward(kept, grad, tables, allowed, block):
    wide = 2 * HEAD_DIM
    rows = kept.shape[0]
    return pl.pallas_call(
        attention_backward,
        grid=(rows // block,),
        in_specs=[row_blocks(block, 3 * wide), row_blocks(block, wide)]
        + [row_blocks(block, wide)] * 3
        + [row_blocks(block, block)],
        out_specs=row_blocks(block, 3 * wide),
        out_shape=jax.ShapeDtypeStruct((rows, 3 * wide), bf16),
        cost_estimate=pl.CostEstimate(flops=rows * block * wide * 20, bytes_accessed=rows * 6000, transcendentals=rows * block * 2),
        name="attention_backward",
    )(kept, grad, *tables, allowed)


def sequence_labels(seq_lengths, seq_device, owner, count_rows):
    index = jnp.arange(seq_lengths.shape[0], dtype=jnp.int32)
    owned = jnp.where(seq_device == owner, seq_lengths, 0)
    earlier = index[None, :] < index[:, None]
    starts = jnp.sum(jnp.where(earlier, owned[None, :], 0), axis=1)
    places = jnp.arange(count_rows, dtype=jnp.int32)
    inside = (places[:, None] >= starts[None, :]) & (places[:, None] < (starts + owned)[None, :])
    return jnp.sum(jnp.where(inside, index[None, :] + 1, 0), axis=1)


def gelu_parts(v):
    c = (2.0 / jnp.pi) ** 0.5
    inner = jnp.tanh(c * (v + 0.044715 * v * v * v))
    value = 0.5 * v * (1.0 + inner)
    slope = 0.5 * (1.0 + inner) + 0.5 * v * (1.0 - inner * inner) * c * (1.0 + 3.0 * 0.044715 * v * v)
    return value, slope


def per_device(
    n_dp,
    hidden_in,
    seq_lengths,
    seq_device,
    positions,
    norm_gain,
    norm_bias,
    qkv_weight,
    qkv_bias,
    out_weight,
    fc1_weight,
    fc1_bias,
    fc2_weight,
    output_bias,
    out_cotangent,
):
    block = hidden_in.shape[0]
    half = block // 2
    width = hidden_in.shape[1]
    piece = norm_gain.shape[1]
    hidden = fc1_weight.shape[2] // GROUP
    groups = n_dp // GROUP
    chips = GROUP // 2
    side = chips // 2 - 1

    if groups == 1:
        ring = [2 * a for a in range(chips // 2)] + [2 * a + 1 for a in reversed(range(chips // 2))]
    else:
        ring = list(range(chips // 2)) + list(reversed(range(chips // 2, chips)))
    ring_pairs = []
    for g in range(groups):
        for place in range(chips):
            for core, step in ((0, 1), (1, -1)):
                ring_pairs.append(
                    (
                        g * GROUP + ring[place] * 2 + core,
                        g * GROUP + ring[(place + step) % chips] * 2 + core,
                    )
                )
    core_pairs = [(i, i ^ 1) for i in range(n_dp)]
    inner = [[g * GROUP + i for i in range(GROUP)] for g in range(groups)]
    outer = [[g * GROUP + i for g in range(groups)] for i in range(GROUP)]
    if groups == 1:
        inner = None

    def along(x):
        return lax.ppermute(x, "dp", ring_pairs)

    def across(x):
        return lax.ppermute(x, "dp", core_pairs)

    def over(x):
        return lax.ppermute(x, "tensor", [(0, 1), (1, 0)])

    index = lax.axis_index("dp")
    group = index // GROUP
    chip = (index % GROUP) // 2
    core = index % 2
    tensor = lax.axis_index("tensor")
    is_first = core == 0
    at = core * half
    off = (1 - core) * half

    def my_half(x, start, axis=0):
        return lax.dynamic_slice_in_dim(x, start, half, axis)

    def in_order(own, other):
        return jnp.where(
            is_first, jnp.concatenate([own, other], 0), jnp.concatenate([other, own], 0)
        )

    def gather_rows(x):
        mine = in_order(x, across(x))
        behind, ahead = [], []
        moving = mine
        for _ in range(side):
            moving = along(moving)
            behind.append(moving)
            ahead.append(across(moving))
        moving = along(my_half(moving, at))
        far = in_order(moving, across(moving))
        return jnp.concatenate([mine] + behind + ahead + [far], axis=0)

    def scatter_rows(partial):
        slots = partial.reshape(chips, block, width)
        give = jnp.concatenate(
            [slots[1 : 1 + side].reshape(side * block, width), my_half(slots[chips - 1], off), my_half(slots[0], off)], 0
        ).astype(bf16)
        took = across(give).astype(f32)
        ahead = slots[1 + side : 1 + 2 * side].astype(f32) + took[: side * block].reshape(side, block, width)
        far = my_half(slots[chips - 1], at).astype(f32) + took[side * block : side * block + half]
        own = my_half(slots[0], at).astype(f32) + took[side * block + half :]
        moving = along(far.astype(bf16)).astype(f32)
        rows = lax.broadcasted_iota(jnp.int32, (block, 1), 0)
        mine_rows = (rows < half) == is_first
        moving = jnp.where(mine_rows, jnp.concatenate([moving, moving], 0), 0.0)
        for step in reversed(range(side)):
            moving = along((moving + ahead[step]).astype(bf16)).astype(f32)
        return own + my_half(moving, at) + across(my_half(moving, off).astype(bf16)).astype(f32)

    def spread(x):
        return lax.all_to_all(x, "dp", 0, 0, axis_index_groups=inner, tiled=True)

    def whole(x):
        if groups > 1:
            x = lax.all_gather(x, "dp", axis=0, axis_index_groups=outer, tiled=True)
        return x.transpose(1, 0, 2).reshape(x.shape[1], width)

    gathered_up, gathered_down = [], []
    for layer in range(LAYERS):
        up = jnp.concatenate(
            [
                qkv_weight[layer].reshape(piece, 3, GROUP, HEAD_DIM).transpose(2, 1, 3, 0).reshape(GROUP, 3 * HEAD_DIM, piece),
                fc1_weight[layer].reshape(piece, GROUP, hidden).transpose(1, 2, 0),
            ],
            axis=1,
        )
        down = jnp.concatenate(
            [
                out_weight[layer].reshape(GROUP, HEAD_DIM, piece),
                fc2_weight[layer].reshape(GROUP, hidden, piece),
            ],
            axis=1,
        )
        up = spread(up)
        up_other = over(up)
        down = spread(down)
        down_other = over(down)
        up, up_other, down, down_other = (whole(x) for x in (up, up_other, down, down_other))
        parts = []
        for p in range(3):
            parts += [up[p * HEAD_DIM : (p + 1) * HEAD_DIM], up_other[p * HEAD_DIM : (p + 1) * HEAD_DIM]]
        gathered_up.append(
            (
                jnp.concatenate(parts, 0),
                jnp.concatenate([up[3 * HEAD_DIM :], up_other[3 * HEAD_DIM :]], 0),
            )
        )
        gathered_down.append(
            (
                jnp.concatenate([down[:HEAD_DIM], down_other[:HEAD_DIM]], 0),
                jnp.concatenate([down[HEAD_DIM:], down_other[HEAD_DIM:]], 0),
            )
        )
    if groups == 1:
        biases = jnp.concatenate([qkv_bias.reshape(LAYERS, 3 * HEAD_DIM), fc1_bias], axis=1)
    else:
        full_qkv = lax.all_gather(qkv_bias, "dp", axis=2, tiled=True)
        full_up = lax.all_gather(fc1_bias, "dp", axis=1, tiled=True)
        member = index % GROUP
        biases = jnp.concatenate(
            [
                lax.dynamic_slice_in_dim(full_qkv, member * HEAD_DIM, HEAD_DIM, 2).reshape(LAYERS, 3 * HEAD_DIM),
                lax.dynamic_slice_in_dim(full_up, member * hidden, hidden, 1),
            ],
            axis=1,
        )
    biases_other = over(biases)
    small = jnp.concatenate(
        [
            norm_gain.reshape(-1),
            norm_bias.reshape(-1),
            output_bias.reshape(-1),
            (positions // 64).astype(bf16),
            (positions % 64).astype(bf16),
        ]
    )
    small = lax.all_gather(small, "dp", axis=0, tiled=False)
    vectors = small[:, : 6 * piece].reshape(n_dp, 3, LAYERS, piece).transpose(1, 2, 0, 3).reshape(3, LAYERS, width).astype(f32)
    gains, shifts, after = vectors[0], vectors[1], vectors[2]

    turned = jnp.where(is_first, 1, -1)
    place = jnp.sum(jnp.where(jnp.asarray(ring) == chip, jnp.arange(chips), 0))
    offsets = [0] + [-(s + 1) for s in range(side)] + [s + 1 for s in range(side)] + [chips // 2]
    places = (place + turned * jnp.asarray(offsets)) % chips
    chip_ids = jnp.sum(
        jnp.where(places[:, None] == jnp.arange(chips)[None, :], jnp.asarray(ring)[None, :], 0), axis=1
    )
    owners = group * GROUP + 2 * chip_ids + tensor
    labels = jax.vmap(lambda owner: sequence_labels(seq_lengths, seq_device, owner, block))(owners)
    rows_at = jnp.arange(block, dtype=jnp.int32)
    allowed = (
        (labels[:, :, None] == labels[:, None, :])
        & (labels[:, :, None] > 0)
        & (rows_at[None, None, :] <= rows_at[None, :, None])
    ) | (rows_at[None, None, :] == rows_at[None, :, None])
    allowed = allowed.astype(f32).reshape(chips * block, block)
    valid = my_half((labels[0] > 0).astype(f32)[:, None], at)
    picked = (owners[:, None] == jnp.arange(n_dp)[None, :]).astype(f32)
    place_parts = jnp.dot(picked, small[:, 6 * piece :].astype(f32), precision=lax.Precision.HIGHEST)
    row_places = (place_parts[:, :block] * 64.0 + place_parts[:, block:]).reshape(chips * block)
    pair = ROT // 2
    frequency = 10000.0 ** (-2.0 * jnp.arange(pair, dtype=f32) / ROT)
    angles = row_places[:, None] * frequency[None, :]
    cosine, sine = jnp.cos(angles), jnp.sin(angles)
    nought = jnp.zeros_like(sine)
    rest = jnp.zeros((chips * block, HEAD_DIM - ROT), f32)
    tables = (
        jnp.concatenate([cosine, cosine, rest + 1.0] * 2, axis=1),
        jnp.concatenate([-sine, nought, rest] * 2, axis=1),
        jnp.concatenate([nought, sine, rest] * 2, axis=1),
    )

    both = jnp.stack([hidden_in, out_cotangent])
    start = jnp.where(tensor == core, my_half(both, at, 1), across(my_half(both, off, 1)))
    state = start[0].astype(f32)
    kept = []
    for layer in range(LAYERS):
        weight_qkv, weight_up = gathered_up[layer]
        weight_out, weight_down = gathered_down[layer]
        mean = jnp.mean(state, axis=1, keepdims=True)
        centred = state - mean
        spread_rows = jnp.mean(centred * centred, axis=1, keepdims=True)
        inverse = lax.rsqrt(spread_rows + norm_epsilon)
        xhat = centred * inverse
        normed = gather_rows((xhat * gains[layer] + shifts[layer]).astype(bf16))
        bias_qkv = jnp.stack(
            [
                biases[layer, : 3 * HEAD_DIM].reshape(3, HEAD_DIM),
                biases_other[layer, : 3 * HEAD_DIM].reshape(3, HEAD_DIM),
            ],
            axis=1,
        ).reshape(6 * HEAD_DIM)
        bias_up = jnp.concatenate([biases[layer, 3 * HEAD_DIM :], biases_other[layer, 3 * HEAD_DIM :]])
        projected = dot(normed, weight_qkv, contract_last) + bias_qkv.astype(f32)
        heads, attended = call_forward(projected, tables, allowed, block)
        hidden_pre = dot(normed, weight_up, contract_last) + bias_up.astype(f32)
        active = gelu_parts(hidden_pre)[0].astype(bf16)
        branch = scatter_rows((dot(attended, weight_out) + dot(active, weight_down)).astype(bf16))
        kept.append((xhat, inverse, normed, heads, attended, hidden_pre, active))
        state = state + branch + after[layer]

    def handed_back(own_rows):
        filled = in_order(own_rows, across(own_rows))
        return jnp.where(tensor == core, filled, over(filled))

    hidden_out = handed_back(state.astype(bf16))

    grad_state = start[1].astype(f32) * valid
    vector_grads = [None] * LAYERS
    weight_grads = [None] * LAYERS
    bias_grads = [None] * LAYERS

    def summed(own, other):
        total = own + over(other.astype(bf16)).astype(f32)
        if groups > 1:
            total = lax.psum_scatter(total, "dp", scatter_dimension=1, axis_index_groups=outer, tiled=True)
        total = total.astype(bf16).reshape(total.shape[0], GROUP, piece).transpose(1, 0, 2)
        return spread(total)

    for layer in reversed(range(LAYERS)):
        xhat, inverse, normed, heads, attended, hidden_pre, active = kept[layer]
        weight_qkv, weight_up = gathered_up[layer]
        weight_out, weight_down = gathered_down[layer]
        grad_branch = gather_rows(grad_state.astype(bf16))
        grad_after = jnp.sum(grad_state, axis=0)
        grad_attended = dot(grad_branch, weight_out, contract_last).astype(bf16)
        grad_pre = (dot(grad_branch, weight_down, contract_last) * gelu_parts(hidden_pre)[1]).astype(bf16)
        grad_proj = call_backward(heads, grad_attended, tables, allowed, block)
        grad_normed = scatter_rows((dot(grad_proj, weight_qkv) + dot(grad_pre, weight_up)).astype(bf16))
        grad_out = dot(attended, grad_branch, contract_first)
        grad_down = dot(active, grad_branch, contract_first)
        grad_qkv = dot(grad_proj, normed, contract_first).reshape(3, 2, HEAD_DIM, width)
        grad_up = dot(grad_pre, normed, contract_first)
        down = summed(
            jnp.concatenate([grad_out[:HEAD_DIM], grad_down[:hidden]], 0),
            jnp.concatenate([grad_out[HEAD_DIM:], grad_down[hidden:]], 0),
        )
        up = summed(
            jnp.concatenate([grad_qkv[:, 0].reshape(3 * HEAD_DIM, width), grad_up[:hidden]], 0),
            jnp.concatenate([grad_qkv[:, 1].reshape(3 * HEAD_DIM, width), grad_up[hidden:]], 0),
        )
        up, down = up.astype(f32), down.astype(f32)
        weight_grads[layer] = (
            up[:, : 3 * HEAD_DIM].reshape(GROUP, 3, HEAD_DIM, piece).transpose(3, 1, 0, 2).reshape(piece, 3, GROUP * HEAD_DIM),
            down[:, :HEAD_DIM].reshape(GROUP * HEAD_DIM, piece),
            up[:, 3 * HEAD_DIM :].transpose(2, 0, 1).reshape(piece, GROUP * hidden),
            down[:, HEAD_DIM:].reshape(GROUP * hidden, piece),
        )
        sums_qkv = jnp.sum(grad_proj, axis=0, dtype=f32).reshape(3, 2, HEAD_DIM)
        sums_up = jnp.sum(grad_pre, axis=0, dtype=f32)
        bias_grads[layer] = (
            jnp.concatenate([sums_qkv[:, 0].reshape(-1), sums_up[:hidden]]),
            jnp.concatenate([sums_qkv[:, 1].reshape(-1), sums_up[hidden:]]),
        )
        vector_grads[layer] = jnp.stack(
            [jnp.sum(grad_normed * xhat, axis=0), jnp.sum(grad_normed, axis=0), grad_after]
        )
        scaled = grad_normed * gains[layer]
        grad_state = grad_state + (
            scaled
            - jnp.mean(scaled, axis=1, keepdims=True)
            - xhat * jnp.mean(scaled * xhat, axis=1, keepdims=True)
        ) * inverse

    grad_hidden = handed_back(grad_state.astype(bf16)).astype(f32)
    vectors = jnp.stack(vector_grads).reshape(LAYERS * 3, n_dp, piece).transpose(1, 0, 2)
    vectors = jnp.sum(lax.all_to_all(vectors, "dp", 0, 0, tiled=True), axis=0)
    vectors = (vectors + over(vectors)).reshape(LAYERS, 3, piece)
    bias_own = jnp.stack([bias_grads[layer][0] for layer in range(LAYERS)])
    bias_other = jnp.stack([bias_grads[layer][1] for layer in range(LAYERS)])
    bias_sums = bias_own + over(bias_other)
    bias_qkv, bias_up = bias_sums[:, : 3 * HEAD_DIM].reshape(LAYERS, 3, HEAD_DIM), bias_sums[:, 3 * HEAD_DIM :]
    if groups > 1:
        bias_qkv = lax.all_gather(lax.psum(bias_qkv, "dp", axis_index_groups=outer), "dp", axis=2, axis_index_groups=inner, tiled=True)
        bias_up = lax.all_gather(lax.psum(bias_up, "dp", axis_index_groups=outer), "dp", axis=1, axis_index_groups=inner, tiled=True)
        bias_qkv = lax.dynamic_slice_in_dim(bias_qkv, index * qkv_bias.shape[2], qkv_bias.shape[2], 2)
        bias_up = lax.dynamic_slice_in_dim(bias_up, index * fc1_bias.shape[1], fc1_bias.shape[1], 1)
    stacked = [jnp.stack([weight_grads[layer][i] for layer in range(LAYERS)]) for i in range(4)]
    return (
        hidden_out,
        grad_hidden,
        vectors[:, 0],
        vectors[:, 1],
        stacked[0],
        bias_qkv,
        stacked[1],
        stacked[2],
        bias_up,
        stacked[3],
        vectors[:, 2],
    )


def solution(mesh):
    placed = (
        P("dp", None),
        P(),
        P(),
        P("dp"),
        P(None, "dp"),
        P(None, "dp"),
        P(None, "dp", None, "tensor"),
        P(None, None, ("tensor", "dp")),
        P(None, "tensor", "dp"),
        P(None, "dp", "tensor"),
        P(None, ("tensor", "dp")),
        P(None, "tensor", "dp"),
        P(None, "dp"),
        P("dp", None),
    )
    return jax.shard_map(
        partial(per_device, mesh.shape["dp"]),
        mesh=mesh,
        in_specs=placed,
        out_specs=(
            P("dp", None),
            P("dp", None),
            P(None, "dp"),
            P(None, "dp"),
            P(None, "dp", None, "tensor"),
            P(None, None, ("tensor", "dp")),
            P(None, "tensor", "dp"),
            P(None, "dp", "tensor"),
            P(None, ("tensor", "dp")),
            P(None, "tensor", "dp"),
            P(None, "dp"),
        ),
        check_vma=False,
    )
```

```python
from functools import partial

import jax
import jax.numpy as jnp
from jax import lax
from jax.experimental import pallas as pl
from jax.experimental.pallas import tpu as pltpu
from jax.sharding import PartitionSpec as P

HEAD_DIM = 64
ROT = 32
LAYERS = 2
GROUP = 16

norm_epsilon = 1e-05
masked_score = -1e30
bf16 = jnp.bfloat16
f32 = jnp.float32

contract_last = (((1,), (1,)), ((), ()))
contract_first = (((0,), (0,)), ((), ()))


def dot(a, b, dims=(((1,), (0,)), ((), ()))):
    return lax.dot_general(a, b, dims, preferred_element_type=f32)


def turn(x, cosine, up, down):
    return x * cosine + pltpu.roll(x, x.shape[1] - ROT // 2, 1) * up + pltpu.roll(x, ROT // 2, 1) * down


def stacked_heads(x):
    lane = lax.broadcasted_iota(jnp.int32, x.shape, 1)
    zero = jnp.zeros_like(x)
    return jnp.concatenate(
        [jnp.where(lane < HEAD_DIM, x, zero), jnp.where(lane < HEAD_DIM, zero, x)], axis=0
    )


def merged_heads(x):
    rows = x.shape[0] // 2
    lane = lax.broadcasted_iota(jnp.int32, (rows, x.shape[1]), 1)
    return jnp.where(lane < HEAD_DIM, x[:rows], x[rows:])


def softmax_rows(queries, keys, allowed):
    scores = dot(stacked_heads(queries), keys, contract_last) * HEAD_DIM ** (-0.5)
    masked = jnp.where(jnp.concatenate([allowed, allowed], axis=0) > 0, scores, masked_score)
    weights = jnp.exp(masked - jnp.max(masked, axis=1, keepdims=True))
    return weights / jnp.sum(weights, axis=1, keepdims=True)


def sequence_labels(seq_lengths, seq_device, owner, count_rows):
    index = jnp.arange(seq_lengths.shape[0], dtype=jnp.int32)
    owned = jnp.where(seq_device == owner, seq_lengths, 0)
    earlier = index[None, :] < index[:, None]
    starts = jnp.sum(jnp.where(earlier, owned[None, :], 0), axis=1)
    places = jnp.arange(count_rows, dtype=jnp.int32)
    inside = (places[:, None] >= starts[None, :]) & (places[:, None] < (starts + owned)[None, :])
    return jnp.sum(jnp.where(inside, index[None, :] + 1, 0), axis=1)


def gelu_parts(v):
    c = (2.0 / jnp.pi) ** 0.5
    inner = jnp.tanh(c * (v + 0.044715 * v * v * v))
    value = 0.5 * v * (1.0 + inner)
    slope = 0.5 * (1.0 + inner) + 0.5 * v * (1.0 - inner * inner) * c * (1.0 + 3.0 * 0.044715 * v * v)
    return value, slope


VMEM_SPEC = pl.BlockSpec(memory_space=pltpu.VMEM)
ANY_SPEC = pl.BlockSpec(memory_space=pl.ANY)
SMEM_SPEC = pl.BlockSpec(memory_space=pltpu.SMEM)
WIDE = 2 * HEAD_DIM


def left_lanes(x):
    return lax.broadcasted_iota(jnp.int32, x.shape, 1) < HEAD_DIM


def swapped(x):
    return pltpu.roll(x, HEAD_DIM, 1)


def zipped(a, b):
    left = left_lanes(a)
    return jnp.where(left, a, swapped(b)).astype(bf16), jnp.where(left, swapped(a), b).astype(bf16)


def pack_up(qkv_ref, fc1_ref, *rest):
    out_ref = rest[-1]
    q, k, v = (qkv_ref[0, p].astype(f32) for p in range(3))
    out_ref[0, :WIDE], out_ref[1, :WIDE] = zipped(q, k)
    rows = q.shape[0] // 2
    out_ref[0, WIDE : WIDE + rows], out_ref[1, WIDE : WIDE + rows] = zipped(v[:rows], v[rows:])
    base = WIDE + rows
    for d in range(2):
        for h in range(2):
            out_ref[d, base + h * 128 : base + (h + 1) * 128] = fc1_ref[0, :, (2 * d + h) * 128 : (2 * d + h + 1) * 128]
        if len(rest) > 1:
            out_ref[d, base + 256 :] = rest[0][...]


def call_pack_up(qkv, fc1, layer, small):
    rows = 3 * HEAD_DIM + 256 + (0 if small is None else small.shape[0])
    specs = [
        pl.BlockSpec((1, 3, 128, 128), lambda i: (layer, 0, 0, i)),
        pl.BlockSpec((1, 128, 512), lambda i: (layer, 0, i)),
    ]
    if small is not None:
        specs.append(pl.BlockSpec(small.shape, lambda i: (0, 0)))
    return pl.pallas_call(
        pack_up,
        grid=(GROUP // 2,),
        in_specs=specs,
        out_specs=pl.BlockSpec((2, rows, 128), lambda i: (i, 0, 0)),
        out_shape=jax.ShapeDtypeStruct((GROUP, rows, 128), bf16),
        name="pack_up",
    )(*([qkv, fc1] + ([] if small is None else [small])))


def pack_down(out_w_ref, fc2_ref, out_ref):
    for d in range(2):
        out_ref[d, :HEAD_DIM] = out_w_ref[0, d * HEAD_DIM : (d + 1) * HEAD_DIM]
        out_ref[d, HEAD_DIM:] = fc2_ref[0, d * 256 : (d + 1) * 256]


def call_pack_down(out_w, fc2, layer):
    return pl.pallas_call(
        pack_down,
        grid=(GROUP // 2,),
        in_specs=[
            pl.BlockSpec((1, 128, 128), lambda i: (layer, i, 0)),
            pl.BlockSpec((1, 512, 128), lambda i: (layer, i, 0)),
        ],
        out_specs=pl.BlockSpec((2, HEAD_DIM + 256, 128), lambda i: (i, 0, 0)),
        out_shape=jax.ShapeDtypeStruct((GROUP, HEAD_DIM + 256, 128), bf16),
        name="pack_down",
    )(out_w, fc2)


def join_up(own_ref, other_ref, out_ref):
    for e in range(2):
        rows = slice(e * 128, (e + 1) * 128)
        a, b = own_ref[e, :WIDE].astype(f32), other_ref[e, :WIDE].astype(f32)
        out_ref[rows, :WIDE], out_ref[rows, WIDE : 2 * WIDE] = zipped(a, b)
        a, b = own_ref[e, WIDE : WIDE + 64].astype(f32), other_ref[e, WIDE : WIDE + 64].astype(f32)
        top, bottom = zipped(a, b)
        out_ref[e * 128 : e * 128 + 64, 2 * WIDE : 3 * WIDE] = top
        out_ref[e * 128 + 64 : (e + 1) * 128, 2 * WIDE : 3 * WIDE] = bottom
        for n, ref in enumerate((own_ref, other_ref)):
            for h in range(2):
                lanes = 3 * WIDE + n * 256 + h * 128
                out_ref[rows, lanes : lanes + 128] = ref[e, WIDE + 64 + h * 128 : WIDE + 64 + (h + 1) * 128]


def call_join_up(own, other):
    rows = own.shape[1]
    return pl.pallas_call(
        join_up,
        grid=(GROUP // 2,),
        in_specs=[pl.BlockSpec((2, rows, 128), lambda i: (i, 0, 0))] * 2,
        out_specs=pl.BlockSpec((256, 3 * WIDE + 512), lambda i: (i, 0)),
        out_shape=jax.ShapeDtypeStruct((GROUP * 128, 3 * WIDE + 512), bf16),
        name="join_up",
    )(own, other)


def join_down(own_ref, other_ref, out_ref):
    for e in range(2):
        lanes = slice(e * 128, (e + 1) * 128)
        for n, ref in enumerate((own_ref, other_ref)):
            out_ref[n * HEAD_DIM : (n + 1) * HEAD_DIM, lanes] = ref[e, :HEAD_DIM]
            out_ref[WIDE + n * 256 : WIDE + (n + 1) * 256, lanes] = ref[e, HEAD_DIM:]


def call_join_down(own, other):
    rows = own.shape[1]
    return pl.pallas_call(
        join_down,
        grid=(GROUP // 2,),
        in_specs=[pl.BlockSpec((2, rows, 128), lambda i: (i, 0, 0))] * 2,
        out_specs=pl.BlockSpec((2 * rows, 256), lambda i: (0, i)),
        out_shape=jax.ShapeDtypeStruct((2 * rows, GROUP * 128), bf16),
        name="join_down",
    )(own, other)


def slot_copies(refs, which, target, core):
    block = target.shape[0] // 8
    half = block // 2
    pairs = []
    for slot in range(7):
        ref = refs[slot] if which is None else refs[slot].at[which]
        pairs.append((ref, target.at[pl.ds(slot * block, block)]))
    for n, at in ((7, core * half), (8, (1 - core) * half)):
        ref = refs[n] if which is None else refs[n].at[which]
        pairs.append((ref, target.at[pl.ds(pl.multiple_of(7 * block + at, half), half)]))
    return pairs


def split_copies(part, far_ref, give_ref, keep_ref, core):
    block = part.shape[0] // 8
    half = block // 2
    at, off = core * half, (1 - core) * half

    def rows(slot, start):
        return part.at[pl.ds(pl.multiple_of(slot * block + start, half), half)]

    return [
        (rows(7, off), far_ref),
        (part.at[pl.ds(block, 3 * block)], give_ref.at[pl.ds(0, 3 * block)]),
        (rows(0, off), give_ref.at[pl.ds(3 * block, half)]),
        (part.at[pl.ds(4 * block, 3 * block)], keep_ref.at[pl.ds(0, 3 * block)]),
        (rows(7, at), keep_ref.at[pl.ds(3 * block, half)]),
        (rows(0, at), keep_ref.at[pl.ds(3 * block + half, half)]),
    ]


def run_copies(pairs, sems, first):
    made = [pltpu.make_async_copy(a, b, sems.at[first + n]) for n, (a, b) in enumerate(pairs)]
    for copy in made:
        copy.start()
    return made


def heads_forward(chances, values):
    return merged_heads(dot(chances.astype(bf16), values)).astype(bf16)


def heads_backward(chances, queries, keys, values, grad, tables):
    grads = stacked_heads(grad)
    grad_chances = dot(grads, values, contract_last)
    grad_values = dot(chances.astype(bf16), grads, contract_first)
    centre = jnp.sum(grad_chances * chances, axis=1, keepdims=True)
    grad_scores = (chances * (grad_chances - centre)).astype(bf16)
    scale = HEAD_DIM ** (-0.5)
    grad_queries = merged_heads(dot(grad_scores, keys)) * scale
    grad_keys = dot(grad_scores, stacked_heads(queries), contract_first) * scale
    cosine, up, down = tables
    back = (cosine, -up, -down)
    return turn(grad_queries, *back).astype(bf16), turn(grad_keys, *back).astype(bf16), grad_values.astype(bf16)


def layer_pass(mode, *refs):
    refs = list(refs)

    def take(n):
        out = refs[:n]
        del refs[:n]
        return out

    forward, backward = mode != "last", mode != "first"
    core_ref, up_ref, down_ref, cos_ref, sin_up_ref, sin_down_ref, allowed_ref = take(7)
    core = core_ref[0]
    if mode == "first":
        bias_ref, gain_ref, shift_ref = take(3)
        rows_in = take(9)
    elif mode == "middle":
        (bias_ref,) = take(1)
        rows_in = take(9)
        grads_in = take(9)
    else:
        heads_ref, hidden_ref = take(2)
        grads_in = take(9)
    if mode == "first":
        normed_ref, heads_ref, hidden_ref, wide_ref = take(4)
        outs = take(3)
        raw, part, sems = take(3)
    elif mode == "middle":
        normed_ref, grad_rows_ref, wide_ref, slim_ref = take(4)
        outs = take(3)
        grad_outs = take(3)
        part, grad_part, sems = take(3)
    else:
        grad_rows_ref, slim_ref = take(2)
        grad_outs = take(3)
        grad_part, sems = take(2)

    pairs = []
    if mode == "first":
        pairs += slot_copies(rows_in, 0, raw, core)
    if mode == "middle":
        pairs += slot_copies(rows_in, None, normed_ref, core)
        pairs += slot_copies(grads_in, 1, grad_rows_ref, core)
    if mode == "last":
        pairs += slot_copies(grads_in, None, grad_rows_ref, core)
    for copy in run_copies(pairs, sems, 0):
        copy.wait()

    total = allowed_ref.shape[0]
    block = allowed_ref.shape[1]
    step = 2 * block

    if mode == "first":
        tile = 32

        def norm_tile(i, carry):
            at = pl.ds(pl.multiple_of(i * tile, tile), tile)
            x = raw[at, :].astype(f32)
            centred = x - jnp.mean(x, axis=1, keepdims=True)
            inverse = lax.rsqrt(jnp.mean(centred * centred, axis=1, keepdims=True) + norm_epsilon)
            normed_ref[at, :] = (centred * inverse * gain_ref[...] + shift_ref[...]).astype(bf16)
            return carry

        lax.fori_loop(0, total // tile, norm_tile, 0)

    def one(p, carry):
        at = pl.ds(pl.multiple_of(p * step, step), step)
        if forward:
            before = dot(normed_ref[at, :], up_ref[...]) + bias_ref[...]
            hidden_pre = before[:, 3 * WIDE :]
        else:
            hidden_pre = hidden_ref[at, :]
        value, slope = gelu_parts(hidden_pre)
        if backward:
            grad_wide = dot(grad_rows_ref[at, :], down_ref[...], contract_last)
            slim_ref[at, 3 * WIDE :] = (grad_wide[:, WIDE:] * slope).astype(bf16)
        if forward:
            wide_ref[at, WIDE:] = value.astype(bf16)
        if mode == "first":
            hidden_ref[at, :] = hidden_pre
        for b in range(2):
            mine = slice(b * block, (b + 1) * block)
            own = pl.ds(pl.multiple_of(p * step + b * block, block), block)
            tables = (cos_ref[own, :], sin_up_ref[own, :], sin_down_ref[own, :])
            if forward:
                queries = turn(before[mine, :WIDE], *tables).astype(bf16)
                keys = turn(before[mine, WIDE : 2 * WIDE], *tables).astype(bf16)
                values = before[mine, 2 * WIDE : 3 * WIDE].astype(bf16)
            else:
                queries = heads_ref[own, :WIDE]
                keys = heads_ref[own, WIDE : 2 * WIDE]
                values = heads_ref[own, 2 * WIDE :]
            if mode == "first":
                heads_ref[own, :WIDE] = queries
                heads_ref[own, WIDE : 2 * WIDE] = keys
                heads_ref[own, 2 * WIDE :] = values
            chances = softmax_rows(queries, keys, allowed_ref[own, :])
            if forward:
                wide_ref[own, :WIDE] = heads_forward(chances, values)
            if backward:
                grads = heads_backward(
                    chances, queries, keys, values, grad_wide[mine, :WIDE].astype(bf16), tables
                )
                for n in range(3):
                    slim_ref[own, n * WIDE : (n + 1) * WIDE] = grads[n]
        if forward:
            part[at, :] = dot(wide_ref[at, :], down_ref[...]).astype(bf16)
        if backward:
            grad_part[at, :] = dot(slim_ref[at, :], up_ref[...], contract_last).astype(bf16)
        return carry

    lax.fori_loop(0, total // step, one, 0)
    pairs = []
    if backward:
        pairs += split_copies(grad_part, *grad_outs, core)
    if forward:
        pairs += split_copies(part, *outs, core)
    for copy in run_copies(pairs, sems, 0):
        copy.wait()


def call_pass(mode, core, weights, tables, allowed, extra, chunks):
    total, block = allowed.shape
    half = block // 2
    width = weights[0].shape[0]
    slim = weights[0].shape[1]
    wide = weights[1].shape[0]
    parts = [
        jax.ShapeDtypeStruct((half, width), bf16),
        jax.ShapeDtypeStruct((3 * block + half, width), bf16),
        jax.ShapeDtypeStruct((4 * block, width), bf16),
    ]
    full = jax.ShapeDtypeStruct((total, width), bf16)
    slim_rows = jax.ShapeDtypeStruct((total, slim), bf16)
    wide_rows = jax.ShapeDtypeStruct((total, wide), bf16)
    if mode == "first":
        kept = [
            full,
            jax.ShapeDtypeStruct((total, 3 * WIDE), bf16),
            jax.ShapeDtypeStruct((total, slim - 3 * WIDE), f32),
            wide_rows,
        ]
        buffers = 2
    elif mode == "middle":
        kept = [full, full, wide_rows, slim_rows]
        parts = parts * 2
        buffers = 2
    else:
        kept = [full, slim_rows]
        buffers = 1
    passes = 2 if mode == "middle" else 1
    return pl.pallas_call(
        partial(layer_pass, mode),
        in_specs=[SMEM_SPEC] + [VMEM_SPEC] * (6 + len(extra)) + [ANY_SPEC] * len(chunks),
        out_specs=[VMEM_SPEC] * len(kept) + [ANY_SPEC] * len(parts),
        out_shape=kept + parts,
        scratch_shapes=[pltpu.VMEM((total, width), bf16)] * buffers + [pltpu.SemaphoreType.DMA((18,))],
        cost_estimate=pl.CostEstimate(
            flops=2 * total * width * (slim + wide) * passes,
            bytes_accessed=20_000_000 * passes,
            transcendentals=total * slim,
        ),
        name="pass_" + mode,
    )(core, *weights, *tables, allowed, *extra, *chunks)


def gradient_slabs(own_rows, other_rows, with_sums, left_ref, right_ref, own_ref, other_ref, *rest):
    turned_ref = rest[-1]

    @pl.when(pl.program_id(0) == 0)
    def _():
        width = left_ref.shape[1]
        for n in range(width // 128):
            lanes = slice(n * 128, (n + 1) * 128)
            left = left_ref[:, lanes].astype(f32)
            if with_sums:
                rest[0][:, lanes] = jnp.sum(left, axis=0, keepdims=True)
            turned_ref[lanes, :] = left.T.astype(bf16)

    product = dot(turned_ref[...], right_ref[...]).astype(bf16)
    for ref, pieces in ((own_ref, own_rows), (other_ref, other_rows)):
        place = 0
        for first, last in pieces:
            for e in range(2):
                ref[e, place : place + last - first] = product[first:last, e * 128 : (e + 1) * 128]
            place += last - first


def call_gradients(left, right, own_rows, other_rows, with_sums, name):
    total, height = left.shape
    width = right.shape[1]
    rows = height // 2
    slab = pl.BlockSpec((2, rows, 128), lambda i: (i, 0, 0))
    shape = jax.ShapeDtypeStruct((width // 128, rows, 128), bf16)
    out_specs, out_shape = [slab, slab], [shape, shape]
    if with_sums:
        out_specs.append(pl.BlockSpec((1, height), lambda i: (0, 0)))
        out_shape.append(jax.ShapeDtypeStruct((1, height), f32))
    return pl.pallas_call(
        partial(gradient_slabs, own_rows, other_rows, with_sums),
        grid=(width // 256,),
        in_specs=[pl.BlockSpec((total, height), lambda i: (0, 0)), pl.BlockSpec((total, 256), lambda i: (0, i))],
        out_specs=out_specs,
        out_shape=out_shape,
        scratch_shapes=[pltpu.VMEM((height, total), bf16)],
        cost_estimate=pl.CostEstimate(
            flops=2 * total * height * width, bytes_accessed=2 * (total * (width + height) + 2 * height * width), transcendentals=0
        ),
        name=name,
    )(left, right)


def spread_gradients(up_ref, down_ref, *rest):
    qkv_ref, out_w_ref, fc1_ref, fc2_ref = rest[-4:]
    for p in range(3):
        rows = slice(p * HEAD_DIM, (p + 1) * HEAD_DIM)
        both = jnp.concatenate([up_ref[0, rows].astype(f32), up_ref[1, rows].astype(f32)], axis=0)
        qkv_ref[0, p] = both.T
    base = 3 * HEAD_DIM
    for d in range(2):
        for h in range(2):
            fc1_ref[0, :, (2 * d + h) * 128 : (2 * d + h + 1) * 128] = (
                up_ref[d, base + h * 128 : base + (h + 1) * 128].astype(f32).T
            )
        out_w_ref[0, d * HEAD_DIM : (d + 1) * HEAD_DIM] = down_ref[d, :HEAD_DIM].astype(f32)
        fc2_ref[0, d * 256 : (d + 1) * 256] = down_ref[d, HEAD_DIM:].astype(f32)


def call_spread(up, down, layer, filled):
    shapes = [
        jax.ShapeDtypeStruct((LAYERS, 3, 128, GROUP * HEAD_DIM), f32),
        jax.ShapeDtypeStruct((LAYERS, GROUP * HEAD_DIM, 128), f32),
        jax.ShapeDtypeStruct((LAYERS, 128, GROUP * 256), f32),
        jax.ShapeDtypeStruct((LAYERS, GROUP * 256, 128), f32),
    ]
    return pl.pallas_call(
        spread_gradients,
        grid=(GROUP // 2,),
        in_specs=[
            pl.BlockSpec((2, up.shape[1], 128), lambda i: (i, 0, 0)),
            pl.BlockSpec((2, down.shape[1], 128), lambda i: (i, 0, 0)),
        ]
        + [ANY_SPEC] * len(filled),
        out_specs=[
            pl.BlockSpec((1, 3, 128, 128), lambda i: (layer, 0, 0, i)),
            pl.BlockSpec((1, 128, 128), lambda i: (layer, i, 0)),
            pl.BlockSpec((1, 128, 512), lambda i: (layer, 0, i)),
            pl.BlockSpec((1, 512, 128), lambda i: (layer, i, 0)),
        ],
        out_shape=shapes,
        input_output_aliases={2 + n: n for n in range(len(filled))},
        name="spread_gradients",
    )(up, down, *filled)


def ring_total(core_ref, keep_ref, took_ref, moving_ref, got_ref):
    half = got_ref.shape[0]
    arrived = moving_ref[pl.ds(pl.multiple_of(core_ref[0] * half, half), half), :]
    return keep_ref[...].astype(f32) + took_ref[...].astype(f32) + arrived.astype(f32) + got_ref[...].astype(f32)


def centred_rows(state):
    centred = state - jnp.mean(state, axis=1, keepdims=True)
    return centred, lax.rsqrt(jnp.mean(centred * centred, axis=1, keepdims=True) + norm_epsilon)


def forward_end(last, core_ref, keep_ref, took_ref, moving_ref, got_ref, state_ref, after_ref, *rest):
    state = state_ref[...].astype(f32) + ring_total(core_ref, keep_ref, took_ref, moving_ref, got_ref) + after_ref[...]
    if last:
        rest[0][...] = state.astype(bf16)
        return
    gain_ref, shift_ref, state_out, normed_ref = rest
    state_out[...] = state
    centred, inverse = centred_rows(state)
    normed_ref[...] = (centred * inverse * gain_ref[...] + shift_ref[...]).astype(bf16)


def backward_end(core_ref, keep_ref, took_ref, moving_ref, got_ref, state_ref, grad_ref, gain_ref, grad_out, low_ref, sums_ref):
    grad_normed = ring_total(core_ref, keep_ref, took_ref, moving_ref, got_ref)
    centred, inverse = centred_rows(state_ref[...].astype(f32))
    xhat = centred * inverse
    before = grad_ref[...].astype(f32)
    sums_ref[0:1] = jnp.sum(grad_normed * xhat, axis=0, keepdims=True)
    sums_ref[1:2] = jnp.sum(grad_normed, axis=0, keepdims=True)
    sums_ref[2:3] = jnp.sum(before, axis=0, keepdims=True)
    scaled = grad_normed * gain_ref[...]
    after = before + (
        scaled - jnp.mean(scaled, axis=1, keepdims=True) - xhat * jnp.mean(scaled * xhat, axis=1, keepdims=True)
    ) * inverse
    grad_out[...] = after
    low_ref[...] = after.astype(bf16)


def call_end(body, core, ring, extra, shapes, name):
    keep, took, moving, got = ring
    half, width = got.shape

    def rows_of(array):
        n = array.shape[0] // half - 1
        return pl.BlockSpec((half, width), lambda i: (n, 0))

    def whole_of(array):
        return pl.BlockSpec(array.shape, lambda i: (0,) * len(array.shape))

    return pl.pallas_call(
        body,
        grid=(1,),
        in_specs=[SMEM_SPEC, rows_of(keep), rows_of(took)] + [whole_of(x) for x in (moving, got, *extra)],
        out_specs=[whole_of(x) for x in shapes],
        out_shape=shapes,
        name=name,
    )(core, keep, took, moving, got, *extra)


def per_device(
    n_dp,
    hidden_in,
    seq_lengths,
    seq_device,
    positions,
    norm_gain,
    norm_bias,
    qkv_weight,
    qkv_bias,
    out_weight,
    fc1_weight,
    fc1_bias,
    fc2_weight,
    output_bias,
    out_cotangent,
):
    block = hidden_in.shape[0]
    half = block // 2
    width = hidden_in.shape[1]
    piece = norm_gain.shape[1]
    hidden = fc1_weight.shape[2] // GROUP
    groups = n_dp // GROUP
    chips = GROUP // 2
    side = chips // 2 - 1

    if groups == 1:
        ring = [2 * a for a in range(chips // 2)] + [2 * a + 1 for a in reversed(range(chips // 2))]
    else:
        ring = list(range(chips // 2)) + list(reversed(range(chips // 2, chips)))
    ring_pairs = []
    for g in range(groups):
        for place in range(chips):
            for core, step in ((0, 1), (1, -1)):
                ring_pairs.append(
                    (
                        g * GROUP + ring[place] * 2 + core,
                        g * GROUP + ring[(place + step) % chips] * 2 + core,
                    )
                )
    core_pairs = [(i, i ^ 1) for i in range(n_dp)]
    inner = [[g * GROUP + i for i in range(GROUP)] for g in range(groups)]
    outer = [[g * GROUP + i for g in range(groups)] for i in range(GROUP)]
    if groups == 1:
        inner = None

    def along(x):
        return lax.ppermute(x, "dp", ring_pairs)

    def across(x):
        return lax.ppermute(x, "dp", core_pairs)

    def over(x):
        return lax.ppermute(x, "tensor", [(0, 1), (1, 0)])

    index = lax.axis_index("dp")
    group = index // GROUP
    chip = (index % GROUP) // 2
    core = index % 2
    tensor = lax.axis_index("tensor")
    is_first = core == 0
    at = core * half
    off = (1 - core) * half
    core_word = core.astype(jnp.int32).reshape(1)

    def my_half(x, start, axis=0):
        return lax.dynamic_slice_in_dim(x, start, half, axis)

    def in_order(own, other):
        return jnp.where(
            is_first, jnp.concatenate([own, other], 0), jnp.concatenate([other, own], 0)
        )

    def gather_rows(mine):
        behind, ahead = [], []
        moving = mine
        for _ in range(side):
            moving = along(moving)
            behind.append(moving)
            ahead.append(across(moving))
        far = along(my_half(moving, at, moving.ndim - 2))
        return [mine] + behind + ahead + [far, across(far)]

    rows = lax.broadcasted_iota(jnp.int32, (block, 1), 0)
    mine_rows = (rows < half) == is_first

    def ring_sum(give_far, give, keep):
        took_far = across(give_far)
        took = across(give)
        far = keep[side * block : side * block + half].astype(f32) + took_far.astype(f32)
        moving = along(far.astype(bf16))
        moving = jnp.where(mine_rows, jnp.concatenate([moving, moving], 0), 0).astype(f32)
        for step in reversed(range(side)):
            here = slice(step * block, (step + 1) * block)
            moving = along((moving + keep[here].astype(f32) + took[here].astype(f32)).astype(bf16))
            if step:
                moving = moving.astype(f32)
        return keep, took, moving, across(my_half(moving, off))

    def spread(x):
        return lax.all_to_all(x, "dp", 0, 0, axis_index_groups=inner, tiled=True)

    small = jnp.concatenate(
        [
            norm_gain.reshape(-1),
            norm_bias.reshape(-1),
            output_bias.reshape(-1),
            (positions // 64).astype(bf16),
            (positions % 64).astype(bf16),
        ]
    )
    slab_rows = 3 * HEAD_DIM + hidden
    small_all = None
    weights = []
    if groups == 1:
        qkv_turned = qkv_weight.transpose(0, 2, 1, 3)
        for layer in range(LAYERS):
            extra = None
            if layer == 0:
                extra = jnp.concatenate([small, jnp.zeros_like(small)]).reshape(-1, 128)
            up = spread(call_pack_up(qkv_turned, fc1_weight, layer, extra))
            if layer == 0:
                small_all = up[:, slab_rows:].reshape(GROUP, -1)[:, : small.shape[0]]
            up_other = over(up)
            down = spread(call_pack_down(out_weight, fc2_weight, layer))
            down_other = over(down)
            weights.append((call_join_up(up, up_other), call_join_down(down, down_other)))
    else:
        small_all = lax.all_gather(small, "dp", axis=0, tiled=False)
        for layer in range(LAYERS):
            up = jnp.concatenate(
                [
                    qkv_weight[layer].reshape(piece, 3, GROUP, HEAD_DIM).transpose(2, 0, 1, 3).reshape(GROUP, piece, -1),
                    fc1_weight[layer].reshape(piece, GROUP, hidden).transpose(1, 0, 2),
                ],
                axis=2,
            )
            up = lax.all_gather(spread(up), "dp", axis=0, axis_index_groups=outer, tiled=True)
            up = up.reshape(width // 128, 128, slab_rows)
            value = up[:, :, WIDE : WIDE + HEAD_DIM]
            first = WIDE + HEAD_DIM
            up = jnp.concatenate(
                [
                    up[:, :, :WIDE],
                    jnp.concatenate([value[:, :HEAD_DIM], value[:, HEAD_DIM:]], axis=2),
                    up[:, :, first : first + 128],
                    up[:, :, first + 128 :],
                ],
                axis=1,
            )
            down = jnp.concatenate(
                [out_weight[layer].reshape(GROUP, HEAD_DIM, piece), fc2_weight[layer].reshape(GROUP, hidden, piece)],
                axis=1,
            )
            down = lax.all_gather(spread(down), "dp", axis=0, axis_index_groups=outer, tiled=True)
            down = down.transpose(1, 0, 2).reshape(-1, width // 128, 128).transpose(1, 0, 2)
            weights.append((call_join_up(up, over(up)), call_join_down(down, over(down))))
    if groups == 1:
        biases = jnp.concatenate([qkv_bias.reshape(LAYERS, 3 * HEAD_DIM), fc1_bias], axis=1)
    else:
        full_qkv = lax.all_gather(qkv_bias, "dp", axis=2, tiled=True)
        full_up = lax.all_gather(fc1_bias, "dp", axis=1, tiled=True)
        member = index % GROUP
        biases = jnp.concatenate(
            [
                lax.dynamic_slice_in_dim(full_qkv, member * HEAD_DIM, HEAD_DIM, 2).reshape(LAYERS, 3 * HEAD_DIM),
                lax.dynamic_slice_in_dim(full_up, member * hidden, hidden, 1),
            ],
            axis=1,
        )
    biases_other = over(biases)
    both_biases = jnp.stack([biases, biases_other], axis=1).astype(f32)
    bias_rows = jnp.concatenate(
        [
            both_biases[:, :, : 3 * HEAD_DIM].reshape(LAYERS, 2, 3, HEAD_DIM).transpose(0, 2, 1, 3).reshape(LAYERS, -1),
            both_biases[:, :, 3 * HEAD_DIM :].reshape(LAYERS, -1),
        ],
        axis=1,
    )
    vectors = small_all[:, : 6 * piece].reshape(n_dp, 3, LAYERS, piece).transpose(1, 2, 0, 3).reshape(3, LAYERS, 1, width).astype(f32)
    gains, shifts, after = vectors[0], vectors[1], vectors[2]

    turned = jnp.where(is_first, 1, -1)
    place = jnp.sum(jnp.where(jnp.asarray(ring) == chip, jnp.arange(chips), 0))
    offsets = [0] + [-(s + 1) for s in range(side)] + [s + 1 for s in range(side)] + [chips // 2]
    places = (place + turned * jnp.asarray(offsets)) % chips
    chip_ids = jnp.sum(
        jnp.where(places[:, None] == jnp.arange(chips)[None, :], jnp.asarray(ring)[None, :], 0), axis=1
    )
    owners = group * GROUP + 2 * chip_ids + tensor
    labels = jax.vmap(lambda owner: sequence_labels(seq_lengths, seq_device, owner, block))(owners)
    rows_at = jnp.arange(block, dtype=jnp.int32)
    allowed = (
        (labels[:, :, None] == labels[:, None, :])
        & (labels[:, :, None] > 0)
        & (rows_at[None, None, :] <= rows_at[None, :, None])
    ) | (rows_at[None, None, :] == rows_at[None, :, None])
    allowed = allowed.astype(f32).reshape(chips * block, block)
    picked = (owners[:, None] == jnp.arange(n_dp)[None, :]).astype(f32)
    place_parts = jnp.dot(picked, small_all[:, 6 * piece :].astype(f32), precision=lax.Precision.HIGHEST)
    row_places = (place_parts[:, :block] * 64.0 + place_parts[:, block:]).reshape(chips * block)
    pair = ROT // 2
    frequency = 10000.0 ** (-2.0 * jnp.arange(pair, dtype=f32) / ROT)
    angles = row_places[:, None] * frequency[None, :]
    cosine, sine = jnp.cos(angles), jnp.sin(angles)
    nought = jnp.zeros_like(sine)
    rest = jnp.zeros((chips * block, HEAD_DIM - ROT), f32)
    tables = (
        jnp.concatenate([cosine, cosine, rest + 1.0] * 2, axis=1),
        jnp.concatenate([-sine, nought, rest] * 2, axis=1),
        jnp.concatenate([nought, sine, rest] * 2, axis=1),
    )

    both = jnp.stack([hidden_in, out_cotangent])
    both = jnp.where(tensor == core, both, across(both))
    keeps = jnp.stack([jnp.ones_like(labels[0]), (labels[0] > 0).astype(labels.dtype)]).astype(bf16)
    both = both * keeps[:, :, None]
    inputs = gather_rows(both)
    mine_inputs = my_half(both, at, 1)
    state, grad_state = mine_inputs[0], mine_inputs[1]

    normed, heads, hidden_pre, wide, *parts = call_pass(
        "first", core_word, weights[0], tables, allowed, [bias_rows[0:1], gains[0], shifts[0]], inputs
    )
    rows_shape = (half, width)
    next_state, normed_own = call_end(
        partial(forward_end, False),
        core_word,
        ring_sum(*parts),
        [state, after[0], gains[1], shifts[1]],
        [jax.ShapeDtypeStruct(rows_shape, f32), jax.ShapeDtypeStruct(rows_shape, bf16)],
        "forward_end",
    )
    normed_chunks = gather_rows(in_order(normed_own, across(normed_own)))

    def handed_back(own_rows):
        filled = in_order(own_rows, across(own_rows))
        return jnp.where(tensor == core, filled, over(filled))

    def summed(own, other):
        total = own.astype(f32) + over(other).astype(f32)
        if groups > 1:
            total = total.transpose(1, 0, 2).reshape(total.shape[1], width)
            total = lax.psum_scatter(total, "dp", scatter_dimension=1, axis_index_groups=outer, tiled=True)
            total = total.reshape(total.shape[0], GROUP, piece).transpose(1, 0, 2)
        return spread(total.astype(bf16))

    down_own = [(0, HEAD_DIM), (WIDE, WIDE + hidden)]
    down_other = [(HEAD_DIM, WIDE), (WIDE + hidden, WIDE + 2 * hidden)]
    up_own = [(p * WIDE, p * WIDE + HEAD_DIM) for p in range(3)] + [(3 * WIDE, 3 * WIDE + hidden)]
    up_other = [(p * WIDE + HEAD_DIM, (p + 1) * WIDE) for p in range(3)] + [(3 * WIDE + hidden, 3 * WIDE + 2 * hidden)]

    def down_gradients(wide_rows, grad_rows):
        own, other = call_gradients(wide_rows, grad_rows, down_own, down_other, False, "down_gradients")
        return summed(own, other)

    def up_gradients(slim_rows, normed_rows):
        own, other, sums = call_gradients(slim_rows, normed_rows, up_own, up_other, True, "up_gradients")
        return summed(own, other), sums

    def backward_finish(parts, state, grad_state, layer):
        return call_end(
            backward_end,
            core_word,
            ring_sum(*parts),
            [state, grad_state, gains[layer]],
            [
                jax.ShapeDtypeStruct(rows_shape, f32),
                jax.ShapeDtypeStruct(rows_shape, bf16),
                jax.ShapeDtypeStruct((3, width), f32),
            ],
            "backward_end",
        )

    normed_last, grad_rows, wide_last, slim, *parts = call_pass(
        "middle", core_word, weights[1], tables, allowed, [bias_rows[1:2]], normed_chunks + inputs
    )
    grad_state, grad_low, sums_last = backward_finish(parts[3:], next_state, grad_state, 1)
    grad_chunks = gather_rows(in_order(grad_low, across(grad_low)))
    down_last = down_gradients(wide_last, grad_rows)
    up_last, bias_last = up_gradients(slim, normed_last)
    (hidden_out,) = call_end(
        partial(forward_end, True),
        core_word,
        ring_sum(*parts[:3]),
        [next_state, after[1]],
        [jax.ShapeDtypeStruct(rows_shape, bf16)],
        "forward_out",
    )
    hidden_out = handed_back(hidden_out)

    grad_rows, slim, *parts = call_pass(
        "last", core_word, weights[0], tables, allowed, [heads, hidden_pre], grad_chunks
    )
    down_first = down_gradients(wide, grad_rows)
    up_first, bias_first = up_gradients(slim, normed)
    _, grad_low, sums_first = backward_finish(parts, state, grad_state, 0)
    grad_hidden = handed_back(grad_low).astype(f32)

    vectors = jnp.stack([sums_first, sums_last]).reshape(LAYERS * 3, n_dp, piece).transpose(1, 0, 2)
    vectors = jnp.sum(lax.all_to_all(vectors, "dp", 0, 0, tiled=True), axis=0)
    vectors = (vectors + over(vectors)).reshape(LAYERS, 3, piece)
    sums = jnp.concatenate([bias_first, bias_last], axis=0)
    sums_qkv = sums[:, : 3 * WIDE].reshape(LAYERS, 3, 2, HEAD_DIM)
    sums_up = sums[:, 3 * WIDE :].reshape(LAYERS, 2, hidden)
    bias_own, bias_other = (
        jnp.concatenate([sums_qkv[:, :, n].reshape(LAYERS, -1), sums_up[:, n]], axis=1) for n in range(2)
    )
    bias_sums = bias_own + over(bias_other)
    bias_qkv, bias_up = bias_sums[:, : 3 * HEAD_DIM].reshape(LAYERS, 3, HEAD_DIM), bias_sums[:, 3 * HEAD_DIM :]
    if groups == 1:
        filled = call_spread(up_last, down_last, 1, [])
        grad_qkv, grad_out, grad_up, grad_down = call_spread(up_first, down_first, 0, filled)
        grad_qkv = grad_qkv.transpose(0, 2, 1, 3)
    else:
        bias_qkv = lax.all_gather(lax.psum(bias_qkv, "dp", axis_index_groups=outer), "dp", axis=2, axis_index_groups=inner, tiled=True)
        bias_up = lax.all_gather(lax.psum(bias_up, "dp", axis_index_groups=outer), "dp", axis=1, axis_index_groups=inner, tiled=True)
        bias_qkv = lax.dynamic_slice_in_dim(bias_qkv, index * qkv_bias.shape[2], qkv_bias.shape[2], 2)
        bias_up = lax.dynamic_slice_in_dim(bias_up, index * fc1_bias.shape[1], fc1_bias.shape[1], 1)
        ups = jnp.stack([up_first, up_last]).astype(f32)
        downs = jnp.stack([down_first, down_last]).astype(f32)
        grad_qkv = ups[:, :, : 3 * HEAD_DIM].reshape(LAYERS, GROUP, 3, HEAD_DIM, piece).transpose(0, 4, 2, 1, 3).reshape(LAYERS, piece, 3, -1)
        grad_up = ups[:, :, 3 * HEAD_DIM :].transpose(0, 3, 1, 2).reshape(LAYERS, piece, -1)
        grad_out = downs[:, :, :HEAD_DIM].reshape(LAYERS, -1, piece)
        grad_down = downs[:, :, HEAD_DIM:].reshape(LAYERS, -1, piece)
    return (
        hidden_out,
        grad_hidden,
        vectors[:, 0],
        vectors[:, 1],
        grad_qkv,
        bias_qkv,
        grad_out,
        grad_up,
        bias_up,
        grad_down,
        vectors[:, 2],
    )


def solution(mesh):
    placed = (
        P("dp", None),
        P(),
        P(),
        P("dp"),
        P(None, "dp"),
        P(None, "dp"),
        P(None, "dp", None, "tensor"),
        P(None, None, ("tensor", "dp")),
        P(None, "tensor", "dp"),
        P(None, "dp", "tensor"),
        P(None, ("tensor", "dp")),
        P(None, "tensor", "dp"),
        P(None, "dp"),
        P("dp", None),
    )
    return jax.shard_map(
        partial(per_device, mesh.shape["dp"]),
        mesh=mesh,
        in_specs=placed,
        out_specs=(
            P("dp", None),
            P("dp", None),
            P(None, "dp"),
            P(None, "dp"),
            P(None, "dp", None, "tensor"),
            P(None, None, ("tensor", "dp")),
            P(None, "tensor", "dp"),
            P(None, "dp", "tensor"),
            P(None, ("tensor", "dp")),
            P(None, "tensor", "dp"),
            P(None, "dp"),
        ),
        check_vma=False,
    )
```

```python
from functools import partial

import jax
import jax.numpy as jnp
from jax import lax
from jax.experimental import pallas as pl
from jax.experimental.pallas import tpu as pltpu
from jax.sharding import PartitionSpec as P

HEAD_DIM = 64
ROT = 32
LAYERS = 2
GROUP = 16

norm_epsilon = 1e-05
masked_score = -1e30
bf16 = jnp.bfloat16
f32 = jnp.float32

contract_last = (((1,), (1,)), ((), ()))
contract_first = (((0,), (0,)), ((), ()))


def dot(a, b, dims=(((1,), (0,)), ((), ()))):
    return lax.dot_general(a, b, dims, preferred_element_type=f32)


def turn(x, cosine, up, down):
    return x * cosine + pltpu.roll(x, x.shape[1] - ROT // 2, 1) * up + pltpu.roll(x, ROT // 2, 1) * down


def stacked_heads(x):
    lane = lax.broadcasted_iota(jnp.int32, x.shape, 1)
    zero = jnp.zeros_like(x)
    return jnp.concatenate(
        [jnp.where(lane < HEAD_DIM, x, zero), jnp.where(lane < HEAD_DIM, zero, x)], axis=0
    )


def merged_heads(x):
    rows = x.shape[0] // 2
    lane = lax.broadcasted_iota(jnp.int32, (rows, x.shape[1]), 1)
    return jnp.where(lane < HEAD_DIM, x[:rows], x[rows:])


def softmax_rows(queries, keys, allowed):
    scores = dot(stacked_heads(queries), keys, contract_last) * HEAD_DIM ** (-0.5)
    masked = jnp.where(jnp.concatenate([allowed, allowed], axis=0) > 0, scores, masked_score)
    weights = jnp.exp(masked - jnp.max(masked, axis=1, keepdims=True))
    return weights / jnp.sum(weights, axis=1, keepdims=True)


def sequence_labels(seq_lengths, seq_device, owner, count_rows):
    index = jnp.arange(seq_lengths.shape[0], dtype=jnp.int32)
    owned = jnp.where(seq_device == owner, seq_lengths, 0)
    earlier = index[None, :] < index[:, None]
    starts = jnp.sum(jnp.where(earlier, owned[None, :], 0), axis=1)
    places = jnp.arange(count_rows, dtype=jnp.int32)
    inside = (places[:, None] >= starts[None, :]) & (places[:, None] < (starts + owned)[None, :])
    return jnp.sum(jnp.where(inside, index[None, :] + 1, 0), axis=1)


def gelu_parts(v):
    c = (2.0 / jnp.pi) ** 0.5
    inner = jnp.tanh(c * (v + 0.044715 * v * v * v))
    value = 0.5 * v * (1.0 + inner)
    slope = 0.5 * (1.0 + inner) + 0.5 * v * (1.0 - inner * inner) * c * (1.0 + 3.0 * 0.044715 * v * v)
    return value, slope


VMEM_SPEC = pl.BlockSpec(memory_space=pltpu.VMEM)
ANY_SPEC = pl.BlockSpec(memory_space=pl.ANY)
SMEM_SPEC = pl.BlockSpec(memory_space=pltpu.SMEM)
WIDE = 2 * HEAD_DIM


def after(x, *others):
    return lax.optimization_barrier((x, *others))[0]


def left_lanes(x):
    return lax.broadcasted_iota(jnp.int32, x.shape, 1) < HEAD_DIM


def swapped(x):
    return pltpu.roll(x, HEAD_DIM, 1)


def zipped(a, b):
    left = left_lanes(a)
    return jnp.where(left, a, swapped(b)).astype(bf16), jnp.where(left, swapped(a), b).astype(bf16)


def pack_up(qkv_ref, fc1_ref, *rest):
    out_ref = rest[-1]
    q, k, v = (qkv_ref[0, p].astype(f32) for p in range(3))
    out_ref[0, :WIDE], out_ref[1, :WIDE] = zipped(q, k)
    rows = q.shape[0] // 2
    out_ref[0, WIDE : WIDE + rows], out_ref[1, WIDE : WIDE + rows] = zipped(v[:rows], v[rows:])
    base = WIDE + rows
    for d in range(2):
        for h in range(2):
            out_ref[d, base + h * 128 : base + (h + 1) * 128] = fc1_ref[0, :, (2 * d + h) * 128 : (2 * d + h + 1) * 128]
        if len(rest) > 1:
            out_ref[d, base + 256 :] = rest[0][...]


def call_pack_up(qkv, fc1, layer, small):
    rows = 3 * HEAD_DIM + 256 + (0 if small is None else small.shape[0])
    specs = [
        pl.BlockSpec((1, 3, 128, 128), lambda i: (layer, 0, 0, i)),
        pl.BlockSpec((1, 128, 512), lambda i: (layer, 0, i)),
    ]
    if small is not None:
        specs.append(pl.BlockSpec(small.shape, lambda i: (0, 0)))
    return pl.pallas_call(
        pack_up,
        grid=(GROUP // 2,),
        in_specs=specs,
        out_specs=pl.BlockSpec((2, rows, 128), lambda i: (i, 0, 0)),
        out_shape=jax.ShapeDtypeStruct((GROUP, rows, 128), bf16),
        name="pack_up",
    )(*([qkv, fc1] + ([] if small is None else [small])))


def pack_down(out_w_ref, fc2_ref, out_ref):
    for d in range(2):
        out_ref[d, :HEAD_DIM] = out_w_ref[0, d * HEAD_DIM : (d + 1) * HEAD_DIM]
        out_ref[d, HEAD_DIM:] = fc2_ref[0, d * 256 : (d + 1) * 256]


def call_pack_down(out_w, fc2, layer):
    return pl.pallas_call(
        pack_down,
        grid=(GROUP // 2,),
        in_specs=[
            pl.BlockSpec((1, 128, 128), lambda i: (layer, i, 0)),
            pl.BlockSpec((1, 512, 128), lambda i: (layer, i, 0)),
        ],
        out_specs=pl.BlockSpec((2, HEAD_DIM + 256, 128), lambda i: (i, 0, 0)),
        out_shape=jax.ShapeDtypeStruct((GROUP, HEAD_DIM + 256, 128), bf16),
        name="pack_down",
    )(out_w, fc2)


def join_up(own_ref, other_ref, out_ref):
    for e in range(2):
        rows = slice(e * 128, (e + 1) * 128)
        a, b = own_ref[e, :WIDE].astype(f32), other_ref[e, :WIDE].astype(f32)
        out_ref[rows, :WIDE], out_ref[rows, WIDE : 2 * WIDE] = zipped(a, b)
        a, b = own_ref[e, WIDE : WIDE + 64].astype(f32), other_ref[e, WIDE : WIDE + 64].astype(f32)
        top, bottom = zipped(a, b)
        out_ref[e * 128 : e * 128 + 64, 2 * WIDE : 3 * WIDE] = top
        out_ref[e * 128 + 64 : (e + 1) * 128, 2 * WIDE : 3 * WIDE] = bottom
        for n, ref in enumerate((own_ref, other_ref)):
            for h in range(2):
                lanes = 3 * WIDE + n * 256 + h * 128
                out_ref[rows, lanes : lanes + 128] = ref[e, WIDE + 64 + h * 128 : WIDE + 64 + (h + 1) * 128]


def call_join_up(own, other):
    rows = own.shape[1]
    return pl.pallas_call(
        join_up,
        grid=(GROUP // 2,),
        in_specs=[pl.BlockSpec((2, rows, 128), lambda i: (i, 0, 0))] * 2,
        out_specs=pl.BlockSpec((256, 3 * WIDE + 512), lambda i: (i, 0)),
        out_shape=jax.ShapeDtypeStruct((GROUP * 128, 3 * WIDE + 512), bf16),
        name="join_up",
    )(own, other)


def join_down(own_ref, other_ref, out_ref):
    for e in range(2):
        lanes = slice(e * 128, (e + 1) * 128)
        for n, ref in enumerate((own_ref, other_ref)):
            out_ref[n * HEAD_DIM : (n + 1) * HEAD_DIM, lanes] = ref[e, :HEAD_DIM]
            out_ref[WIDE + n * 256 : WIDE + (n + 1) * 256, lanes] = ref[e, HEAD_DIM:]


def call_join_down(own, other):
    rows = own.shape[1]
    return pl.pallas_call(
        join_down,
        grid=(GROUP // 2,),
        in_specs=[pl.BlockSpec((2, rows, 128), lambda i: (i, 0, 0))] * 2,
        out_specs=pl.BlockSpec((2 * rows, 256), lambda i: (0, i)),
        out_shape=jax.ShapeDtypeStruct((2 * rows, GROUP * 128), bf16),
        name="join_down",
    )(own, other)


def slot_copies(refs, which, target, core):
    block = target.shape[0] // 8
    half = block // 2
    pairs = []
    for slot in range(7):
        ref = refs[slot] if which is None else refs[slot].at[which]
        pairs.append((ref, target.at[pl.ds(slot * block, block)]))
    for n, at in ((7, core * half), (8, (1 - core) * half)):
        ref = refs[n] if which is None else refs[n].at[which]
        pairs.append((ref, target.at[pl.ds(pl.multiple_of(7 * block + at, half), half)]))
    return pairs


def split_copies(part, far_ref, give_ref, keep_ref, core):
    block = part.shape[0] // 8
    half = block // 2
    at, off = core * half, (1 - core) * half

    def rows(slot, start):
        return part.at[pl.ds(pl.multiple_of(slot * block + start, half), half)]

    return [
        (rows(7, off), far_ref),
        (part.at[pl.ds(block, 3 * block)], give_ref.at[pl.ds(0, 3 * block)]),
        (rows(0, off), give_ref.at[pl.ds(3 * block, half)]),
        (part.at[pl.ds(4 * block, 3 * block)], keep_ref.at[pl.ds(0, 3 * block)]),
        (rows(7, at), keep_ref.at[pl.ds(3 * block, half)]),
        (rows(0, at), keep_ref.at[pl.ds(3 * block + half, half)]),
    ]


def run_copies(pairs, sems, first):
    made = [pltpu.make_async_copy(a, b, sems.at[first + n]) for n, (a, b) in enumerate(pairs)]
    for copy in made:
        copy.start()
    return made


def heads_forward(chances, values):
    return merged_heads(dot(chances.astype(bf16), values)).astype(bf16)


def heads_backward(chances, queries, keys, values, grad, tables):
    grads = stacked_heads(grad)
    grad_chances = dot(grads, values, contract_last)
    grad_values = dot(chances.astype(bf16), grads, contract_first)
    centre = jnp.sum(grad_chances * chances, axis=1, keepdims=True)
    grad_scores = (chances * (grad_chances - centre)).astype(bf16)
    scale = HEAD_DIM ** (-0.5)
    grad_queries = merged_heads(dot(grad_scores, keys)) * scale
    grad_keys = dot(grad_scores, stacked_heads(queries), contract_first) * scale
    cosine, up, down = tables
    back = (cosine, -up, -down)
    return turn(grad_queries, *back).astype(bf16), turn(grad_keys, *back).astype(bf16), grad_values.astype(bf16)


def layer_pass(mode, *refs):
    refs = list(refs)

    def take(n):
        out = refs[:n]
        del refs[:n]
        return out

    forward, backward = mode != "last", mode != "first"
    core_ref, up_ref, down_ref, cos_ref, sin_up_ref, sin_down_ref, allowed_ref = take(7)
    core = core_ref[0]
    if mode == "first":
        bias_ref, gain_ref, shift_ref = take(3)
        rows_in = take(9)
    elif mode == "middle":
        (bias_ref,) = take(1)
        rows_in = take(9)
        grads_in = take(9)
    else:
        heads_ref, hidden_ref = take(2)
        grads_in = take(9)
    if mode == "first":
        normed_ref, heads_ref, hidden_ref, wide_ref = take(4)
        outs = take(3)
        raw, part, sems = take(3)
    elif mode == "middle":
        normed_ref, grad_rows_ref, wide_ref, slim_ref = take(4)
        outs = take(3)
        grad_outs = take(3)
        part, grad_part, sems = take(3)
    else:
        grad_rows_ref, slim_ref = take(2)
        grad_outs = take(3)
        grad_part, sems = take(2)

    pairs = []
    if mode == "first":
        pairs += slot_copies(rows_in, 0, raw, core)
    if mode == "middle":
        pairs += slot_copies(rows_in, None, normed_ref, core)
        pairs += slot_copies(grads_in, 1, grad_rows_ref, core)
    if mode == "last":
        pairs += slot_copies(grads_in, None, grad_rows_ref, core)
    for copy in run_copies(pairs, sems, 0):
        copy.wait()

    total = allowed_ref.shape[0]
    block = allowed_ref.shape[1]
    step = 2 * block

    if mode == "first":
        tile = 32

        def norm_tile(i, carry):
            at = pl.ds(pl.multiple_of(i * tile, tile), tile)
            x = raw[at, :].astype(f32)
            centred = x - jnp.mean(x, axis=1, keepdims=True)
            inverse = lax.rsqrt(jnp.mean(centred * centred, axis=1, keepdims=True) + norm_epsilon)
            normed_ref[at, :] = (centred * inverse * gain_ref[...] + shift_ref[...]).astype(bf16)
            return carry

        lax.fori_loop(0, total // tile, norm_tile, 0)

    def one(p, carry):
        at = pl.ds(pl.multiple_of(p * step, step), step)
        if forward:
            before = dot(normed_ref[at, :], up_ref[...]) + bias_ref[...]
            hidden_pre = before[:, 3 * WIDE :]
        else:
            hidden_pre = hidden_ref[at, :]
        value, slope = gelu_parts(hidden_pre)
        if backward:
            grad_wide = dot(grad_rows_ref[at, :], down_ref[...], contract_last)
            slim_ref[at, 3 * WIDE :] = (grad_wide[:, WIDE:] * slope).astype(bf16)
        if forward:
            wide_ref[at, WIDE:] = value.astype(bf16)
        if mode == "first":
            hidden_ref[at, :] = hidden_pre
        for b in range(2):
            mine = slice(b * block, (b + 1) * block)
            own = pl.ds(pl.multiple_of(p * step + b * block, block), block)
            tables = (cos_ref[own, :], sin_up_ref[own, :], sin_down_ref[own, :])
            if forward:
                queries = turn(before[mine, :WIDE], *tables).astype(bf16)
                keys = turn(before[mine, WIDE : 2 * WIDE], *tables).astype(bf16)
                values = before[mine, 2 * WIDE : 3 * WIDE].astype(bf16)
            else:
                queries = heads_ref[own, :WIDE]
                keys = heads_ref[own, WIDE : 2 * WIDE]
                values = heads_ref[own, 2 * WIDE :]
            if mode == "first":
                heads_ref[own, :WIDE] = queries
                heads_ref[own, WIDE : 2 * WIDE] = keys
                heads_ref[own, 2 * WIDE :] = values
            chances = softmax_rows(queries, keys, allowed_ref[own, :])
            if forward:
                wide_ref[own, :WIDE] = heads_forward(chances, values)
            if backward:
                grads = heads_backward(
                    chances, queries, keys, values, grad_wide[mine, :WIDE].astype(bf16), tables
                )
                for n in range(3):
                    slim_ref[own, n * WIDE : (n + 1) * WIDE] = grads[n]
        if forward:
            part[at, :] = dot(wide_ref[at, :], down_ref[...]).astype(bf16)
        if backward:
            grad_part[at, :] = dot(slim_ref[at, :], up_ref[...], contract_last).astype(bf16)
        return carry

    lax.fori_loop(0, total // step, one, 0)
    pairs = []
    if backward:
        pairs += split_copies(grad_part, *grad_outs, core)
    if forward:
        pairs += split_copies(part, *outs, core)
    for copy in run_copies(pairs, sems, 0):
        copy.wait()


def call_pass(mode, core, weights, tables, allowed, extra, chunks):
    total, block = allowed.shape
    half = block // 2
    width = weights[0].shape[0]
    slim = weights[0].shape[1]
    wide = weights[1].shape[0]
    parts = [
        jax.ShapeDtypeStruct((half, width), bf16),
        jax.ShapeDtypeStruct((3 * block + half, width), bf16),
        jax.ShapeDtypeStruct((4 * block, width), bf16),
    ]
    full = jax.ShapeDtypeStruct((total, width), bf16)
    slim_rows = jax.ShapeDtypeStruct((total, slim), bf16)
    wide_rows = jax.ShapeDtypeStruct((total, wide), bf16)
    if mode == "first":
        kept = [
            full,
            jax.ShapeDtypeStruct((total, 3 * WIDE), bf16),
            jax.ShapeDtypeStruct((total, slim - 3 * WIDE), f32),
            wide_rows,
        ]
        buffers = 2
    elif mode == "middle":
        kept = [full, full, wide_rows, slim_rows]
        parts = parts * 2
        buffers = 2
    else:
        kept = [full, slim_rows]
        buffers = 1
    passes = 2 if mode == "middle" else 1
    return pl.pallas_call(
        partial(layer_pass, mode),
        in_specs=[SMEM_SPEC] + [VMEM_SPEC] * (6 + len(extra)) + [ANY_SPEC] * len(chunks),
        out_specs=[VMEM_SPEC] * len(kept) + [ANY_SPEC] * len(parts),
        out_shape=kept + parts,
        scratch_shapes=[pltpu.VMEM((total, width), bf16)] * buffers + [pltpu.SemaphoreType.DMA((18,))],
        cost_estimate=pl.CostEstimate(
            flops=6 * total * width * (slim + wide) * passes,
            bytes_accessed=20_000_000 * passes,
            transcendentals=total * slim,
        ),
        name="pass_" + mode,
    )(core, *weights, *tables, allowed, *extra, *chunks)


def gradient_slabs(own_rows, other_rows, with_sums, pieces_in, core_ref, left_ref, *rest):
    right_refs, (own_ref, other_ref, *rest) = rest[:pieces_in], rest[pieces_in:]
    turned_ref = rest[-1]
    if pieces_in == 1:
        right = right_refs[0][...]
    else:
        a, b = right_refs[-2][...], right_refs[-1][...]
        first = jnp.full(a.shape, core_ref[0]) == 0
        halves = [jnp.where(first, a, b), jnp.where(first, b, a)]
        right = jnp.concatenate([ref[...] for ref in right_refs[:-2]] + halves, axis=0)

    @pl.when(pl.program_id(0) == 0)
    def _():
        width = left_ref.shape[1]
        for n in range(width // 128):
            lanes = slice(n * 128, (n + 1) * 128)
            left = left_ref[:, lanes].astype(f32)
            if with_sums:
                rest[0][:, lanes] = jnp.sum(left, axis=0, keepdims=True)
            turned_ref[lanes, :] = left.T.astype(bf16)

    product = dot(turned_ref[...], right).astype(bf16)
    for ref, pieces in ((own_ref, own_rows), (other_ref, other_rows)):
        place = 0
        for first, last in pieces:
            for e in range(2):
                ref[e, place : place + last - first] = product[first:last, e * 128 : (e + 1) * 128]
            place += last - first


def call_gradients(core, left, right, own_rows, other_rows, with_sums, name):
    total, height = left.shape
    width = right[0].shape[1]
    rows = height // 2
    slab = pl.BlockSpec((2, rows, 128), lambda i: (i, 0, 0))
    shape = jax.ShapeDtypeStruct((width // 128, rows, 128), bf16)
    out_specs, out_shape = [slab, slab], [shape, shape]
    if with_sums:
        out_specs.append(pl.BlockSpec((1, height), lambda i: (0, 0)))
        out_shape.append(jax.ShapeDtypeStruct((1, height), f32))
    return pl.pallas_call(
        partial(gradient_slabs, own_rows, other_rows, with_sums, len(right)),
        grid=(width // 256,),
        in_specs=[SMEM_SPEC, pl.BlockSpec((total, height), lambda i: (0, 0))]
        + [pl.BlockSpec((x.shape[0], 256), lambda i: (0, i)) for x in right],
        out_specs=out_specs,
        out_shape=out_shape,
        scratch_shapes=[pltpu.VMEM((height, total), bf16)],
        cost_estimate=pl.CostEstimate(
            flops=4 * total * height * width, bytes_accessed=2 * (total * (width + height) + 2 * height * width), transcendentals=0
        ),
        name=name,
    )(core, left, *right)


def spread_gradients(up_ref, down_ref, *rest):
    qkv_ref, out_w_ref, fc1_ref, fc2_ref = rest[-4:]
    for p in range(3):
        rows = slice(p * HEAD_DIM, (p + 1) * HEAD_DIM)
        both = jnp.concatenate([up_ref[0, rows].astype(f32), up_ref[1, rows].astype(f32)], axis=0)
        qkv_ref[0, p] = both.T
    base = 3 * HEAD_DIM
    for d in range(2):
        for h in range(2):
            fc1_ref[0, :, (2 * d + h) * 128 : (2 * d + h + 1) * 128] = (
                up_ref[d, base + h * 128 : base + (h + 1) * 128].astype(f32).T
            )
        out_w_ref[0, d * HEAD_DIM : (d + 1) * HEAD_DIM] = down_ref[d, :HEAD_DIM].astype(f32)
        fc2_ref[0, d * 256 : (d + 1) * 256] = down_ref[d, HEAD_DIM:].astype(f32)


def call_spread(up, down, layer, filled):
    shapes = [
        jax.ShapeDtypeStruct((LAYERS, 3, 128, GROUP * HEAD_DIM), f32),
        jax.ShapeDtypeStruct((LAYERS, GROUP * HEAD_DIM, 128), f32),
        jax.ShapeDtypeStruct((LAYERS, 128, GROUP * 256), f32),
        jax.ShapeDtypeStruct((LAYERS, GROUP * 256, 128), f32),
    ]
    return pl.pallas_call(
        spread_gradients,
        grid=(GROUP // 2,),
        in_specs=[
            pl.BlockSpec((2, up.shape[1], 128), lambda i: (i, 0, 0)),
            pl.BlockSpec((2, down.shape[1], 128), lambda i: (i, 0, 0)),
        ]
        + [ANY_SPEC] * len(filled),
        out_specs=[
            pl.BlockSpec((1, 3, 128, 128), lambda i: (layer, 0, 0, i)),
            pl.BlockSpec((1, 128, 128), lambda i: (layer, i, 0)),
            pl.BlockSpec((1, 128, 512), lambda i: (layer, 0, i)),
            pl.BlockSpec((1, 512, 128), lambda i: (layer, i, 0)),
        ],
        out_shape=shapes,
        input_output_aliases={2 + n: n for n in range(len(filled))},
        name="spread_gradients",
    )(up, down, *filled)


def ring_total(core_ref, keep_ref, took_ref, moving_ref, got_ref):
    half = got_ref.shape[0]
    arrived = moving_ref[pl.ds(pl.multiple_of(core_ref[0] * half, half), half), :]
    return keep_ref[...].astype(f32) + took_ref[...].astype(f32) + arrived.astype(f32) + got_ref[...].astype(f32)


def centred_rows(state):
    centred = state - jnp.mean(state, axis=1, keepdims=True)
    return centred, lax.rsqrt(jnp.mean(centred * centred, axis=1, keepdims=True) + norm_epsilon)


def forward_end(last, core_ref, keep_ref, took_ref, moving_ref, got_ref, state_ref, after_ref, *rest):
    state = state_ref[...].astype(f32) + ring_total(core_ref, keep_ref, took_ref, moving_ref, got_ref) + after_ref[...]
    if last:
        rest[0][...] = state.astype(bf16)
        return
    gain_ref, shift_ref, state_out, normed_ref = rest
    state_out[...] = state
    centred, inverse = centred_rows(state)
    normed_ref[...] = (centred * inverse * gain_ref[...] + shift_ref[...]).astype(bf16)


def backward_end(core_ref, keep_ref, took_ref, moving_ref, got_ref, state_ref, grad_ref, gain_ref, grad_out, low_ref, sums_ref):
    grad_normed = ring_total(core_ref, keep_ref, took_ref, moving_ref, got_ref)
    centred, inverse = centred_rows(state_ref[...].astype(f32))
    xhat = centred * inverse
    before = grad_ref[...].astype(f32)
    sums_ref[0:1] = jnp.sum(grad_normed * xhat, axis=0, keepdims=True)
    sums_ref[1:2] = jnp.sum(grad_normed, axis=0, keepdims=True)
    sums_ref[2:3] = jnp.sum(before, axis=0, keepdims=True)
    scaled = grad_normed * gain_ref[...]
    after = before + (
        scaled - jnp.mean(scaled, axis=1, keepdims=True) - xhat * jnp.mean(scaled * xhat, axis=1, keepdims=True)
    ) * inverse
    grad_out[...] = after
    low_ref[...] = after.astype(bf16)


def call_end(body, core, ring, extra, shapes, name):
    keep, took, moving, got, n_sum = ring
    _, half, width = got.shape

    def rows_of(array):
        n = array.shape[0] // half - 1
        return pl.BlockSpec((half, width), lambda i: (n, 0))

    def whole_of(array):
        return pl.BlockSpec(array.shape, lambda i: (0,) * len(array.shape))

    def one_of(array):
        return pl.BlockSpec((None,) + array.shape[1:], lambda i: (n_sum, 0, 0))

    return pl.pallas_call(
        body,
        grid=(1,),
        in_specs=[SMEM_SPEC, rows_of(keep), rows_of(took), one_of(moving), one_of(got)] + [whole_of(x) for x in extra],
        out_specs=[whole_of(x) for x in shapes],
        out_shape=shapes,
        name=name,
    )(core, keep, took, moving, got, *extra)


def per_device(
    n_dp,
    hidden_in,
    seq_lengths,
    seq_device,
    positions,
    norm_gain,
    norm_bias,
    qkv_weight,
    qkv_bias,
    out_weight,
    fc1_weight,
    fc1_bias,
    fc2_weight,
    output_bias,
    out_cotangent,
):
    block = hidden_in.shape[0]
    half = block // 2
    width = hidden_in.shape[1]
    piece = norm_gain.shape[1]
    hidden = fc1_weight.shape[2] // GROUP
    groups = n_dp // GROUP
    chips = GROUP // 2
    side = chips // 2 - 1

    if groups == 1:
        ring = [2 * a for a in range(chips // 2)] + [2 * a + 1 for a in reversed(range(chips // 2))]
    else:
        ring = list(range(chips // 2)) + list(reversed(range(chips // 2, chips)))
    ring_pairs = []
    for g in range(groups):
        for place in range(chips):
            for core, step in ((0, 1), (1, -1)):
                ring_pairs.append(
                    (
                        g * GROUP + ring[place] * 2 + core,
                        g * GROUP + ring[(place + step) % chips] * 2 + core,
                    )
                )
    core_pairs = [(i, i ^ 1) for i in range(n_dp)]
    inner = [[g * GROUP + i for i in range(GROUP)] for g in range(groups)]
    outer = [[g * GROUP + i for g in range(groups)] for i in range(GROUP)]
    if groups == 1:
        inner = None

    def along(x):
        return lax.ppermute(x, "dp", ring_pairs)

    def across(x):
        return lax.ppermute(x, "dp", core_pairs)

    def over(x):
        return lax.ppermute(x, "tensor", [(0, 1), (1, 0)])

    index = lax.axis_index("dp")
    group = index // GROUP
    chip = (index % GROUP) // 2
    core = index % 2
    tensor = lax.axis_index("tensor")
    is_first = core == 0
    at = core * half
    off = (1 - core) * half
    core_word = core.astype(jnp.int32).reshape(1)

    def my_half(x, start, axis=0):
        return lax.dynamic_slice_in_dim(x, start, half, axis)

    def in_order(own, other):
        return jnp.where(
            is_first, jnp.concatenate([own, other], 0), jnp.concatenate([other, own], 0)
        )

    def gather_rows(mine):
        behind, ahead = [], []
        moving = mine
        for _ in range(side):
            moving = along(moving)
            behind.append(moving)
            ahead.append(across(moving))
        far = along(my_half(moving, at, moving.ndim - 2))
        return [mine] + behind + ahead + [far, across(far)]

    rows = lax.broadcasted_iota(jnp.int32, (block, 1), 0)
    mine_rows = (rows < half) == is_first

    def ring_sum(*sets):
        took_far = [across(give_far) for give_far, _, _ in sets]
        took = [across(give) for _, give, _ in sets]
        keep = [x for _, _, x in sets]
        far = [k[side * block : side * block + half].astype(f32) + t.astype(f32) for k, t in zip(keep, took_far)]
        moving = along(jnp.stack(far).astype(bf16))
        moving = jnp.where(mine_rows, jnp.concatenate([moving, moving], 1), 0).astype(f32)
        for step in reversed(range(side)):
            here = slice(step * block, (step + 1) * block)
            added = [k[here].astype(f32) + t[here].astype(f32) for k, t in zip(keep, took)]
            moving = along((moving + jnp.stack(added)).astype(bf16))
            if step:
                moving = moving.astype(f32)
        got = across(my_half(moving, off, 1))
        return [(k, t, moving, got, n) for n, (k, t) in enumerate(zip(keep, took))]

    def spread(x):
        return lax.all_to_all(x, "dp", 0, 0, axis_index_groups=inner, tiled=True)

    small = jnp.concatenate(
        [
            norm_gain.reshape(-1),
            norm_bias.reshape(-1),
            output_bias.reshape(-1),
            (positions // 64).astype(bf16),
            (positions % 64).astype(bf16),
        ]
    )
    slab_rows = 3 * HEAD_DIM + hidden
    small_all = None
    weights = []
    arrivals = []
    if groups == 1:
        qkv_turned = qkv_weight.transpose(0, 2, 1, 3)
        previous = ()
        for layer in range(LAYERS):
            extra = None
            if layer == 0:
                extra = jnp.concatenate([small, jnp.zeros_like(small)]).reshape(-1, 128)
            up = spread(after(call_pack_up(qkv_turned, fc1_weight, layer, extra), *previous))
            if layer == 0:
                small_all = up[:, slab_rows:].reshape(GROUP, -1)[:, : small.shape[0]]
            up_other = over(up)
            down = spread(after(call_pack_down(out_weight, fc2_weight, layer), up))
            down_other = over(down)
            previous = (down,)
            arrivals.append((up, down))
            weights.append((call_join_up(up, up_other), call_join_down(down, down_other)))
    else:
        small_all = lax.all_gather(small, "dp", axis=0, tiled=False)
        for layer in range(LAYERS):
            up = jnp.concatenate(
                [
                    qkv_weight[layer].reshape(piece, 3, GROUP, HEAD_DIM).transpose(2, 0, 1, 3).reshape(GROUP, piece, -1),
                    fc1_weight[layer].reshape(piece, GROUP, hidden).transpose(1, 0, 2),
                ],
                axis=2,
            )
            up = lax.all_gather(spread(up), "dp", axis=0, axis_index_groups=outer, tiled=True)
            up = up.reshape(width // 128, 128, slab_rows)
            value = up[:, :, WIDE : WIDE + HEAD_DIM]
            first = WIDE + HEAD_DIM
            up = jnp.concatenate(
                [
                    up[:, :, :WIDE],
                    jnp.concatenate([value[:, :HEAD_DIM], value[:, HEAD_DIM:]], axis=2),
                    up[:, :, first : first + 128],
                    up[:, :, first + 128 :],
                ],
                axis=1,
            )
            down = jnp.concatenate(
                [out_weight[layer].reshape(GROUP, HEAD_DIM, piece), fc2_weight[layer].reshape(GROUP, hidden, piece)],
                axis=1,
            )
            down = lax.all_gather(spread(down), "dp", axis=0, axis_index_groups=outer, tiled=True)
            down = down.transpose(1, 0, 2).reshape(-1, width // 128, 128).transpose(1, 0, 2)
            arrivals.append((up, down))
            weights.append((call_join_up(up, over(up)), call_join_down(down, over(down))))
    if groups == 1:
        biases = jnp.concatenate([qkv_bias.reshape(LAYERS, 3 * HEAD_DIM), fc1_bias], axis=1)
    else:
        full_qkv = lax.all_gather(qkv_bias, "dp", axis=2, tiled=True)
        full_up = lax.all_gather(fc1_bias, "dp", axis=1, tiled=True)
        member = index % GROUP
        biases = jnp.concatenate(
            [
                lax.dynamic_slice_in_dim(full_qkv, member * HEAD_DIM, HEAD_DIM, 2).reshape(LAYERS, 3 * HEAD_DIM),
                lax.dynamic_slice_in_dim(full_up, member * hidden, hidden, 1),
            ],
            axis=1,
        )
    biases_other = over(biases)
    both_biases = jnp.stack([biases, biases_other], axis=1).astype(f32)
    bias_rows = jnp.concatenate(
        [
            both_biases[:, :, : 3 * HEAD_DIM].reshape(LAYERS, 2, 3, HEAD_DIM).transpose(0, 2, 1, 3).reshape(LAYERS, -1),
            both_biases[:, :, 3 * HEAD_DIM :].reshape(LAYERS, -1),
        ],
        axis=1,
    )
    vectors = small_all[:, : 6 * piece].reshape(n_dp, 3, LAYERS, piece).transpose(1, 2, 0, 3).reshape(3, LAYERS, 1, width).astype(f32)
    gains, shifts, added_bias = vectors[0], vectors[1], vectors[2]

    turned = jnp.where(is_first, 1, -1)
    place = jnp.sum(jnp.where(jnp.asarray(ring) == chip, jnp.arange(chips), 0))
    offsets = [0] + [-(s + 1) for s in range(side)] + [s + 1 for s in range(side)] + [chips // 2]
    places = (place + turned * jnp.asarray(offsets)) % chips
    chip_ids = jnp.sum(
        jnp.where(places[:, None] == jnp.arange(chips)[None, :], jnp.asarray(ring)[None, :], 0), axis=1
    )
    owners = group * GROUP + 2 * chip_ids + tensor
    labels = jax.vmap(lambda owner: sequence_labels(seq_lengths, seq_device, owner, block))(owners)
    rows_at = jnp.arange(block, dtype=jnp.int32)
    allowed = (
        (labels[:, :, None] == labels[:, None, :])
        & (labels[:, :, None] > 0)
        & (rows_at[None, None, :] <= rows_at[None, :, None])
    ) | (rows_at[None, None, :] == rows_at[None, :, None])
    allowed = allowed.astype(f32).reshape(chips * block, block)
    picked = (owners[:, None] == jnp.arange(n_dp)[None, :]).astype(f32)
    place_parts = jnp.dot(picked, small_all[:, 6 * piece :].astype(f32), precision=lax.Precision.HIGHEST)
    row_places = (place_parts[:, :block] * 64.0 + place_parts[:, block:]).reshape(chips * block)
    pair = ROT // 2
    frequency = 10000.0 ** (-2.0 * jnp.arange(pair, dtype=f32) / ROT)
    angles = row_places[:, None] * frequency[None, :]
    cosine, sine = jnp.cos(angles), jnp.sin(angles)
    nought = jnp.zeros_like(sine)
    rest = jnp.zeros((chips * block, HEAD_DIM - ROT), f32)
    tables = (
        jnp.concatenate([cosine, cosine, rest + 1.0] * 2, axis=1),
        jnp.concatenate([-sine, nought, rest] * 2, axis=1),
        jnp.concatenate([nought, sine, rest] * 2, axis=1),
    )

    both = jnp.stack([hidden_in, out_cotangent])
    both = jnp.where(tensor == core, both, across(both))
    keeps = jnp.stack([jnp.ones_like(labels[0]), (labels[0] > 0).astype(labels.dtype)]).astype(bf16)
    both = both * keeps[:, :, None]
    inputs = gather_rows(both)
    mine_inputs = my_half(both, at, 1)
    state, grad_state = mine_inputs[0], mine_inputs[1]

    normed, heads, hidden_pre, wide, *parts = call_pass(
        "first", core_word, weights[0], tables, allowed, [bias_rows[0:1], gains[0], shifts[0]], inputs
    )
    rows_shape = (half, width)
    next_state, normed_own = call_end(
        partial(forward_end, False),
        core_word,
        ring_sum((after(parts[0], arrivals[1][0]), parts[1], parts[2]))[0],
        [state, added_bias[0], gains[1], shifts[1]],
        [jax.ShapeDtypeStruct(rows_shape, f32), jax.ShapeDtypeStruct(rows_shape, bf16)],
        "forward_end",
    )
    normed_own = after(normed_own, arrivals[1][1])
    normed_chunks = gather_rows(in_order(normed_own, across(normed_own)))

    def handed_back(own_rows):
        filled = in_order(own_rows, across(own_rows))
        return jnp.where(tensor == core, filled, over(filled))

    def summed(own, other, *earlier):
        total = own.astype(f32) + over(other).astype(f32)
        if groups > 1:
            total = total.transpose(1, 0, 2).reshape(total.shape[1], width)
            total = lax.psum_scatter(total, "dp", scatter_dimension=1, axis_index_groups=outer, tiled=True)
            total = total.reshape(total.shape[0], GROUP, piece).transpose(1, 0, 2)
        return spread(after(total.astype(bf16), *earlier))

    down_own = [(0, HEAD_DIM), (WIDE, WIDE + hidden)]
    down_other = [(HEAD_DIM, WIDE), (WIDE + hidden, WIDE + 2 * hidden)]
    up_own = [(p * WIDE, p * WIDE + HEAD_DIM) for p in range(3)] + [(3 * WIDE, 3 * WIDE + hidden)]
    up_other = [(p * WIDE + HEAD_DIM, (p + 1) * WIDE) for p in range(3)] + [(3 * WIDE + hidden, 3 * WIDE + 2 * hidden)]

    def down_gradients(wide_rows, grad_rows):
        return call_gradients(core_word, wide_rows, grad_rows, down_own, down_other, False, "down_gradients")

    def up_gradients(slim_rows, normed_rows):
        return call_gradients(core_word, slim_rows, [normed_rows], up_own, up_other, True, "up_gradients")

    def backward_finish(ring_end, state, grad_state, layer):
        return call_end(
            backward_end,
            core_word,
            ring_end,
            [state, grad_state, gains[layer]],
            [
                jax.ShapeDtypeStruct(rows_shape, f32),
                jax.ShapeDtypeStruct(rows_shape, bf16),
                jax.ShapeDtypeStruct((3, width), f32),
            ],
            "backward_end",
        )

    normed_last, grad_rows, wide_last, slim, *parts = call_pass(
        "middle", core_word, weights[1], tables, allowed, [bias_rows[1:2]], normed_chunks + inputs
    )
    out_parts = parts[:3]
    down_pair = down_gradients(wide_last, [grad_rows])
    *up_pair, bias_last = up_gradients(slim, normed_last)
    grad_state, grad_low, sums_last = backward_finish(
        ring_sum(parts[3:])[0], after(next_state, down_pair[0], up_pair[0]), grad_state, 1
    )
    grad_chunks = gather_rows(in_order(grad_low, across(grad_low)))
    down_last = summed(*down_pair)
    up_last = summed(*up_pair, down_last)

    down_pair = down_gradients(wide, grad_chunks)
    grad_rows, slim, *parts = call_pass(
        "last", core_word, weights[0], tables, allowed, [heads, after(hidden_pre, down_pair[0], down_last)], grad_chunks
    )
    down_first = summed(*down_pair, up_last)
    *up_pair, bias_first = up_gradients(slim, normed)
    up_first = summed(*up_pair, down_first)
    grad_end, out_end = ring_sum((after(parts[0], up_pair[0]), parts[1], parts[2]), out_parts)
    _, grad_low, sums_first = backward_finish(grad_end, state, grad_state, 0)
    grad_hidden = handed_back(grad_low).astype(f32)
    (hidden_out,) = call_end(
        partial(forward_end, True),
        core_word,
        out_end,
        [next_state, added_bias[1]],
        [jax.ShapeDtypeStruct(rows_shape, bf16)],
        "forward_out",
    )
    hidden_out = handed_back(hidden_out)

    vectors = jnp.stack([sums_first, sums_last]).reshape(LAYERS * 3, n_dp, piece).transpose(1, 0, 2)
    vectors = jnp.sum(lax.all_to_all(vectors, "dp", 0, 0, tiled=True), axis=0)
    vectors = (vectors + over(vectors)).reshape(LAYERS, 3, piece)
    sums = jnp.concatenate([bias_first, bias_last], axis=0)
    sums_qkv = sums[:, : 3 * WIDE].reshape(LAYERS, 3, 2, HEAD_DIM)
    sums_up = sums[:, 3 * WIDE :].reshape(LAYERS, 2, hidden)
    bias_own, bias_other = (
        jnp.concatenate([sums_qkv[:, :, n].reshape(LAYERS, -1), sums_up[:, n]], axis=1) for n in range(2)
    )
    bias_sums = bias_own + over(bias_other)
    bias_qkv, bias_up = bias_sums[:, : 3 * HEAD_DIM].reshape(LAYERS, 3, HEAD_DIM), bias_sums[:, 3 * HEAD_DIM :]
    if groups == 1:
        filled = call_spread(up_last, down_last, 1, [])
        grad_qkv, grad_out, grad_up, grad_down = call_spread(up_first, down_first, 0, filled)
        grad_qkv = grad_qkv.transpose(0, 2, 1, 3)
    else:
        bias_qkv = lax.all_gather(lax.psum(bias_qkv, "dp", axis_index_groups=outer), "dp", axis=2, axis_index_groups=inner, tiled=True)
        bias_up = lax.all_gather(lax.psum(bias_up, "dp", axis_index_groups=outer), "dp", axis=1, axis_index_groups=inner, tiled=True)
        bias_qkv = lax.dynamic_slice_in_dim(bias_qkv, index * qkv_bias.shape[2], qkv_bias.shape[2], 2)
        bias_up = lax.dynamic_slice_in_dim(bias_up, index * fc1_bias.shape[1], fc1_bias.shape[1], 1)
        ups = jnp.stack([up_first, up_last]).astype(f32)
        downs = jnp.stack([down_first, down_last]).astype(f32)
        grad_qkv = ups[:, :, : 3 * HEAD_DIM].reshape(LAYERS, GROUP, 3, HEAD_DIM, piece).transpose(0, 4, 2, 1, 3).reshape(LAYERS, piece, 3, -1)
        grad_up = ups[:, :, 3 * HEAD_DIM :].transpose(0, 3, 1, 2).reshape(LAYERS, piece, -1)
        grad_out = downs[:, :, :HEAD_DIM].reshape(LAYERS, -1, piece)
        grad_down = downs[:, :, HEAD_DIM:].reshape(LAYERS, -1, piece)
    return (
        hidden_out,
        grad_hidden,
        vectors[:, 0],
        vectors[:, 1],
        grad_qkv,
        bias_qkv,
        grad_out,
        grad_up,
        bias_up,
        grad_down,
        vectors[:, 2],
    )


def solution(mesh):
    placed = (
        P("dp", None),
        P(),
        P(),
        P("dp"),
        P(None, "dp"),
        P(None, "dp"),
        P(None, "dp", None, "tensor"),
        P(None, None, ("tensor", "dp")),
        P(None, "tensor", "dp"),
        P(None, "dp", "tensor"),
        P(None, ("tensor", "dp")),
        P(None, "tensor", "dp"),
        P(None, "dp"),
        P("dp", None),
    )
    return jax.shard_map(
        partial(per_device, mesh.shape["dp"]),
        mesh=mesh,
        in_specs=placed,
        out_specs=(
            P("dp", None),
            P("dp", None),
            P(None, "dp"),
            P(None, "dp"),
            P(None, "dp", None, "tensor"),
            P(None, None, ("tensor", "dp")),
            P(None, "tensor", "dp"),
            P(None, "dp", "tensor"),
            P(None, ("tensor", "dp")),
            P(None, "tensor", "dp"),
            P(None, "dp"),
        ),
        check_vma=False,
    )
```

```python
from functools import partial

import jax
import jax.numpy as jnp
from jax import lax
from jax.experimental import pallas as pl
from jax.experimental.pallas import tpu as pltpu
from jax.sharding import PartitionSpec as P

HEAD_DIM = 64
ROT = 32
LAYERS = 2
GROUP = 16

norm_epsilon = 1e-05
masked_score = -1e30
bf16 = jnp.bfloat16
f32 = jnp.float32

contract_last = (((1,), (1,)), ((), ()))
contract_first = (((0,), (0,)), ((), ()))


def dot(a, b, dims=(((1,), (0,)), ((), ()))):
    return lax.dot_general(a, b, dims, preferred_element_type=f32)


def turn(x, cosine, up, down):
    return x * cosine + pltpu.roll(x, x.shape[1] - ROT // 2, 1) * up + pltpu.roll(x, ROT // 2, 1) * down


def stacked_heads(x):
    lane = lax.broadcasted_iota(jnp.int32, x.shape, 1)
    zero = jnp.zeros_like(x)
    return jnp.concatenate(
        [jnp.where(lane < HEAD_DIM, x, zero), jnp.where(lane < HEAD_DIM, zero, x)], axis=0
    )


def merged_heads(x):
    rows = x.shape[0] // 2
    lane = lax.broadcasted_iota(jnp.int32, (rows, x.shape[1]), 1)
    return jnp.where(lane < HEAD_DIM, x[:rows], x[rows:])


def softmax_rows(queries, keys, allowed):
    scores = dot(stacked_heads(queries), keys, contract_last) * HEAD_DIM ** (-0.5)
    masked = jnp.where(jnp.concatenate([allowed, allowed], axis=0) > 0, scores, masked_score)
    weights = jnp.exp(masked - jnp.max(masked, axis=1, keepdims=True))
    return weights / jnp.sum(weights, axis=1, keepdims=True)


def sequence_labels(seq_lengths, seq_device, owner, count_rows):
    index = jnp.arange(seq_lengths.shape[0], dtype=jnp.int32)
    owned = jnp.where(seq_device == owner, seq_lengths, 0)
    earlier = index[None, :] < index[:, None]
    starts = jnp.sum(jnp.where(earlier, owned[None, :], 0), axis=1)
    places = jnp.arange(count_rows, dtype=jnp.int32)
    inside = (places[:, None] >= starts[None, :]) & (places[:, None] < (starts + owned)[None, :])
    return jnp.sum(jnp.where(inside, index[None, :] + 1, 0), axis=1)


def gelu_parts(v):
    c = (2.0 / jnp.pi) ** 0.5
    inner = jnp.tanh(c * (v + 0.044715 * v * v * v))
    value = 0.5 * v * (1.0 + inner)
    slope = 0.5 * (1.0 + inner) + 0.5 * v * (1.0 - inner * inner) * c * (1.0 + 3.0 * 0.044715 * v * v)
    return value, slope


VMEM_SPEC = pl.BlockSpec(memory_space=pltpu.VMEM)
ANY_SPEC = pl.BlockSpec(memory_space=pl.ANY)
SMEM_SPEC = pl.BlockSpec(memory_space=pltpu.SMEM)
WIDE = 2 * HEAD_DIM
UP_ROWS = 3 * HEAD_DIM + 256
DOWN_ROWS = HEAD_DIM + 256
MEMBERS = 4


def after(x, *others):
    if not others:
        return x
    return lax.optimization_barrier((x, *others))[0]


def left_lanes(x):
    return lax.broadcasted_iota(jnp.int32, x.shape, 1) < HEAD_DIM


def swapped(x):
    return pltpu.roll(x, HEAD_DIM, 1)


def zipped(a, b):
    left = left_lanes(a)
    return jnp.where(left, a, swapped(b)).astype(bf16), jnp.where(left, swapped(a), b).astype(bf16)


def pack_up(qkv_ref, fc1_ref, *rest):
    out_ref = rest[-1]
    for pair in range(MEMBERS // 2):
        lanes = slice(pair * 128, (pair + 1) * 128)
        q, k, v = (qkv_ref[0, p, :, lanes].astype(f32) for p in range(3))
        here, there = 2 * pair, 2 * pair + 1
        out_ref[here, :WIDE], out_ref[there, :WIDE] = zipped(q, k)
        rows = q.shape[0] // 2
        out_ref[here, WIDE : WIDE + rows], out_ref[there, WIDE : WIDE + rows] = zipped(v[:rows], v[rows:])
        base = WIDE + rows
        for d in (here, there):
            for h in range(2):
                out_ref[d, base + h * 128 : base + (h + 1) * 128] = fc1_ref[0, :, (2 * d + h) * 128 : (2 * d + h + 1) * 128]


def pack_first(qkv_ref, fc1_ref, small_ref, out_ref):
    pack_up(qkv_ref, fc1_ref, out_ref)
    for d in range(MEMBERS):
        out_ref[d, UP_ROWS:] = small_ref[...]


def pack_both(qkv_ref, fc1_ref, out_w_ref, fc2_ref, out_ref):
    pack_up(qkv_ref, fc1_ref, out_ref)
    pack_down(out_w_ref, fc2_ref, out_ref.at[:, UP_ROWS:])


def pack_down(out_w_ref, fc2_ref, out_ref):
    for d in range(MEMBERS):
        out_ref[d, :HEAD_DIM] = out_w_ref[0, d * HEAD_DIM : (d + 1) * HEAD_DIM]
        out_ref[d, HEAD_DIM:] = fc2_ref[0, d * 256 : (d + 1) * 256]


def call_pack(body, layer, ups, downs, small):
    rows, specs = 0, []
    if ups:
        rows += UP_ROWS
        specs += [
            pl.BlockSpec((1, 3, 128, MEMBERS * HEAD_DIM), lambda i: (layer, 0, 0, i)),
            pl.BlockSpec((1, 128, MEMBERS * 256), lambda i: (layer, 0, i)),
        ]
    if downs:
        rows += DOWN_ROWS
        specs += [
            pl.BlockSpec((1, MEMBERS * HEAD_DIM, 128), lambda i: (layer, i, 0)),
            pl.BlockSpec((1, MEMBERS * 256, 128), lambda i: (layer, i, 0)),
        ]
    if small:
        rows += small[0].shape[0]
        specs.append(pl.BlockSpec(small[0].shape, lambda i: (0, 0)))
    return pl.pallas_call(
        body,
        grid=(GROUP // MEMBERS,),
        in_specs=specs,
        out_specs=pl.BlockSpec((MEMBERS, rows, 128), lambda i: (i, 0, 0)),
        out_shape=jax.ShapeDtypeStruct((GROUP, rows, 128), bf16),
        cost_estimate=pl.CostEstimate(flops=0, bytes_accessed=GROUP * rows * 128 * 8, transcendentals=0),
        name=body.__name__,
    )(*ups, *downs, *small)


def join_up(own_ref, other_ref, out_ref):
    for e in range(MEMBERS):
        rows = slice(e * 128, (e + 1) * 128)
        a, b = own_ref[e, :WIDE].astype(f32), other_ref[e, :WIDE].astype(f32)
        out_ref[rows, :WIDE], out_ref[rows, WIDE : 2 * WIDE] = zipped(a, b)
        a, b = own_ref[e, WIDE : WIDE + 64].astype(f32), other_ref[e, WIDE : WIDE + 64].astype(f32)
        top, bottom = zipped(a, b)
        out_ref[e * 128 : e * 128 + 64, 2 * WIDE : 3 * WIDE] = top
        out_ref[e * 128 + 64 : (e + 1) * 128, 2 * WIDE : 3 * WIDE] = bottom
        for n, ref in enumerate((own_ref, other_ref)):
            for h in range(2):
                lanes = 3 * WIDE + n * 256 + h * 128
                out_ref[rows, lanes : lanes + 128] = ref[e, WIDE + 64 + h * 128 : WIDE + 64 + (h + 1) * 128]


def join_down(own_ref, other_ref, out_ref):
    base = own_ref.shape[1] - DOWN_ROWS
    for e in range(MEMBERS):
        lanes = slice(e * 128, (e + 1) * 128)
        for n, ref in enumerate((own_ref, other_ref)):
            out_ref[n * HEAD_DIM : (n + 1) * HEAD_DIM, lanes] = ref[e, base : base + HEAD_DIM]
            out_ref[WIDE + n * 256 : WIDE + (n + 1) * 256, lanes] = ref[e, base + HEAD_DIM :]


def join_both(own_ref, other_ref, up_ref, down_ref):
    join_up(own_ref, other_ref, up_ref)
    join_down(own_ref, other_ref, down_ref)


def call_join(body, own, other, ups, downs):
    rows = own.shape[1]
    specs, shapes = [], []
    if ups:
        specs.append(pl.BlockSpec((MEMBERS * 128, 2 * UP_ROWS), lambda i: (i, 0)))
        shapes.append(jax.ShapeDtypeStruct((GROUP * 128, 2 * UP_ROWS), bf16))
    if downs:
        specs.append(pl.BlockSpec((2 * DOWN_ROWS, MEMBERS * 128), lambda i: (0, i)))
        shapes.append(jax.ShapeDtypeStruct((2 * DOWN_ROWS, GROUP * 128), bf16))
    return pl.pallas_call(
        body,
        grid=(GROUP // MEMBERS,),
        in_specs=[pl.BlockSpec((MEMBERS, rows, 128), lambda i: (i, 0, 0))] * 2,
        out_specs=specs,
        out_shape=shapes,
        cost_estimate=pl.CostEstimate(flops=0, bytes_accessed=GROUP * rows * 128 * 12, transcendentals=0),
        name=body.__name__,
    )(own, other)


def slot_copies(refs, which, target, core):
    block = target.shape[0] // 8
    half = block // 2
    pairs = []
    for slot in range(7):
        ref = refs[slot] if which is None else refs[slot].at[which]
        pairs.append((ref, target.at[pl.ds(slot * block, block)]))
    for n, at in ((7, core * half), (8, (1 - core) * half)):
        ref = refs[n] if which is None else refs[n].at[which]
        pairs.append((ref, target.at[pl.ds(pl.multiple_of(7 * block + at, half), half)]))
    return pairs


def split_copies(part, far_ref, give_ref, keep_ref, core):
    block = part.shape[0] // 8
    half = block // 2
    at, off = core * half, (1 - core) * half

    def rows(slot, start):
        return part.at[pl.ds(pl.multiple_of(slot * block + start, half), half)]

    return [
        (rows(7, off), far_ref),
        (part.at[pl.ds(block, 3 * block)], give_ref.at[pl.ds(0, 3 * block)]),
        (rows(0, off), give_ref.at[pl.ds(3 * block, half)]),
        (part.at[pl.ds(4 * block, 3 * block)], keep_ref.at[pl.ds(0, 3 * block)]),
        (rows(7, at), keep_ref.at[pl.ds(3 * block, half)]),
        (rows(0, at), keep_ref.at[pl.ds(3 * block + half, half)]),
    ]


def run_copies(pairs, sems, first):
    made = [pltpu.make_async_copy(a, b, sems.at[first + n]) for n, (a, b) in enumerate(pairs)]
    for copy in made:
        copy.start()
    return made


def heads_forward(chances, values):
    return merged_heads(dot(chances.astype(bf16), values)).astype(bf16)


def heads_backward(chances, queries, keys, values, grad, tables):
    grads = stacked_heads(grad)
    grad_chances = dot(grads, values, contract_last)
    grad_values = dot(chances.astype(bf16), grads, contract_first)
    centre = jnp.sum(grad_chances * chances, axis=1, keepdims=True)
    grad_scores = (chances * (grad_chances - centre)).astype(bf16)
    scale = HEAD_DIM ** (-0.5)
    grad_queries = merged_heads(dot(grad_scores, keys)) * scale
    grad_keys = dot(grad_scores, stacked_heads(queries), contract_first) * scale
    cosine, up, down = tables
    back = (cosine, -up, -down)
    return turn(grad_queries, *back).astype(bf16), turn(grad_keys, *back).astype(bf16), grad_values.astype(bf16)


def layer_pass(mode, *refs):
    refs = list(refs)

    def take(n):
        out = refs[:n]
        del refs[:n]
        return out

    forward, backward = mode != "last", mode != "first"
    core_ref, up_ref, down_ref, cos_ref, sin_up_ref, sin_down_ref, allowed_ref = take(7)
    core = core_ref[0]
    if mode == "first":
        bias_ref, gain_ref, shift_ref = take(3)
        rows_in = take(9)
    elif mode == "middle":
        (bias_ref,) = take(1)
        rows_in = take(9)
        grads_in = take(9)
    else:
        heads_ref, hidden_ref = take(2)
        grads_in = take(9)
    if mode == "first":
        normed_ref, heads_ref, hidden_ref, wide_ref = take(4)
        outs = take(3)
        raw, part, sems = take(3)
    elif mode == "middle":
        normed_ref, grad_rows_ref, wide_ref, slim_ref = take(4)
        outs = take(3)
        grad_outs = take(3)
        part, grad_part, sems = take(3)
    else:
        grad_rows_ref, slim_ref = take(2)
        grad_outs = take(3)
        grad_part, sems = take(2)

    pairs = []
    if mode == "first":
        pairs += slot_copies(rows_in, 0, raw, core)
    if mode == "middle":
        pairs += slot_copies(rows_in, None, normed_ref, core)
        pairs += slot_copies(grads_in, 1, grad_rows_ref, core)
    if mode == "last":
        pairs += slot_copies(grads_in, None, grad_rows_ref, core)
    for copy in run_copies(pairs, sems, 0):
        copy.wait()

    total = allowed_ref.shape[0]
    block = allowed_ref.shape[1]
    step = 2 * block

    if mode == "first":
        tile = 32

        def norm_tile(i, carry):
            at = pl.ds(pl.multiple_of(i * tile, tile), tile)
            x = raw[at, :].astype(f32)
            centred = x - jnp.mean(x, axis=1, keepdims=True)
            inverse = lax.rsqrt(jnp.mean(centred * centred, axis=1, keepdims=True) + norm_epsilon)
            normed_ref[at, :] = (centred * inverse * gain_ref[...] + shift_ref[...]).astype(bf16)
            return carry

        lax.fori_loop(0, total // tile, norm_tile, 0)

    def one(p, carry):
        at = pl.ds(pl.multiple_of(p * step, step), step)
        if forward:
            before = dot(normed_ref[at, :], up_ref[...]) + bias_ref[...]
            hidden_pre = before[:, 3 * WIDE :]
        else:
            hidden_pre = hidden_ref[at, :]
        value, slope = gelu_parts(hidden_pre)
        if backward:
            grad_wide = dot(grad_rows_ref[at, :], down_ref[...], contract_last)
            slim_ref[at, 3 * WIDE :] = (grad_wide[:, WIDE:] * slope).astype(bf16)
        if forward:
            wide_ref[at, WIDE:] = value.astype(bf16)
        if mode == "first":
            hidden_ref[at, :] = hidden_pre
        for b in range(2):
            mine = slice(b * block, (b + 1) * block)
            own = pl.ds(pl.multiple_of(p * step + b * block, block), block)
            tables = (cos_ref[own, :], sin_up_ref[own, :], sin_down_ref[own, :])
            if forward:
                queries = turn(before[mine, :WIDE], *tables).astype(bf16)
                keys = turn(before[mine, WIDE : 2 * WIDE], *tables).astype(bf16)
                values = before[mine, 2 * WIDE : 3 * WIDE].astype(bf16)
            else:
                queries = heads_ref[own, :WIDE]
                keys = heads_ref[own, WIDE : 2 * WIDE]
                values = heads_ref[own, 2 * WIDE :]
            if mode == "first":
                heads_ref[own, :WIDE] = queries
                heads_ref[own, WIDE : 2 * WIDE] = keys
                heads_ref[own, 2 * WIDE :] = values
            chances = softmax_rows(queries, keys, allowed_ref[own, :])
            if forward:
                wide_ref[own, :WIDE] = heads_forward(chances, values)
            if backward:
                grads = heads_backward(
                    chances, queries, keys, values, grad_wide[mine, :WIDE].astype(bf16), tables
                )
                for n in range(3):
                    slim_ref[own, n * WIDE : (n + 1) * WIDE] = grads[n]
        if forward:
            part[at, :] = dot(wide_ref[at, :], down_ref[...]).astype(bf16)
        if backward:
            grad_part[at, :] = dot(slim_ref[at, :], up_ref[...], contract_last).astype(bf16)
        return carry

    lax.fori_loop(0, total // step, one, 0)
    pairs = []
    if backward:
        pairs += split_copies(grad_part, *grad_outs, core)
    if forward:
        pairs += split_copies(part, *outs, core)
    for copy in run_copies(pairs, sems, 0):
        copy.wait()


def call_pass(mode, core, weights, tables, allowed, extra, chunks):
    total, block = allowed.shape
    half = block // 2
    width = weights[0].shape[0]
    slim = weights[0].shape[1]
    wide = weights[1].shape[0]
    parts = [
        jax.ShapeDtypeStruct((half, width), bf16),
        jax.ShapeDtypeStruct((3 * block + half, width), bf16),
        jax.ShapeDtypeStruct((4 * block, width), bf16),
    ]
    full = jax.ShapeDtypeStruct((total, width), bf16)
    slim_rows = jax.ShapeDtypeStruct((total, slim), bf16)
    wide_rows = jax.ShapeDtypeStruct((total, wide), bf16)
    if mode == "first":
        kept = [
            full,
            jax.ShapeDtypeStruct((total, 3 * WIDE), bf16),
            jax.ShapeDtypeStruct((total, slim - 3 * WIDE), f32),
            wide_rows,
        ]
        buffers = 2
    elif mode == "middle":
        kept = [full, full, wide_rows, slim_rows]
        parts = parts * 2
        buffers = 2
    else:
        kept = [full, slim_rows]
        buffers = 1
    passes = 2 if mode == "middle" else 1
    return pl.pallas_call(
        partial(layer_pass, mode),
        in_specs=[SMEM_SPEC] + [VMEM_SPEC] * (6 + len(extra)) + [ANY_SPEC] * len(chunks),
        out_specs=[VMEM_SPEC] * len(kept) + [ANY_SPEC] * len(parts),
        out_shape=kept + parts,
        scratch_shapes=[pltpu.VMEM((total, width), bf16)] * buffers + [pltpu.SemaphoreType.DMA((18,))],
        cost_estimate=pl.CostEstimate(
            flops=6 * total * width * (slim + wide) * passes,
            bytes_accessed=20_000_000 * passes,
            transcendentals=total * slim,
        ),
        name="pass_" + mode,
    )(core, *weights, *tables, allowed, *extra, *chunks)


def gradient_slabs(own_rows, other_rows, with_sums, pieces_in, core_ref, left_ref, *rest):
    right_refs, (own_ref, other_ref, *rest) = rest[:pieces_in], rest[pieces_in:]
    turned_ref = rest[-1]
    if pieces_in == 1:
        right = right_refs[0][...]
    else:
        a, b = right_refs[-2][...], right_refs[-1][...]
        first = jnp.full(a.shape, core_ref[0]) == 0
        halves = [jnp.where(first, a, b), jnp.where(first, b, a)]
        right = jnp.concatenate([ref[...] for ref in right_refs[:-2]] + halves, axis=0)

    @pl.when(pl.program_id(0) == 0)
    def _():
        width = left_ref.shape[1]
        for n in range(width // 128):
            lanes = slice(n * 128, (n + 1) * 128)
            left = left_ref[:, lanes].astype(f32)
            if with_sums:
                rest[0][:, lanes] = jnp.sum(left, axis=0, keepdims=True)
            turned_ref[lanes, :] = left.T.astype(bf16)

    product = dot(turned_ref[...], right).astype(bf16)
    for ref, pieces in ((own_ref, own_rows), (other_ref, other_rows)):
        place = 0
        for first, last in pieces:
            for e in range(2):
                ref[e, place : place + last - first] = product[first:last, e * 128 : (e + 1) * 128]
            place += last - first


def call_gradients(core, left, right, own_rows, other_rows, with_sums, name):
    total, height = left.shape
    width = right[0].shape[1]
    rows = height // 2
    slab = pl.BlockSpec((2, rows, 128), lambda i: (i, 0, 0))
    shape = jax.ShapeDtypeStruct((width // 128, rows, 128), bf16)
    out_specs, out_shape = [slab, slab], [shape, shape]
    if with_sums:
        out_specs.append(pl.BlockSpec((1, height), lambda i: (0, 0)))
        out_shape.append(jax.ShapeDtypeStruct((1, height), f32))
    return pl.pallas_call(
        partial(gradient_slabs, own_rows, other_rows, with_sums, len(right)),
        grid=(width // 256,),
        in_specs=[SMEM_SPEC, pl.BlockSpec((total, height), lambda i: (0, 0))]
        + [pl.BlockSpec((x.shape[0], 256), lambda i: (0, i)) for x in right],
        out_specs=out_specs,
        out_shape=out_shape,
        scratch_shapes=[pltpu.VMEM((height, total), bf16)],
        cost_estimate=pl.CostEstimate(
            flops=4 * total * height * width, bytes_accessed=2 * (total * (width + height) + 2 * height * width), transcendentals=0
        ),
        name=name,
    )(core, left, *right)


def spread_gradients(up_ref, down_ref, *rest):
    qkv_ref, out_w_ref, fc1_ref, fc2_ref = rest[-4:]
    for p in range(3):
        rows = slice(p * HEAD_DIM, (p + 1) * HEAD_DIM)
        both = jnp.concatenate([up_ref[0, rows].astype(f32), up_ref[1, rows].astype(f32)], axis=0)
        qkv_ref[0, p] = both.T
    base = 3 * HEAD_DIM
    for d in range(2):
        for h in range(2):
            fc1_ref[0, :, (2 * d + h) * 128 : (2 * d + h + 1) * 128] = (
                up_ref[d, base + h * 128 : base + (h + 1) * 128].astype(f32).T
            )
        out_w_ref[0, d * HEAD_DIM : (d + 1) * HEAD_DIM] = down_ref[d, :HEAD_DIM].astype(f32)
        fc2_ref[0, d * 256 : (d + 1) * 256] = down_ref[d, HEAD_DIM:].astype(f32)


def call_spread(up, down, layer, filled):
    shapes = [
        jax.ShapeDtypeStruct((LAYERS, 3, 128, GROUP * HEAD_DIM), f32),
        jax.ShapeDtypeStruct((LAYERS, GROUP * HEAD_DIM, 128), f32),
        jax.ShapeDtypeStruct((LAYERS, 128, GROUP * 256), f32),
        jax.ShapeDtypeStruct((LAYERS, GROUP * 256, 128), f32),
    ]
    return pl.pallas_call(
        spread_gradients,
        grid=(GROUP // 2,),
        in_specs=[
            pl.BlockSpec((2, up.shape[1], 128), lambda i: (i, 0, 0)),
            pl.BlockSpec((2, down.shape[1], 128), lambda i: (i, 0, 0)),
        ]
        + [ANY_SPEC] * len(filled),
        out_specs=[
            pl.BlockSpec((1, 3, 128, 128), lambda i: (layer, 0, 0, i)),
            pl.BlockSpec((1, 128, 128), lambda i: (layer, i, 0)),
            pl.BlockSpec((1, 128, 512), lambda i: (layer, 0, i)),
            pl.BlockSpec((1, 512, 128), lambda i: (layer, i, 0)),
        ],
        out_shape=shapes,
        input_output_aliases={2 + n: n for n in range(len(filled))},
        name="spread_gradients",
    )(up, down, *filled)


def ring_total(core_ref, keep_ref, took_ref, moving_ref, got_ref):
    half = got_ref.shape[0]
    arrived = moving_ref[pl.ds(pl.multiple_of(core_ref[0] * half, half), half), :]
    return keep_ref[...].astype(f32) + took_ref[...].astype(f32) + arrived.astype(f32) + got_ref[...].astype(f32)


def centred_rows(state):
    centred = state - jnp.mean(state, axis=1, keepdims=True)
    return centred, lax.rsqrt(jnp.mean(centred * centred, axis=1, keepdims=True) + norm_epsilon)


def forward_end(last, core_ref, keep_ref, took_ref, moving_ref, got_ref, state_ref, after_ref, *rest):
    state = state_ref[...].astype(f32) + ring_total(core_ref, keep_ref, took_ref, moving_ref, got_ref) + after_ref[...]
    if last:
        rest[0][...] = state.astype(bf16)
        return
    gain_ref, shift_ref, state_out, normed_ref = rest
    state_out[...] = state
    centred, inverse = centred_rows(state)
    normed_ref[...] = (centred * inverse * gain_ref[...] + shift_ref[...]).astype(bf16)


def backward_end(core_ref, keep_ref, took_ref, moving_ref, got_ref, state_ref, grad_ref, gain_ref, grad_out, low_ref, sums_ref):
    grad_normed = ring_total(core_ref, keep_ref, took_ref, moving_ref, got_ref)
    centred, inverse = centred_rows(state_ref[...].astype(f32))
    xhat = centred * inverse
    before = grad_ref[...].astype(f32)
    sums_ref[0:1] = jnp.sum(grad_normed * xhat, axis=0, keepdims=True)
    sums_ref[1:2] = jnp.sum(grad_normed, axis=0, keepdims=True)
    sums_ref[2:3] = jnp.sum(before, axis=0, keepdims=True)
    scaled = grad_normed * gain_ref[...]
    after = before + (
        scaled - jnp.mean(scaled, axis=1, keepdims=True) - xhat * jnp.mean(scaled * xhat, axis=1, keepdims=True)
    ) * inverse
    grad_out[...] = after
    low_ref[...] = after.astype(bf16)


def call_end(body, core, ring, extra, shapes, name):
    keep, took, moving, got, n_sum = ring
    _, half, width = got.shape

    def rows_of(array):
        n = array.shape[0] // half - 1
        return pl.BlockSpec((half, width), lambda i: (n, 0))

    def whole_of(array):
        return pl.BlockSpec(array.shape, lambda i: (0,) * len(array.shape))

    def one_of(array):
        return pl.BlockSpec((None,) + array.shape[1:], lambda i: (n_sum, 0, 0))

    return pl.pallas_call(
        body,
        grid=(1,),
        in_specs=[SMEM_SPEC, rows_of(keep), rows_of(took), one_of(moving), one_of(got)] + [whole_of(x) for x in extra],
        out_specs=[whole_of(x) for x in shapes],
        out_shape=shapes,
        name=name,
    )(core, keep, took, moving, got, *extra)


def per_device(
    n_dp,
    hidden_in,
    seq_lengths,
    seq_device,
    positions,
    norm_gain,
    norm_bias,
    qkv_weight,
    qkv_bias,
    out_weight,
    fc1_weight,
    fc1_bias,
    fc2_weight,
    output_bias,
    out_cotangent,
):
    block = hidden_in.shape[0]
    half = block // 2
    width = hidden_in.shape[1]
    piece = norm_gain.shape[1]
    hidden = fc1_weight.shape[2] // GROUP
    groups = n_dp // GROUP
    chips = GROUP // 2
    side = chips // 2 - 1

    if groups == 1:
        ring = [2 * a for a in range(chips // 2)] + [2 * a + 1 for a in reversed(range(chips // 2))]
    else:
        ring = list(range(chips // 2)) + list(reversed(range(chips // 2, chips)))
    ring_pairs = []
    for g in range(groups):
        for place in range(chips):
            for core, step in ((0, 1), (1, -1)):
                ring_pairs.append(
                    (
                        g * GROUP + ring[place] * 2 + core,
                        g * GROUP + ring[(place + step) % chips] * 2 + core,
                    )
                )
    core_pairs = [(i, i ^ 1) for i in range(n_dp)]
    inner = [[g * GROUP + i for i in range(GROUP)] for g in range(groups)]
    outer = [[g * GROUP + i for g in range(groups)] for i in range(GROUP)]
    if groups == 1:
        inner = None

    def along(x):
        return lax.ppermute(x, "dp", ring_pairs)

    def across(x):
        return lax.ppermute(x, "dp", core_pairs)

    def over(x):
        return lax.ppermute(x, "tensor", [(0, 1), (1, 0)])

    index = lax.axis_index("dp")
    group = index // GROUP
    chip = (index % GROUP) // 2
    core = index % 2
    tensor = lax.axis_index("tensor")
    is_first = core == 0
    at = core * half
    off = (1 - core) * half
    core_word = core.astype(jnp.int32).reshape(1)

    def my_half(x, start, axis=0):
        return lax.dynamic_slice_in_dim(x, start, half, axis)

    def in_order(own, other):
        return jnp.where(
            is_first, jnp.concatenate([own, other], 0), jnp.concatenate([other, own], 0)
        )

    def gather_rows(mine, needed={}):
        behind, ahead = [], []
        moving = mine
        for step in range(side):
            moving = along(after(moving, *needed.get(step, ())))
            behind.append(moving)
            ahead.append(across(moving))
        far = along(after(my_half(moving, at, moving.ndim - 2), *needed.get(side, ())))
        return [mine] + behind + ahead + [far, across(far)]

    rows = lax.broadcasted_iota(jnp.int32, (block, 1), 0)
    mine_rows = (rows < half) == is_first

    def ring_sum(*sets, needed=()):
        took_far = [across(give_far) for give_far, _, _ in sets]
        took = [across(give) for _, give, _ in sets]
        keep = [x for _, _, x in sets]
        far = [k[side * block : side * block + half].astype(f32) + t.astype(f32) for k, t in zip(keep, took_far)]
        moving = along(jnp.stack(far).astype(bf16))
        moving = jnp.where(mine_rows, jnp.concatenate([moving, moving], 1), 0).astype(f32)
        for step in reversed(range(side)):
            here = slice(step * block, (step + 1) * block)
            if step == side - 2 and needed:
                moving = after(moving, *needed)
            added = [k[here].astype(f32) + t[here].astype(f32) for k, t in zip(keep, took)]
            moving = along((moving + jnp.stack(added)).astype(bf16))
            if step:
                moving = moving.astype(f32)
        got = across(my_half(moving, off, 1))
        return [(k, t, moving, got, n) for n, (k, t) in enumerate(zip(keep, took))]

    def spread(x):
        return lax.all_to_all(x, "dp", 0, 0, axis_index_groups=inner, tiled=True)

    small = jnp.concatenate(
        [
            norm_gain.reshape(-1),
            norm_bias.reshape(-1),
            output_bias.reshape(-1),
            (positions // 64).astype(bf16),
            (positions % 64).astype(bf16),
        ]
    )
    weights = []
    if groups == 1:
        qkv_turned = qkv_weight.transpose(0, 2, 1, 3)
        ups, downs = (qkv_turned, fc1_weight), (out_weight, fc2_weight)
        extra = jnp.concatenate([small, jnp.zeros_like(small)]).reshape(-1, 128)
        up = spread(call_pack(pack_first, 0, ups, (), (extra,)))
        small_all = up[:, UP_ROWS:].reshape(GROUP, -1)[:, : small.shape[0]]
        up_other = over(up)
        packed_down = call_pack(pack_down, 0, (), downs, ())
        down = spread(after(packed_down, up))
        down_other = over(down)
        weights.append(call_join(join_up, up, up_other, True, False) + call_join(join_down, down, down_other, False, True))
        packed_last = call_pack(pack_both, 1, ups, downs, ())
        first_up, first_other, first_down = up, up_other, down
    else:
        small_all = lax.all_gather(small, "dp", axis=0, tiled=False)
        for layer in range(LAYERS):
            up = jnp.concatenate(
                [
                    qkv_weight[layer].reshape(piece, 3, GROUP, HEAD_DIM).transpose(2, 0, 1, 3).reshape(GROUP, piece, -1),
                    fc1_weight[layer].reshape(piece, GROUP, hidden).transpose(1, 0, 2),
                ],
                axis=2,
            )
            up = lax.all_gather(spread(up), "dp", axis=0, axis_index_groups=outer, tiled=True)
            up = up.reshape(width // 128, 128, UP_ROWS)
            value = up[:, :, WIDE : WIDE + HEAD_DIM]
            first = WIDE + HEAD_DIM
            up = jnp.concatenate(
                [
                    up[:, :, :WIDE],
                    jnp.concatenate([value[:, :HEAD_DIM], value[:, HEAD_DIM:]], axis=2),
                    up[:, :, first : first + 128],
                    up[:, :, first + 128 :],
                ],
                axis=1,
            )
            down = jnp.concatenate(
                [out_weight[layer].reshape(GROUP, HEAD_DIM, piece), fc2_weight[layer].reshape(GROUP, hidden, piece)],
                axis=1,
            )
            down = lax.all_gather(spread(down), "dp", axis=0, axis_index_groups=outer, tiled=True)
            down = down.transpose(1, 0, 2).reshape(-1, width // 128, 128).transpose(1, 0, 2)
            weights.append(call_join(join_up, up, over(up), True, False) + call_join(join_down, down, over(down), False, True))
    if groups == 1:
        biases = jnp.concatenate([qkv_bias.reshape(LAYERS, 3 * HEAD_DIM), fc1_bias], axis=1)
    else:
        full_qkv = lax.all_gather(qkv_bias, "dp", axis=2, tiled=True)
        full_up = lax.all_gather(fc1_bias, "dp", axis=1, tiled=True)
        member = index % GROUP
        biases = jnp.concatenate(
            [
                lax.dynamic_slice_in_dim(full_qkv, member * HEAD_DIM, HEAD_DIM, 2).reshape(LAYERS, 3 * HEAD_DIM),
                lax.dynamic_slice_in_dim(full_up, member * hidden, hidden, 1),
            ],
            axis=1,
        )
    biases_other = over(biases)
    both_biases = jnp.stack([biases, biases_other], axis=1).astype(f32)
    bias_rows = jnp.concatenate(
        [
            both_biases[:, :, : 3 * HEAD_DIM].reshape(LAYERS, 2, 3, HEAD_DIM).transpose(0, 2, 1, 3).reshape(LAYERS, -1),
            both_biases[:, :, 3 * HEAD_DIM :].reshape(LAYERS, -1),
        ],
        axis=1,
    )
    vectors = small_all[:, : 6 * piece].reshape(n_dp, 3, LAYERS, piece).transpose(1, 2, 0, 3).reshape(3, LAYERS, 1, width).astype(f32)
    gains, shifts, added_bias = vectors[0], vectors[1], vectors[2]

    turned = jnp.where(is_first, 1, -1)
    place = jnp.sum(jnp.where(jnp.asarray(ring) == chip, jnp.arange(chips), 0))
    offsets = [0] + [-(s + 1) for s in range(side)] + [s + 1 for s in range(side)] + [chips // 2]
    places = (place + turned * jnp.asarray(offsets)) % chips
    chip_ids = jnp.sum(
        jnp.where(places[:, None] == jnp.arange(chips)[None, :], jnp.asarray(ring)[None, :], 0), axis=1
    )
    owners = group * GROUP + 2 * chip_ids + tensor
    labels = jax.vmap(lambda owner: sequence_labels(seq_lengths, seq_device, owner, block))(owners)
    rows_at = jnp.arange(block, dtype=jnp.int32)
    allowed = (
        (labels[:, :, None] == labels[:, None, :])
        & (labels[:, :, None] > 0)
        & (rows_at[None, None, :] <= rows_at[None, :, None])
    ) | (rows_at[None, None, :] == rows_at[None, :, None])
    allowed = allowed.astype(f32).reshape(chips * block, block)
    picked = (owners[:, None] == jnp.arange(n_dp)[None, :]).astype(f32)
    place_parts = jnp.dot(picked, small_all[:, 6 * piece :].astype(f32), precision=lax.Precision.HIGHEST)
    row_places = (place_parts[:, :block] * 64.0 + place_parts[:, block:]).reshape(chips * block)
    pair = ROT // 2
    frequency = 10000.0 ** (-2.0 * jnp.arange(pair, dtype=f32) / ROT)
    angles = row_places[:, None] * frequency[None, :]
    cosine, sine = jnp.cos(angles), jnp.sin(angles)
    nought = jnp.zeros_like(sine)
    rest = jnp.zeros((chips * block, HEAD_DIM - ROT), f32)
    tables = (
        jnp.concatenate([cosine, cosine, rest + 1.0] * 2, axis=1),
        jnp.concatenate([-sine, nought, rest] * 2, axis=1),
        jnp.concatenate([nought, sine, rest] * 2, axis=1),
    )

    both = jnp.stack([hidden_in, out_cotangent])
    both = jnp.where(tensor == core, both, across(both))
    keeps = jnp.stack([jnp.ones_like(labels[0]), (labels[0] > 0).astype(labels.dtype)]).astype(bf16)
    both = both * keeps[:, :, None]
    if groups == 1:
        inputs = gather_rows(after(both, packed_down, packed_last, first_up), {side: (first_other,)})
        slab = spread(after(packed_last, first_down, inputs[-2]))
        slab_other = over(slab)
        weights.append(call_join(join_both, slab, slab_other, True, True))
        slabs, others = (slab,), (slab_other,)
    else:
        inputs = gather_rows(both)
        slabs, others = (), ()
    mine_inputs = my_half(both, at, 1)
    state, grad_state = mine_inputs[0], mine_inputs[1]

    normed, heads, hidden_pre, wide, *parts = call_pass(
        "first", core_word, weights[0], tables, allowed, [bias_rows[0:1], gains[0], shifts[0]], inputs
    )
    rows_shape = (half, width)
    next_state, normed_own = call_end(
        partial(forward_end, False),
        core_word,
        ring_sum((after(parts[0], *slabs), parts[1], parts[2]))[0],
        [state, added_bias[0], gains[1], shifts[1]],
        [jax.ShapeDtypeStruct(rows_shape, f32), jax.ShapeDtypeStruct(rows_shape, bf16)],
        "forward_end",
    )
    normed_chunks = gather_rows(in_order(normed_own, across(normed_own)), {1: others})

    def handed_back(own_rows):
        filled = in_order(own_rows, across(own_rows))
        return jnp.where(tensor == core, filled, over(filled))

    def summed(own, other, *earlier, extra=None):
        total = own.astype(f32) + over(other).astype(f32)
        if groups > 1:
            total = total.transpose(1, 0, 2).reshape(total.shape[1], width)
            total = lax.psum_scatter(total, "dp", scatter_dimension=1, axis_index_groups=outer, tiled=True)
            total = total.reshape(total.shape[0], GROUP, piece).transpose(1, 0, 2)
        total = total.astype(bf16)
        if extra is not None:
            total = jnp.concatenate([total, extra], axis=1)
        return spread(after(total, *earlier))

    down_own = [(0, HEAD_DIM), (WIDE, WIDE + hidden)]
    down_other = [(HEAD_DIM, WIDE), (WIDE + hidden, WIDE + 2 * hidden)]
    up_own = [(p * WIDE, p * WIDE + HEAD_DIM) for p in range(3)] + [(3 * WIDE, 3 * WIDE + hidden)]
    up_other = [(p * WIDE + HEAD_DIM, (p + 1) * WIDE) for p in range(3)] + [(3 * WIDE + hidden, 3 * WIDE + 2 * hidden)]

    def down_gradients(wide_rows, grad_rows):
        return call_gradients(core_word, wide_rows, grad_rows, down_own, down_other, False, "down_gradients")

    def up_gradients(slim_rows, normed_rows):
        return call_gradients(core_word, slim_rows, [normed_rows], up_own, up_other, True, "up_gradients")

    def backward_finish(ring_end, state, grad_state, layer):
        return call_end(
            backward_end,
            core_word,
            ring_end,
            [state, grad_state, gains[layer]],
            [
                jax.ShapeDtypeStruct(rows_shape, f32),
                jax.ShapeDtypeStruct(rows_shape, bf16),
                jax.ShapeDtypeStruct((3, width), f32),
            ],
            "backward_end",
        )

    normed_last, grad_rows, wide_last, slim, *parts = call_pass(
        "middle", core_word, weights[1], tables, allowed, [bias_rows[1:2]], normed_chunks + inputs
    )
    out_parts = parts[:3]
    down_pair = down_gradients(wide_last, [grad_rows])
    *up_pair, bias_last = up_gradients(slim, normed_last)
    grad_end, out_end = ring_sum(parts[3:], out_parts, needed=(down_pair[0], up_pair[0]))
    grad_state, grad_low, sums_last = backward_finish(grad_end, next_state, grad_state, 1)
    grad_chunks = gather_rows(in_order(grad_low, across(grad_low)))
    down_last = summed(*down_pair)
    up_last = summed(*up_pair, down_last)

    down_pair = down_gradients(wide, grad_chunks)
    grad_rows, slim, *parts = call_pass(
        "last", core_word, weights[0], tables, allowed, [heads, after(hidden_pre, down_pair[0], down_last)], grad_chunks
    )
    down_first = summed(*down_pair, up_last)
    *up_pair, bias_first = up_gradients(slim, after(normed, up_last))
    (grad_end,) = ring_sum((after(parts[0], up_pair[0]), parts[1], parts[2]), needed=(down_first,))
    _, grad_low, sums_first = backward_finish(grad_end, state, grad_state, 0)
    grad_hidden = handed_back(grad_low).astype(f32)
    (hidden_out,) = call_end(
        partial(forward_end, True),
        core_word,
        out_end,
        [next_state, added_bias[1]],
        [jax.ShapeDtypeStruct(rows_shape, bf16)],
        "forward_out",
    )
    hidden_out = handed_back(hidden_out)

    vectors = jnp.stack([sums_first, sums_last]).reshape(LAYERS * 3, n_dp, piece).transpose(1, 0, 2)
    if groups == 1:
        extra = jnp.pad(vectors, ((0, 0), (0, 16 - LAYERS * 3), (0, 0))).astype(bf16)
        up_first = summed(*up_pair, down_first, extra=extra)
        vectors = up_first[:, UP_ROWS : UP_ROWS + LAYERS * 3].astype(f32)
    else:
        up_first = summed(*up_pair, down_first)
        vectors = lax.all_to_all(vectors, "dp", 0, 0, tiled=True)
    vectors = jnp.sum(vectors, axis=0)
    vectors = (vectors + over(vectors)).reshape(LAYERS, 3, piece)
    sums = jnp.concatenate([bias_first, bias_last], axis=0)
    sums_qkv = sums[:, : 3 * WIDE].reshape(LAYERS, 3, 2, HEAD_DIM)
    sums_up = sums[:, 3 * WIDE :].reshape(LAYERS, 2, hidden)
    bias_own, bias_other = (
        jnp.concatenate([sums_qkv[:, :, n].reshape(LAYERS, -1), sums_up[:, n]], axis=1) for n in range(2)
    )
    bias_sums = bias_own + over(bias_other)
    bias_qkv, bias_up = bias_sums[:, : 3 * HEAD_DIM].reshape(LAYERS, 3, HEAD_DIM), bias_sums[:, 3 * HEAD_DIM :]
    if groups == 1:
        filled = call_spread(up_last, down_last, 1, [])
        grad_qkv, grad_out, grad_up, grad_down = call_spread(up_first, down_first, 0, filled)
        grad_qkv = grad_qkv.transpose(0, 2, 1, 3)
    else:
        bias_qkv = lax.all_gather(lax.psum(bias_qkv, "dp", axis_index_groups=outer), "dp", axis=2, axis_index_groups=inner, tiled=True)
        bias_up = lax.all_gather(lax.psum(bias_up, "dp", axis_index_groups=outer), "dp", axis=1, axis_index_groups=inner, tiled=True)
        bias_qkv = lax.dynamic_slice_in_dim(bias_qkv, index * qkv_bias.shape[2], qkv_bias.shape[2], 2)
        bias_up = lax.dynamic_slice_in_dim(bias_up, index * fc1_bias.shape[1], fc1_bias.shape[1], 1)
        ups = jnp.stack([up_first, up_last]).astype(f32)
        downs = jnp.stack([down_first, down_last]).astype(f32)
        grad_qkv = ups[:, :, : 3 * HEAD_DIM].reshape(LAYERS, GROUP, 3, HEAD_DIM, piece).transpose(0, 4, 2, 1, 3).reshape(LAYERS, piece, 3, -1)
        grad_up = ups[:, :, 3 * HEAD_DIM :].transpose(0, 3, 1, 2).reshape(LAYERS, piece, -1)
        grad_out = downs[:, :, :HEAD_DIM].reshape(LAYERS, -1, piece)
        grad_down = downs[:, :, HEAD_DIM:].reshape(LAYERS, -1, piece)
    return (
        hidden_out,
        grad_hidden,
        vectors[:, 0],
        vectors[:, 1],
        grad_qkv,
        bias_qkv,
        grad_out,
        grad_up,
        bias_up,
        grad_down,
        vectors[:, 2],
    )


def solution(mesh):
    placed = (
        P("dp", None),
        P(),
        P(),
        P("dp"),
        P(None, "dp"),
        P(None, "dp"),
        P(None, "dp", None, "tensor"),
        P(None, None, ("tensor", "dp")),
        P(None, "tensor", "dp"),
        P(None, "dp", "tensor"),
        P(None, ("tensor", "dp")),
        P(None, "tensor", "dp"),
        P(None, "dp"),
        P("dp", None),
    )
    return jax.shard_map(
        partial(per_device, mesh.shape["dp"]),
        mesh=mesh,
        in_specs=placed,
        out_specs=(
            P("dp", None),
            P("dp", None),
            P(None, "dp"),
            P(None, "dp"),
            P(None, "dp", None, "tensor"),
            P(None, None, ("tensor", "dp")),
            P(None, "tensor", "dp"),
            P(None, "dp", "tensor"),
            P(None, ("tensor", "dp")),
            P(None, "tensor", "dp"),
            P(None, "dp"),
        ),
        check_vma=False,
    )
```

```python
from functools import partial

import jax
import jax.numpy as jnp
from jax import lax
from jax.experimental import pallas as pl
from jax.experimental.pallas import tpu as pltpu
from jax.sharding import PartitionSpec as P

HEAD_DIM = 64
ROT = 32
LAYERS = 2
GROUP = 16

norm_epsilon = 1e-05
masked_score = -1e30
bf16 = jnp.bfloat16
f32 = jnp.float32

contract_last = (((1,), (1,)), ((), ()))
contract_first = (((0,), (0,)), ((), ()))


def dot(a, b, dims=(((1,), (0,)), ((), ()))):
    return lax.dot_general(a, b, dims, preferred_element_type=f32)


def turn(x, cosine, up, down):
    return x * cosine + pltpu.roll(x, x.shape[1] - ROT // 2, 1) * up + pltpu.roll(x, ROT // 2, 1) * down


def stacked_heads(x):
    lane = lax.broadcasted_iota(jnp.int32, x.shape, 1)
    zero = jnp.zeros_like(x)
    return jnp.concatenate(
        [jnp.where(lane < HEAD_DIM, x, zero), jnp.where(lane < HEAD_DIM, zero, x)], axis=0
    )


def merged_heads(x):
    rows = x.shape[0] // 2
    lane = lax.broadcasted_iota(jnp.int32, (rows, x.shape[1]), 1)
    return jnp.where(lane < HEAD_DIM, x[:rows], x[rows:])


def softmax_rows(queries, keys, allowed):
    scores = dot(stacked_heads(queries), keys, contract_last) * HEAD_DIM ** (-0.5)
    masked = jnp.where(jnp.concatenate([allowed, allowed], axis=0) > 0, scores, masked_score)
    weights = jnp.exp(masked - jnp.max(masked, axis=1, keepdims=True))
    return weights / jnp.sum(weights, axis=1, keepdims=True)


def sequence_labels(seq_lengths, seq_device, owner, count_rows):
    index = jnp.arange(seq_lengths.shape[0], dtype=jnp.int32)
    owned = jnp.where(seq_device == owner, seq_lengths, 0)
    earlier = index[None, :] < index[:, None]
    starts = jnp.sum(jnp.where(earlier, owned[None, :], 0), axis=1)
    places = jnp.arange(count_rows, dtype=jnp.int32)
    inside = (places[:, None] >= starts[None, :]) & (places[:, None] < (starts + owned)[None, :])
    return jnp.sum(jnp.where(inside, index[None, :] + 1, 0), axis=1)


def gelu_parts(v):
    c = (2.0 / jnp.pi) ** 0.5
    inner = jnp.tanh(c * (v + 0.044715 * v * v * v))
    value = 0.5 * v * (1.0 + inner)
    slope = 0.5 * (1.0 + inner) + 0.5 * v * (1.0 - inner * inner) * c * (1.0 + 3.0 * 0.044715 * v * v)
    return value, slope


VMEM_SPEC = pl.BlockSpec(memory_space=pltpu.VMEM)
ANY_SPEC = pl.BlockSpec(memory_space=pl.ANY)
SMEM_SPEC = pl.BlockSpec(memory_space=pltpu.SMEM)
WIDE = 2 * HEAD_DIM
UP_ROWS = 3 * HEAD_DIM + 256
DOWN_ROWS = HEAD_DIM + 256
MEMBERS = 4


def after(x, *others):
    if not others:
        return x
    return lax.optimization_barrier((x, *others))[0]


def left_lanes(x):
    return lax.broadcasted_iota(jnp.int32, x.shape, 1) < HEAD_DIM


def swapped(x):
    return pltpu.roll(x, HEAD_DIM, 1)


def zipped(a, b):
    left = left_lanes(a)
    return jnp.where(left, a, swapped(b)).astype(bf16), jnp.where(left, swapped(a), b).astype(bf16)


def pack_up(qkv_ref, fc1_ref, *rest):
    out_ref = rest[-1]
    for pair in range(MEMBERS // 2):
        lanes = slice(pair * 128, (pair + 1) * 128)
        q, k, v = (qkv_ref[0, p, :, lanes].astype(f32) for p in range(3))
        here, there = 2 * pair, 2 * pair + 1
        out_ref[here, :WIDE], out_ref[there, :WIDE] = zipped(q, k)
        rows = q.shape[0] // 2
        out_ref[here, WIDE : WIDE + rows], out_ref[there, WIDE : WIDE + rows] = zipped(v[:rows], v[rows:])
        base = WIDE + rows
        for d in (here, there):
            for h in range(2):
                out_ref[d, base + h * 128 : base + (h + 1) * 128] = fc1_ref[0, :, (2 * d + h) * 128 : (2 * d + h + 1) * 128]


def pack_first(qkv_ref, fc1_ref, small_ref, out_ref):
    pack_up(qkv_ref, fc1_ref, out_ref)
    for d in range(MEMBERS):
        out_ref[d, UP_ROWS:] = small_ref[...]


def pack_both(qkv_ref, fc1_ref, out_w_ref, fc2_ref, out_ref):
    pack_up(qkv_ref, fc1_ref, out_ref)
    pack_down(out_w_ref, fc2_ref, out_ref.at[:, UP_ROWS:])


def pack_down(out_w_ref, fc2_ref, out_ref):
    for d in range(MEMBERS):
        out_ref[d, :HEAD_DIM] = out_w_ref[0, d * HEAD_DIM : (d + 1) * HEAD_DIM]
        out_ref[d, HEAD_DIM:] = fc2_ref[0, d * 256 : (d + 1) * 256]


def call_pack(body, layer, ups, downs, small):
    rows, specs = 0, []
    if ups:
        rows += UP_ROWS
        specs += [
            pl.BlockSpec((1, 3, 128, MEMBERS * HEAD_DIM), lambda i: (layer, 0, 0, i)),
            pl.BlockSpec((1, 128, MEMBERS * 256), lambda i: (layer, 0, i)),
        ]
    if downs:
        rows += DOWN_ROWS
        specs += [
            pl.BlockSpec((1, MEMBERS * HEAD_DIM, 128), lambda i: (layer, i, 0)),
            pl.BlockSpec((1, MEMBERS * 256, 128), lambda i: (layer, i, 0)),
        ]
    if small:
        rows += small[0].shape[0]
        specs.append(pl.BlockSpec(small[0].shape, lambda i: (0, 0)))
    return pl.pallas_call(
        body,
        grid=(GROUP // MEMBERS,),
        in_specs=specs,
        out_specs=pl.BlockSpec((MEMBERS, rows, 128), lambda i: (i, 0, 0)),
        out_shape=jax.ShapeDtypeStruct((GROUP, rows, 128), bf16),
        cost_estimate=pl.CostEstimate(flops=0, bytes_accessed=GROUP * rows * 128 * 8, transcendentals=0),
        name=body.__name__,
    )(*ups, *downs, *small)


def join_up(own_ref, other_ref, out_ref):
    for e in range(MEMBERS):
        rows = slice(e * 128, (e + 1) * 128)
        a, b = own_ref[e, :WIDE].astype(f32), other_ref[e, :WIDE].astype(f32)
        out_ref[rows, :WIDE], out_ref[rows, WIDE : 2 * WIDE] = zipped(a, b)
        a, b = own_ref[e, WIDE : WIDE + 64].astype(f32), other_ref[e, WIDE : WIDE + 64].astype(f32)
        top, bottom = zipped(a, b)
        out_ref[e * 128 : e * 128 + 64, 2 * WIDE : 3 * WIDE] = top
        out_ref[e * 128 + 64 : (e + 1) * 128, 2 * WIDE : 3 * WIDE] = bottom
        for n, ref in enumerate((own_ref, other_ref)):
            for h in range(2):
                lanes = 3 * WIDE + n * 256 + h * 128
                out_ref[rows, lanes : lanes + 128] = ref[e, WIDE + 64 + h * 128 : WIDE + 64 + (h + 1) * 128]


def join_down(own_ref, other_ref, out_ref):
    base = own_ref.shape[1] - DOWN_ROWS
    for e in range(MEMBERS):
        lanes = slice(e * 128, (e + 1) * 128)
        for n, ref in enumerate((own_ref, other_ref)):
            out_ref[n * HEAD_DIM : (n + 1) * HEAD_DIM, lanes] = ref[e, base : base + HEAD_DIM]
            out_ref[WIDE + n * 256 : WIDE + (n + 1) * 256, lanes] = ref[e, base + HEAD_DIM :]


def join_both(own_ref, other_ref, up_ref, down_ref):
    join_up(own_ref, other_ref, up_ref)
    join_down(own_ref, other_ref, down_ref)


def join_halves(own_ref, lower_ref, upper_ref, up_ref, down_ref):
    lower = pl.program_id(0) < GROUP // MEMBERS // 2

    @pl.when(lower)
    def _():
        join_both(own_ref, lower_ref, up_ref, down_ref)

    @pl.when(jnp.logical_not(lower))
    def _():
        join_both(own_ref, upper_ref, up_ref, down_ref)


def call_join(body, own, others, ups, downs):
    rows = own.shape[1]
    steps = GROUP // MEMBERS
    spec = pl.BlockSpec((MEMBERS, rows, 128), lambda i: (i, 0, 0))
    other_specs = [spec]
    if len(others) == 2:
        other_specs = [
            pl.BlockSpec((MEMBERS, rows, 128), lambda i: (jnp.minimum(i, steps // 2 - 1), 0, 0)),
            pl.BlockSpec((MEMBERS, rows, 128), lambda i: (jnp.maximum(i - steps // 2, 0), 0, 0)),
        ]
    specs, shapes = [], []
    if ups:
        specs.append(pl.BlockSpec((MEMBERS * 128, 2 * UP_ROWS), lambda i: (i, 0)))
        shapes.append(jax.ShapeDtypeStruct((GROUP * 128, 2 * UP_ROWS), bf16))
    if downs:
        specs.append(pl.BlockSpec((2 * DOWN_ROWS, MEMBERS * 128), lambda i: (0, i)))
        shapes.append(jax.ShapeDtypeStruct((2 * DOWN_ROWS, GROUP * 128), bf16))
    return pl.pallas_call(
        body,
        grid=(GROUP // MEMBERS,),
        in_specs=[spec] + other_specs,
        out_specs=specs,
        out_shape=shapes,
        cost_estimate=pl.CostEstimate(flops=0, bytes_accessed=GROUP * rows * 128 * 12, transcendentals=0),
        name=body.__name__,
    )(own, *others)


def slot_copies(refs, which, target, core):
    block = target.shape[0] // 8
    half = block // 2
    pairs = []
    for slot in range(7):
        ref = refs[slot] if which is None else refs[slot].at[which]
        pairs.append((ref, target.at[pl.ds(slot * block, block)]))
    for n, at in ((7, core * half), (8, (1 - core) * half)):
        ref = refs[n] if which is None else refs[n].at[which]
        pairs.append((ref, target.at[pl.ds(pl.multiple_of(7 * block + at, half), half)]))
    return pairs


def split_copies(part, far_ref, give_ref, keep_ref, core):
    block = part.shape[0] // 8
    half = block // 2
    at, off = core * half, (1 - core) * half

    def rows(slot, start):
        return part.at[pl.ds(pl.multiple_of(slot * block + start, half), half)]

    return [
        (rows(7, off), far_ref),
        (part.at[pl.ds(block, 3 * block)], give_ref.at[pl.ds(0, 3 * block)]),
        (rows(0, off), give_ref.at[pl.ds(3 * block, half)]),
        (part.at[pl.ds(4 * block, 3 * block)], keep_ref.at[pl.ds(0, 3 * block)]),
        (rows(7, at), keep_ref.at[pl.ds(3 * block, half)]),
        (rows(0, at), keep_ref.at[pl.ds(3 * block + half, half)]),
    ]


def run_copies(pairs, sems, first):
    made = [pltpu.make_async_copy(a, b, sems.at[first + n]) for n, (a, b) in enumerate(pairs)]
    for copy in made:
        copy.start()
    return made


def heads_forward(chances, values):
    return merged_heads(dot(chances.astype(bf16), values)).astype(bf16)


def heads_backward(chances, queries, keys, values, grad, tables):
    grads = stacked_heads(grad)
    grad_chances = dot(grads, values, contract_last)
    grad_values = dot(chances.astype(bf16), grads, contract_first)
    centre = jnp.sum(grad_chances * chances, axis=1, keepdims=True)
    grad_scores = (chances * (grad_chances - centre)).astype(bf16)
    scale = HEAD_DIM ** (-0.5)
    grad_queries = merged_heads(dot(grad_scores, keys)) * scale
    grad_keys = dot(grad_scores, stacked_heads(queries), contract_first) * scale
    cosine, up, down = tables
    back = (cosine, -up, -down)
    return turn(grad_queries, *back).astype(bf16), turn(grad_keys, *back).astype(bf16), grad_values.astype(bf16)


def layer_pass(mode, *refs):
    refs = list(refs)

    def take(n):
        out = refs[:n]
        del refs[:n]
        return out

    forward, backward = mode != "last", mode != "first"
    core_ref, up_ref, down_ref, cos_ref, sin_up_ref, sin_down_ref, allowed_ref = take(7)
    core = core_ref[0]
    if mode == "first":
        bias_ref, gain_ref, shift_ref = take(3)
        rows_in = take(9)
    elif mode == "middle":
        (bias_ref,) = take(1)
        rows_in = take(9)
        grads_in = take(9)
    else:
        heads_ref, hidden_ref = take(2)
        grads_in = take(9)
    if mode == "first":
        normed_ref, heads_ref, hidden_ref, wide_ref = take(4)
        outs = take(3)
        raw, part, sems = take(3)
    elif mode == "middle":
        normed_ref, grad_rows_ref, wide_ref, slim_ref = take(4)
        outs = take(3)
        grad_outs = take(3)
        part, grad_part, sems = take(3)
    else:
        grad_rows_ref, slim_ref = take(2)
        grad_outs = take(3)
        grad_part, sems = take(2)

    pairs = []
    if mode == "first":
        pairs += slot_copies(rows_in, 0, raw, core)
    if mode == "middle":
        pairs += slot_copies(rows_in, None, normed_ref, core)
        pairs += slot_copies(grads_in, 1, grad_rows_ref, core)
    if mode == "last":
        pairs += slot_copies(grads_in, None, grad_rows_ref, core)
    for copy in run_copies(pairs, sems, 0):
        copy.wait()

    total = allowed_ref.shape[0]
    block = allowed_ref.shape[1]
    step = 2 * block

    if mode == "first":
        tile = 32

        def norm_tile(i, carry):
            at = pl.ds(pl.multiple_of(i * tile, tile), tile)
            x = raw[at, :].astype(f32)
            centred = x - jnp.mean(x, axis=1, keepdims=True)
            inverse = lax.rsqrt(jnp.mean(centred * centred, axis=1, keepdims=True) + norm_epsilon)
            normed_ref[at, :] = (centred * inverse * gain_ref[...] + shift_ref[...]).astype(bf16)
            return carry

        lax.fori_loop(0, total // tile, norm_tile, 0)

    def one(p, carry):
        at = pl.ds(pl.multiple_of(p * step, step), step)
        if forward:
            before = dot(normed_ref[at, :], up_ref[...]) + bias_ref[...]
            hidden_pre = before[:, 3 * WIDE :]
        else:
            hidden_pre = hidden_ref[at, :]
        value, slope = gelu_parts(hidden_pre)
        if backward:
            grad_wide = dot(grad_rows_ref[at, :], down_ref[...], contract_last)
            slim_ref[at, 3 * WIDE :] = (grad_wide[:, WIDE:] * slope).astype(bf16)
        if forward:
            wide_ref[at, WIDE:] = value.astype(bf16)
        if mode == "first":
            hidden_ref[at, :] = hidden_pre
        for b in range(2):
            mine = slice(b * block, (b + 1) * block)
            own = pl.ds(pl.multiple_of(p * step + b * block, block), block)
            tables = (cos_ref[own, :], sin_up_ref[own, :], sin_down_ref[own, :])
            if forward:
                queries = turn(before[mine, :WIDE], *tables).astype(bf16)
                keys = turn(before[mine, WIDE : 2 * WIDE], *tables).astype(bf16)
                values = before[mine, 2 * WIDE : 3 * WIDE].astype(bf16)
            else:
                queries = heads_ref[own, :WIDE]
                keys = heads_ref[own, WIDE : 2 * WIDE]
                values = heads_ref[own, 2 * WIDE :]
            if mode == "first":
                heads_ref[own, :WIDE] = queries
                heads_ref[own, WIDE : 2 * WIDE] = keys
                heads_ref[own, 2 * WIDE :] = values
            chances = softmax_rows(queries, keys, allowed_ref[own, :])
            if forward:
                wide_ref[own, :WIDE] = heads_forward(chances, values)
            if backward:
                grads = heads_backward(
                    chances, queries, keys, values, grad_wide[mine, :WIDE].astype(bf16), tables
                )
                for n in range(3):
                    slim_ref[own, n * WIDE : (n + 1) * WIDE] = grads[n]
        if forward:
            part[at, :] = dot(wide_ref[at, :], down_ref[...]).astype(bf16)
        if backward:
            grad_part[at, :] = dot(slim_ref[at, :], up_ref[...], contract_last).astype(bf16)
        return carry

    lax.fori_loop(0, total // step, one, 0)
    pairs = []
    if backward:
        pairs += split_copies(grad_part, *grad_outs, core)
    if forward:
        pairs += split_copies(part, *outs, core)
    for copy in run_copies(pairs, sems, 0):
        copy.wait()


def call_pass(mode, core, weights, tables, allowed, extra, chunks):
    total, block = allowed.shape
    half = block // 2
    width = weights[0].shape[0]
    slim = weights[0].shape[1]
    wide = weights[1].shape[0]
    parts = [
        jax.ShapeDtypeStruct((half, width), bf16),
        jax.ShapeDtypeStruct((3 * block + half, width), bf16),
        jax.ShapeDtypeStruct((4 * block, width), bf16),
    ]
    full = jax.ShapeDtypeStruct((total, width), bf16)
    slim_rows = jax.ShapeDtypeStruct((total, slim), bf16)
    wide_rows = jax.ShapeDtypeStruct((total, wide), bf16)
    if mode == "first":
        kept = [
            full,
            jax.ShapeDtypeStruct((total, 3 * WIDE), bf16),
            jax.ShapeDtypeStruct((total, slim - 3 * WIDE), f32),
            wide_rows,
        ]
        buffers = 2
    elif mode == "middle":
        kept = [full, full, wide_rows, slim_rows]
        parts = parts * 2
        buffers = 2
    else:
        kept = [full, slim_rows]
        buffers = 1
    passes = 2 if mode == "middle" else 1
    return pl.pallas_call(
        partial(layer_pass, mode),
        in_specs=[SMEM_SPEC] + [VMEM_SPEC] * (6 + len(extra)) + [ANY_SPEC] * len(chunks),
        out_specs=[VMEM_SPEC] * len(kept) + [ANY_SPEC] * len(parts),
        out_shape=kept + parts,
        scratch_shapes=[pltpu.VMEM((total, width), bf16)] * buffers + [pltpu.SemaphoreType.DMA((18,))],
        cost_estimate=pl.CostEstimate(
            flops=6 * total * width * (slim + wide) * passes,
            bytes_accessed=20_000_000 * passes,
            transcendentals=total * slim,
        ),
        name="pass_" + mode,
    )(core, *weights, *tables, allowed, *extra, *chunks)


def gradient_slabs(own_rows, other_rows, with_sums, pieces_in, core_ref, left_ref, *rest):
    right_refs, (own_ref, other_ref, *rest) = rest[:pieces_in], rest[pieces_in:]
    turned_ref = rest[-1]
    if pieces_in == 1:
        right = right_refs[0][...]
    else:
        a, b = right_refs[-2][...], right_refs[-1][...]
        first = jnp.full(a.shape, core_ref[0]) == 0
        halves = [jnp.where(first, a, b), jnp.where(first, b, a)]
        right = jnp.concatenate([ref[...] for ref in right_refs[:-2]] + halves, axis=0)

    @pl.when(pl.program_id(0) == 0)
    def _():
        width = left_ref.shape[1]
        for n in range(width // 128):
            lanes = slice(n * 128, (n + 1) * 128)
            left = left_ref[:, lanes].astype(f32)
            if with_sums:
                rest[0][:, lanes] = jnp.sum(left, axis=0, keepdims=True)
            turned_ref[lanes, :] = left.T.astype(bf16)

    product = dot(turned_ref[...], right).astype(bf16)
    for ref, pieces in ((own_ref, own_rows), (other_ref, other_rows)):
        place = 0
        for first, last in pieces:
            for e in range(2):
                ref[e, place : place + last - first] = product[first:last, e * 128 : (e + 1) * 128]
            place += last - first


def call_gradients(core, left, right, own_rows, other_rows, with_sums, name):
    total, height = left.shape
    width = right[0].shape[1]
    rows = height // 2
    slab = pl.BlockSpec((2, rows, 128), lambda i: (i, 0, 0))
    shape = jax.ShapeDtypeStruct((width // 128, rows, 128), bf16)
    out_specs, out_shape = [slab, slab], [shape, shape]
    if with_sums:
        out_specs.append(pl.BlockSpec((1, height), lambda i: (0, 0)))
        out_shape.append(jax.ShapeDtypeStruct((1, height), f32))
    return pl.pallas_call(
        partial(gradient_slabs, own_rows, other_rows, with_sums, len(right)),
        grid=(width // 256,),
        in_specs=[SMEM_SPEC, pl.BlockSpec((total, height), lambda i: (0, 0))]
        + [pl.BlockSpec((x.shape[0], 256), lambda i: (0, i)) for x in right],
        out_specs=out_specs,
        out_shape=out_shape,
        scratch_shapes=[pltpu.VMEM((height, total), bf16)],
        cost_estimate=pl.CostEstimate(
            flops=4 * total * height * width, bytes_accessed=2 * (total * (width + height) + 2 * height * width), transcendentals=0
        ),
        name=name,
    )(core, left, *right)


def spread_gradients(up_ref, down_ref, *rest):
    qkv_ref, out_w_ref, fc1_ref, fc2_ref = rest[-4:]
    for p in range(3):
        rows = slice(p * HEAD_DIM, (p + 1) * HEAD_DIM)
        both = jnp.concatenate([up_ref[0, rows].astype(f32), up_ref[1, rows].astype(f32)], axis=0)
        qkv_ref[0, p] = both.T
    base = 3 * HEAD_DIM
    for d in range(2):
        for h in range(2):
            fc1_ref[0, :, (2 * d + h) * 128 : (2 * d + h + 1) * 128] = (
                up_ref[d, base + h * 128 : base + (h + 1) * 128].astype(f32).T
            )
        out_w_ref[0, d * HEAD_DIM : (d + 1) * HEAD_DIM] = down_ref[d, :HEAD_DIM].astype(f32)
        fc2_ref[0, d * 256 : (d + 1) * 256] = down_ref[d, HEAD_DIM:].astype(f32)


def call_spread(up, down, layer, filled):
    shapes = [
        jax.ShapeDtypeStruct((LAYERS, 3, 128, GROUP * HEAD_DIM), f32),
        jax.ShapeDtypeStruct((LAYERS, GROUP * HEAD_DIM, 128), f32),
        jax.ShapeDtypeStruct((LAYERS, 128, GROUP * 256), f32),
        jax.ShapeDtypeStruct((LAYERS, GROUP * 256, 128), f32),
    ]
    return pl.pallas_call(
        spread_gradients,
        grid=(GROUP // 2,),
        in_specs=[
            pl.BlockSpec((2, up.shape[1], 128), lambda i: (i, 0, 0)),
            pl.BlockSpec((2, down.shape[1], 128), lambda i: (i, 0, 0)),
        ]
        + [ANY_SPEC] * len(filled),
        out_specs=[
            pl.BlockSpec((1, 3, 128, 128), lambda i: (layer, 0, 0, i)),
            pl.BlockSpec((1, 128, 128), lambda i: (layer, i, 0)),
            pl.BlockSpec((1, 128, 512), lambda i: (layer, 0, i)),
            pl.BlockSpec((1, 512, 128), lambda i: (layer, i, 0)),
        ],
        out_shape=shapes,
        input_output_aliases={2 + n: n for n in range(len(filled))},
        name="spread_gradients",
    )(up, down, *filled)


def ring_total(core_ref, keep_ref, took_ref, moving_ref, got_ref):
    half = got_ref.shape[0]
    arrived = moving_ref[pl.ds(pl.multiple_of(core_ref[0] * half, half), half), :]
    return keep_ref[...].astype(f32) + took_ref[...].astype(f32) + arrived.astype(f32) + got_ref[...].astype(f32)


def centred_rows(state):
    centred = state - jnp.mean(state, axis=1, keepdims=True)
    return centred, lax.rsqrt(jnp.mean(centred * centred, axis=1, keepdims=True) + norm_epsilon)


def forward_end(last, core_ref, keep_ref, took_ref, moving_ref, got_ref, state_ref, after_ref, *rest):
    state = state_ref[...].astype(f32) + ring_total(core_ref, keep_ref, took_ref, moving_ref, got_ref) + after_ref[...]
    if last:
        rest[0][...] = state.astype(bf16)
        return
    gain_ref, shift_ref, state_out, normed_ref = rest
    state_out[...] = state
    centred, inverse = centred_rows(state)
    normed_ref[...] = (centred * inverse * gain_ref[...] + shift_ref[...]).astype(bf16)


def backward_end(core_ref, keep_ref, took_ref, moving_ref, got_ref, state_ref, grad_ref, gain_ref, grad_out, low_ref, sums_ref):
    grad_normed = ring_total(core_ref, keep_ref, took_ref, moving_ref, got_ref)
    centred, inverse = centred_rows(state_ref[...].astype(f32))
    xhat = centred * inverse
    before = grad_ref[...].astype(f32)
    sums_ref[0:1] = jnp.sum(grad_normed * xhat, axis=0, keepdims=True)
    sums_ref[1:2] = jnp.sum(grad_normed, axis=0, keepdims=True)
    sums_ref[2:3] = jnp.sum(before, axis=0, keepdims=True)
    scaled = grad_normed * gain_ref[...]
    after = before + (
        scaled - jnp.mean(scaled, axis=1, keepdims=True) - xhat * jnp.mean(scaled * xhat, axis=1, keepdims=True)
    ) * inverse
    grad_out[...] = after
    low_ref[...] = after.astype(bf16)


def call_end(body, core, ring, extra, shapes, name):
    keep, took, moving, got, n_sum = ring
    _, half, width = got.shape

    def rows_of(array):
        n = array.shape[0] // half - 1
        return pl.BlockSpec((half, width), lambda i: (n, 0))

    def whole_of(array):
        return pl.BlockSpec(array.shape, lambda i: (0,) * len(array.shape))

    def one_of(array):
        return pl.BlockSpec((None,) + array.shape[1:], lambda i: (n_sum, 0, 0))

    return pl.pallas_call(
        body,
        grid=(1,),
        in_specs=[SMEM_SPEC, rows_of(keep), rows_of(took), one_of(moving), one_of(got)] + [whole_of(x) for x in extra],
        out_specs=[whole_of(x) for x in shapes],
        out_shape=shapes,
        name=name,
    )(core, keep, took, moving, got, *extra)


def per_device(
    n_dp,
    hidden_in,
    seq_lengths,
    seq_device,
    positions,
    norm_gain,
    norm_bias,
    qkv_weight,
    qkv_bias,
    out_weight,
    fc1_weight,
    fc1_bias,
    fc2_weight,
    output_bias,
    out_cotangent,
):
    block = hidden_in.shape[0]
    half = block // 2
    width = hidden_in.shape[1]
    piece = norm_gain.shape[1]
    hidden = fc1_weight.shape[2] // GROUP
    groups = n_dp // GROUP
    chips = GROUP // 2
    side = chips // 2 - 1

    if groups == 1:
        ring = [2 * a for a in range(chips // 2)] + [2 * a + 1 for a in reversed(range(chips // 2))]
    else:
        ring = list(range(chips // 2)) + list(reversed(range(chips // 2, chips)))
    ring_pairs = []
    for g in range(groups):
        for place in range(chips):
            for core, step in ((0, 1), (1, -1)):
                ring_pairs.append(
                    (
                        g * GROUP + ring[place] * 2 + core,
                        g * GROUP + ring[(place + step) % chips] * 2 + core,
                    )
                )
    core_pairs = [(i, i ^ 1) for i in range(n_dp)]
    inner = [[g * GROUP + i for i in range(GROUP)] for g in range(groups)]
    outer = [[g * GROUP + i for g in range(groups)] for i in range(GROUP)]
    if groups == 1:
        inner = None

    def along(x):
        return lax.ppermute(x, "dp", ring_pairs)

    def across(x):
        return lax.ppermute(x, "dp", core_pairs)

    def over(x):
        return lax.ppermute(x, "tensor", [(0, 1), (1, 0)])

    index = lax.axis_index("dp")
    group = index // GROUP
    chip = (index % GROUP) // 2
    core = index % 2
    tensor = lax.axis_index("tensor")
    is_first = core == 0
    at = core * half
    off = (1 - core) * half
    core_word = core.astype(jnp.int32).reshape(1)

    def my_half(x, start, axis=0):
        return lax.dynamic_slice_in_dim(x, start, half, axis)

    def in_order(own, other):
        return jnp.where(
            is_first, jnp.concatenate([own, other], 0), jnp.concatenate([other, own], 0)
        )

    def gather_rows(mine, needed={}):
        behind, ahead = [], []
        moving = mine
        for step in range(side):
            moving = along(after(moving, *needed.get(step, ())))
            behind.append(moving)
            ahead.append(across(moving))
        far = along(after(my_half(moving, at, moving.ndim - 2), *needed.get(side, ())))
        return [mine] + behind + ahead + [far, across(far)]

    rows = lax.broadcasted_iota(jnp.int32, (block, 1), 0)
    mine_rows = (rows < half) == is_first

    def ring_sum(*sets, needed={}):
        took_far = [across(give_far) for give_far, _, _ in sets]
        took = [across(give) for _, give, _ in sets]
        keep = [x for _, _, x in sets]
        far = [k[side * block : side * block + half].astype(f32) + t.astype(f32) for k, t in zip(keep, took_far)]
        moving = along(jnp.stack(far).astype(bf16))
        moving = jnp.where(mine_rows, jnp.concatenate([moving, moving], 1), 0).astype(f32)
        for step in reversed(range(side)):
            here = slice(step * block, (step + 1) * block)
            moving = after(moving, *needed.get(step, ()))
            added = [k[here].astype(f32) + t[here].astype(f32) for k, t in zip(keep, took)]
            moving = along((moving + jnp.stack(added)).astype(bf16))
            if step:
                moving = moving.astype(f32)
        got = across(my_half(moving, off, 1))
        return [(k, t, moving, got, n) for n, (k, t) in enumerate(zip(keep, took))]

    def spread(x):
        return lax.all_to_all(x, "dp", 0, 0, axis_index_groups=inner, tiled=True)

    small = jnp.concatenate(
        [
            norm_gain.reshape(-1),
            norm_bias.reshape(-1),
            output_bias.reshape(-1),
            (positions // 64).astype(bf16),
            (positions % 64).astype(bf16),
        ]
    )
    weights = []
    if groups == 1:
        qkv_turned = qkv_weight.transpose(0, 2, 1, 3)
        ups, downs = (qkv_turned, fc1_weight), (out_weight, fc2_weight)
        extra = jnp.concatenate([small, jnp.zeros_like(small)]).reshape(-1, 128)
        up = spread(call_pack(pack_first, 0, ups, (), (extra,)))
        small_all = up[:, UP_ROWS:].reshape(GROUP, -1)[:, : small.shape[0]]
        up_other = over(up)
        packed_down = call_pack(pack_down, 0, (), downs, ())
        down = spread(after(packed_down, up))
        down_other = over(down)
        weights.append(call_join(join_up, up, [up_other], True, False) + call_join(join_down, down, [down_other], False, True))
        packed_last = call_pack(pack_both, 1, ups, downs, ())
        firsts = (up, up_other, down)
    else:
        small_all = lax.all_gather(small, "dp", axis=0, tiled=False)
        for layer in range(LAYERS):
            up = jnp.concatenate(
                [
                    qkv_weight[layer].reshape(piece, 3, GROUP, HEAD_DIM).transpose(2, 0, 1, 3).reshape(GROUP, piece, -1),
                    fc1_weight[layer].reshape(piece, GROUP, hidden).transpose(1, 0, 2),
                ],
                axis=2,
            )
            up = lax.all_gather(spread(up), "dp", axis=0, axis_index_groups=outer, tiled=True)
            up = up.reshape(width // 128, 128, UP_ROWS)
            value = up[:, :, WIDE : WIDE + HEAD_DIM]
            first = WIDE + HEAD_DIM
            up = jnp.concatenate(
                [
                    up[:, :, :WIDE],
                    jnp.concatenate([value[:, :HEAD_DIM], value[:, HEAD_DIM:]], axis=2),
                    up[:, :, first : first + 128],
                    up[:, :, first + 128 :],
                ],
                axis=1,
            )
            down = jnp.concatenate(
                [out_weight[layer].reshape(GROUP, HEAD_DIM, piece), fc2_weight[layer].reshape(GROUP, hidden, piece)],
                axis=1,
            )
            down = lax.all_gather(spread(down), "dp", axis=0, axis_index_groups=outer, tiled=True)
            down = down.transpose(1, 0, 2).reshape(-1, width // 128, 128).transpose(1, 0, 2)
            weights.append(call_join(join_up, up, [over(up)], True, False) + call_join(join_down, down, [over(down)], False, True))
    if groups == 1:
        biases = jnp.concatenate([qkv_bias.reshape(LAYERS, 3 * HEAD_DIM), fc1_bias], axis=1)
    else:
        full_qkv = lax.all_gather(qkv_bias, "dp", axis=2, tiled=True)
        full_up = lax.all_gather(fc1_bias, "dp", axis=1, tiled=True)
        member = index % GROUP
        biases = jnp.concatenate(
            [
                lax.dynamic_slice_in_dim(full_qkv, member * HEAD_DIM, HEAD_DIM, 2).reshape(LAYERS, 3 * HEAD_DIM),
                lax.dynamic_slice_in_dim(full_up, member * hidden, hidden, 1),
            ],
            axis=1,
        )
    biases_other = over(biases)
    both_biases = jnp.stack([biases, biases_other], axis=1).astype(f32)
    bias_rows = jnp.concatenate(
        [
            both_biases[:, :, : 3 * HEAD_DIM].reshape(LAYERS, 2, 3, HEAD_DIM).transpose(0, 2, 1, 3).reshape(LAYERS, -1),
            both_biases[:, :, 3 * HEAD_DIM :].reshape(LAYERS, -1),
        ],
        axis=1,
    )
    vectors = small_all[:, : 6 * piece].reshape(n_dp, 3, LAYERS, piece).transpose(1, 2, 0, 3).reshape(3, LAYERS, 1, width).astype(f32)
    gains, shifts, added_bias = vectors[0], vectors[1], vectors[2]

    turned = jnp.where(is_first, 1, -1)
    place = jnp.sum(jnp.where(jnp.asarray(ring) == chip, jnp.arange(chips), 0))
    offsets = [0] + [-(s + 1) for s in range(side)] + [s + 1 for s in range(side)] + [chips // 2]
    places = (place + turned * jnp.asarray(offsets)) % chips
    chip_ids = jnp.sum(
        jnp.where(places[:, None] == jnp.arange(chips)[None, :], jnp.asarray(ring)[None, :], 0), axis=1
    )
    owners = group * GROUP + 2 * chip_ids + tensor
    labels = jax.vmap(lambda owner: sequence_labels(seq_lengths, seq_device, owner, block))(owners)
    rows_at = jnp.arange(block, dtype=jnp.int32)
    allowed = (
        (labels[:, :, None] == labels[:, None, :])
        & (labels[:, :, None] > 0)
        & (rows_at[None, None, :] <= rows_at[None, :, None])
    ) | (rows_at[None, None, :] == rows_at[None, :, None])
    allowed = allowed.astype(f32).reshape(chips * block, block)
    picked = (owners[:, None] == jnp.arange(n_dp)[None, :]).astype(f32)
    place_parts = jnp.dot(picked, small_all[:, 6 * piece :].astype(f32), precision=lax.Precision.HIGHEST)
    row_places = (place_parts[:, :block] * 64.0 + place_parts[:, block:]).reshape(chips * block)
    pair = ROT // 2
    frequency = 10000.0 ** (-2.0 * jnp.arange(pair, dtype=f32) / ROT)
    angles = row_places[:, None] * frequency[None, :]
    cosine, sine = jnp.cos(angles), jnp.sin(angles)
    nought = jnp.zeros_like(sine)
    rest = jnp.zeros((chips * block, HEAD_DIM - ROT), f32)
    tables = (
        jnp.concatenate([cosine, cosine, rest + 1.0] * 2, axis=1),
        jnp.concatenate([-sine, nought, rest] * 2, axis=1),
        jnp.concatenate([nought, sine, rest] * 2, axis=1),
    )

    both = jnp.stack([hidden_in, out_cotangent])
    both = jnp.where(tensor == core, both, across(both))
    keeps = jnp.stack([jnp.ones_like(labels[0]), (labels[0] > 0).astype(labels.dtype)]).astype(bf16)
    both = both * keeps[:, :, None]
    if groups == 1:
        inputs = gather_rows(after(both, packed_down, packed_last, *firsts), {side: (down_other,)})
        slab = spread(after(packed_last, inputs[-2]))
        others = tuple(over(slab[n * GROUP // 2 : (n + 1) * GROUP // 2]) for n in range(2))
        weights.append(call_join(join_halves, slab, others, True, True))
        slabs = (slab,)
    else:
        inputs = gather_rows(both)
        slabs, others = (), ()
    mine_inputs = my_half(both, at, 1)
    state, grad_state = mine_inputs[0], mine_inputs[1]

    normed, heads, hidden_pre, wide, *parts = call_pass(
        "first", core_word, weights[0], tables, allowed, [bias_rows[0:1], gains[0], shifts[0]], inputs
    )
    rows_shape = (half, width)
    next_state, normed_own = call_end(
        partial(forward_end, False),
        core_word,
        ring_sum((after(parts[0], *slabs), parts[1], parts[2]), needed={0: others[:1]})[0],
        [state, added_bias[0], gains[1], shifts[1]],
        [jax.ShapeDtypeStruct(rows_shape, f32), jax.ShapeDtypeStruct(rows_shape, bf16)],
        "forward_end",
    )
    normed_chunks = gather_rows(in_order(normed_own, across(normed_own)), {1: others[1:]})

    def handed_back(own_rows):
        filled = in_order(own_rows, across(own_rows))
        return jnp.where(tensor == core, filled, over(filled))

    def summed(own, other, *earlier, extra=None):
        total = own.astype(f32) + other.astype(f32)
        if groups > 1:
            total = total.transpose(1, 0, 2).reshape(total.shape[1], width)
            total = lax.psum_scatter(total, "dp", scatter_dimension=1, axis_index_groups=outer, tiled=True)
            total = total.reshape(total.shape[0], GROUP, piece).transpose(1, 0, 2)
        total = total.astype(bf16)
        if extra is not None:
            total = jnp.concatenate([total, extra], axis=1)
        return spread(after(total, *earlier))

    down_own = [(0, HEAD_DIM), (WIDE, WIDE + hidden)]
    down_other = [(HEAD_DIM, WIDE), (WIDE + hidden, WIDE + 2 * hidden)]
    up_own = [(p * WIDE, p * WIDE + HEAD_DIM) for p in range(3)] + [(3 * WIDE, 3 * WIDE + hidden)]
    up_other = [(p * WIDE + HEAD_DIM, (p + 1) * WIDE) for p in range(3)] + [(3 * WIDE + hidden, 3 * WIDE + 2 * hidden)]

    def down_gradients(wide_rows, grad_rows):
        return call_gradients(core_word, wide_rows, grad_rows, down_own, down_other, False, "down_gradients")

    def up_gradients(slim_rows, normed_rows):
        return call_gradients(core_word, slim_rows, [normed_rows], up_own, up_other, True, "up_gradients")

    def backward_finish(ring_end, state, grad_state, layer):
        return call_end(
            backward_end,
            core_word,
            ring_end,
            [state, grad_state, gains[layer]],
            [
                jax.ShapeDtypeStruct(rows_shape, f32),
                jax.ShapeDtypeStruct(rows_shape, bf16),
                jax.ShapeDtypeStruct((3, width), f32),
            ],
            "backward_end",
        )

    normed_last, grad_rows, wide_last, slim, *parts = call_pass(
        "middle", core_word, weights[1], tables, allowed, [bias_rows[1:2]], normed_chunks + inputs
    )
    out_parts = parts[:3]
    down_pair = down_gradients(wide_last, [grad_rows])
    *up_pair, bias_last = up_gradients(slim, normed_last)
    down_sent, up_sent = over(down_pair[1]), over(up_pair[1])
    grad_end, out_end = ring_sum(parts[3:], out_parts, needed={1: (down_pair[0], up_pair[0]), 0: (down_sent,)})
    grad_state, grad_low, sums_last = backward_finish(grad_end, next_state, grad_state, 1)
    (hidden_out,) = call_end(
        partial(forward_end, True),
        core_word,
        out_end,
        [next_state, added_bias[1]],
        [jax.ShapeDtypeStruct(rows_shape, bf16)],
        "forward_out",
    )
    hidden_out = handed_back(hidden_out)
    down_last = summed(down_pair[0], after(down_sent, grad_low))
    grad_chunks = gather_rows(in_order(grad_low, across(grad_low)), {2: (up_sent,), side: (down_last, hidden_out)})
    up_last = summed(up_pair[0], after(up_sent, grad_chunks[-2]), down_last)

    down_pair = down_gradients(wide, grad_chunks)
    down_sent = over(down_pair[1])
    grad_rows, slim, *parts = call_pass(
        "last", core_word, weights[0], tables, allowed, [heads, after(hidden_pre, down_pair[0])], grad_chunks
    )
    down_first = summed(down_pair[0], after(down_sent, slim), up_last)
    *up_pair, bias_first = up_gradients(slim, after(normed, up_last))
    up_sent = over(up_pair[1])
    (grad_end,) = ring_sum((after(parts[0], up_pair[0]), parts[1], parts[2]), needed={1: (down_first,)})
    _, grad_low, sums_first = backward_finish(grad_end, state, grad_state, 0)
    grad_hidden = handed_back(grad_low).astype(f32)

    vectors = jnp.stack([sums_first, sums_last]).reshape(LAYERS * 3, n_dp, piece).transpose(1, 0, 2)
    if groups == 1:
        extra = jnp.pad(vectors, ((0, 0), (0, 16 - LAYERS * 3), (0, 0))).astype(bf16)
        up_first = summed(up_pair[0], up_sent, down_first, extra=extra)
        vectors = up_first[:, UP_ROWS : UP_ROWS + LAYERS * 3].astype(f32)
    else:
        up_first = summed(up_pair[0], up_sent, down_first)
        vectors = lax.all_to_all(vectors, "dp", 0, 0, tiled=True)
    vectors = jnp.sum(vectors, axis=0)
    vectors = (vectors + over(vectors)).reshape(LAYERS, 3, piece)
    sums = jnp.concatenate([bias_first, bias_last], axis=0)
    sums_qkv = sums[:, : 3 * WIDE].reshape(LAYERS, 3, 2, HEAD_DIM)
    sums_up = sums[:, 3 * WIDE :].reshape(LAYERS, 2, hidden)
    bias_own, bias_other = (
        jnp.concatenate([sums_qkv[:, :, n].reshape(LAYERS, -1), sums_up[:, n]], axis=1) for n in range(2)
    )
    bias_sums = bias_own + over(bias_other)
    bias_qkv, bias_up = bias_sums[:, : 3 * HEAD_DIM].reshape(LAYERS, 3, HEAD_DIM), bias_sums[:, 3 * HEAD_DIM :]
    if groups == 1:
        filled = call_spread(up_last, down_last, 1, [])
        grad_qkv, grad_out, grad_up, grad_down = call_spread(up_first, down_first, 0, filled)
        grad_qkv = grad_qkv.transpose(0, 2, 1, 3)
    else:
        bias_qkv = lax.all_gather(lax.psum(bias_qkv, "dp", axis_index_groups=outer), "dp", axis=2, axis_index_groups=inner, tiled=True)
        bias_up = lax.all_gather(lax.psum(bias_up, "dp", axis_index_groups=outer), "dp", axis=1, axis_index_groups=inner, tiled=True)
        bias_qkv = lax.dynamic_slice_in_dim(bias_qkv, index * qkv_bias.shape[2], qkv_bias.shape[2], 2)
        bias_up = lax.dynamic_slice_in_dim(bias_up, index * fc1_bias.shape[1], fc1_bias.shape[1], 1)
        ups = jnp.stack([up_first, up_last]).astype(f32)
        downs = jnp.stack([down_first, down_last]).astype(f32)
        grad_qkv = ups[:, :, : 3 * HEAD_DIM].reshape(LAYERS, GROUP, 3, HEAD_DIM, piece).transpose(0, 4, 2, 1, 3).reshape(LAYERS, piece, 3, -1)
        grad_up = ups[:, :, 3 * HEAD_DIM :].transpose(0, 3, 1, 2).reshape(LAYERS, piece, -1)
        grad_out = downs[:, :, :HEAD_DIM].reshape(LAYERS, -1, piece)
        grad_down = downs[:, :, HEAD_DIM:].reshape(LAYERS, -1, piece)
    return (
        hidden_out,
        grad_hidden,
        vectors[:, 0],
        vectors[:, 1],
        grad_qkv,
        bias_qkv,
        grad_out,
        grad_up,
        bias_up,
        grad_down,
        vectors[:, 2],
    )


def solution(mesh):
    placed = (
        P("dp", None),
        P(),
        P(),
        P("dp"),
        P(None, "dp"),
        P(None, "dp"),
        P(None, "dp", None, "tensor"),
        P(None, None, ("tensor", "dp")),
        P(None, "tensor", "dp"),
        P(None, "dp", "tensor"),
        P(None, ("tensor", "dp")),
        P(None, "tensor", "dp"),
        P(None, "dp"),
        P("dp", None),
    )
    return jax.shard_map(
        partial(per_device, mesh.shape["dp"]),
        mesh=mesh,
        in_specs=placed,
        out_specs=(
            P("dp", None),
            P("dp", None),
            P(None, "dp"),
            P(None, "dp"),
            P(None, "dp", None, "tensor"),
            P(None, None, ("tensor", "dp")),
            P(None, "tensor", "dp"),
            P(None, "dp", "tensor"),
            P(None, ("tensor", "dp")),
            P(None, "tensor", "dp"),
            P(None, "dp"),
        ),
        check_vma=False,
    )
```

```python
from functools import partial

import jax
import jax.numpy as jnp
from jax import lax
from jax.experimental import pallas as pl
from jax.experimental.pallas import tpu as pltpu
from jax.sharding import PartitionSpec as P

HEAD_DIM = 64
ROT = 32
LAYERS = 2
GROUP = 16

norm_epsilon = 1e-05
masked_score = -1e30
bf16 = jnp.bfloat16
f32 = jnp.float32

contract_last = (((1,), (1,)), ((), ()))
contract_first = (((0,), (0,)), ((), ()))


def dot(a, b, dims=(((1,), (0,)), ((), ()))):
    return lax.dot_general(a, b, dims, preferred_element_type=f32)


def turn(x, cosine, up, down):
    return x * cosine + pltpu.roll(x, x.shape[1] - ROT // 2, 1) * up + pltpu.roll(x, ROT // 2, 1) * down


def stacked_heads(x):
    lane = lax.broadcasted_iota(jnp.int32, x.shape, 1)
    zero = jnp.zeros_like(x)
    return jnp.concatenate(
        [jnp.where(lane < HEAD_DIM, x, zero), jnp.where(lane < HEAD_DIM, zero, x)], axis=0
    )


def merged_heads(x):
    rows = x.shape[0] // 2
    lane = lax.broadcasted_iota(jnp.int32, (rows, x.shape[1]), 1)
    return jnp.where(lane < HEAD_DIM, x[:rows], x[rows:])


def softmax_rows(queries, keys, allowed):
    scores = dot(stacked_heads(queries), keys, contract_last) * HEAD_DIM ** (-0.5)
    masked = jnp.where(jnp.concatenate([allowed, allowed], axis=0) > 0, scores, masked_score)
    weights = jnp.exp(masked - jnp.max(masked, axis=1, keepdims=True))
    return weights / jnp.sum(weights, axis=1, keepdims=True)


def sequence_labels(seq_lengths, seq_device, owner, count_rows):
    index = jnp.arange(seq_lengths.shape[0], dtype=jnp.int32)
    owned = jnp.where(seq_device == owner, seq_lengths, 0)
    earlier = index[None, :] < index[:, None]
    starts = jnp.sum(jnp.where(earlier, owned[None, :], 0), axis=1)
    places = jnp.arange(count_rows, dtype=jnp.int32)
    inside = (places[:, None] >= starts[None, :]) & (places[:, None] < (starts + owned)[None, :])
    return jnp.sum(jnp.where(inside, index[None, :] + 1, 0), axis=1)


def gelu_parts(v):
    c = (2.0 / jnp.pi) ** 0.5
    inner = jnp.tanh(c * (v + 0.044715 * v * v * v))
    value = 0.5 * v * (1.0 + inner)
    slope = 0.5 * (1.0 + inner) + 0.5 * v * (1.0 - inner * inner) * c * (1.0 + 3.0 * 0.044715 * v * v)
    return value, slope


VMEM_SPEC = pl.BlockSpec(memory_space=pltpu.VMEM)
ANY_SPEC = pl.BlockSpec(memory_space=pl.ANY)
SMEM_SPEC = pl.BlockSpec(memory_space=pltpu.SMEM)
WIDE = 2 * HEAD_DIM
UP_ROWS = 3 * HEAD_DIM + 256
DOWN_ROWS = HEAD_DIM + 256
SUM_ROWS = 16
MEMBERS = 4


def after(x, *others):
    if not others:
        return x
    return lax.optimization_barrier((x, *others))[0]


def left_lanes(x):
    return lax.broadcasted_iota(jnp.int32, x.shape, 1) < HEAD_DIM


def swapped(x):
    return pltpu.roll(x, HEAD_DIM, 1)


def zipped(a, b):
    left = left_lanes(a)
    return jnp.where(left, a, swapped(b)).astype(bf16), jnp.where(left, swapped(a), b).astype(bf16)


def pack_up(qkv_ref, fc1_ref, *rest):
    out_ref = rest[-1]
    for pair in range(MEMBERS // 2):
        lanes = slice(pair * 128, (pair + 1) * 128)
        q, k, v = (qkv_ref[0, p, :, lanes].astype(f32) for p in range(3))
        here, there = 2 * pair, 2 * pair + 1
        out_ref[here, :WIDE], out_ref[there, :WIDE] = zipped(q, k)
        rows = q.shape[0] // 2
        out_ref[here, WIDE : WIDE + rows], out_ref[there, WIDE : WIDE + rows] = zipped(v[:rows], v[rows:])
        base = WIDE + rows
        for d in (here, there):
            for h in range(2):
                out_ref[d, base + h * 128 : base + (h + 1) * 128] = fc1_ref[0, :, (2 * d + h) * 128 : (2 * d + h + 1) * 128]


def pack_first(qkv_ref, fc1_ref, small_ref, out_ref):
    pack_up(qkv_ref, fc1_ref, out_ref)
    for d in range(MEMBERS):
        out_ref[d, UP_ROWS:] = small_ref[...]


def pack_both(qkv_ref, fc1_ref, out_w_ref, fc2_ref, out_ref):
    pack_up(qkv_ref, fc1_ref, out_ref)
    pack_down(out_w_ref, fc2_ref, out_ref.at[:, UP_ROWS:])


def pack_down(out_w_ref, fc2_ref, out_ref):
    for d in range(MEMBERS):
        out_ref[d, :HEAD_DIM] = out_w_ref[0, d * HEAD_DIM : (d + 1) * HEAD_DIM]
        out_ref[d, HEAD_DIM:] = fc2_ref[0, d * 256 : (d + 1) * 256]


def call_pack(body, layer, ups, downs, small):
    rows, specs = 0, []
    if ups:
        rows += UP_ROWS
        specs += [
            pl.BlockSpec((1, 3, 128, MEMBERS * HEAD_DIM), lambda i: (layer, 0, 0, i)),
            pl.BlockSpec((1, 128, MEMBERS * 256), lambda i: (layer, 0, i)),
        ]
    if downs:
        rows += DOWN_ROWS
        specs += [
            pl.BlockSpec((1, MEMBERS * HEAD_DIM, 128), lambda i: (layer, i, 0)),
            pl.BlockSpec((1, MEMBERS * 256, 128), lambda i: (layer, i, 0)),
        ]
    if small:
        rows += small[0].shape[0]
        specs.append(pl.BlockSpec(small[0].shape, lambda i: (0, 0)))
    return pl.pallas_call(
        body,
        grid=(GROUP // MEMBERS,),
        in_specs=specs,
        out_specs=pl.BlockSpec((MEMBERS, rows, 128), lambda i: (i, 0, 0)),
        out_shape=jax.ShapeDtypeStruct((GROUP, rows, 128), bf16),
        cost_estimate=pl.CostEstimate(flops=0, bytes_accessed=GROUP * rows * 128 * 8, transcendentals=0),
        name=body.__name__,
    )(*ups, *downs, *small)


def join_up(own_ref, other_ref, out_ref):
    for e in range(MEMBERS):
        rows = slice(e * 128, (e + 1) * 128)
        a, b = own_ref[e, :WIDE].astype(f32), other_ref[e, :WIDE].astype(f32)
        out_ref[rows, :WIDE], out_ref[rows, WIDE : 2 * WIDE] = zipped(a, b)
        a, b = own_ref[e, WIDE : WIDE + 64].astype(f32), other_ref[e, WIDE : WIDE + 64].astype(f32)
        top, bottom = zipped(a, b)
        out_ref[e * 128 : e * 128 + 64, 2 * WIDE : 3 * WIDE] = top
        out_ref[e * 128 + 64 : (e + 1) * 128, 2 * WIDE : 3 * WIDE] = bottom
        for n, ref in enumerate((own_ref, other_ref)):
            for h in range(2):
                lanes = 3 * WIDE + n * 256 + h * 128
                out_ref[rows, lanes : lanes + 128] = ref[e, WIDE + 64 + h * 128 : WIDE + 64 + (h + 1) * 128]


def join_down(own_ref, other_ref, out_ref):
    base = own_ref.shape[1] - DOWN_ROWS
    for e in range(MEMBERS):
        lanes = slice(e * 128, (e + 1) * 128)
        for n, ref in enumerate((own_ref, other_ref)):
            out_ref[n * HEAD_DIM : (n + 1) * HEAD_DIM, lanes] = ref[e, base : base + HEAD_DIM]
            out_ref[WIDE + n * 256 : WIDE + (n + 1) * 256, lanes] = ref[e, base + HEAD_DIM :]


def join_both(own_ref, other_ref, up_ref, down_ref):
    join_up(own_ref, other_ref, up_ref)
    join_down(own_ref, other_ref, down_ref)


def join_halves(own_ref, lower_ref, upper_ref, up_ref, down_ref):
    lower = pl.program_id(0) < GROUP // MEMBERS // 2

    @pl.when(lower)
    def _():
        join_both(own_ref, lower_ref, up_ref, down_ref)

    @pl.when(jnp.logical_not(lower))
    def _():
        join_both(own_ref, upper_ref, up_ref, down_ref)


def call_join(body, own, others, ups, downs):
    rows = own.shape[1]
    steps = GROUP // MEMBERS
    spec = pl.BlockSpec((MEMBERS, rows, 128), lambda i: (i, 0, 0))
    other_specs = [spec]
    if len(others) == 2:
        other_specs = [
            pl.BlockSpec((MEMBERS, rows, 128), lambda i: (jnp.minimum(i, steps // 2 - 1), 0, 0)),
            pl.BlockSpec((MEMBERS, rows, 128), lambda i: (jnp.maximum(i - steps // 2, 0), 0, 0)),
        ]
    specs, shapes = [], []
    if ups:
        specs.append(pl.BlockSpec((MEMBERS * 128, 2 * UP_ROWS), lambda i: (i, 0)))
        shapes.append(jax.ShapeDtypeStruct((GROUP * 128, 2 * UP_ROWS), bf16))
    if downs:
        specs.append(pl.BlockSpec((2 * DOWN_ROWS, MEMBERS * 128), lambda i: (0, i)))
        shapes.append(jax.ShapeDtypeStruct((2 * DOWN_ROWS, GROUP * 128), bf16))
    return pl.pallas_call(
        body,
        grid=(GROUP // MEMBERS,),
        in_specs=[spec] + other_specs,
        out_specs=specs,
        out_shape=shapes,
        cost_estimate=pl.CostEstimate(flops=0, bytes_accessed=GROUP * rows * 128 * 12, transcendentals=0),
        name=body.__name__,
    )(own, *others)


def slot_copies(refs, which, target, core):
    block = target.shape[0] // 8
    half = block // 2
    pairs = []
    for slot in range(7):
        ref = refs[slot] if which is None else refs[slot].at[which]
        pairs.append((ref, target.at[pl.ds(slot * block, block)]))
    for n, at in ((7, core * half), (8, (1 - core) * half)):
        ref = refs[n] if which is None else refs[n].at[which]
        pairs.append((ref, target.at[pl.ds(pl.multiple_of(7 * block + at, half), half)]))
    return pairs


def split_copies(part, far_ref, give_ref, keep_ref, core):
    block = part.shape[0] // 8
    half = block // 2
    at, off = core * half, (1 - core) * half

    def rows(slot, start):
        return part.at[pl.ds(pl.multiple_of(slot * block + start, half), half)]

    return [
        (rows(7, off), far_ref),
        (part.at[pl.ds(block, 3 * block)], give_ref.at[pl.ds(0, 3 * block)]),
        (rows(0, off), give_ref.at[pl.ds(3 * block, half)]),
        (part.at[pl.ds(4 * block, 3 * block)], keep_ref.at[pl.ds(0, 3 * block)]),
        (rows(7, at), keep_ref.at[pl.ds(3 * block, half)]),
        (rows(0, at), keep_ref.at[pl.ds(3 * block + half, half)]),
    ]


def run_copies(pairs, sems, first):
    made = [pltpu.make_async_copy(a, b, sems.at[first + n]) for n, (a, b) in enumerate(pairs)]
    for copy in made:
        copy.start()
    return made


def heads_forward(chances, values):
    return merged_heads(dot(chances.astype(bf16), values)).astype(bf16)


def heads_backward(chances, queries, keys, values, grad, tables):
    grads = stacked_heads(grad)
    grad_chances = dot(grads, values, contract_last)
    grad_values = dot(chances.astype(bf16), grads, contract_first)
    centre = jnp.sum(grad_chances * chances, axis=1, keepdims=True)
    grad_scores = (chances * (grad_chances - centre)).astype(bf16)
    scale = HEAD_DIM ** (-0.5)
    grad_queries = merged_heads(dot(grad_scores, keys)) * scale
    grad_keys = dot(grad_scores, stacked_heads(queries), contract_first) * scale
    cosine, up, down = tables
    back = (cosine, -up, -down)
    return turn(grad_queries, *back).astype(bf16), turn(grad_keys, *back).astype(bf16), grad_values.astype(bf16)


def layer_pass(mode, *refs):
    refs = list(refs)

    def take(n):
        out = refs[:n]
        del refs[:n]
        return out

    forward, backward = mode != "last", mode != "first"
    core_ref, up_ref, down_ref, cos_ref, sin_up_ref, sin_down_ref, allowed_ref = take(7)
    core = core_ref[0]
    if mode == "first":
        bias_ref, gain_ref, shift_ref = take(3)
        rows_in = take(9)
    elif mode == "middle":
        (bias_ref,) = take(1)
        rows_in = take(9)
        grads_in = take(9)
    else:
        heads_ref, hidden_ref, normed_ref = take(3)
        grads_in = take(9)
    if mode == "first":
        normed_ref, heads_ref, hidden_ref, wide_ref = take(4)
        outs = take(3)
        raw, part, sems = take(3)
    elif mode == "middle":
        normed_ref, grad_rows_ref, wide_ref, slim_ref, sums_ref = take(5)
        outs = take(3)
        grad_outs = take(3)
        part, grad_part, sems = take(3)
    else:
        grad_rows_ref, slim_ref, sums_ref = take(3)
        grad_outs = take(3)
        grad_part, sems = take(2)

    pairs = []
    if mode == "first":
        pairs += slot_copies(rows_in, 0, raw, core)
    if mode == "middle":
        pairs += slot_copies(rows_in, None, normed_ref, core)
        pairs += slot_copies(grads_in, 1, grad_rows_ref, core)
    if mode == "last":
        pairs += slot_copies(grads_in, None, grad_rows_ref, core)
    for copy in run_copies(pairs, sems, 0):
        copy.wait()

    total = allowed_ref.shape[0]
    block = allowed_ref.shape[1]
    step = 2 * block

    if mode == "first":
        tile = 32

        def norm_tile(i, carry):
            at = pl.ds(pl.multiple_of(i * tile, tile), tile)
            x = raw[at, :].astype(f32)
            centred = x - jnp.mean(x, axis=1, keepdims=True)
            inverse = lax.rsqrt(jnp.mean(centred * centred, axis=1, keepdims=True) + norm_epsilon)
            normed_ref[at, :] = (centred * inverse * gain_ref[...] + shift_ref[...]).astype(bf16)
            return carry

        lax.fori_loop(0, total // tile, norm_tile, 0)

    if backward:
        sums_ref[...] = jnp.zeros_like(sums_ref)

    def one(p, carry):
        at = pl.ds(pl.multiple_of(p * step, step), step)
        if forward:
            before = dot(normed_ref[at, :], up_ref[...]) + bias_ref[...]
            hidden_pre = before[:, 3 * WIDE :]
        else:
            hidden_pre = hidden_ref[at, :]
        value, slope = gelu_parts(hidden_pre)
        if backward:
            grad_wide = dot(grad_rows_ref[at, :], down_ref[...], contract_last)
            slim_ref[at, 3 * WIDE :] = (grad_wide[:, WIDE:] * slope).astype(bf16)
        if forward:
            wide_ref[at, WIDE:] = value.astype(bf16)
        if mode == "first":
            hidden_ref[at, :] = hidden_pre
        for b in range(2):
            mine = slice(b * block, (b + 1) * block)
            own = pl.ds(pl.multiple_of(p * step + b * block, block), block)
            tables = (cos_ref[own, :], sin_up_ref[own, :], sin_down_ref[own, :])
            if forward:
                queries = turn(before[mine, :WIDE], *tables).astype(bf16)
                keys = turn(before[mine, WIDE : 2 * WIDE], *tables).astype(bf16)
                values = before[mine, 2 * WIDE : 3 * WIDE].astype(bf16)
            else:
                queries = heads_ref[own, :WIDE]
                keys = heads_ref[own, WIDE : 2 * WIDE]
                values = heads_ref[own, 2 * WIDE :]
            if mode == "first":
                heads_ref[own, :WIDE] = queries
                heads_ref[own, WIDE : 2 * WIDE] = keys
                heads_ref[own, 2 * WIDE :] = values
            chances = softmax_rows(queries, keys, allowed_ref[own, :])
            if forward:
                wide_ref[own, :WIDE] = heads_forward(chances, values)
            if backward:
                grads = heads_backward(
                    chances, queries, keys, values, grad_wide[mine, :WIDE].astype(bf16), tables
                )
                for n in range(3):
                    slim_ref[own, n * WIDE : (n + 1) * WIDE] = grads[n]
        if forward:
            part[at, :] = dot(wide_ref[at, :], down_ref[...]).astype(bf16)
        if backward:
            grad_normed = dot(slim_ref[at, :], up_ref[...], contract_last)
            grad_part[at, :] = grad_normed.astype(bf16)
            for n, rows in enumerate(
                (grad_normed, grad_normed * normed_ref[at, :].astype(f32), grad_rows_ref[at, :].astype(f32))
            ):
                sums_ref[n : n + 1] += jnp.sum(rows, axis=0, keepdims=True)
        return carry

    lax.fori_loop(0, total // step, one, 0)
    pairs = []
    if backward:
        pairs += split_copies(grad_part, *grad_outs, core)
    if forward:
        pairs += split_copies(part, *outs, core)
    for copy in run_copies(pairs, sems, 0):
        copy.wait()


def call_pass(mode, core, weights, tables, allowed, extra, chunks):
    total, block = allowed.shape
    half = block // 2
    width = weights[0].shape[0]
    slim = weights[0].shape[1]
    wide = weights[1].shape[0]
    parts = [
        jax.ShapeDtypeStruct((half, width), bf16),
        jax.ShapeDtypeStruct((3 * block + half, width), bf16),
        jax.ShapeDtypeStruct((4 * block, width), bf16),
    ]
    full = jax.ShapeDtypeStruct((total, width), bf16)
    sums = jax.ShapeDtypeStruct((SUM_ROWS, width), f32)
    slim_rows = jax.ShapeDtypeStruct((total, slim), bf16)
    wide_rows = jax.ShapeDtypeStruct((total, wide), bf16)
    if mode == "first":
        kept = [
            full,
            jax.ShapeDtypeStruct((total, 3 * WIDE), bf16),
            jax.ShapeDtypeStruct((total, slim - 3 * WIDE), f32),
            wide_rows,
        ]
        buffers = 2
    elif mode == "middle":
        kept = [full, full, wide_rows, slim_rows, sums]
        parts = parts * 2
        buffers = 2
    else:
        kept = [full, slim_rows, sums]
        buffers = 1
    passes = 2 if mode == "middle" else 1
    return pl.pallas_call(
        partial(layer_pass, mode),
        in_specs=[SMEM_SPEC] + [VMEM_SPEC] * (6 + len(extra)) + [ANY_SPEC] * len(chunks),
        out_specs=[VMEM_SPEC] * len(kept) + [ANY_SPEC] * len(parts),
        out_shape=kept + parts,
        scratch_shapes=[pltpu.VMEM((total, width), bf16)] * buffers + [pltpu.SemaphoreType.DMA((18,))],
        cost_estimate=pl.CostEstimate(
            flops=6 * total * width * (slim + wide) * passes,
            bytes_accessed=20_000_000 * passes,
            transcendentals=total * slim,
        ),
        name="pass_" + mode,
    )(core, *weights, *tables, allowed, *extra, *chunks)


def gradient_slabs(own_rows, other_rows, with_sums, pieces_in, core_ref, left_ref, *rest):
    right_refs, rest = rest[:pieces_in], rest[pieces_in:]
    if with_sums:
        sums_ref, *rest = rest
    own_ref, other_ref, *rest = rest
    turned_ref = rest[-1]
    if pieces_in == 1:
        right = right_refs[0][...]
    else:
        a, b = right_refs[-2][...], right_refs[-1][...]
        first = jnp.full(a.shape, core_ref[0]) == 0
        halves = [jnp.where(first, a, b), jnp.where(first, b, a)]
        right = jnp.concatenate([ref[...] for ref in right_refs[:-2]] + halves, axis=0)

    @pl.when(pl.program_id(0) == 0)
    def _():
        width = left_ref.shape[1]
        for n in range(width // 128):
            lanes = slice(n * 128, (n + 1) * 128)
            left = left_ref[:, lanes].astype(f32)
            if with_sums:
                rest[0][:, lanes] = jnp.sum(left, axis=0, keepdims=True)
            turned_ref[lanes, :] = left.T.astype(bf16)

    product = dot(turned_ref[...], right).astype(bf16)
    for ref, pieces in ((own_ref, own_rows), (other_ref, other_rows)):
        place = 0
        for first, last in pieces:
            for e in range(2):
                ref[e, place : place + last - first] = product[first:last, e * 128 : (e + 1) * 128]
            place += last - first
        if with_sums:
            for e in range(2):
                ref[e, place:] = sums_ref[:, e * 128 : (e + 1) * 128].astype(bf16)


def call_gradients(core, left, right, own_rows, other_rows, sums, name):
    total, height = left.shape
    width = right[0].shape[1]
    with_sums = len(sums) > 0
    rows = height // 2 + (SUM_ROWS if with_sums else 0)
    slab = pl.BlockSpec((2, rows, 128), lambda i: (i, 0, 0))
    shape = jax.ShapeDtypeStruct((width // 128, rows, 128), bf16)
    out_specs, out_shape = [slab, slab], [shape, shape]
    if with_sums:
        out_specs.append(pl.BlockSpec((1, height), lambda i: (0, 0)))
        out_shape.append(jax.ShapeDtypeStruct((1, height), f32))
    return pl.pallas_call(
        partial(gradient_slabs, own_rows, other_rows, with_sums, len(right)),
        grid=(width // 256,),
        in_specs=[SMEM_SPEC, pl.BlockSpec((total, height), lambda i: (0, 0))]
        + [pl.BlockSpec((x.shape[0], 256), lambda i: (0, i)) for x in (*right, *sums)],
        out_specs=out_specs,
        out_shape=out_shape,
        scratch_shapes=[pltpu.VMEM((height, total), bf16)],
        cost_estimate=pl.CostEstimate(
            flops=4 * total * height * width, bytes_accessed=2 * (total * (width + height) + 2 * height * width), transcendentals=0
        ),
        name=name,
    )(core, left, *right, *sums)


def spread_gradients(up_ref, down_ref, *rest):
    qkv_ref, out_w_ref, fc1_ref, fc2_ref = rest[-4:]
    for p in range(3):
        rows = slice(p * HEAD_DIM, (p + 1) * HEAD_DIM)
        both = jnp.concatenate([up_ref[0, rows].astype(f32), up_ref[1, rows].astype(f32)], axis=0)
        qkv_ref[0, p] = both.T
    base = 3 * HEAD_DIM
    for d in range(2):
        for h in range(2):
            fc1_ref[0, :, (2 * d + h) * 128 : (2 * d + h + 1) * 128] = (
                up_ref[d, base + h * 128 : base + (h + 1) * 128].astype(f32).T
            )
        out_w_ref[0, d * HEAD_DIM : (d + 1) * HEAD_DIM] = down_ref[d, :HEAD_DIM].astype(f32)
        fc2_ref[0, d * 256 : (d + 1) * 256] = down_ref[d, HEAD_DIM:].astype(f32)


def call_spread(up, down, layer, filled):
    shapes = [
        jax.ShapeDtypeStruct((LAYERS, 3, 128, GROUP * HEAD_DIM), f32),
        jax.ShapeDtypeStruct((LAYERS, GROUP * HEAD_DIM, 128), f32),
        jax.ShapeDtypeStruct((LAYERS, 128, GROUP * 256), f32),
        jax.ShapeDtypeStruct((LAYERS, GROUP * 256, 128), f32),
    ]
    return pl.pallas_call(
        spread_gradients,
        grid=(GROUP // 2,),
        in_specs=[
            pl.BlockSpec((2, up.shape[1], 128), lambda i: (i, 0, 0)),
            pl.BlockSpec((2, down.shape[1], 128), lambda i: (i, 0, 0)),
        ]
        + [ANY_SPEC] * len(filled),
        out_specs=[
            pl.BlockSpec((1, 3, 128, 128), lambda i: (layer, 0, 0, i)),
            pl.BlockSpec((1, 128, 128), lambda i: (layer, i, 0)),
            pl.BlockSpec((1, 128, 512), lambda i: (layer, 0, i)),
            pl.BlockSpec((1, 512, 128), lambda i: (layer, i, 0)),
        ],
        out_shape=shapes,
        input_output_aliases={2 + n: n for n in range(len(filled))},
        name="spread_gradients",
    )(up, down, *filled)


def ring_total(core_ref, keep_ref, took_ref, moving_ref, got_ref):
    half = got_ref.shape[0]
    arrived = moving_ref[pl.ds(pl.multiple_of(core_ref[0] * half, half), half), :]
    return keep_ref[...].astype(f32) + took_ref[...].astype(f32) + arrived.astype(f32) + got_ref[...].astype(f32)


def centred_rows(state):
    centred = state - jnp.mean(state, axis=1, keepdims=True)
    return centred, lax.rsqrt(jnp.mean(centred * centred, axis=1, keepdims=True) + norm_epsilon)


def forward_end(last, core_ref, keep_ref, took_ref, moving_ref, got_ref, state_ref, after_ref, *rest):
    state = state_ref[...].astype(f32) + ring_total(core_ref, keep_ref, took_ref, moving_ref, got_ref) + after_ref[...]
    if last:
        rest[0][...] = state.astype(bf16)
        return
    gain_ref, shift_ref, state_out, normed_ref = rest
    state_out[...] = state
    centred, inverse = centred_rows(state)
    normed_ref[...] = (centred * inverse * gain_ref[...] + shift_ref[...]).astype(bf16)


def backward_end(core_ref, keep_ref, took_ref, moving_ref, got_ref, state_ref, grad_ref, gain_ref, grad_out, low_ref):
    grad_normed = ring_total(core_ref, keep_ref, took_ref, moving_ref, got_ref)
    centred, inverse = centred_rows(state_ref[...].astype(f32))
    xhat = centred * inverse
    before = grad_ref[...].astype(f32)
    scaled = grad_normed * gain_ref[...]
    after = before + (
        scaled - jnp.mean(scaled, axis=1, keepdims=True) - xhat * jnp.mean(scaled * xhat, axis=1, keepdims=True)
    ) * inverse
    grad_out[...] = after
    low_ref[...] = after.astype(bf16)


def call_end(body, core, ring, extra, shapes, name):
    keep, took, moving, got, n_sum = ring
    _, half, width = got.shape

    def rows_of(array):
        n = array.shape[0] // half - 1
        return pl.BlockSpec((half, width), lambda i: (n, 0))

    def whole_of(array):
        return pl.BlockSpec(array.shape, lambda i: (0,) * len(array.shape))

    def one_of(array):
        return pl.BlockSpec((None,) + array.shape[1:], lambda i: (n_sum, 0, 0))

    return pl.pallas_call(
        body,
        grid=(1,),
        in_specs=[SMEM_SPEC, rows_of(keep), rows_of(took), one_of(moving), one_of(got)] + [whole_of(x) for x in extra],
        out_specs=[whole_of(x) for x in shapes],
        out_shape=shapes,
        name=name,
    )(core, keep, took, moving, got, *extra)


def per_device(
    n_dp,
    hidden_in,
    seq_lengths,
    seq_device,
    positions,
    norm_gain,
    norm_bias,
    qkv_weight,
    qkv_bias,
    out_weight,
    fc1_weight,
    fc1_bias,
    fc2_weight,
    output_bias,
    out_cotangent,
):
    block = hidden_in.shape[0]
    half = block // 2
    width = hidden_in.shape[1]
    piece = norm_gain.shape[1]
    hidden = fc1_weight.shape[2] // GROUP
    groups = n_dp // GROUP
    chips = GROUP // 2
    side = chips // 2 - 1

    if groups == 1:
        ring = [2 * a for a in range(chips // 2)] + [2 * a + 1 for a in reversed(range(chips // 2))]
    else:
        ring = list(range(chips // 2)) + list(reversed(range(chips // 2, chips)))
    ring_pairs = []
    for g in range(groups):
        for place in range(chips):
            for core, step in ((0, 1), (1, -1)):
                ring_pairs.append(
                    (
                        g * GROUP + ring[place] * 2 + core,
                        g * GROUP + ring[(place + step) % chips] * 2 + core,
                    )
                )
    core_pairs = [(i, i ^ 1) for i in range(n_dp)]
    inner = [[g * GROUP + i for i in range(GROUP)] for g in range(groups)]
    outer = [[g * GROUP + i for g in range(groups)] for i in range(GROUP)]
    if groups == 1:
        inner = None

    def along(x):
        return lax.ppermute(x, "dp", ring_pairs)

    def across(x):
        return lax.ppermute(x, "dp", core_pairs)

    def over(x):
        return lax.ppermute(x, "tensor", [(0, 1), (1, 0)])

    index = lax.axis_index("dp")
    group = index // GROUP
    chip = (index % GROUP) // 2
    core = index % 2
    tensor = lax.axis_index("tensor")
    is_first = core == 0
    at = core * half
    off = (1 - core) * half
    core_word = core.astype(jnp.int32).reshape(1)

    def my_half(x, start, axis=0):
        return lax.dynamic_slice_in_dim(x, start, half, axis)

    def in_order(own, other):
        return jnp.where(
            is_first, jnp.concatenate([own, other], 0), jnp.concatenate([other, own], 0)
        )

    def gather_rows(mine, needed={}):
        behind, ahead = [], []
        moving = mine
        for step in range(side):
            moving = along(after(moving, *needed.get(step, ())))
            behind.append(moving)
            ahead.append(across(moving))
        far = along(after(my_half(moving, at, moving.ndim - 2), *needed.get(side, ())))
        return [mine] + behind + ahead + [far, across(far)]

    rows = lax.broadcasted_iota(jnp.int32, (block, 1), 0)
    mine_rows = (rows < half) == is_first

    def ring_sum(*sets, needed={}):
        took_far = [across(give_far) for give_far, _, _ in sets]
        took = [across(give) for _, give, _ in sets]
        keep = [x for _, _, x in sets]
        far = [k[side * block : side * block + half].astype(f32) + t.astype(f32) for k, t in zip(keep, took_far)]
        moving = along(jnp.stack(far).astype(bf16))
        moving = jnp.where(mine_rows, jnp.concatenate([moving, moving], 1), 0).astype(f32)
        for step in reversed(range(side)):
            here = slice(step * block, (step + 1) * block)
            moving = after(moving, *needed.get(step, ()))
            added = [k[here].astype(f32) + t[here].astype(f32) for k, t in zip(keep, took)]
            moving = along((moving + jnp.stack(added)).astype(bf16))
            if step:
                moving = moving.astype(f32)
        got = across(my_half(moving, off, 1))
        return [(k, t, moving, got, n) for n, (k, t) in enumerate(zip(keep, took))]

    def spread(x):
        return lax.all_to_all(x, "dp", 0, 0, axis_index_groups=inner, tiled=True)

    small = jnp.concatenate(
        [
            norm_gain.reshape(-1),
            norm_bias.reshape(-1),
            output_bias.reshape(-1),
            (positions // 64).astype(bf16),
            (positions % 64).astype(bf16),
        ]
    )
    weights = []
    if groups == 1:
        qkv_turned = qkv_weight.transpose(0, 2, 1, 3)
        ups, downs = (qkv_turned, fc1_weight), (out_weight, fc2_weight)
        extra = jnp.concatenate([small, jnp.zeros_like(small)]).reshape(-1, 128)
        up = spread(call_pack(pack_first, 0, ups, (), (extra,)))
        small_all = up[:, UP_ROWS:].reshape(GROUP, -1)[:, : small.shape[0]]
        up_other = over(up)
        packed_down = call_pack(pack_down, 0, (), downs, ())
        down = spread(after(packed_down, up))
        down_other = over(down)
        weights.append(call_join(join_up, up, [up_other], True, False) + call_join(join_down, down, [down_other], False, True))
        packed_last = call_pack(pack_both, 1, ups, downs, ())
        firsts = (up, up_other, down)
    else:
        small_all = lax.all_gather(small, "dp", axis=0, tiled=False)
        for layer in range(LAYERS):
            up = jnp.concatenate(
                [
                    qkv_weight[layer].reshape(piece, 3, GROUP, HEAD_DIM).transpose(2, 0, 1, 3).reshape(GROUP, piece, -1),
                    fc1_weight[layer].reshape(piece, GROUP, hidden).transpose(1, 0, 2),
                ],
                axis=2,
            )
            up = lax.all_gather(spread(up), "dp", axis=0, axis_index_groups=outer, tiled=True)
            up = up.reshape(width // 128, 128, UP_ROWS)
            value = up[:, :, WIDE : WIDE + HEAD_DIM]
            first = WIDE + HEAD_DIM
            up = jnp.concatenate(
                [
                    up[:, :, :WIDE],
                    jnp.concatenate([value[:, :HEAD_DIM], value[:, HEAD_DIM:]], axis=2),
                    up[:, :, first : first + 128],
                    up[:, :, first + 128 :],
                ],
                axis=1,
            )
            down = jnp.concatenate(
                [out_weight[layer].reshape(GROUP, HEAD_DIM, piece), fc2_weight[layer].reshape(GROUP, hidden, piece)],
                axis=1,
            )
            down = lax.all_gather(spread(down), "dp", axis=0, axis_index_groups=outer, tiled=True)
            down = down.transpose(1, 0, 2).reshape(-1, width // 128, 128).transpose(1, 0, 2)
            weights.append(call_join(join_up, up, [over(up)], True, False) + call_join(join_down, down, [over(down)], False, True))
    if groups == 1:
        biases = jnp.concatenate([qkv_bias.reshape(LAYERS, 3 * HEAD_DIM), fc1_bias], axis=1)
    else:
        full_qkv = lax.all_gather(qkv_bias, "dp", axis=2, tiled=True)
        full_up = lax.all_gather(fc1_bias, "dp", axis=1, tiled=True)
        member = index % GROUP
        biases = jnp.concatenate(
            [
                lax.dynamic_slice_in_dim(full_qkv, member * HEAD_DIM, HEAD_DIM, 2).reshape(LAYERS, 3 * HEAD_DIM),
                lax.dynamic_slice_in_dim(full_up, member * hidden, hidden, 1),
            ],
            axis=1,
        )
    biases_other = over(biases)
    both_biases = jnp.stack([biases, biases_other], axis=1).astype(f32)
    bias_rows = jnp.concatenate(
        [
            both_biases[:, :, : 3 * HEAD_DIM].reshape(LAYERS, 2, 3, HEAD_DIM).transpose(0, 2, 1, 3).reshape(LAYERS, -1),
            both_biases[:, :, 3 * HEAD_DIM :].reshape(LAYERS, -1),
        ],
        axis=1,
    )
    vectors = small_all[:, : 6 * piece].reshape(n_dp, 3, LAYERS, piece).transpose(1, 2, 0, 3).reshape(3, LAYERS, 1, width).astype(f32)
    gains, shifts, added_bias = vectors[0], vectors[1], vectors[2]

    turned = jnp.where(is_first, 1, -1)
    place = jnp.sum(jnp.where(jnp.asarray(ring) == chip, jnp.arange(chips), 0))
    offsets = [0] + [-(s + 1) for s in range(side)] + [s + 1 for s in range(side)] + [chips // 2]
    places = (place + turned * jnp.asarray(offsets)) % chips
    chip_ids = jnp.sum(
        jnp.where(places[:, None] == jnp.arange(chips)[None, :], jnp.asarray(ring)[None, :], 0), axis=1
    )
    owners = group * GROUP + 2 * chip_ids + tensor
    labels = jax.vmap(lambda owner: sequence_labels(seq_lengths, seq_device, owner, block))(owners)
    rows_at = jnp.arange(block, dtype=jnp.int32)
    allowed = (
        (labels[:, :, None] == labels[:, None, :])
        & (labels[:, :, None] > 0)
        & (rows_at[None, None, :] <= rows_at[None, :, None])
    ) | (rows_at[None, None, :] == rows_at[None, :, None])
    allowed = allowed.astype(f32).reshape(chips * block, block)
    picked = (owners[:, None] == jnp.arange(n_dp)[None, :]).astype(f32)
    place_parts = jnp.dot(picked, small_all[:, 6 * piece :].astype(f32), precision=lax.Precision.HIGHEST)
    row_places = (place_parts[:, :block] * 64.0 + place_parts[:, block:]).reshape(chips * block)
    pair = ROT // 2
    frequency = 10000.0 ** (-2.0 * jnp.arange(pair, dtype=f32) / ROT)
    angles = row_places[:, None] * frequency[None, :]
    cosine, sine = jnp.cos(angles), jnp.sin(angles)
    nought = jnp.zeros_like(sine)
    rest = jnp.zeros((chips * block, HEAD_DIM - ROT), f32)
    tables = (
        jnp.concatenate([cosine, cosine, rest + 1.0] * 2, axis=1),
        jnp.concatenate([-sine, nought, rest] * 2, axis=1),
        jnp.concatenate([nought, sine, rest] * 2, axis=1),
    )

    both = jnp.stack([hidden_in, out_cotangent])
    both = jnp.where(tensor == core, both, across(both))
    keeps = jnp.stack([jnp.ones_like(labels[0]), (labels[0] > 0).astype(labels.dtype)]).astype(bf16)
    both = both * keeps[:, :, None]
    if groups == 1:
        inputs = gather_rows(
            after(both, packed_down, packed_last, firsts[0], firsts[2]),
            {1: (firsts[1], tables[0]), 2: (tables[1], tables[2], allowed), side: (down_other, weights[0][0])},
        )
        slab = spread(after(packed_last, inputs[-2]))
        others = tuple(over(slab[n * GROUP // 2 : (n + 1) * GROUP // 2]) for n in range(2))
        weights.append(call_join(join_halves, slab, others, True, True))
        slabs = (slab,)
    else:
        inputs = gather_rows(both)
        slabs, others = (), ()
    mine_inputs = my_half(both, at, 1)
    state, grad_state = mine_inputs[0], mine_inputs[1]

    normed, heads, hidden_pre, wide, *parts = call_pass(
        "first", core_word, weights[0], tables, allowed, [bias_rows[0:1], gains[0], shifts[0]], inputs
    )
    rows_shape = (half, width)
    next_state, normed_own = call_end(
        partial(forward_end, False),
        core_word,
        ring_sum((after(parts[0], *slabs), parts[1], parts[2]), needed={})[0],
        [state, added_bias[0], gains[1], shifts[1]],
        [jax.ShapeDtypeStruct(rows_shape, f32), jax.ShapeDtypeStruct(rows_shape, bf16)],
        "forward_end",
    )
    normed_chunks = gather_rows(in_order(normed_own, across(normed_own)), {0: others[:1], 2: others[1:]})

    def handed_back(own_rows):
        filled = in_order(own_rows, across(own_rows))
        return jnp.where(tensor == core, filled, over(filled))

    def summed(own, other, *earlier):
        total = own.astype(f32) + other.astype(f32)
        if groups > 1:
            total = total.transpose(1, 0, 2).reshape(total.shape[1], width)
            total = lax.psum_scatter(total, "dp", scatter_dimension=1, axis_index_groups=outer, tiled=True)
            total = total.reshape(total.shape[0], GROUP, piece).transpose(1, 0, 2)
        return spread(after(total.astype(bf16), *earlier))

    down_own = [(0, HEAD_DIM), (WIDE, WIDE + hidden)]
    down_other = [(HEAD_DIM, WIDE), (WIDE + hidden, WIDE + 2 * hidden)]
    up_own = [(p * WIDE, p * WIDE + HEAD_DIM) for p in range(3)] + [(3 * WIDE, 3 * WIDE + hidden)]
    up_other = [(p * WIDE + HEAD_DIM, (p + 1) * WIDE) for p in range(3)] + [(3 * WIDE + hidden, 3 * WIDE + 2 * hidden)]

    def down_gradients(wide_rows, grad_rows):
        return call_gradients(core_word, wide_rows, grad_rows, down_own, down_other, [], "down_gradients")

    def up_gradients(slim_rows, normed_rows, sums):
        return call_gradients(core_word, slim_rows, [normed_rows], up_own, up_other, [sums], "up_gradients")

    def backward_finish(ring_end, state, grad_state, layer):
        return call_end(
            backward_end,
            core_word,
            ring_end,
            [state, grad_state, gains[layer]],
            [jax.ShapeDtypeStruct(rows_shape, f32), jax.ShapeDtypeStruct(rows_shape, bf16)],
            "backward_end",
        )

    normed_last, grad_rows, wide_last, slim, sums, *parts = call_pass(
        "middle", core_word, weights[1], tables, allowed, [bias_rows[1:2]], normed_chunks + inputs
    )
    out_parts = parts[:3]
    down_pair = down_gradients(wide_last, [grad_rows])
    *up_pair, bias_last = up_gradients(slim, normed_last, sums)
    down_sent, up_sent = over(down_pair[1]), over(up_pair[1])
    grad_end, out_end = ring_sum(parts[3:], out_parts, needed={1: (down_pair[0],), 0: (up_pair[0],)})
    grad_state, grad_low = backward_finish(grad_end, next_state, grad_state, 1)
    (hidden_out,) = call_end(
        partial(forward_end, True),
        core_word,
        out_end,
        [next_state, added_bias[1]],
        [jax.ShapeDtypeStruct(rows_shape, bf16)],
        "forward_out",
    )
    hidden_out = handed_back(hidden_out)
    down_last = summed(down_pair[0], after(down_sent, grad_low))
    grad_chunks = gather_rows(in_order(grad_low, across(grad_low)), {0: (down_sent,), 2: (up_sent,), side: (down_last, hidden_out)})
    up_last = summed(up_pair[0], after(up_sent, grad_chunks[-2]), down_last)

    down_pair = down_gradients(wide, grad_chunks)
    down_sent = over(down_pair[1])
    grad_rows, slim, sums, *parts = call_pass(
        "last", core_word, weights[0], tables, allowed, [heads, after(hidden_pre, down_pair[0]), normed], grad_chunks
    )
    down_first = summed(down_pair[0], after(down_sent, slim), up_last)
    *up_pair, bias_first = up_gradients(slim, after(normed, up_last), sums)
    up_sent = over(up_pair[1])
    (grad_end,) = ring_sum((after(parts[0], up_pair[0]), parts[1], parts[2]), needed={1: (down_first,)})
    up_first = summed(up_pair[0], up_sent, down_first)
    _, grad_low = backward_finish(grad_end, state, grad_state, 0)
    grad_hidden = handed_back(grad_low).astype(f32)

    ends = jnp.stack([jnp.sum(x[:, UP_ROWS : UP_ROWS + 3].astype(f32), axis=0) for x in (up_first, up_last)])
    shift_grads = ends[:, 0]
    gain_grads = (ends[:, 1] - norm_bias.astype(f32) * ends[:, 0]) / norm_gain.astype(f32)
    after_grads = ends[:, 2] / GROUP
    sums = jnp.concatenate([bias_first, bias_last], axis=0)
    sums_qkv = sums[:, : 3 * WIDE].reshape(LAYERS, 3, 2, HEAD_DIM)
    sums_up = sums[:, 3 * WIDE :].reshape(LAYERS, 2, hidden)
    bias_own, bias_other = (
        jnp.concatenate([sums_qkv[:, :, n].reshape(LAYERS, -1), sums_up[:, n]], axis=1) for n in range(2)
    )
    bias_sums = bias_own + over(bias_other)
    bias_qkv, bias_up = bias_sums[:, : 3 * HEAD_DIM].reshape(LAYERS, 3, HEAD_DIM), bias_sums[:, 3 * HEAD_DIM :]
    if groups == 1:
        filled = call_spread(up_last, down_last, 1, [])
        grad_qkv, grad_out, grad_up, grad_down = call_spread(up_first, down_first, 0, filled)
        grad_qkv = grad_qkv.transpose(0, 2, 1, 3)
    else:
        bias_qkv = lax.all_gather(lax.psum(bias_qkv, "dp", axis_index_groups=outer), "dp", axis=2, axis_index_groups=inner, tiled=True)
        bias_up = lax.all_gather(lax.psum(bias_up, "dp", axis_index_groups=outer), "dp", axis=1, axis_index_groups=inner, tiled=True)
        bias_qkv = lax.dynamic_slice_in_dim(bias_qkv, index * qkv_bias.shape[2], qkv_bias.shape[2], 2)
        bias_up = lax.dynamic_slice_in_dim(bias_up, index * fc1_bias.shape[1], fc1_bias.shape[1], 1)
        ups = jnp.stack([up_first, up_last]).astype(f32)
        downs = jnp.stack([down_first, down_last]).astype(f32)
        grad_qkv = ups[:, :, : 3 * HEAD_DIM].reshape(LAYERS, GROUP, 3, HEAD_DIM, piece).transpose(0, 4, 2, 1, 3).reshape(LAYERS, piece, 3, -1)
        grad_up = ups[:, :, 3 * HEAD_DIM : UP_ROWS].transpose(0, 3, 1, 2).reshape(LAYERS, piece, -1)
        grad_out = downs[:, :, :HEAD_DIM].reshape(LAYERS, -1, piece)
        grad_down = downs[:, :, HEAD_DIM:].reshape(LAYERS, -1, piece)
    return (
        hidden_out,
        grad_hidden,
        gain_grads,
        shift_grads,
        grad_qkv,
        bias_qkv,
        grad_out,
        grad_up,
        bias_up,
        grad_down,
        after_grads,
    )


def solution(mesh):
    placed = (
        P("dp", None),
        P(),
        P(),
        P("dp"),
        P(None, "dp"),
        P(None, "dp"),
        P(None, "dp", None, "tensor"),
        P(None, None, ("tensor", "dp")),
        P(None, "tensor", "dp"),
        P(None, "dp", "tensor"),
        P(None, ("tensor", "dp")),
        P(None, "tensor", "dp"),
        P(None, "dp"),
        P("dp", None),
    )
    return jax.shard_map(
        partial(per_device, mesh.shape["dp"]),
        mesh=mesh,
        in_specs=placed,
        out_specs=(
            P("dp", None),
            P("dp", None),
            P(None, "dp"),
            P(None, "dp"),
            P(None, "dp", None, "tensor"),
            P(None, None, ("tensor", "dp")),
            P(None, "tensor", "dp"),
            P(None, "dp", "tensor"),
            P(None, ("tensor", "dp")),
            P(None, "tensor", "dp"),
            P(None, "dp"),
        ),
        check_vma=False,
    )
```

```python
from functools import partial

import jax
import jax.numpy as jnp
from jax import lax
from jax.experimental import pallas as pl
from jax.experimental.pallas import tpu as pltpu
from jax.sharding import PartitionSpec as P

HEAD_DIM = 64
ROT = 32
LAYERS = 2
GROUP = 16

norm_epsilon = 1e-05
masked_score = -1e30
bf16 = jnp.bfloat16
f32 = jnp.float32

contract_last = (((1,), (1,)), ((), ()))
contract_first = (((0,), (0,)), ((), ()))


def dot(a, b, dims=(((1,), (0,)), ((), ()))):
    return lax.dot_general(a, b, dims, preferred_element_type=f32)


def turn(x, cosine, up, down):
    return x * cosine + pltpu.roll(x, x.shape[1] - ROT // 2, 1) * up + pltpu.roll(x, ROT // 2, 1) * down


def stacked_heads(x):
    lane = lax.broadcasted_iota(jnp.int32, x.shape, 1)
    zero = jnp.zeros_like(x)
    return jnp.concatenate(
        [jnp.where(lane < HEAD_DIM, x, zero), jnp.where(lane < HEAD_DIM, zero, x)], axis=0
    )


def merged_heads(x):
    rows = x.shape[0] // 2
    lane = lax.broadcasted_iota(jnp.int32, (rows, x.shape[1]), 1)
    return jnp.where(lane < HEAD_DIM, x[:rows], x[rows:])


def softmax_rows(queries, keys, allowed):
    scores = dot(stacked_heads(queries), keys, contract_last) * HEAD_DIM ** (-0.5)
    masked = jnp.where(jnp.concatenate([allowed, allowed], axis=0) > 0, scores, masked_score)
    weights = jnp.exp(masked - jnp.max(masked, axis=1, keepdims=True))
    return weights / jnp.sum(weights, axis=1, keepdims=True)


def sequence_labels(seq_lengths, seq_device, owner, count_rows):
    index = jnp.arange(seq_lengths.shape[0], dtype=jnp.int32)
    owned = jnp.where(seq_device == owner, seq_lengths, 0)
    earlier = index[None, :] < index[:, None]
    starts = jnp.sum(jnp.where(earlier, owned[None, :], 0), axis=1)
    places = jnp.arange(count_rows, dtype=jnp.int32)
    inside = (places[:, None] >= starts[None, :]) & (places[:, None] < (starts + owned)[None, :])
    return jnp.sum(jnp.where(inside, index[None, :] + 1, 0), axis=1)


def gelu_parts(v):
    c = (2.0 / jnp.pi) ** 0.5
    inner = jnp.tanh(c * (v + 0.044715 * v * v * v))
    value = 0.5 * v * (1.0 + inner)
    slope = 0.5 * (1.0 + inner) + 0.5 * v * (1.0 - inner * inner) * c * (1.0 + 3.0 * 0.044715 * v * v)
    return value, slope


VMEM_SPEC = pl.BlockSpec(memory_space=pltpu.VMEM)
ANY_SPEC = pl.BlockSpec(memory_space=pl.ANY)
SMEM_SPEC = pl.BlockSpec(memory_space=pltpu.SMEM)
WIDE = 2 * HEAD_DIM
UP_ROWS = 3 * HEAD_DIM + 256
DOWN_ROWS = HEAD_DIM + 256
SUM_ROWS = 16
MEMBERS = 4


def after(x, *others):
    if not others:
        return x
    return lax.optimization_barrier((x, *others))[0]


def left_lanes(x):
    return lax.broadcasted_iota(jnp.int32, x.shape, 1) < HEAD_DIM


def swapped(x):
    return pltpu.roll(x, HEAD_DIM, 1)


def zipped(a, b):
    left = left_lanes(a)
    return jnp.where(left, a, swapped(b)).astype(bf16), jnp.where(left, swapped(a), b).astype(bf16)


def pack_up(qkv_ref, fc1_ref, *rest):
    out_ref = rest[-1]
    for pair in range(MEMBERS // 2):
        lanes = slice(pair * 128, (pair + 1) * 128)
        q, k, v = (qkv_ref[0, p, :, lanes].astype(f32) for p in range(3))
        here, there = 2 * pair, 2 * pair + 1
        out_ref[here, :WIDE], out_ref[there, :WIDE] = zipped(q, k)
        rows = q.shape[0] // 2
        out_ref[here, WIDE : WIDE + rows], out_ref[there, WIDE : WIDE + rows] = zipped(v[:rows], v[rows:])
        base = WIDE + rows
        for d in (here, there):
            for h in range(2):
                out_ref[d, base + h * 128 : base + (h + 1) * 128] = fc1_ref[0, :, (2 * d + h) * 128 : (2 * d + h + 1) * 128]


def pack_first(qkv_ref, fc1_ref, small_ref, out_ref):
    pack_up(qkv_ref, fc1_ref, out_ref)
    for d in range(MEMBERS):
        out_ref[d, UP_ROWS:] = small_ref[...]


def pack_both(qkv_ref, fc1_ref, out_w_ref, fc2_ref, out_ref):
    pack_up(qkv_ref, fc1_ref, out_ref)
    pack_down(out_w_ref, fc2_ref, out_ref.at[:, UP_ROWS:])


def pack_down(out_w_ref, fc2_ref, out_ref):
    for d in range(MEMBERS):
        out_ref[d, :HEAD_DIM] = out_w_ref[0, d * HEAD_DIM : (d + 1) * HEAD_DIM]
        out_ref[d, HEAD_DIM:] = fc2_ref[0, d * 256 : (d + 1) * 256]


def call_pack(body, layer, ups, downs, small):
    rows, specs = 0, []
    if ups:
        rows += UP_ROWS
        specs += [
            pl.BlockSpec((1, 3, 128, MEMBERS * HEAD_DIM), lambda i: (layer, 0, 0, i)),
            pl.BlockSpec((1, 128, MEMBERS * 256), lambda i: (layer, 0, i)),
        ]
    if downs:
        rows += DOWN_ROWS
        specs += [
            pl.BlockSpec((1, MEMBERS * HEAD_DIM, 128), lambda i: (layer, i, 0)),
            pl.BlockSpec((1, MEMBERS * 256, 128), lambda i: (layer, i, 0)),
        ]
    if small:
        rows += small[0].shape[0]
        specs.append(pl.BlockSpec(small[0].shape, lambda i: (0, 0)))
    return pl.pallas_call(
        body,
        grid=(GROUP // MEMBERS,),
        in_specs=specs,
        out_specs=pl.BlockSpec((MEMBERS, rows, 128), lambda i: (i, 0, 0)),
        out_shape=jax.ShapeDtypeStruct((GROUP, rows, 128), bf16),
        cost_estimate=pl.CostEstimate(flops=0, bytes_accessed=GROUP * rows * 128 * 8, transcendentals=0),
        name=body.__name__,
    )(*ups, *downs, *small)


def join_up(own_ref, other_ref, out_ref):
    for e in range(MEMBERS):
        rows = slice(e * 128, (e + 1) * 128)
        a, b = own_ref[e, :WIDE].astype(f32), other_ref[e, :WIDE].astype(f32)
        out_ref[rows, :WIDE], out_ref[rows, WIDE : 2 * WIDE] = zipped(a, b)
        a, b = own_ref[e, WIDE : WIDE + 64].astype(f32), other_ref[e, WIDE : WIDE + 64].astype(f32)
        top, bottom = zipped(a, b)
        out_ref[e * 128 : e * 128 + 64, 2 * WIDE : 3 * WIDE] = top
        out_ref[e * 128 + 64 : (e + 1) * 128, 2 * WIDE : 3 * WIDE] = bottom
        for n, ref in enumerate((own_ref, other_ref)):
            for h in range(2):
                lanes = 3 * WIDE + n * 256 + h * 128
                out_ref[rows, lanes : lanes + 128] = ref[e, WIDE + 64 + h * 128 : WIDE + 64 + (h + 1) * 128]


def join_down(own_ref, other_ref, out_ref):
    base = own_ref.shape[1] - DOWN_ROWS
    for e in range(MEMBERS):
        lanes = slice(e * 128, (e + 1) * 128)
        for n, ref in enumerate((own_ref, other_ref)):
            out_ref[n * HEAD_DIM : (n + 1) * HEAD_DIM, lanes] = ref[e, base : base + HEAD_DIM]
            out_ref[WIDE + n * 256 : WIDE + (n + 1) * 256, lanes] = ref[e, base + HEAD_DIM :]


def join_both(own_ref, other_ref, up_ref, down_ref):
    join_up(own_ref, other_ref, up_ref)
    join_down(own_ref, other_ref, down_ref)


def join_halves(own_ref, lower_ref, upper_ref, up_ref, down_ref):
    lower = pl.program_id(0) < GROUP // MEMBERS // 2

    @pl.when(lower)
    def _():
        join_both(own_ref, lower_ref, up_ref, down_ref)

    @pl.when(jnp.logical_not(lower))
    def _():
        join_both(own_ref, upper_ref, up_ref, down_ref)


def call_join(body, own, others, ups, downs):
    rows = own.shape[1]
    steps = GROUP // MEMBERS
    spec = pl.BlockSpec((MEMBERS, rows, 128), lambda i: (i, 0, 0))
    other_specs = [spec]
    if len(others) == 2:
        other_specs = [
            pl.BlockSpec((MEMBERS, rows, 128), lambda i: (jnp.minimum(i, steps // 2 - 1), 0, 0)),
            pl.BlockSpec((MEMBERS, rows, 128), lambda i: (jnp.maximum(i - steps // 2, 0), 0, 0)),
        ]
    specs, shapes = [], []
    if ups:
        specs.append(pl.BlockSpec((MEMBERS * 128, 2 * UP_ROWS), lambda i: (i, 0)))
        shapes.append(jax.ShapeDtypeStruct((GROUP * 128, 2 * UP_ROWS), bf16))
    if downs:
        specs.append(pl.BlockSpec((2 * DOWN_ROWS, MEMBERS * 128), lambda i: (0, i)))
        shapes.append(jax.ShapeDtypeStruct((2 * DOWN_ROWS, GROUP * 128), bf16))
    return pl.pallas_call(
        body,
        grid=(GROUP // MEMBERS,),
        in_specs=[spec] + other_specs,
        out_specs=specs,
        out_shape=shapes,
        cost_estimate=pl.CostEstimate(flops=0, bytes_accessed=GROUP * rows * 128 * 12, transcendentals=0),
        name=body.__name__,
    )(own, *others)


def slot_copies(refs, which, target, core):
    block = target.shape[0] // 8
    half = block // 2
    pairs = []
    for slot in range(7):
        ref = refs[slot] if which is None else refs[slot].at[which]
        pairs.append((ref, target.at[pl.ds(slot * block, block)]))
    for n, at in ((7, core * half), (8, (1 - core) * half)):
        ref = refs[n] if which is None else refs[n].at[which]
        pairs.append((ref, target.at[pl.ds(pl.multiple_of(7 * block + at, half), half)]))
    return pairs


def split_copies(part, far_ref, give_ref, keep_ref, core):
    block = part.shape[0] // 8
    half = block // 2
    at, off = core * half, (1 - core) * half

    def rows(slot, start):
        return part.at[pl.ds(pl.multiple_of(slot * block + start, half), half)]

    return [
        (rows(7, off), far_ref),
        (part.at[pl.ds(block, 3 * block)], give_ref.at[pl.ds(0, 3 * block)]),
        (rows(0, off), give_ref.at[pl.ds(3 * block, half)]),
        (part.at[pl.ds(4 * block, 3 * block)], keep_ref.at[pl.ds(0, 3 * block)]),
        (rows(7, at), keep_ref.at[pl.ds(3 * block, half)]),
        (rows(0, at), keep_ref.at[pl.ds(3 * block + half, half)]),
    ]


def run_copies(pairs, sems, first):
    made = [pltpu.make_async_copy(a, b, sems.at[first + n]) for n, (a, b) in enumerate(pairs)]
    for copy in made:
        copy.start()
    return made


def heads_forward(chances, values):
    return merged_heads(dot(chances.astype(bf16), values)).astype(bf16)


def heads_backward(chances, queries, keys, values, grad, tables):
    grads = stacked_heads(grad)
    grad_chances = dot(grads, values, contract_last)
    grad_values = dot(chances.astype(bf16), grads, contract_first)
    centre = jnp.sum(grad_chances * chances, axis=1, keepdims=True)
    grad_scores = (chances * (grad_chances - centre)).astype(bf16)
    scale = HEAD_DIM ** (-0.5)
    grad_queries = merged_heads(dot(grad_scores, keys)) * scale
    grad_keys = dot(grad_scores, stacked_heads(queries), contract_first) * scale
    cosine, up, down = tables
    back = (cosine, -up, -down)
    return turn(grad_queries, *back).astype(bf16), turn(grad_keys, *back).astype(bf16), grad_values.astype(bf16)


def layer_pass(mode, *refs):
    refs = list(refs)

    def take(n):
        out = refs[:n]
        del refs[:n]
        return out

    forward, backward = mode != "last", mode != "first"
    core_ref, up_ref, down_ref, cos_ref, sin_up_ref, sin_down_ref, allowed_ref = take(7)
    core = core_ref[0]
    if mode == "first":
        bias_ref, gain_ref, shift_ref = take(3)
        rows_in = take(9)
    elif mode == "middle":
        (bias_ref,) = take(1)
        rows_in = take(9)
    else:
        heads_ref, hidden_ref, normed_ref = take(3)
        grads_in = take(9)
    if mode == "first":
        normed_ref, heads_ref, hidden_ref, wide_ref = take(4)
        outs = take(3)
        raw, part, sems = take(3)
    elif mode == "middle":
        normed_ref, grad_rows_ref, wide_ref, slim_ref, sums_ref = take(5)
        outs = take(3)
        grad_outs = take(3)
        part, grad_part, sems = take(3)
    else:
        grad_rows_ref, slim_ref, sums_ref = take(3)
        grad_outs = take(3)
        grad_part, sems = take(2)

    pairs = []
    if mode == "first":
        pairs += slot_copies(rows_in, None, raw, core)
    if mode == "middle":
        pairs += slot_copies(rows_in, 0, normed_ref, core)
        pairs += slot_copies(rows_in, 1, grad_rows_ref, core)
    if mode == "last":
        pairs += slot_copies(grads_in, None, grad_rows_ref, core)
    for copy in run_copies(pairs, sems, 0):
        copy.wait()

    total = allowed_ref.shape[0]
    block = allowed_ref.shape[1]
    step = 2 * block

    if mode == "first":
        tile = 32

        def norm_tile(i, carry):
            at = pl.ds(pl.multiple_of(i * tile, tile), tile)
            x = raw[at, :].astype(f32)
            centred = x - jnp.mean(x, axis=1, keepdims=True)
            inverse = lax.rsqrt(jnp.mean(centred * centred, axis=1, keepdims=True) + norm_epsilon)
            normed_ref[at, :] = (centred * inverse * gain_ref[...] + shift_ref[...]).astype(bf16)
            return carry

        lax.fori_loop(0, total // tile, norm_tile, 0)

    if backward:
        sums_ref[...] = jnp.zeros_like(sums_ref)

    def one(p, carry):
        at = pl.ds(pl.multiple_of(p * step, step), step)
        if forward:
            before = dot(normed_ref[at, :], up_ref[...]) + bias_ref[...]
            hidden_pre = before[:, 3 * WIDE :]
        else:
            hidden_pre = hidden_ref[at, :]
        value, slope = gelu_parts(hidden_pre)
        if backward:
            grad_wide = dot(grad_rows_ref[at, :], down_ref[...], contract_last)
            slim_ref[at, 3 * WIDE :] = (grad_wide[:, WIDE:] * slope).astype(bf16)
        if forward:
            wide_ref[at, WIDE:] = value.astype(bf16)
        if mode == "first":
            hidden_ref[at, :] = hidden_pre
        for b in range(2):
            mine = slice(b * block, (b + 1) * block)
            own = pl.ds(pl.multiple_of(p * step + b * block, block), block)
            tables = (cos_ref[own, :], sin_up_ref[own, :], sin_down_ref[own, :])
            if forward:
                queries = turn(before[mine, :WIDE], *tables).astype(bf16)
                keys = turn(before[mine, WIDE : 2 * WIDE], *tables).astype(bf16)
                values = before[mine, 2 * WIDE : 3 * WIDE].astype(bf16)
            else:
                queries = heads_ref[own, :WIDE]
                keys = heads_ref[own, WIDE : 2 * WIDE]
                values = heads_ref[own, 2 * WIDE :]
            if mode == "first":
                heads_ref[own, :WIDE] = queries
                heads_ref[own, WIDE : 2 * WIDE] = keys
                heads_ref[own, 2 * WIDE :] = values
            chances = softmax_rows(queries, keys, allowed_ref[own, :])
            if forward:
                wide_ref[own, :WIDE] = heads_forward(chances, values)
            if backward:
                grads = heads_backward(
                    chances, queries, keys, values, grad_wide[mine, :WIDE].astype(bf16), tables
                )
                for n in range(3):
                    slim_ref[own, n * WIDE : (n + 1) * WIDE] = grads[n]
        if forward:
            part[at, :] = dot(wide_ref[at, :], down_ref[...]).astype(bf16)
        if backward:
            grad_normed = dot(slim_ref[at, :], up_ref[...], contract_last)
            grad_part[at, :] = grad_normed.astype(bf16)
            for n, rows in enumerate(
                (grad_normed, grad_normed * normed_ref[at, :].astype(f32), grad_rows_ref[at, :].astype(f32))
            ):
                sums_ref[n : n + 1] += jnp.sum(rows, axis=0, keepdims=True)
        return carry

    lax.fori_loop(0, total // step, one, 0)
    pairs = []
    if backward:
        pairs += split_copies(grad_part, *grad_outs, core)
    if forward:
        pairs += split_copies(part, *outs, core)
    for copy in run_copies(pairs, sems, 0):
        copy.wait()


def call_pass(mode, core, weights, tables, allowed, extra, chunks):
    total, block = allowed.shape
    half = block // 2
    width = weights[0].shape[0]
    slim = weights[0].shape[1]
    wide = weights[1].shape[0]
    parts = [
        jax.ShapeDtypeStruct((half, width), bf16),
        jax.ShapeDtypeStruct((3 * block + half, width), bf16),
        jax.ShapeDtypeStruct((4 * block, width), bf16),
    ]
    full = jax.ShapeDtypeStruct((total, width), bf16)
    sums = jax.ShapeDtypeStruct((SUM_ROWS, width), f32)
    slim_rows = jax.ShapeDtypeStruct((total, slim), bf16)
    wide_rows = jax.ShapeDtypeStruct((total, wide), bf16)
    if mode == "first":
        kept = [
            full,
            jax.ShapeDtypeStruct((total, 3 * WIDE), bf16),
            jax.ShapeDtypeStruct((total, slim - 3 * WIDE), f32),
            wide_rows,
        ]
        buffers = 2
    elif mode == "middle":
        kept = [full, full, wide_rows, slim_rows, sums]
        parts = parts * 2
        buffers = 2
    else:
        kept = [full, slim_rows, sums]
        buffers = 1
    passes = 2 if mode == "middle" else 1
    return pl.pallas_call(
        partial(layer_pass, mode),
        in_specs=[SMEM_SPEC] + [VMEM_SPEC] * (6 + len(extra)) + [ANY_SPEC] * len(chunks),
        out_specs=[VMEM_SPEC] * len(kept) + [ANY_SPEC] * len(parts),
        out_shape=kept + parts,
        scratch_shapes=[pltpu.VMEM((total, width), bf16)] * buffers + [pltpu.SemaphoreType.DMA((18,))],
        cost_estimate=pl.CostEstimate(
            flops=6 * total * width * (slim + wide) * passes,
            bytes_accessed=20_000_000 * passes,
            transcendentals=total * slim,
        ),
        name="pass_" + mode,
    )(core, *weights, *tables, allowed, *extra, *chunks)


def gradient_slabs(own_rows, other_rows, with_sums, pieces_in, core_ref, left_ref, *rest):
    right_refs, rest = rest[:pieces_in], rest[pieces_in:]
    if with_sums:
        sums_ref, *rest = rest
    own_ref, other_ref, *rest = rest
    turned_ref = rest[-1]
    if pieces_in == 1:
        right = right_refs[0][...]
    else:
        a, b = right_refs[-2][...], right_refs[-1][...]
        first = jnp.full(a.shape, core_ref[0]) == 0
        halves = [jnp.where(first, a, b), jnp.where(first, b, a)]
        right = jnp.concatenate([ref[...] for ref in right_refs[:-2]] + halves, axis=0)

    @pl.when(pl.program_id(0) == 0)
    def _():
        width = left_ref.shape[1]
        for n in range(width // 128):
            lanes = slice(n * 128, (n + 1) * 128)
            left = left_ref[:, lanes].astype(f32)
            if with_sums:
                rest[0][:, lanes] = jnp.sum(left, axis=0, keepdims=True)
            turned_ref[lanes, :] = left.T.astype(bf16)

    product = dot(turned_ref[...], right).astype(bf16)
    for ref, pieces in ((own_ref, own_rows), (other_ref, other_rows)):
        place = 0
        for first, last in pieces:
            for e in range(2):
                ref[e, place : place + last - first] = product[first:last, e * 128 : (e + 1) * 128]
            place += last - first
        if with_sums:
            for e in range(2):
                ref[e, place:] = sums_ref[:, e * 128 : (e + 1) * 128].astype(bf16)


def call_gradients(core, left, right, own_rows, other_rows, sums, name):
    total, height = left.shape
    width = right[0].shape[1]
    with_sums = len(sums) > 0
    rows = height // 2 + (SUM_ROWS if with_sums else 0)
    slab = pl.BlockSpec((2, rows, 128), lambda i: (i, 0, 0))
    shape = jax.ShapeDtypeStruct((width // 128, rows, 128), bf16)
    out_specs, out_shape = [slab, slab], [shape, shape]
    if with_sums:
        out_specs.append(pl.BlockSpec((1, height), lambda i: (0, 0)))
        out_shape.append(jax.ShapeDtypeStruct((1, height), f32))
    return pl.pallas_call(
        partial(gradient_slabs, own_rows, other_rows, with_sums, len(right)),
        grid=(width // 256,),
        in_specs=[SMEM_SPEC, pl.BlockSpec((total, height), lambda i: (0, 0))]
        + [pl.BlockSpec((x.shape[0], 256), lambda i: (0, i)) for x in (*right, *sums)],
        out_specs=out_specs,
        out_shape=out_shape,
        scratch_shapes=[pltpu.VMEM((height, total), bf16)],
        cost_estimate=pl.CostEstimate(
            flops=4 * total * height * width, bytes_accessed=2 * (total * (width + height) + 2 * height * width), transcendentals=0
        ),
        name=name,
    )(core, left, *right, *sums)


def spread_gradients(up_ref, down_ref, *rest):
    qkv_ref, out_w_ref, fc1_ref, fc2_ref = rest[-4:]
    down = down_ref.shape[1] - DOWN_ROWS
    for p in range(3):
        rows = slice(p * HEAD_DIM, (p + 1) * HEAD_DIM)
        both = jnp.concatenate([up_ref[0, rows].astype(f32), up_ref[1, rows].astype(f32)], axis=0)
        qkv_ref[0, p] = both.T
    base = 3 * HEAD_DIM
    for d in range(2):
        for h in range(2):
            fc1_ref[0, :, (2 * d + h) * 128 : (2 * d + h + 1) * 128] = (
                up_ref[d, base + h * 128 : base + (h + 1) * 128].astype(f32).T
            )
        out_w_ref[0, d * HEAD_DIM : (d + 1) * HEAD_DIM] = down_ref[d, down : down + HEAD_DIM].astype(f32)
        fc2_ref[0, d * 256 : (d + 1) * 256] = down_ref[d, down + HEAD_DIM :].astype(f32)


def call_spread(up, down, layer, filled):
    shapes = [
        jax.ShapeDtypeStruct((LAYERS, 3, 128, GROUP * HEAD_DIM), f32),
        jax.ShapeDtypeStruct((LAYERS, GROUP * HEAD_DIM, 128), f32),
        jax.ShapeDtypeStruct((LAYERS, 128, GROUP * 256), f32),
        jax.ShapeDtypeStruct((LAYERS, GROUP * 256, 128), f32),
    ]
    return pl.pallas_call(
        spread_gradients,
        grid=(GROUP // 2,),
        in_specs=[
            pl.BlockSpec((2, up.shape[1], 128), lambda i: (i, 0, 0)),
            pl.BlockSpec((2, down.shape[1], 128), lambda i: (i, 0, 0)),
        ]
        + [ANY_SPEC] * len(filled),
        out_specs=[
            pl.BlockSpec((1, 3, 128, 128), lambda i: (layer, 0, 0, i)),
            pl.BlockSpec((1, 128, 128), lambda i: (layer, i, 0)),
            pl.BlockSpec((1, 128, 512), lambda i: (layer, 0, i)),
            pl.BlockSpec((1, 512, 128), lambda i: (layer, i, 0)),
        ],
        out_shape=shapes,
        input_output_aliases={2 + n: n for n in range(len(filled))},
        name="spread_gradients",
    )(up, down, *filled)


def ring_total(core_ref, keep_ref, took_ref, moving_ref, got_ref):
    half = got_ref.shape[0]
    arrived = moving_ref[pl.ds(pl.multiple_of(core_ref[0] * half, half), half), :]
    return keep_ref[...].astype(f32) + took_ref[...].astype(f32) + arrived.astype(f32) + got_ref[...].astype(f32)


def centred_rows(state):
    centred = state - jnp.mean(state, axis=1, keepdims=True)
    return centred, lax.rsqrt(jnp.mean(centred * centred, axis=1, keepdims=True) + norm_epsilon)


def forward_end(last, core_ref, keep_ref, took_ref, moving_ref, got_ref, state_ref, after_ref, *rest):
    state = state_ref[...].astype(f32) + ring_total(core_ref, keep_ref, took_ref, moving_ref, got_ref) + after_ref[...]
    if last:
        rest[0][...] = state.astype(bf16)
        return
    gain_ref, shift_ref, state_out, normed_ref = rest
    state_out[...] = state
    centred, inverse = centred_rows(state)
    normed_ref[...] = (centred * inverse * gain_ref[...] + shift_ref[...]).astype(bf16)


def backward_end(core_ref, keep_ref, took_ref, moving_ref, got_ref, state_ref, grad_ref, gain_ref, grad_out, low_ref):
    grad_normed = ring_total(core_ref, keep_ref, took_ref, moving_ref, got_ref)
    centred, inverse = centred_rows(state_ref[...].astype(f32))
    xhat = centred * inverse
    before = grad_ref[...].astype(f32)
    scaled = grad_normed * gain_ref[...]
    after = before + (
        scaled - jnp.mean(scaled, axis=1, keepdims=True) - xhat * jnp.mean(scaled * xhat, axis=1, keepdims=True)
    ) * inverse
    grad_out[...] = after
    low_ref[...] = after.astype(bf16)


def call_end(body, core, ring, extra, shapes, name):
    keep, took, moving, got, n_sum = ring
    _, half, width = got.shape

    def rows_of(array):
        n = array.shape[0] // half - 1
        return pl.BlockSpec((half, width), lambda i: (n, 0))

    def whole_of(array):
        return pl.BlockSpec(array.shape, lambda i: (0,) * len(array.shape))

    def one_of(array):
        return pl.BlockSpec((None,) + array.shape[1:], lambda i: (n_sum, 0, 0))

    return pl.pallas_call(
        body,
        grid=(1,),
        in_specs=[SMEM_SPEC, rows_of(keep), rows_of(took), one_of(moving), one_of(got)] + [whole_of(x) for x in extra],
        out_specs=[whole_of(x) for x in shapes],
        out_shape=shapes,
        cost_estimate=pl.CostEstimate(flops=0, bytes_accessed=half * width, transcendentals=0),
        name=name,
    )(core, keep, took, moving, got, *extra)


def per_device(
    n_dp,
    hidden_in,
    seq_lengths,
    seq_device,
    positions,
    norm_gain,
    norm_bias,
    qkv_weight,
    qkv_bias,
    out_weight,
    fc1_weight,
    fc1_bias,
    fc2_weight,
    output_bias,
    out_cotangent,
):
    block = hidden_in.shape[0]
    half = block // 2
    width = hidden_in.shape[1]
    piece = norm_gain.shape[1]
    hidden = fc1_weight.shape[2] // GROUP
    groups = n_dp // GROUP
    chips = GROUP // 2
    side = chips // 2 - 1

    if groups == 1:
        ring = [2 * a for a in range(chips // 2)] + [2 * a + 1 for a in reversed(range(chips // 2))]
    else:
        ring = list(range(chips // 2)) + list(reversed(range(chips // 2, chips)))
    ring_pairs = []
    for g in range(groups):
        for place in range(chips):
            for core, step in ((0, 1), (1, -1)):
                ring_pairs.append(
                    (
                        g * GROUP + ring[place] * 2 + core,
                        g * GROUP + ring[(place + step) % chips] * 2 + core,
                    )
                )
    core_pairs = [(i, i ^ 1) for i in range(n_dp)]
    inner = [[g * GROUP + i for i in range(GROUP)] for g in range(groups)]
    outer = [[g * GROUP + i for g in range(groups)] for i in range(GROUP)]
    if groups == 1:
        inner = None

    def along(x):
        return lax.ppermute(x, "dp", ring_pairs)

    def across(x):
        return lax.ppermute(x, "dp", core_pairs)

    def over(x):
        return lax.ppermute(x, "tensor", [(0, 1), (1, 0)])

    index = lax.axis_index("dp")
    group = index // GROUP
    chip = (index % GROUP) // 2
    core = index % 2
    tensor = lax.axis_index("tensor")
    is_first = core == 0
    at = core * half
    off = (1 - core) * half
    core_word = core.astype(jnp.int32).reshape(1)

    def my_half(x, start, axis=0):
        return lax.dynamic_slice_in_dim(x, start, half, axis)

    def in_order(own, other):
        return jnp.where(
            is_first, jnp.concatenate([own, other], 0), jnp.concatenate([other, own], 0)
        )

    def gather_rows(mine, needed={}):
        behind, ahead = [], []
        moving = mine
        for step in range(side):
            moving = along(after(moving, *needed.get(step, ())))
            behind.append(moving)
            ahead.append(across(moving))
        far = along(after(my_half(moving, at, moving.ndim - 2), *needed.get(side, ())))
        return [mine] + behind + ahead + [far, across(far)]

    rows = lax.broadcasted_iota(jnp.int32, (block, 1), 0)
    mine_rows = (rows < half) == is_first

    def ring_sum(*sets, needed={}):
        took_far = [across(give_far) for give_far, _, _ in sets]
        took = [across(give) for _, give, _ in sets]
        keep = [x for _, _, x in sets]
        far = [k[side * block : side * block + half].astype(f32) + t.astype(f32) for k, t in zip(keep, took_far)]
        moving = along(jnp.stack(far).astype(bf16))
        moving = jnp.where(mine_rows, jnp.concatenate([moving, moving], 1), 0).astype(f32)
        for step in reversed(range(side)):
            here = slice(step * block, (step + 1) * block)
            moving = after(moving, *needed.get(step, ()))
            added = [k[here].astype(f32) + t[here].astype(f32) for k, t in zip(keep, took)]
            moving = along((moving + jnp.stack(added)).astype(bf16))
            if step:
                moving = moving.astype(f32)
        got = across(my_half(moving, off, 1))
        return [(k, t, moving, got, n) for n, (k, t) in enumerate(zip(keep, took))]

    def spread(x):
        return lax.all_to_all(x, "dp", 0, 0, axis_index_groups=inner, tiled=True)

    small = jnp.concatenate(
        [
            norm_gain.reshape(-1),
            norm_bias.reshape(-1),
            output_bias.reshape(-1),
            (positions // 64).astype(bf16),
            (positions % 64).astype(bf16),
        ]
    )
    weights = []
    if groups == 1:
        qkv_turned = qkv_weight.transpose(0, 2, 1, 3)
        ups, downs = (qkv_turned, fc1_weight), (out_weight, fc2_weight)
        extra = jnp.concatenate([small, jnp.zeros_like(small)]).reshape(-1, 128)
        up = spread(call_pack(pack_first, 0, ups, (), (extra,)))
        small_all = up[:, UP_ROWS:].reshape(GROUP, -1)[:, : small.shape[0]]
        up_other = over(up)
        packed_down = call_pack(pack_down, 0, (), downs, ())
        down = spread(after(packed_down, up))
        down_other = over(down)
        weights.append(call_join(join_up, up, [up_other], True, False) + call_join(join_down, down, [down_other], False, True))
        packed_last = call_pack(pack_both, 1, ups, downs, ())
        firsts = (up, up_other, down)
    else:
        small_all = lax.all_gather(small, "dp", axis=0, tiled=False)
        for layer in range(LAYERS):
            up = jnp.concatenate(
                [
                    qkv_weight[layer].reshape(piece, 3, GROUP, HEAD_DIM).transpose(2, 0, 1, 3).reshape(GROUP, piece, -1),
                    fc1_weight[layer].reshape(piece, GROUP, hidden).transpose(1, 0, 2),
                ],
                axis=2,
            )
            up = lax.all_gather(spread(up), "dp", axis=0, axis_index_groups=outer, tiled=True)
            up = up.reshape(width // 128, 128, UP_ROWS)
            value = up[:, :, WIDE : WIDE + HEAD_DIM]
            first = WIDE + HEAD_DIM
            up = jnp.concatenate(
                [
                    up[:, :, :WIDE],
                    jnp.concatenate([value[:, :HEAD_DIM], value[:, HEAD_DIM:]], axis=2),
                    up[:, :, first : first + 128],
                    up[:, :, first + 128 :],
                ],
                axis=1,
            )
            down = jnp.concatenate(
                [out_weight[layer].reshape(GROUP, HEAD_DIM, piece), fc2_weight[layer].reshape(GROUP, hidden, piece)],
                axis=1,
            )
            down = lax.all_gather(spread(down), "dp", axis=0, axis_index_groups=outer, tiled=True)
            down = down.transpose(1, 0, 2).reshape(-1, width // 128, 128).transpose(1, 0, 2)
            weights.append(call_join(join_up, up, [over(up)], True, False) + call_join(join_down, down, [over(down)], False, True))
    if groups == 1:
        biases = jnp.concatenate([qkv_bias.reshape(LAYERS, 3 * HEAD_DIM), fc1_bias], axis=1)
    else:
        full_qkv = lax.all_gather(qkv_bias, "dp", axis=2, tiled=True)
        full_up = lax.all_gather(fc1_bias, "dp", axis=1, tiled=True)
        member = index % GROUP
        biases = jnp.concatenate(
            [
                lax.dynamic_slice_in_dim(full_qkv, member * HEAD_DIM, HEAD_DIM, 2).reshape(LAYERS, 3 * HEAD_DIM),
                lax.dynamic_slice_in_dim(full_up, member * hidden, hidden, 1),
            ],
            axis=1,
        )
    biases_other = over(biases)
    both_biases = jnp.stack([biases, biases_other], axis=1).astype(f32)
    bias_rows = jnp.concatenate(
        [
            both_biases[:, :, : 3 * HEAD_DIM].reshape(LAYERS, 2, 3, HEAD_DIM).transpose(0, 2, 1, 3).reshape(LAYERS, -1),
            both_biases[:, :, 3 * HEAD_DIM :].reshape(LAYERS, -1),
        ],
        axis=1,
    )
    vectors = small_all[:, : 6 * piece].reshape(n_dp, 3, LAYERS, piece).transpose(1, 2, 0, 3).reshape(3, LAYERS, 1, width).astype(f32)
    gains, shifts, added_bias = vectors[0], vectors[1], vectors[2]

    turned = jnp.where(is_first, 1, -1)
    place = jnp.sum(jnp.where(jnp.asarray(ring) == chip, jnp.arange(chips), 0))
    offsets = [0] + [-(s + 1) for s in range(side)] + [s + 1 for s in range(side)] + [chips // 2]
    places = (place + turned * jnp.asarray(offsets)) % chips
    chip_ids = jnp.sum(
        jnp.where(places[:, None] == jnp.arange(chips)[None, :], jnp.asarray(ring)[None, :], 0), axis=1
    )
    owners = group * GROUP + 2 * chip_ids + tensor
    labels = jax.vmap(lambda owner: sequence_labels(seq_lengths, seq_device, owner, block))(owners)
    rows_at = jnp.arange(block, dtype=jnp.int32)
    allowed = (
        (labels[:, :, None] == labels[:, None, :])
        & (labels[:, :, None] > 0)
        & (rows_at[None, None, :] <= rows_at[None, :, None])
    ) | (rows_at[None, None, :] == rows_at[None, :, None])
    allowed = allowed.astype(f32).reshape(chips * block, block)
    picked = (owners[:, None] == jnp.arange(n_dp)[None, :]).astype(f32)
    place_parts = jnp.dot(picked, small_all[:, 6 * piece :].astype(f32), precision=lax.Precision.HIGHEST)
    row_places = (place_parts[:, :block] * 64.0 + place_parts[:, block:]).reshape(chips * block)
    pair = ROT // 2
    frequency = 10000.0 ** (-2.0 * jnp.arange(pair, dtype=f32) / ROT)
    angles = row_places[:, None] * frequency[None, :]
    cosine, sine = jnp.cos(angles), jnp.sin(angles)
    nought = jnp.zeros_like(sine)
    rest = jnp.zeros((chips * block, HEAD_DIM - ROT), f32)
    tables = (
        jnp.concatenate([cosine, cosine, rest + 1.0] * 2, axis=1),
        jnp.concatenate([-sine, nought, rest] * 2, axis=1),
        jnp.concatenate([nought, sine, rest] * 2, axis=1),
    )

    mine = jnp.where(tensor == core, hidden_in, across(hidden_in))
    cotangent = jnp.where(tensor == core, out_cotangent, across(out_cotangent))
    cotangent = jnp.where(labels[0][:, None] > 0, cotangent, jnp.zeros_like(cotangent))
    if groups == 1:
        inputs = gather_rows(
            after(mine, packed_down, packed_last, firsts[0], firsts[2]),
            {1: (firsts[1], tables[0]), 2: (tables[1], tables[2], allowed), side: (down_other, weights[0][0])},
        )
        slab = spread(after(packed_last, inputs[-2]))
        others = tuple(over(slab[n * GROUP // 2 : (n + 1) * GROUP // 2]) for n in range(2))
        weights.append(call_join(join_halves, slab, others, True, True))
        slabs = (slab,)
    else:
        inputs = gather_rows(mine)
        slabs, others = (), ()
    state, grad_state = my_half(mine, at), my_half(cotangent, at)

    normed, heads, hidden_pre, wide, *parts = call_pass(
        "first", core_word, weights[0], tables, allowed, [bias_rows[0:1], gains[0], shifts[0]], inputs
    )
    rows_shape = (half, width)
    next_state, normed_own = call_end(
        partial(forward_end, False),
        core_word,
        ring_sum((after(parts[0], *slabs), parts[1], parts[2]), needed={})[0],
        [state, added_bias[0], gains[1], shifts[1]],
        [jax.ShapeDtypeStruct(rows_shape, f32), jax.ShapeDtypeStruct(rows_shape, bf16)],
        "forward_end",
    )
    normed_chunks = gather_rows(
        jnp.stack([in_order(normed_own, across(normed_own)), cotangent]), {0: others[:1], 2: others[1:]}
    )

    def handed_back(own_rows):
        filled = in_order(own_rows, across(own_rows))
        return jnp.where(tensor == core, filled, over(filled))

    def summed(pairs, *earlier):
        total = jnp.concatenate([own.astype(f32) + other.astype(f32) for own, other in pairs], axis=1)
        if groups > 1:
            total = total.transpose(1, 0, 2).reshape(total.shape[1], width)
            total = lax.psum_scatter(total, "dp", scatter_dimension=1, axis_index_groups=outer, tiled=True)
            total = total.reshape(total.shape[0], GROUP, piece).transpose(1, 0, 2)
        return spread(after(total.astype(bf16), *earlier))

    down_own = [(0, HEAD_DIM), (WIDE, WIDE + hidden)]
    down_other = [(HEAD_DIM, WIDE), (WIDE + hidden, WIDE + 2 * hidden)]
    up_own = [(p * WIDE, p * WIDE + HEAD_DIM) for p in range(3)] + [(3 * WIDE, 3 * WIDE + hidden)]
    up_other = [(p * WIDE + HEAD_DIM, (p + 1) * WIDE) for p in range(3)] + [(3 * WIDE + hidden, 3 * WIDE + 2 * hidden)]

    def down_gradients(wide_rows, grad_rows):
        return call_gradients(core_word, wide_rows, grad_rows, down_own, down_other, [], "down_gradients")

    def up_gradients(slim_rows, normed_rows, sums):
        return call_gradients(core_word, slim_rows, [normed_rows], up_own, up_other, [sums], "up_gradients")

    def backward_finish(ring_end, state, grad_state, layer):
        return call_end(
            backward_end,
            core_word,
            ring_end,
            [state, grad_state, gains[layer]],
            [jax.ShapeDtypeStruct(rows_shape, f32), jax.ShapeDtypeStruct(rows_shape, bf16)],
            "backward_end",
        )

    normed_last, grad_rows, wide_last, slim, sums, *parts = call_pass(
        "middle", core_word, weights[1], tables, allowed, [bias_rows[1:2]], normed_chunks
    )
    out_parts = parts[:3]
    down_pair = down_gradients(wide_last, [grad_rows])
    *up_pair, bias_last = up_gradients(slim, normed_last, sums)
    down_sent, up_sent = over(down_pair[1]), over(up_pair[1])
    grad_end, out_end = ring_sum(parts[3:], out_parts, needed={1: (down_pair[0],), 0: (up_pair[0],)})
    grad_state, grad_low = backward_finish(grad_end, next_state, grad_state, 1)
    (hidden_out,) = call_end(
        partial(forward_end, True),
        core_word,
        out_end,
        [next_state, added_bias[1]],
        [jax.ShapeDtypeStruct(rows_shape, bf16)],
        "forward_out",
    )
    hidden_out = handed_back(hidden_out)
    grad_chunks = gather_rows(in_order(grad_low, across(grad_low)), {0: (down_sent,), side: (up_sent, hidden_out)})
    both_last = summed([(up_pair[0], after(up_sent, grad_chunks[-2])), (down_pair[0], down_sent)])
    up_last, down_last = both_last[:, : UP_ROWS + SUM_ROWS], both_last[:, UP_ROWS + SUM_ROWS :]

    down_pair = down_gradients(wide, grad_chunks)
    down_sent = over(down_pair[1])
    grad_rows, slim, sums, *parts = call_pass(
        "last", core_word, weights[0], tables, allowed, [heads, after(hidden_pre, down_pair[0]), normed], grad_chunks
    )
    *up_pair, bias_first = up_gradients(slim, normed, sums)
    up_sent = over(up_pair[1])
    down_first = summed([(down_pair[0], after(down_sent, up_pair[0]))], both_last)
    needed = {1: (down_first,)}
    if groups == 1:
        filled = call_spread(both_last, both_last, 1, [])
        needed[0] = (filled[1][:, :8],)
    (grad_end,) = ring_sum((after(parts[0], up_pair[0], both_last), parts[1], parts[2]), needed=needed)
    up_first = summed([(up_pair[0], up_sent)], down_first)
    _, grad_low = backward_finish(grad_end, state, grad_state, 0)
    grad_hidden = handed_back(grad_low).astype(f32)

    ends = jnp.stack([jnp.sum(x[:, UP_ROWS : UP_ROWS + 3].astype(f32), axis=0) for x in (up_first, up_last)])
    shift_grads = ends[:, 0]
    gain_grads = (ends[:, 1] - norm_bias.astype(f32) * ends[:, 0]) / norm_gain.astype(f32)
    after_grads = ends[:, 2] / GROUP
    sums = jnp.concatenate([bias_first, bias_last], axis=0)
    sums_qkv = sums[:, : 3 * WIDE].reshape(LAYERS, 3, 2, HEAD_DIM)
    sums_up = sums[:, 3 * WIDE :].reshape(LAYERS, 2, hidden)
    bias_own, bias_other = (
        jnp.concatenate([sums_qkv[:, :, n].reshape(LAYERS, -1), sums_up[:, n]], axis=1) for n in range(2)
    )
    bias_sums = bias_own + over(bias_other)
    bias_qkv, bias_up = bias_sums[:, : 3 * HEAD_DIM].reshape(LAYERS, 3, HEAD_DIM), bias_sums[:, 3 * HEAD_DIM :]
    if groups == 1:
        grad_qkv, grad_out, grad_up, grad_down = call_spread(up_first, down_first, 0, filled)
        grad_qkv = grad_qkv.transpose(0, 2, 1, 3)
    else:
        bias_qkv = lax.all_gather(lax.psum(bias_qkv, "dp", axis_index_groups=outer), "dp", axis=2, axis_index_groups=inner, tiled=True)
        bias_up = lax.all_gather(lax.psum(bias_up, "dp", axis_index_groups=outer), "dp", axis=1, axis_index_groups=inner, tiled=True)
        bias_qkv = lax.dynamic_slice_in_dim(bias_qkv, index * qkv_bias.shape[2], qkv_bias.shape[2], 2)
        bias_up = lax.dynamic_slice_in_dim(bias_up, index * fc1_bias.shape[1], fc1_bias.shape[1], 1)
        ups = jnp.stack([up_first, up_last]).astype(f32)
        downs = jnp.stack([down_first, down_last]).astype(f32)
        grad_qkv = ups[:, :, : 3 * HEAD_DIM].reshape(LAYERS, GROUP, 3, HEAD_DIM, piece).transpose(0, 4, 2, 1, 3).reshape(LAYERS, piece, 3, -1)
        grad_up = ups[:, :, 3 * HEAD_DIM : UP_ROWS].transpose(0, 3, 1, 2).reshape(LAYERS, piece, -1)
        grad_out = downs[:, :, :HEAD_DIM].reshape(LAYERS, -1, piece)
        grad_down = downs[:, :, HEAD_DIM:].reshape(LAYERS, -1, piece)
    return (
        hidden_out,
        grad_hidden,
        gain_grads,
        shift_grads,
        grad_qkv,
        bias_qkv,
        grad_out,
        grad_up,
        bias_up,
        grad_down,
        after_grads,
    )


def solution(mesh):
    placed = (
        P("dp", None),
        P(),
        P(),
        P("dp"),
        P(None, "dp"),
        P(None, "dp"),
        P(None, "dp", None, "tensor"),
        P(None, None, ("tensor", "dp")),
        P(None, "tensor", "dp"),
        P(None, "dp", "tensor"),
        P(None, ("tensor", "dp")),
        P(None, "tensor", "dp"),
        P(None, "dp"),
        P("dp", None),
    )
    return jax.shard_map(
        partial(per_device, mesh.shape["dp"]),
        mesh=mesh,
        in_specs=placed,
        out_specs=(
            P("dp", None),
            P("dp", None),
            P(None, "dp"),
            P(None, "dp"),
            P(None, "dp", None, "tensor"),
            P(None, None, ("tensor", "dp")),
            P(None, "tensor", "dp"),
            P(None, "dp", "tensor"),
            P(None, ("tensor", "dp")),
            P(None, "tensor", "dp"),
            P(None, "dp"),
        ),
        check_vma=False,
    )
```

```python
from functools import partial

import jax
import jax.numpy as jnp
from jax import lax
from jax.experimental import pallas as pl
from jax.experimental.pallas import tpu as pltpu
from jax.sharding import PartitionSpec as P

HEAD_DIM = 64
ROT = 32
LAYERS = 2
GROUP = 16

norm_epsilon = 1e-05
masked_score = -1e30
bf16 = jnp.bfloat16
f32 = jnp.float32

contract_last = (((1,), (1,)), ((), ()))
contract_first = (((0,), (0,)), ((), ()))


def dot(a, b, dims=(((1,), (0,)), ((), ()))):
    return lax.dot_general(a, b, dims, preferred_element_type=f32)


def turn(x, cosine, up, down):
    return x * cosine + pltpu.roll(x, x.shape[1] - ROT // 2, 1) * up + pltpu.roll(x, ROT // 2, 1) * down


def stacked_heads(x):
    lane = lax.broadcasted_iota(jnp.int32, x.shape, 1)
    zero = jnp.zeros_like(x)
    return jnp.concatenate(
        [jnp.where(lane < HEAD_DIM, x, zero), jnp.where(lane < HEAD_DIM, zero, x)], axis=0
    )


def merged_heads(x):
    rows = x.shape[0] // 2
    lane = lax.broadcasted_iota(jnp.int32, (rows, x.shape[1]), 1)
    return jnp.where(lane < HEAD_DIM, x[:rows], x[rows:])


def softmax_rows(queries, keys, allowed):
    scores = dot(stacked_heads(queries), keys, contract_last) * HEAD_DIM ** (-0.5)
    masked = jnp.where(jnp.concatenate([allowed, allowed], axis=0) > 0, scores, masked_score)
    weights = jnp.exp(masked - jnp.max(masked, axis=1, keepdims=True))
    return weights / jnp.sum(weights, axis=1, keepdims=True)


def sequence_labels(seq_lengths, seq_device, owner, count_rows):
    index = jnp.arange(seq_lengths.shape[0], dtype=jnp.int32)
    owned = jnp.where(seq_device == owner, seq_lengths, 0)
    earlier = index[None, :] < index[:, None]
    starts = jnp.sum(jnp.where(earlier, owned[None, :], 0), axis=1)
    places = jnp.arange(count_rows, dtype=jnp.int32)
    inside = (places[:, None] >= starts[None, :]) & (places[:, None] < (starts + owned)[None, :])
    return jnp.sum(jnp.where(inside, index[None, :] + 1, 0), axis=1)


def gelu_parts(v):
    c = (2.0 / jnp.pi) ** 0.5
    inner = jnp.tanh(c * (v + 0.044715 * v * v * v))
    value = 0.5 * v * (1.0 + inner)
    slope = 0.5 * (1.0 + inner) + 0.5 * v * (1.0 - inner * inner) * c * (1.0 + 3.0 * 0.044715 * v * v)
    return value, slope


VMEM_SPEC = pl.BlockSpec(memory_space=pltpu.VMEM)
ANY_SPEC = pl.BlockSpec(memory_space=pl.ANY)
SMEM_SPEC = pl.BlockSpec(memory_space=pltpu.SMEM)
WIDE = 2 * HEAD_DIM
UP_ROWS = 3 * HEAD_DIM + 256
DOWN_ROWS = HEAD_DIM + 256
SUM_ROWS = 16
MEMBERS = 4


def after(x, *others):
    if not others:
        return x
    return lax.optimization_barrier((x, *others))[0]


def left_lanes(x):
    return lax.broadcasted_iota(jnp.int32, x.shape, 1) < HEAD_DIM


def swapped(x):
    return pltpu.roll(x, HEAD_DIM, 1)


def zipped(a, b):
    left = left_lanes(a)
    return jnp.where(left, a, swapped(b)).astype(bf16), jnp.where(left, swapped(a), b).astype(bf16)


def pack_up(qkv_ref, fc1_ref, *rest):
    out_ref = rest[-1]
    for pair in range(MEMBERS // 2):
        lanes = slice(pair * 128, (pair + 1) * 128)
        q, k, v = (qkv_ref[0, p, :, lanes].astype(f32) for p in range(3))
        here, there = 2 * pair, 2 * pair + 1
        out_ref[here, :WIDE], out_ref[there, :WIDE] = zipped(q, k)
        rows = q.shape[0] // 2
        out_ref[here, WIDE : WIDE + rows], out_ref[there, WIDE : WIDE + rows] = zipped(v[:rows], v[rows:])
        base = WIDE + rows
        for d in (here, there):
            for h in range(2):
                out_ref[d, base + h * 128 : base + (h + 1) * 128] = fc1_ref[0, :, (2 * d + h) * 128 : (2 * d + h + 1) * 128]


def pack_first(qkv_ref, fc1_ref, small_ref, out_ref):
    pack_up(qkv_ref, fc1_ref, out_ref)
    for d in range(MEMBERS):
        out_ref[d, UP_ROWS:] = small_ref[...]


def pack_both(qkv_ref, fc1_ref, out_w_ref, fc2_ref, out_ref):
    pack_up(qkv_ref, fc1_ref, out_ref)
    pack_down(out_w_ref, fc2_ref, out_ref.at[:, UP_ROWS:])


def pack_down(out_w_ref, fc2_ref, out_ref):
    for d in range(MEMBERS):
        out_ref[d, :HEAD_DIM] = out_w_ref[0, d * HEAD_DIM : (d + 1) * HEAD_DIM]
        out_ref[d, HEAD_DIM:] = fc2_ref[0, d * 256 : (d + 1) * 256]


def call_pack(body, layer, ups, downs, small):
    rows, specs = 0, []
    if ups:
        rows += UP_ROWS
        specs += [
            pl.BlockSpec((1, 3, 128, MEMBERS * HEAD_DIM), lambda i: (layer, 0, 0, i)),
            pl.BlockSpec((1, 128, MEMBERS * 256), lambda i: (layer, 0, i)),
        ]
    if downs:
        rows += DOWN_ROWS
        specs += [
            pl.BlockSpec((1, MEMBERS * HEAD_DIM, 128), lambda i: (layer, i, 0)),
            pl.BlockSpec((1, MEMBERS * 256, 128), lambda i: (layer, i, 0)),
        ]
    if small:
        rows += small[0].shape[0]
        specs.append(pl.BlockSpec(small[0].shape, lambda i: (0, 0)))
    return pl.pallas_call(
        body,
        grid=(GROUP // MEMBERS,),
        in_specs=specs,
        out_specs=pl.BlockSpec((MEMBERS, rows, 128), lambda i: (i, 0, 0)),
        out_shape=jax.ShapeDtypeStruct((GROUP, rows, 128), bf16),
        cost_estimate=pl.CostEstimate(flops=0, bytes_accessed=GROUP * rows * 128 * 8, transcendentals=0),
        name=body.__name__,
    )(*ups, *downs, *small)


def join_up(own_ref, other_ref, out_ref):
    for e in range(MEMBERS):
        rows = slice(e * 128, (e + 1) * 128)
        a, b = own_ref[e, :WIDE].astype(f32), other_ref[e, :WIDE].astype(f32)
        out_ref[rows, :WIDE], out_ref[rows, WIDE : 2 * WIDE] = zipped(a, b)
        a, b = own_ref[e, WIDE : WIDE + 64].astype(f32), other_ref[e, WIDE : WIDE + 64].astype(f32)
        top, bottom = zipped(a, b)
        out_ref[e * 128 : e * 128 + 64, 2 * WIDE : 3 * WIDE] = top
        out_ref[e * 128 + 64 : (e + 1) * 128, 2 * WIDE : 3 * WIDE] = bottom
        for n, ref in enumerate((own_ref, other_ref)):
            for h in range(2):
                lanes = 3 * WIDE + n * 256 + h * 128
                out_ref[rows, lanes : lanes + 128] = ref[e, WIDE + 64 + h * 128 : WIDE + 64 + (h + 1) * 128]


def join_down(own_ref, other_ref, out_ref):
    base = own_ref.shape[1] - DOWN_ROWS
    for e in range(MEMBERS):
        lanes = slice(e * 128, (e + 1) * 128)
        for n, ref in enumerate((own_ref, other_ref)):
            out_ref[n * HEAD_DIM : (n + 1) * HEAD_DIM, lanes] = ref[e, base : base + HEAD_DIM]
            out_ref[WIDE + n * 256 : WIDE + (n + 1) * 256, lanes] = ref[e, base + HEAD_DIM :]


def join_both(own_ref, other_ref, up_ref, down_ref):
    join_up(own_ref, other_ref, up_ref)
    join_down(own_ref, other_ref, down_ref)


def join_halves(own_ref, lower_ref, upper_ref, up_ref, down_ref):
    lower = pl.program_id(0) < GROUP // MEMBERS // 2

    @pl.when(lower)
    def _():
        join_both(own_ref, lower_ref, up_ref, down_ref)

    @pl.when(jnp.logical_not(lower))
    def _():
        join_both(own_ref, upper_ref, up_ref, down_ref)


def call_join(body, own, others, ups, downs):
    rows = own.shape[1]
    steps = GROUP // MEMBERS
    spec = pl.BlockSpec((MEMBERS, rows, 128), lambda i: (i, 0, 0))
    other_specs = [spec]
    if len(others) == 2:
        other_specs = [
            pl.BlockSpec((MEMBERS, rows, 128), lambda i: (jnp.minimum(i, steps // 2 - 1), 0, 0)),
            pl.BlockSpec((MEMBERS, rows, 128), lambda i: (jnp.maximum(i - steps // 2, 0), 0, 0)),
        ]
    specs, shapes = [], []
    if ups:
        specs.append(pl.BlockSpec((MEMBERS * 128, 2 * UP_ROWS), lambda i: (i, 0)))
        shapes.append(jax.ShapeDtypeStruct((GROUP * 128, 2 * UP_ROWS), bf16))
    if downs:
        specs.append(pl.BlockSpec((2 * DOWN_ROWS, MEMBERS * 128), lambda i: (0, i)))
        shapes.append(jax.ShapeDtypeStruct((2 * DOWN_ROWS, GROUP * 128), bf16))
    return pl.pallas_call(
        body,
        grid=(GROUP // MEMBERS,),
        in_specs=[spec] + other_specs,
        out_specs=specs,
        out_shape=shapes,
        cost_estimate=pl.CostEstimate(flops=0, bytes_accessed=GROUP * rows * 128 * 12, transcendentals=0),
        name=body.__name__,
    )(own, *others)


def slot_copies(refs, which, target, core):
    block = target.shape[0] // 8
    half = block // 2
    pairs = []
    for slot in range(7):
        ref = refs[slot] if which is None else refs[slot].at[which]
        pairs.append((ref, target.at[pl.ds(slot * block, block)]))
    for n, at in ((7, core * half), (8, (1 - core) * half)):
        ref = refs[n] if which is None else refs[n].at[which]
        pairs.append((ref, target.at[pl.ds(pl.multiple_of(7 * block + at, half), half)]))
    return pairs


def split_copies(part, far_ref, give_ref, keep_ref, core):
    block = part.shape[0] // 8
    half = block // 2
    at, off = core * half, (1 - core) * half

    def rows(slot, start):
        return part.at[pl.ds(pl.multiple_of(slot * block + start, half), half)]

    return [
        (rows(7, off), far_ref),
        (part.at[pl.ds(block, 3 * block)], give_ref.at[pl.ds(0, 3 * block)]),
        (rows(0, off), give_ref.at[pl.ds(3 * block, half)]),
        (part.at[pl.ds(4 * block, 3 * block)], keep_ref.at[pl.ds(0, 3 * block)]),
        (rows(7, at), keep_ref.at[pl.ds(3 * block, half)]),
        (rows(0, at), keep_ref.at[pl.ds(3 * block + half, half)]),
    ]


def run_copies(pairs, sems, first):
    made = [pltpu.make_async_copy(a, b, sems.at[first + n]) for n, (a, b) in enumerate(pairs)]
    for copy in made:
        copy.start()
    return made


def heads_forward(chances, values):
    return merged_heads(dot(chances.astype(bf16), values)).astype(bf16)


def heads_backward(chances, queries, keys, values, grad, tables):
    grads = stacked_heads(grad)
    grad_chances = dot(grads, values, contract_last)
    grad_values = dot(chances.astype(bf16), grads, contract_first)
    centre = jnp.sum(grad_chances * chances, axis=1, keepdims=True)
    grad_scores = (chances * (grad_chances - centre)).astype(bf16)
    scale = HEAD_DIM ** (-0.5)
    grad_queries = merged_heads(dot(grad_scores, keys)) * scale
    grad_keys = dot(grad_scores, stacked_heads(queries), contract_first) * scale
    cosine, up, down = tables
    back = (cosine, -up, -down)
    return turn(grad_queries, *back).astype(bf16), turn(grad_keys, *back).astype(bf16), grad_values.astype(bf16)


def layer_pass(mode, *refs):
    refs = list(refs)

    def take(n):
        out = refs[:n]
        del refs[:n]
        return out

    forward, backward = mode != "last", mode != "first"
    core_ref, up_ref, down_ref, cos_ref, sin_up_ref, sin_down_ref, allowed_ref = take(7)
    core = core_ref[0]
    if mode == "first":
        bias_ref, gain_ref, shift_ref = take(3)
        rows_in = take(9)
    elif mode == "middle":
        (bias_ref,) = take(1)
        rows_in = take(9)
        grads_in = take(9)
    else:
        heads_ref, hidden_ref, normed_ref = take(3)
        grads_in = take(9)
    if mode == "first":
        normed_ref, heads_ref, hidden_ref, wide_ref = take(4)
        outs = take(3)
        raw, part, sems = take(3)
    elif mode == "middle":
        normed_ref, grad_rows_ref, wide_ref, slim_ref, sums_ref = take(5)
        outs = take(3)
        grad_outs = take(3)
        part, grad_part, sems = take(3)
    else:
        grad_rows_ref, slim_ref, sums_ref = take(3)
        grad_outs = take(3)
        grad_part, sems = take(2)

    pairs = []
    if mode == "first":
        pairs += slot_copies(rows_in, 0, raw, core)
    if mode == "middle":
        pairs += slot_copies(rows_in, None, normed_ref, core)
        pairs += slot_copies(grads_in, 1, grad_rows_ref, core)
    if mode == "last":
        pairs += slot_copies(grads_in, None, grad_rows_ref, core)
    for copy in run_copies(pairs, sems, 0):
        copy.wait()

    total = allowed_ref.shape[0]
    block = allowed_ref.shape[1]
    step = 2 * block

    if mode == "first":
        tile = 32

        def norm_tile(i, carry):
            at = pl.ds(pl.multiple_of(i * tile, tile), tile)
            x = raw[at, :].astype(f32)
            centred = x - jnp.mean(x, axis=1, keepdims=True)
            inverse = lax.rsqrt(jnp.mean(centred * centred, axis=1, keepdims=True) + norm_epsilon)
            normed_ref[at, :] = (centred * inverse * gain_ref[...] + shift_ref[...]).astype(bf16)
            return carry

        lax.fori_loop(0, total // tile, norm_tile, 0)

    if backward:
        sums_ref[...] = jnp.zeros_like(sums_ref)

    def one(p, carry):
        at = pl.ds(pl.multiple_of(p * step, step), step)
        if forward:
            before = dot(normed_ref[at, :], up_ref[...]) + bias_ref[...]
            hidden_pre = before[:, 3 * WIDE :]
        else:
            hidden_pre = hidden_ref[at, :]
        value, slope = gelu_parts(hidden_pre)
        if backward:
            grad_wide = dot(grad_rows_ref[at, :], down_ref[...], contract_last)
            slim_ref[at, 3 * WIDE :] = (grad_wide[:, WIDE:] * slope).astype(bf16)
        if forward:
            wide_ref[at, WIDE:] = value.astype(bf16)
        if mode == "first":
            hidden_ref[at, :] = hidden_pre
        for b in range(2):
            mine = slice(b * block, (b + 1) * block)
            own = pl.ds(pl.multiple_of(p * step + b * block, block), block)
            tables = (cos_ref[own, :], sin_up_ref[own, :], sin_down_ref[own, :])
            if forward:
                queries = turn(before[mine, :WIDE], *tables).astype(bf16)
                keys = turn(before[mine, WIDE : 2 * WIDE], *tables).astype(bf16)
                values = before[mine, 2 * WIDE : 3 * WIDE].astype(bf16)
            else:
                queries = heads_ref[own, :WIDE]
                keys = heads_ref[own, WIDE : 2 * WIDE]
                values = heads_ref[own, 2 * WIDE :]
            if mode == "first":
                heads_ref[own, :WIDE] = queries
                heads_ref[own, WIDE : 2 * WIDE] = keys
                heads_ref[own, 2 * WIDE :] = values
            chances = softmax_rows(queries, keys, allowed_ref[own, :])
            if forward:
                wide_ref[own, :WIDE] = heads_forward(chances, values)
            if backward:
                grads = heads_backward(
                    chances, queries, keys, values, grad_wide[mine, :WIDE].astype(bf16), tables
                )
                for n in range(3):
                    slim_ref[own, n * WIDE : (n + 1) * WIDE] = grads[n]
        if forward:
            part[at, :] = dot(wide_ref[at, :], down_ref[...]).astype(bf16)
        if backward:
            grad_normed = dot(slim_ref[at, :], up_ref[...], contract_last)
            grad_part[at, :] = grad_normed.astype(bf16)
            for n, rows in enumerate(
                (grad_normed, grad_normed * normed_ref[at, :].astype(f32), grad_rows_ref[at, :].astype(f32))
            ):
                sums_ref[n : n + 1] += jnp.sum(rows, axis=0, keepdims=True)
        return carry

    lax.fori_loop(0, total // step, one, 0)
    pairs = []
    if backward:
        pairs += split_copies(grad_part, *grad_outs, core)
    if forward:
        pairs += split_copies(part, *outs, core)
    for copy in run_copies(pairs, sems, 0):
        copy.wait()


def call_pass(mode, core, weights, tables, allowed, extra, chunks):
    total, block = allowed.shape
    half = block // 2
    width = weights[0].shape[0]
    slim = weights[0].shape[1]
    wide = weights[1].shape[0]
    parts = [
        jax.ShapeDtypeStruct((half, width), bf16),
        jax.ShapeDtypeStruct((3 * block + half, width), bf16),
        jax.ShapeDtypeStruct((4 * block, width), bf16),
    ]
    full = jax.ShapeDtypeStruct((total, width), bf16)
    sums = jax.ShapeDtypeStruct((SUM_ROWS, width), f32)
    slim_rows = jax.ShapeDtypeStruct((total, slim), bf16)
    wide_rows = jax.ShapeDtypeStruct((total, wide), bf16)
    if mode == "first":
        kept = [
            full,
            jax.ShapeDtypeStruct((total, 3 * WIDE), bf16),
            jax.ShapeDtypeStruct((total, slim - 3 * WIDE), f32),
            wide_rows,
        ]
        buffers = 2
    elif mode == "middle":
        kept = [full, full, wide_rows, slim_rows, sums]
        parts = parts * 2
        buffers = 2
    else:
        kept = [full, slim_rows, sums]
        buffers = 1
    passes = 2 if mode == "middle" else 1
    return pl.pallas_call(
        partial(layer_pass, mode),
        in_specs=[SMEM_SPEC] + [VMEM_SPEC] * (6 + len(extra)) + [ANY_SPEC] * len(chunks),
        out_specs=[VMEM_SPEC] * len(kept) + [ANY_SPEC] * len(parts),
        out_shape=kept + parts,
        scratch_shapes=[pltpu.VMEM((total, width), bf16)] * buffers + [pltpu.SemaphoreType.DMA((18,))],
        cost_estimate=pl.CostEstimate(
            flops=6 * total * width * (slim + wide) * passes,
            bytes_accessed=20_000_000 * passes,
            transcendentals=total * slim,
        ),
        name="pass_" + mode,
    )(core, *weights, *tables, allowed, *extra, *chunks)


def gradient_slabs(own_rows, other_rows, with_sums, pieces_in, core_ref, left_ref, *rest):
    right_refs, rest = rest[:pieces_in], rest[pieces_in:]
    if with_sums:
        sums_ref, *rest = rest
    own_ref, other_ref, *rest = rest
    turned_ref = rest[-1]
    if pieces_in == 1:
        right = right_refs[0][...]
    else:
        a, b = right_refs[-2][...], right_refs[-1][...]
        first = jnp.full(a.shape, core_ref[0]) == 0
        halves = [jnp.where(first, a, b), jnp.where(first, b, a)]
        right = jnp.concatenate([ref[...] for ref in right_refs[:-2]] + halves, axis=0)

    @pl.when(pl.program_id(0) == 0)
    def _():
        width = left_ref.shape[1]
        for n in range(width // 128):
            lanes = slice(n * 128, (n + 1) * 128)
            left = left_ref[:, lanes].astype(f32)
            if with_sums:
                rest[0][:, lanes] = jnp.sum(left, axis=0, keepdims=True)
            turned_ref[lanes, :] = left.T.astype(bf16)

    product = dot(turned_ref[...], right).astype(bf16)
    for ref, pieces in ((own_ref, own_rows), (other_ref, other_rows)):
        place = 0
        for first, last in pieces:
            for e in range(2):
                ref[e, place : place + last - first] = product[first:last, e * 128 : (e + 1) * 128]
            place += last - first
        if with_sums:
            for e in range(2):
                ref[e, place:] = sums_ref[:, e * 128 : (e + 1) * 128].astype(bf16)


def call_gradients(core, left, right, own_rows, other_rows, sums, name):
    total, height = left.shape
    width = right[0].shape[1]
    with_sums = len(sums) > 0
    rows = height // 2 + (SUM_ROWS if with_sums else 0)
    slab = pl.BlockSpec((2, rows, 128), lambda i: (i, 0, 0))
    shape = jax.ShapeDtypeStruct((width // 128, rows, 128), bf16)
    out_specs, out_shape = [slab, slab], [shape, shape]
    if with_sums:
        out_specs.append(pl.BlockSpec((1, height), lambda i: (0, 0)))
        out_shape.append(jax.ShapeDtypeStruct((1, height), f32))
    return pl.pallas_call(
        partial(gradient_slabs, own_rows, other_rows, with_sums, len(right)),
        grid=(width // 256,),
        in_specs=[SMEM_SPEC, pl.BlockSpec((total, height), lambda i: (0, 0))]
        + [pl.BlockSpec((x.shape[0], 256), lambda i: (0, i)) for x in (*right, *sums)],
        out_specs=out_specs,
        out_shape=out_shape,
        scratch_shapes=[pltpu.VMEM((height, total), bf16)],
        cost_estimate=pl.CostEstimate(
            flops=4 * total * height * width, bytes_accessed=2 * (total * (width + height) + 2 * height * width), transcendentals=0
        ),
        name=name,
    )(core, left, *right, *sums)


def spread_gradients(up_ref, down_ref, *rest):
    qkv_ref, out_w_ref, fc1_ref, fc2_ref, mark_ref = rest[-5:]
    mark_ref[...] = jnp.zeros_like(mark_ref)
    down = down_ref.shape[1] - DOWN_ROWS
    for p in range(3):
        rows = slice(p * HEAD_DIM, (p + 1) * HEAD_DIM)
        both = jnp.concatenate([up_ref[0, rows].astype(f32), up_ref[1, rows].astype(f32)], axis=0)
        qkv_ref[0, p] = both.T
    base = 3 * HEAD_DIM
    for d in range(2):
        for h in range(2):
            fc1_ref[0, :, (2 * d + h) * 128 : (2 * d + h + 1) * 128] = (
                up_ref[d, base + h * 128 : base + (h + 1) * 128].astype(f32).T
            )
        out_w_ref[0, d * HEAD_DIM : (d + 1) * HEAD_DIM] = down_ref[d, down : down + HEAD_DIM].astype(f32)
        fc2_ref[0, d * 256 : (d + 1) * 256] = down_ref[d, down + HEAD_DIM :].astype(f32)


def call_spread(up, down, layer, filled):
    shapes = [
        jax.ShapeDtypeStruct((LAYERS, 3, 128, GROUP * HEAD_DIM), f32),
        jax.ShapeDtypeStruct((LAYERS, GROUP * HEAD_DIM, 128), f32),
        jax.ShapeDtypeStruct((LAYERS, 128, GROUP * 256), f32),
        jax.ShapeDtypeStruct((LAYERS, GROUP * 256, 128), f32),
        jax.ShapeDtypeStruct((8, 128), f32),
    ]
    return pl.pallas_call(
        spread_gradients,
        grid=(GROUP // 2,),
        in_specs=[
            pl.BlockSpec((2, up.shape[1], 128), lambda i: (i, 0, 0)),
            pl.BlockSpec((2, down.shape[1], 128), lambda i: (i, 0, 0)),
        ]
        + [ANY_SPEC] * len(filled),
        out_specs=[
            pl.BlockSpec((1, 3, 128, 128), lambda i: (layer, 0, 0, i)),
            pl.BlockSpec((1, 128, 128), lambda i: (layer, i, 0)),
            pl.BlockSpec((1, 128, 512), lambda i: (layer, 0, i)),
            pl.BlockSpec((1, 512, 128), lambda i: (layer, i, 0)),
            pl.BlockSpec((8, 128), lambda i: (0, 0)),
        ],
        out_shape=shapes,
        input_output_aliases={2 + n: n for n in range(len(filled))},
        name="spread_gradients",
    )(up, down, *filled)


def ring_total(core_ref, keep_ref, took_ref, moving_ref, got_ref):
    half = got_ref.shape[0]
    arrived = moving_ref[pl.ds(pl.multiple_of(core_ref[0] * half, half), half), :]
    return keep_ref[...].astype(f32) + took_ref[...].astype(f32) + arrived.astype(f32) + got_ref[...].astype(f32)


def centred_rows(state):
    centred = state - jnp.mean(state, axis=1, keepdims=True)
    return centred, lax.rsqrt(jnp.mean(centred * centred, axis=1, keepdims=True) + norm_epsilon)


def forward_end(last, core_ref, keep_ref, took_ref, moving_ref, got_ref, state_ref, after_ref, *rest):
    state = state_ref[...].astype(f32) + ring_total(core_ref, keep_ref, took_ref, moving_ref, got_ref) + after_ref[...]
    if last:
        rest[0][...] = state.astype(bf16)
        return
    gain_ref, shift_ref, state_out, normed_ref = rest
    state_out[...] = state
    centred, inverse = centred_rows(state)
    normed_ref[...] = (centred * inverse * gain_ref[...] + shift_ref[...]).astype(bf16)


def backward_end(core_ref, keep_ref, took_ref, moving_ref, got_ref, state_ref, grad_ref, gain_ref, grad_out, low_ref):
    grad_normed = ring_total(core_ref, keep_ref, took_ref, moving_ref, got_ref)
    centred, inverse = centred_rows(state_ref[...].astype(f32))
    xhat = centred * inverse
    before = grad_ref[...].astype(f32)
    scaled = grad_normed * gain_ref[...]
    after = before + (
        scaled - jnp.mean(scaled, axis=1, keepdims=True) - xhat * jnp.mean(scaled * xhat, axis=1, keepdims=True)
    ) * inverse
    grad_out[...] = after
    low_ref[...] = after.astype(bf16)


def call_end(body, core, ring, extra, shapes, name):
    keep, took, moving, got, n_sum = ring
    _, half, width = got.shape

    def rows_of(array):
        n = array.shape[0] // half - 1
        return pl.BlockSpec((half, width), lambda i: (n, 0))

    def whole_of(array):
        return pl.BlockSpec(array.shape, lambda i: (0,) * len(array.shape))

    def one_of(array):
        return pl.BlockSpec((None,) + array.shape[1:], lambda i: (n_sum, 0, 0))

    return pl.pallas_call(
        body,
        grid=(1,),
        in_specs=[SMEM_SPEC, rows_of(keep), rows_of(took), one_of(moving), one_of(got)] + [whole_of(x) for x in extra],
        out_specs=[whole_of(x) for x in shapes],
        out_shape=shapes,
        cost_estimate=pl.CostEstimate(flops=0, bytes_accessed=half * width, transcendentals=0),
        name=name,
    )(core, keep, took, moving, got, *extra)


def per_device(
    n_dp,
    hidden_in,
    seq_lengths,
    seq_device,
    positions,
    norm_gain,
    norm_bias,
    qkv_weight,
    qkv_bias,
    out_weight,
    fc1_weight,
    fc1_bias,
    fc2_weight,
    output_bias,
    out_cotangent,
):
    block = hidden_in.shape[0]
    half = block // 2
    width = hidden_in.shape[1]
    piece = norm_gain.shape[1]
    hidden = fc1_weight.shape[2] // GROUP
    groups = n_dp // GROUP
    chips = GROUP // 2
    side = chips // 2 - 1

    if groups == 1:
        ring = [2 * a for a in range(chips // 2)] + [2 * a + 1 for a in reversed(range(chips // 2))]
    else:
        ring = list(range(chips // 2)) + list(reversed(range(chips // 2, chips)))
    ring_pairs = []
    for g in range(groups):
        for place in range(chips):
            for core, step in ((0, 1), (1, -1)):
                ring_pairs.append(
                    (
                        g * GROUP + ring[place] * 2 + core,
                        g * GROUP + ring[(place + step) % chips] * 2 + core,
                    )
                )
    core_pairs = [(i, i ^ 1) for i in range(n_dp)]
    inner = [[g * GROUP + i for i in range(GROUP)] for g in range(groups)]
    outer = [[g * GROUP + i for g in range(groups)] for i in range(GROUP)]
    if groups == 1:
        inner = None

    def along(x):
        return lax.ppermute(x, "dp", ring_pairs)

    def across(x):
        return lax.ppermute(x, "dp", core_pairs)

    def over(x):
        return lax.ppermute(x, "tensor", [(0, 1), (1, 0)])

    index = lax.axis_index("dp")
    group = index // GROUP
    chip = (index % GROUP) // 2
    core = index % 2
    tensor = lax.axis_index("tensor")
    is_first = core == 0
    at = core * half
    off = (1 - core) * half
    core_word = core.astype(jnp.int32).reshape(1)

    def my_half(x, start, axis=0):
        return lax.dynamic_slice_in_dim(x, start, half, axis)

    def in_order(own, other):
        return jnp.where(
            is_first, jnp.concatenate([own, other], 0), jnp.concatenate([other, own], 0)
        )

    def gather_rows(mine, needed={}):
        behind, ahead = [], []
        moving = mine
        for step in range(side):
            moving = along(after(moving, *needed.get(step, ())))
            behind.append(moving)
            ahead.append(across(moving))
        far = along(after(my_half(moving, at, moving.ndim - 2), *needed.get(side, ())))
        return [mine] + behind + ahead + [far, across(far)]

    rows = lax.broadcasted_iota(jnp.int32, (block, 1), 0)
    mine_rows = (rows < half) == is_first

    def ring_sum(*sets, needed={}):
        took_far = [across(give_far) for give_far, _, _ in sets]
        took = [across(give) for _, give, _ in sets]
        keep = [x for _, _, x in sets]
        far = [k[side * block : side * block + half].astype(f32) + t.astype(f32) for k, t in zip(keep, took_far)]
        moving = along(jnp.stack(far).astype(bf16))
        moving = jnp.where(mine_rows, jnp.concatenate([moving, moving], 1), 0).astype(f32)
        for step in reversed(range(side)):
            here = slice(step * block, (step + 1) * block)
            moving = after(moving, *needed.get(step, ()))
            added = [k[here].astype(f32) + t[here].astype(f32) for k, t in zip(keep, took)]
            moving = along((moving + jnp.stack(added)).astype(bf16))
            if step:
                moving = moving.astype(f32)
        got = across(my_half(moving, off, 1))
        return [(k, t, moving, got, n) for n, (k, t) in enumerate(zip(keep, took))]

    def spread(x):
        return lax.all_to_all(x, "dp", 0, 0, axis_index_groups=inner, tiled=True)

    small = jnp.concatenate(
        [
            norm_gain.reshape(-1),
            norm_bias.reshape(-1),
            output_bias.reshape(-1),
            (positions // 64).astype(bf16),
            (positions % 64).astype(bf16),
        ]
    )
    weights = []
    if groups == 1:
        qkv_turned = qkv_weight.transpose(0, 2, 1, 3)
        ups, downs = (qkv_turned, fc1_weight), (out_weight, fc2_weight)
        extra = jnp.concatenate([small, jnp.zeros_like(small)]).reshape(-1, 128)
        up = spread(call_pack(pack_first, 0, ups, (), (extra,)))
        small_all = up[:, UP_ROWS:].reshape(GROUP, -1)[:, : small.shape[0]]
        up_other = over(up)
        packed_down = call_pack(pack_down, 0, (), downs, ())
        down = spread(after(packed_down, up))
        down_other = over(down)
        weights.append(call_join(join_up, up, [up_other], True, False) + call_join(join_down, down, [down_other], False, True))
        packed_last = call_pack(pack_both, 1, ups, downs, ())
        firsts = (up, up_other, down)
    else:
        small_all = lax.all_gather(small, "dp", axis=0, tiled=False)
        for layer in range(LAYERS):
            up = jnp.concatenate(
                [
                    qkv_weight[layer].reshape(piece, 3, GROUP, HEAD_DIM).transpose(2, 0, 1, 3).reshape(GROUP, piece, -1),
                    fc1_weight[layer].reshape(piece, GROUP, hidden).transpose(1, 0, 2),
                ],
                axis=2,
            )
            up = lax.all_gather(spread(up), "dp", axis=0, axis_index_groups=outer, tiled=True)
            up = up.reshape(width // 128, 128, UP_ROWS)
            value = up[:, :, WIDE : WIDE + HEAD_DIM]
            first = WIDE + HEAD_DIM
            up = jnp.concatenate(
                [
                    up[:, :, :WIDE],
                    jnp.concatenate([value[:, :HEAD_DIM], value[:, HEAD_DIM:]], axis=2),
                    up[:, :, first : first + 128],
                    up[:, :, first + 128 :],
                ],
                axis=1,
            )
            down = jnp.concatenate(
                [out_weight[layer].reshape(GROUP, HEAD_DIM, piece), fc2_weight[layer].reshape(GROUP, hidden, piece)],
                axis=1,
            )
            down = lax.all_gather(spread(down), "dp", axis=0, axis_index_groups=outer, tiled=True)
            down = down.transpose(1, 0, 2).reshape(-1, width // 128, 128).transpose(1, 0, 2)
            weights.append(call_join(join_up, up, [over(up)], True, False) + call_join(join_down, down, [over(down)], False, True))
    if groups == 1:
        biases = jnp.concatenate([qkv_bias.reshape(LAYERS, 3 * HEAD_DIM), fc1_bias], axis=1)
    else:
        full_qkv = lax.all_gather(qkv_bias, "dp", axis=2, tiled=True)
        full_up = lax.all_gather(fc1_bias, "dp", axis=1, tiled=True)
        member = index % GROUP
        biases = jnp.concatenate(
            [
                lax.dynamic_slice_in_dim(full_qkv, member * HEAD_DIM, HEAD_DIM, 2).reshape(LAYERS, 3 * HEAD_DIM),
                lax.dynamic_slice_in_dim(full_up, member * hidden, hidden, 1),
            ],
            axis=1,
        )
    biases_other = over(biases)
    both_biases = jnp.stack([biases, biases_other], axis=1).astype(f32)
    bias_rows = jnp.concatenate(
        [
            both_biases[:, :, : 3 * HEAD_DIM].reshape(LAYERS, 2, 3, HEAD_DIM).transpose(0, 2, 1, 3).reshape(LAYERS, -1),
            both_biases[:, :, 3 * HEAD_DIM :].reshape(LAYERS, -1),
        ],
        axis=1,
    )
    vectors = small_all[:, : 6 * piece].reshape(n_dp, 3, LAYERS, piece).transpose(1, 2, 0, 3).reshape(3, LAYERS, 1, width).astype(f32)
    gains, shifts, added_bias = vectors[0], vectors[1], vectors[2]

    turned = jnp.where(is_first, 1, -1)
    place = jnp.sum(jnp.where(jnp.asarray(ring) == chip, jnp.arange(chips), 0))
    offsets = [0] + [-(s + 1) for s in range(side)] + [s + 1 for s in range(side)] + [chips // 2]
    places = (place + turned * jnp.asarray(offsets)) % chips
    chip_ids = jnp.sum(
        jnp.where(places[:, None] == jnp.arange(chips)[None, :], jnp.asarray(ring)[None, :], 0), axis=1
    )
    owners = group * GROUP + 2 * chip_ids + tensor
    labels = jax.vmap(lambda owner: sequence_labels(seq_lengths, seq_device, owner, block))(owners)
    rows_at = jnp.arange(block, dtype=jnp.int32)
    allowed = (
        (labels[:, :, None] == labels[:, None, :])
        & (labels[:, :, None] > 0)
        & (rows_at[None, None, :] <= rows_at[None, :, None])
    ) | (rows_at[None, None, :] == rows_at[None, :, None])
    allowed = allowed.astype(f32).reshape(chips * block, block)
    picked = (owners[:, None] == jnp.arange(n_dp)[None, :]).astype(f32)
    place_parts = jnp.dot(picked, small_all[:, 6 * piece :].astype(f32), precision=lax.Precision.HIGHEST)
    row_places = (place_parts[:, :block] * 64.0 + place_parts[:, block:]).reshape(chips * block)
    pair = ROT // 2
    frequency = 10000.0 ** (-2.0 * jnp.arange(pair, dtype=f32) / ROT)
    angles = row_places[:, None] * frequency[None, :]
    cosine, sine = jnp.cos(angles), jnp.sin(angles)
    nought = jnp.zeros_like(sine)
    rest = jnp.zeros((chips * block, HEAD_DIM - ROT), f32)
    tables = (
        jnp.concatenate([cosine, cosine, rest + 1.0] * 2, axis=1),
        jnp.concatenate([-sine, nought, rest] * 2, axis=1),
        jnp.concatenate([nought, sine, rest] * 2, axis=1),
    )

    both = jnp.stack([hidden_in, out_cotangent])
    both = jnp.where(tensor == core, both, across(both))
    keeps = jnp.stack([jnp.ones_like(labels[0]), (labels[0] > 0).astype(labels.dtype)]).astype(bf16)
    both = both * keeps[:, :, None]
    if groups == 1:
        inputs = gather_rows(
            after(both, packed_down, packed_last, firsts[0], firsts[2]),
            {1: (firsts[1], tables[0]), 2: (tables[1], tables[2], allowed), side: (down_other, weights[0][0])},
        )
        slab = spread(after(packed_last, inputs[-2]))
        others = tuple(over(slab[n * GROUP // 2 : (n + 1) * GROUP // 2]) for n in range(2))
        weights.append(call_join(join_halves, slab, others, True, True))
        slabs = (slab,)
    else:
        inputs = gather_rows(both)
        slabs, others = (), ()
    state, grad_state = my_half(both, at, 1)

    normed, heads, hidden_pre, wide, *parts = call_pass(
        "first", core_word, weights[0], tables, allowed, [bias_rows[0:1], gains[0], shifts[0]], inputs
    )
    rows_shape = (half, width)
    next_state, normed_own = call_end(
        partial(forward_end, False),
        core_word,
        ring_sum((after(parts[0], *slabs), parts[1], parts[2]), needed={0: others[:1]})[0],
        [state, added_bias[0], gains[1], shifts[1]],
        [jax.ShapeDtypeStruct(rows_shape, f32), jax.ShapeDtypeStruct(rows_shape, bf16)],
        "forward_end",
    )
    normed_chunks = gather_rows(in_order(normed_own, across(normed_own)), {1: others[1:]})

    def handed_back(own_rows):
        filled = in_order(own_rows, across(own_rows))
        return jnp.where(tensor == core, filled, over(filled))

    def summed(pairs, *earlier):
        total = jnp.concatenate([own.astype(f32) + other.astype(f32) for own, other in pairs], axis=1)
        if groups > 1:
            total = total.transpose(1, 0, 2).reshape(total.shape[1], width)
            total = lax.psum_scatter(total, "dp", scatter_dimension=1, axis_index_groups=outer, tiled=True)
            total = total.reshape(total.shape[0], GROUP, piece).transpose(1, 0, 2)
        return spread(after(total.astype(bf16), *earlier))

    down_own = [(0, HEAD_DIM), (WIDE, WIDE + hidden)]
    down_other = [(HEAD_DIM, WIDE), (WIDE + hidden, WIDE + 2 * hidden)]
    up_own = [(p * WIDE, p * WIDE + HEAD_DIM) for p in range(3)] + [(3 * WIDE, 3 * WIDE + hidden)]
    up_other = [(p * WIDE + HEAD_DIM, (p + 1) * WIDE) for p in range(3)] + [(3 * WIDE + hidden, 3 * WIDE + 2 * hidden)]

    def down_gradients(wide_rows, grad_rows):
        return call_gradients(core_word, wide_rows, grad_rows, down_own, down_other, [], "down_gradients")

    def up_gradients(slim_rows, normed_rows, sums):
        return call_gradients(core_word, slim_rows, [normed_rows], up_own, up_other, [sums], "up_gradients")

    def backward_finish(ring_end, state, grad_state, layer):
        return call_end(
            backward_end,
            core_word,
            ring_end,
            [state, grad_state, gains[layer]],
            [jax.ShapeDtypeStruct(rows_shape, f32), jax.ShapeDtypeStruct(rows_shape, bf16)],
            "backward_end",
        )

    normed_last, grad_rows, wide_last, slim, sums, *parts = call_pass(
        "middle", core_word, weights[1], tables, allowed, [bias_rows[1:2]], normed_chunks + inputs
    )
    out_parts = parts[:3]
    down_pair = down_gradients(wide_last, [grad_rows])
    *up_pair, bias_last = up_gradients(slim, normed_last, sums)
    down_sent, up_sent = over(down_pair[1]), over(up_pair[1])
    grad_end, out_end = ring_sum(parts[3:], out_parts, needed={1: (down_pair[0],), 0: (up_pair[0],)})
    grad_state, grad_low = backward_finish(grad_end, next_state, grad_state, 1)
    (hidden_out,) = call_end(
        partial(forward_end, True),
        core_word,
        out_end,
        [next_state, added_bias[1]],
        [jax.ShapeDtypeStruct(rows_shape, bf16)],
        "forward_out",
    )
    hidden_out = handed_back(hidden_out)
    grad_chunks = gather_rows(in_order(grad_low, across(grad_low)), {0: (down_sent,), 2: (up_sent,)})
    both_last = summed([(up_pair[0], after(up_sent, grad_chunks[-2])), (down_pair[0], down_sent)])
    up_last, down_last = both_last[:, : UP_ROWS + SUM_ROWS], both_last[:, UP_ROWS + SUM_ROWS :]

    down_pair = down_gradients(wide, grad_chunks)
    down_sent = over(down_pair[1])
    grad_rows, slim, sums, *parts = call_pass(
        "last", core_word, weights[0], tables, allowed, [heads, after(hidden_pre, down_pair[0]), normed], grad_chunks
    )
    *up_pair, bias_first = up_gradients(slim, normed, sums)
    up_sent = over(up_pair[1])
    down_first = summed([(down_pair[0], after(down_sent, up_pair[0]))], both_last)
    needed = {1: (down_first,)}
    if groups == 1:
        *filled, mark = call_spread(both_last, both_last, 1, [])
        needed[0] = (mark, hidden_out)
    (grad_end,) = ring_sum((after(parts[0], up_pair[0], both_last), parts[1], parts[2]), needed=needed)
    up_first = summed([(up_pair[0], up_sent)], down_first)
    _, grad_low = backward_finish(grad_end, state, grad_state, 0)
    grad_hidden = handed_back(grad_low).astype(f32)

    ends = jnp.stack([jnp.sum(x[:, UP_ROWS : UP_ROWS + 3].astype(f32), axis=0) for x in (up_first, up_last)])
    shift_grads = ends[:, 0]
    gain_grads = (ends[:, 1] - norm_bias.astype(f32) * ends[:, 0]) / norm_gain.astype(f32)
    after_grads = ends[:, 2] / GROUP
    sums = jnp.concatenate([bias_first, bias_last], axis=0)
    sums_qkv = sums[:, : 3 * WIDE].reshape(LAYERS, 3, 2, HEAD_DIM)
    sums_up = sums[:, 3 * WIDE :].reshape(LAYERS, 2, hidden)
    bias_own, bias_other = (
        jnp.concatenate([sums_qkv[:, :, n].reshape(LAYERS, -1), sums_up[:, n]], axis=1) for n in range(2)
    )
    bias_sums = bias_own + over(bias_other)
    bias_qkv, bias_up = bias_sums[:, : 3 * HEAD_DIM].reshape(LAYERS, 3, HEAD_DIM), bias_sums[:, 3 * HEAD_DIM :]
    if groups == 1:
        grad_qkv, grad_out, grad_up, grad_down, _ = call_spread(up_first, down_first, 0, filled)
        grad_qkv = grad_qkv.transpose(0, 2, 1, 3)
    else:
        bias_qkv = lax.all_gather(lax.psum(bias_qkv, "dp", axis_index_groups=outer), "dp", axis=2, axis_index_groups=inner, tiled=True)
        bias_up = lax.all_gather(lax.psum(bias_up, "dp", axis_index_groups=outer), "dp", axis=1, axis_index_groups=inner, tiled=True)
        bias_qkv = lax.dynamic_slice_in_dim(bias_qkv, index * qkv_bias.shape[2], qkv_bias.shape[2], 2)
        bias_up = lax.dynamic_slice_in_dim(bias_up, index * fc1_bias.shape[1], fc1_bias.shape[1], 1)
        ups = jnp.stack([up_first, up_last]).astype(f32)
        downs = jnp.stack([down_first, down_last]).astype(f32)
        grad_qkv = ups[:, :, : 3 * HEAD_DIM].reshape(LAYERS, GROUP, 3, HEAD_DIM, piece).transpose(0, 4, 2, 1, 3).reshape(LAYERS, piece, 3, -1)
        grad_up = ups[:, :, 3 * HEAD_DIM : UP_ROWS].transpose(0, 3, 1, 2).reshape(LAYERS, piece, -1)
        grad_out = downs[:, :, :HEAD_DIM].reshape(LAYERS, -1, piece)
        grad_down = downs[:, :, HEAD_DIM:].reshape(LAYERS, -1, piece)
    return (
        hidden_out,
        grad_hidden,
        gain_grads,
        shift_grads,
        grad_qkv,
        bias_qkv,
        grad_out,
        grad_up,
        bias_up,
        grad_down,
        after_grads,
    )


def solution(mesh):
    placed = (
        P("dp", None),
        P(),
        P(),
        P("dp"),
        P(None, "dp"),
        P(None, "dp"),
        P(None, "dp", None, "tensor"),
        P(None, None, ("tensor", "dp")),
        P(None, "tensor", "dp"),
        P(None, "dp", "tensor"),
        P(None, ("tensor", "dp")),
        P(None, "tensor", "dp"),
        P(None, "dp"),
        P("dp", None),
    )
    return jax.shard_map(
        partial(per_device, mesh.shape["dp"]),
        mesh=mesh,
        in_specs=placed,
        out_specs=(
            P("dp", None),
            P("dp", None),
            P(None, "dp"),
            P(None, "dp"),
            P(None, "dp", None, "tensor"),
            P(None, None, ("tensor", "dp")),
            P(None, "tensor", "dp"),
            P(None, "dp", "tensor"),
            P(None, ("tensor", "dp")),
            P(None, "tensor", "dp"),
            P(None, "dp"),
        ),
        check_vma=False,
    )
```

```python
from functools import partial

import jax
import jax.numpy as jnp
from jax import lax
from jax.experimental import pallas as pl
from jax.experimental.pallas import tpu as pltpu
from jax.sharding import PartitionSpec as P

HEAD_DIM = 64
ROT = 32
LAYERS = 2
GROUP = 16

norm_epsilon = 1e-05
masked_score = -1e30
bf16 = jnp.bfloat16
f32 = jnp.float32

contract_last = (((1,), (1,)), ((), ()))
contract_first = (((0,), (0,)), ((), ()))


def dot(a, b, dims=(((1,), (0,)), ((), ()))):
    return lax.dot_general(a, b, dims, preferred_element_type=f32)


def turn(x, cosine, up, down):
    return x * cosine + pltpu.roll(x, x.shape[1] - ROT // 2, 1) * up + pltpu.roll(x, ROT // 2, 1) * down


def stacked_heads(x):
    lane = lax.broadcasted_iota(jnp.int32, x.shape, 1)
    zero = jnp.zeros_like(x)
    return jnp.concatenate(
        [jnp.where(lane < HEAD_DIM, x, zero), jnp.where(lane < HEAD_DIM, zero, x)], axis=0
    )


def merged_heads(x):
    rows = x.shape[0] // 2
    lane = lax.broadcasted_iota(jnp.int32, (rows, x.shape[1]), 1)
    return jnp.where(lane < HEAD_DIM, x[:rows], x[rows:])


def softmax_rows(queries, keys, allowed):
    scores = dot(stacked_heads(queries), keys, contract_last) * HEAD_DIM ** (-0.5)
    masked = jnp.where(jnp.concatenate([allowed, allowed], axis=0) > 0, scores, masked_score)
    weights = jnp.exp(masked - jnp.max(masked, axis=1, keepdims=True))
    return weights / jnp.sum(weights, axis=1, keepdims=True)


def sequence_labels(seq_lengths, seq_device, owner, count_rows):
    index = jnp.arange(seq_lengths.shape[0], dtype=jnp.int32)
    owned = jnp.where(seq_device == owner, seq_lengths, 0)
    earlier = index[None, :] < index[:, None]
    starts = jnp.sum(jnp.where(earlier, owned[None, :], 0), axis=1)
    places = jnp.arange(count_rows, dtype=jnp.int32)
    inside = (places[:, None] >= starts[None, :]) & (places[:, None] < (starts + owned)[None, :])
    return jnp.sum(jnp.where(inside, index[None, :] + 1, 0), axis=1)


def gelu_parts(v):
    c = (2.0 / jnp.pi) ** 0.5
    inner = jnp.tanh(c * (v + 0.044715 * v * v * v))
    value = 0.5 * v * (1.0 + inner)
    slope = 0.5 * (1.0 + inner) + 0.5 * v * (1.0 - inner * inner) * c * (1.0 + 3.0 * 0.044715 * v * v)
    return value, slope


VMEM_SPEC = pl.BlockSpec(memory_space=pltpu.VMEM)
ANY_SPEC = pl.BlockSpec(memory_space=pl.ANY)
SMEM_SPEC = pl.BlockSpec(memory_space=pltpu.SMEM)
WIDE = 2 * HEAD_DIM
UP_ROWS = 3 * HEAD_DIM + 256
DOWN_ROWS = HEAD_DIM + 256
SUM_ROWS = 16
MEMBERS = 4


def after(x, *others):
    if not others:
        return x
    return lax.optimization_barrier((x, *others))[0]


def left_lanes(x):
    return lax.broadcasted_iota(jnp.int32, x.shape, 1) < HEAD_DIM


def swapped(x):
    return pltpu.roll(x, HEAD_DIM, 1)


def zipped(a, b):
    left = left_lanes(a)
    return jnp.where(left, a, swapped(b)).astype(bf16), jnp.where(left, swapped(a), b).astype(bf16)


def pack_up(qkv_ref, fc1_ref, *rest):
    out_ref = rest[-1]
    for pair in range(MEMBERS // 2):
        lanes = slice(pair * 128, (pair + 1) * 128)
        q, k, v = (qkv_ref[0, p, :, lanes].astype(f32) for p in range(3))
        here, there = 2 * pair, 2 * pair + 1
        out_ref[here, :WIDE], out_ref[there, :WIDE] = zipped(q, k)
        rows = q.shape[0] // 2
        out_ref[here, WIDE : WIDE + rows], out_ref[there, WIDE : WIDE + rows] = zipped(v[:rows], v[rows:])
        base = WIDE + rows
        for d in (here, there):
            for h in range(2):
                out_ref[d, base + h * 128 : base + (h + 1) * 128] = fc1_ref[0, :, (2 * d + h) * 128 : (2 * d + h + 1) * 128]


def pack_first(qkv_ref, fc1_ref, small_ref, out_ref):
    pack_up(qkv_ref, fc1_ref, out_ref)
    for d in range(MEMBERS):
        out_ref[d, UP_ROWS:] = small_ref[...]


def pack_both(qkv_ref, fc1_ref, out_w_ref, fc2_ref, out_ref):
    pack_up(qkv_ref, fc1_ref, out_ref)
    pack_down(out_w_ref, fc2_ref, out_ref.at[:, UP_ROWS:])


def pack_down(out_w_ref, fc2_ref, out_ref):
    for d in range(MEMBERS):
        out_ref[d, :HEAD_DIM] = out_w_ref[0, d * HEAD_DIM : (d + 1) * HEAD_DIM]
        out_ref[d, HEAD_DIM:] = fc2_ref[0, d * 256 : (d + 1) * 256]


def call_pack(body, layer, ups, downs, small):
    rows, specs = 0, []
    if ups:
        rows += UP_ROWS
        specs += [
            pl.BlockSpec((1, 3, 128, MEMBERS * HEAD_DIM), lambda i: (layer, 0, 0, i)),
            pl.BlockSpec((1, 128, MEMBERS * 256), lambda i: (layer, 0, i)),
        ]
    if downs:
        rows += DOWN_ROWS
        specs += [
            pl.BlockSpec((1, MEMBERS * HEAD_DIM, 128), lambda i: (layer, i, 0)),
            pl.BlockSpec((1, MEMBERS * 256, 128), lambda i: (layer, i, 0)),
        ]
    if small:
        rows += small[0].shape[0]
        specs.append(pl.BlockSpec(small[0].shape, lambda i: (0, 0)))
    return pl.pallas_call(
        body,
        grid=(GROUP // MEMBERS,),
        in_specs=specs,
        out_specs=pl.BlockSpec((MEMBERS, rows, 128), lambda i: (i, 0, 0)),
        out_shape=jax.ShapeDtypeStruct((GROUP, rows, 128), bf16),
        cost_estimate=pl.CostEstimate(flops=0, bytes_accessed=GROUP * rows * 128 * 8, transcendentals=0),
        name=body.__name__,
    )(*ups, *downs, *small)


def join_up(own_ref, other_ref, out_ref):
    for e in range(MEMBERS):
        rows = slice(e * 128, (e + 1) * 128)
        a, b = own_ref[e, :WIDE].astype(f32), other_ref[e, :WIDE].astype(f32)
        out_ref[rows, :WIDE], out_ref[rows, WIDE : 2 * WIDE] = zipped(a, b)
        a, b = own_ref[e, WIDE : WIDE + 64].astype(f32), other_ref[e, WIDE : WIDE + 64].astype(f32)
        top, bottom = zipped(a, b)
        out_ref[e * 128 : e * 128 + 64, 2 * WIDE : 3 * WIDE] = top
        out_ref[e * 128 + 64 : (e + 1) * 128, 2 * WIDE : 3 * WIDE] = bottom
        for n, ref in enumerate((own_ref, other_ref)):
            for h in range(2):
                lanes = 3 * WIDE + n * 256 + h * 128
                out_ref[rows, lanes : lanes + 128] = ref[e, WIDE + 64 + h * 128 : WIDE + 64 + (h + 1) * 128]


def join_down(own_ref, other_ref, out_ref):
    base = own_ref.shape[1] - DOWN_ROWS
    for e in range(MEMBERS):
        lanes = slice(e * 128, (e + 1) * 128)
        for n, ref in enumerate((own_ref, other_ref)):
            out_ref[n * HEAD_DIM : (n + 1) * HEAD_DIM, lanes] = ref[e, base : base + HEAD_DIM]
            out_ref[WIDE + n * 256 : WIDE + (n + 1) * 256, lanes] = ref[e, base + HEAD_DIM :]


def join_both(own_ref, other_ref, up_ref, down_ref):
    join_up(own_ref, other_ref, up_ref)
    join_down(own_ref, other_ref, down_ref)


def join_halves(own_ref, lower_ref, upper_ref, up_ref, down_ref):
    lower = pl.program_id(0) < GROUP // MEMBERS // 2

    @pl.when(lower)
    def _():
        join_both(own_ref, lower_ref, up_ref, down_ref)

    @pl.when(jnp.logical_not(lower))
    def _():
        join_both(own_ref, upper_ref, up_ref, down_ref)


def call_join(body, own, others, ups, downs):
    rows = own.shape[1]
    steps = GROUP // MEMBERS
    spec = pl.BlockSpec((MEMBERS, rows, 128), lambda i: (i, 0, 0))
    other_specs = [spec]
    if len(others) == 2:
        other_specs = [
            pl.BlockSpec((MEMBERS, rows, 128), lambda i: (jnp.minimum(i, steps // 2 - 1), 0, 0)),
            pl.BlockSpec((MEMBERS, rows, 128), lambda i: (jnp.maximum(i - steps // 2, 0), 0, 0)),
        ]
    specs, shapes = [], []
    if ups:
        specs.append(pl.BlockSpec((MEMBERS * 128, 2 * UP_ROWS), lambda i: (i, 0)))
        shapes.append(jax.ShapeDtypeStruct((GROUP * 128, 2 * UP_ROWS), bf16))
    if downs:
        specs.append(pl.BlockSpec((2 * DOWN_ROWS, MEMBERS * 128), lambda i: (0, i)))
        shapes.append(jax.ShapeDtypeStruct((2 * DOWN_ROWS, GROUP * 128), bf16))
    return pl.pallas_call(
        body,
        grid=(GROUP // MEMBERS,),
        in_specs=[spec] + other_specs,
        out_specs=specs,
        out_shape=shapes,
        cost_estimate=pl.CostEstimate(flops=0, bytes_accessed=GROUP * rows * 128 * 12, transcendentals=0),
        name=body.__name__,
    )(own, *others)


def slot_copies(refs, which, target, core):
    block = target.shape[0] // 8
    half = block // 2
    pairs = []
    for slot in range(7):
        ref = refs[slot] if which is None else refs[slot].at[which]
        pairs.append((ref, target.at[pl.ds(slot * block, block)]))
    for n, at in ((7, core * half), (8, (1 - core) * half)):
        ref = refs[n] if which is None else refs[n].at[which]
        pairs.append((ref, target.at[pl.ds(pl.multiple_of(7 * block + at, half), half)]))
    return pairs


def split_copies(part, far_ref, give_ref, keep_ref, core):
    block = part.shape[0] // 8
    half = block // 2
    at, off = core * half, (1 - core) * half

    def rows(slot, start):
        return part.at[pl.ds(pl.multiple_of(slot * block + start, half), half)]

    return [
        (rows(7, off), far_ref),
        (part.at[pl.ds(block, 3 * block)], give_ref.at[pl.ds(0, 3 * block)]),
        (rows(0, off), give_ref.at[pl.ds(3 * block, half)]),
        (part.at[pl.ds(4 * block, 3 * block)], keep_ref.at[pl.ds(0, 3 * block)]),
        (rows(7, at), keep_ref.at[pl.ds(3 * block, half)]),
        (rows(0, at), keep_ref.at[pl.ds(3 * block + half, half)]),
    ]


def run_copies(pairs, sems, first):
    made = [pltpu.make_async_copy(a, b, sems.at[first + n]) for n, (a, b) in enumerate(pairs)]
    for copy in made:
        copy.start()
    return made


def heads_forward(chances, values):
    return merged_heads(dot(chances.astype(bf16), values)).astype(bf16)


def heads_backward(chances, queries, keys, values, grad, tables):
    grads = stacked_heads(grad)
    grad_chances = dot(grads, values, contract_last)
    grad_values = dot(chances.astype(bf16), grads, contract_first)
    centre = jnp.sum(grad_chances * chances, axis=1, keepdims=True)
    grad_scores = (chances * (grad_chances - centre)).astype(bf16)
    scale = HEAD_DIM ** (-0.5)
    grad_queries = merged_heads(dot(grad_scores, keys)) * scale
    grad_keys = dot(grad_scores, stacked_heads(queries), contract_first) * scale
    cosine, up, down = tables
    back = (cosine, -up, -down)
    return turn(grad_queries, *back).astype(bf16), turn(grad_keys, *back).astype(bf16), grad_values.astype(bf16)


def layer_pass(mode, *refs):
    refs = list(refs)

    def take(n):
        out = refs[:n]
        del refs[:n]
        return out

    forward, backward = mode != "last", mode != "first"
    core_ref, up_ref, down_ref, cos_ref, sin_up_ref, sin_down_ref, allowed_ref = take(7)
    core = core_ref[0]
    if mode == "first":
        bias_ref, gain_ref, shift_ref = take(3)
        rows_in = take(9)
    elif mode == "middle":
        (bias_ref,) = take(1)
        rows_in = take(9)
        grads_in = take(9)
    else:
        heads_ref, hidden_ref, normed_ref = take(3)
        grads_in = take(9)
    if mode == "first":
        normed_ref, heads_ref, hidden_ref, wide_ref = take(4)
        outs = take(3)
        raw, part, sems = take(3)
    elif mode == "middle":
        normed_ref, grad_rows_ref, wide_ref, slim_ref, sums_ref = take(5)
        outs = take(3)
        grad_outs = take(3)
        part, grad_part, sems = take(3)
    else:
        grad_rows_ref, slim_ref, sums_ref = take(3)
        grad_outs = take(3)
        grad_part, sems = take(2)

    pairs = []
    if mode == "first":
        pairs += slot_copies(rows_in, 0, raw, core)
    if mode == "middle":
        pairs += slot_copies(rows_in, None, normed_ref, core)
        pairs += slot_copies(grads_in, 1, grad_rows_ref, core)
    if mode == "last":
        pairs += slot_copies(grads_in, None, grad_rows_ref, core)
    for copy in run_copies(pairs, sems, 0):
        copy.wait()

    total = allowed_ref.shape[0]
    block = allowed_ref.shape[1]
    step = 2 * block

    if mode == "first":
        tile = 32

        def norm_tile(i, carry):
            at = pl.ds(pl.multiple_of(i * tile, tile), tile)
            x = raw[at, :].astype(f32)
            centred = x - jnp.mean(x, axis=1, keepdims=True)
            inverse = lax.rsqrt(jnp.mean(centred * centred, axis=1, keepdims=True) + norm_epsilon)
            normed_ref[at, :] = (centred * inverse * gain_ref[...] + shift_ref[...]).astype(bf16)
            return carry

        lax.fori_loop(0, total // tile, norm_tile, 0)

    if backward:
        sums_ref[...] = jnp.zeros_like(sums_ref)

    def one(p, carry):
        at = pl.ds(pl.multiple_of(p * step, step), step)
        if forward:
            before = dot(normed_ref[at, :], up_ref[...]) + bias_ref[...]
            hidden_pre = before[:, 3 * WIDE :]
        else:
            hidden_pre = hidden_ref[at, :]
        value, slope = gelu_parts(hidden_pre)
        if backward:
            grad_wide = dot(grad_rows_ref[at, :], down_ref[...], contract_last)
            slim_ref[at, 3 * WIDE :] = (grad_wide[:, WIDE:] * slope).astype(bf16)
        if forward:
            wide_ref[at, WIDE:] = value.astype(bf16)
        if mode == "first":
            hidden_ref[at, :] = hidden_pre
        for b in range(2):
            mine = slice(b * block, (b + 1) * block)
            own = pl.ds(pl.multiple_of(p * step + b * block, block), block)
            tables = (cos_ref[own, :], sin_up_ref[own, :], sin_down_ref[own, :])
            if forward:
                queries = turn(before[mine, :WIDE], *tables).astype(bf16)
                keys = turn(before[mine, WIDE : 2 * WIDE], *tables).astype(bf16)
                values = before[mine, 2 * WIDE : 3 * WIDE].astype(bf16)
            else:
                queries = heads_ref[own, :WIDE]
                keys = heads_ref[own, WIDE : 2 * WIDE]
                values = heads_ref[own, 2 * WIDE :]
            if mode == "first":
                heads_ref[own, :WIDE] = queries
                heads_ref[own, WIDE : 2 * WIDE] = keys
                heads_ref[own, 2 * WIDE :] = values
            chances = softmax_rows(queries, keys, allowed_ref[own, :])
            if forward:
                wide_ref[own, :WIDE] = heads_forward(chances, values)
            if backward:
                grads = heads_backward(
                    chances, queries, keys, values, grad_wide[mine, :WIDE].astype(bf16), tables
                )
                for n in range(3):
                    slim_ref[own, n * WIDE : (n + 1) * WIDE] = grads[n]
        if forward:
            part[at, :] = dot(wide_ref[at, :], down_ref[...]).astype(bf16)
        if backward:
            grad_normed = dot(slim_ref[at, :], up_ref[...], contract_last)
            grad_part[at, :] = grad_normed.astype(bf16)
            for n, rows in enumerate(
                (grad_normed, grad_normed * normed_ref[at, :].astype(f32), grad_rows_ref[at, :].astype(f32))
            ):
                sums_ref[n : n + 1] += jnp.sum(rows, axis=0, keepdims=True)
        return carry

    lax.fori_loop(0, total // step, one, 0)
    pairs = []
    if backward:
        pairs += split_copies(grad_part, *grad_outs, core)
    if forward:
        pairs += split_copies(part, *outs, core)
    for copy in run_copies(pairs, sems, 0):
        copy.wait()


def call_pass(mode, core, weights, tables, allowed, extra, chunks):
    total, block = allowed.shape
    half = block // 2
    width = weights[0].shape[0]
    slim = weights[0].shape[1]
    wide = weights[1].shape[0]
    parts = [
        jax.ShapeDtypeStruct((half, width), bf16),
        jax.ShapeDtypeStruct((3 * block + half, width), bf16),
        jax.ShapeDtypeStruct((4 * block, width), bf16),
    ]
    full = jax.ShapeDtypeStruct((total, width), bf16)
    sums = jax.ShapeDtypeStruct((SUM_ROWS, width), f32)
    slim_rows = jax.ShapeDtypeStruct((total, slim), bf16)
    wide_rows = jax.ShapeDtypeStruct((total, wide), bf16)
    if mode == "first":
        kept = [
            full,
            jax.ShapeDtypeStruct((total, 3 * WIDE), bf16),
            jax.ShapeDtypeStruct((total, slim - 3 * WIDE), f32),
            wide_rows,
        ]
        buffers = 2
    elif mode == "middle":
        kept = [full, full, wide_rows, slim_rows, sums]
        parts = parts * 2
        buffers = 2
    else:
        kept = [full, slim_rows, sums]
        buffers = 1
    passes = 2 if mode == "middle" else 1
    return pl.pallas_call(
        partial(layer_pass, mode),
        in_specs=[SMEM_SPEC] + [VMEM_SPEC] * (6 + len(extra)) + [ANY_SPEC] * len(chunks),
        out_specs=[VMEM_SPEC] * len(kept) + [ANY_SPEC] * len(parts),
        out_shape=kept + parts,
        scratch_shapes=[pltpu.VMEM((total, width), bf16)] * buffers + [pltpu.SemaphoreType.DMA((18,))],
        cost_estimate=pl.CostEstimate(
            flops=6 * total * width * (slim + wide) * passes,
            bytes_accessed=20_000_000 * passes,
            transcendentals=total * slim,
        ),
        name="pass_" + mode,
    )(core, *weights, *tables, allowed, *extra, *chunks)


def gradient_slabs(own_rows, other_rows, with_sums, pieces_in, core_ref, left_ref, *rest):
    right_refs, rest = rest[:pieces_in], rest[pieces_in:]
    if with_sums:
        sums_ref, *rest = rest
    own_ref, other_ref, *rest = rest
    turned_ref = rest[-1]
    if pieces_in == 1:
        right = right_refs[0][...]
    else:
        a, b = right_refs[-2][...], right_refs[-1][...]
        first = jnp.full(a.shape, core_ref[0]) == 0
        halves = [jnp.where(first, a, b), jnp.where(first, b, a)]
        right = jnp.concatenate([ref[...] for ref in right_refs[:-2]] + halves, axis=0)

    @pl.when(pl.program_id(0) == 0)
    def _():
        width = left_ref.shape[1]
        for n in range(width // 128):
            lanes = slice(n * 128, (n + 1) * 128)
            left = left_ref[:, lanes].astype(f32)
            if with_sums:
                rest[0][:, lanes] = jnp.sum(left, axis=0, keepdims=True)
            turned_ref[lanes, :] = left.T.astype(bf16)

    product = dot(turned_ref[...], right).astype(bf16)
    for ref, pieces in ((own_ref, own_rows), (other_ref, other_rows)):
        place = 0
        for first, last in pieces:
            for e in range(2):
                ref[e, place : place + last - first] = product[first:last, e * 128 : (e + 1) * 128]
            place += last - first
        if with_sums:
            for e in range(2):
                ref[e, place:] = sums_ref[:, e * 128 : (e + 1) * 128].astype(bf16)


def call_gradients(core, left, right, own_rows, other_rows, sums, name):
    total, height = left.shape
    width = right[0].shape[1]
    with_sums = len(sums) > 0
    rows = height // 2 + (SUM_ROWS if with_sums else 0)
    slab = pl.BlockSpec((2, rows, 128), lambda i: (i, 0, 0))
    shape = jax.ShapeDtypeStruct((width // 128, rows, 128), bf16)
    out_specs, out_shape = [slab, slab], [shape, shape]
    if with_sums:
        out_specs.append(pl.BlockSpec((1, height), lambda i: (0, 0)))
        out_shape.append(jax.ShapeDtypeStruct((1, height), f32))
    return pl.pallas_call(
        partial(gradient_slabs, own_rows, other_rows, with_sums, len(right)),
        grid=(width // 256,),
        in_specs=[SMEM_SPEC, pl.BlockSpec((total, height), lambda i: (0, 0))]
        + [pl.BlockSpec((x.shape[0], 256), lambda i: (0, i)) for x in (*right, *sums)],
        out_specs=out_specs,
        out_shape=out_shape,
        scratch_shapes=[pltpu.VMEM((height, total), bf16)],
        cost_estimate=pl.CostEstimate(
            flops=4 * total * height * width, bytes_accessed=2 * (total * (width + height) + 2 * height * width), transcendentals=0
        ),
        name=name,
    )(core, left, *right, *sums)


def spread_gradients(up_ref, down_ref, *rest):
    qkv_ref, out_w_ref, fc1_ref, fc2_ref, mark_ref = rest[-5:]
    mark_ref[...] = jnp.zeros_like(mark_ref)
    for p in range(3):
        rows = slice(p * HEAD_DIM, (p + 1) * HEAD_DIM)
        both = jnp.concatenate([up_ref[0, rows].astype(f32), up_ref[1, rows].astype(f32)], axis=0)
        qkv_ref[0, p] = both.T
    base = 3 * HEAD_DIM
    for d in range(2):
        for h in range(2):
            fc1_ref[0, :, (2 * d + h) * 128 : (2 * d + h + 1) * 128] = (
                up_ref[d, base + h * 128 : base + (h + 1) * 128].astype(f32).T
            )
        out_w_ref[0, d * HEAD_DIM : (d + 1) * HEAD_DIM] = down_ref[d, :HEAD_DIM].astype(f32)
        fc2_ref[0, d * 256 : (d + 1) * 256] = down_ref[d, HEAD_DIM:].astype(f32)


def call_spread(up, down, layer, filled):
    shapes = [
        jax.ShapeDtypeStruct((LAYERS, 3, 128, GROUP * HEAD_DIM), f32),
        jax.ShapeDtypeStruct((LAYERS, GROUP * HEAD_DIM, 128), f32),
        jax.ShapeDtypeStruct((LAYERS, 128, GROUP * 256), f32),
        jax.ShapeDtypeStruct((LAYERS, GROUP * 256, 128), f32),
        jax.ShapeDtypeStruct((8, 128), f32),
    ]
    return pl.pallas_call(
        spread_gradients,
        grid=(GROUP // 2,),
        in_specs=[
            pl.BlockSpec((2, up.shape[1], 128), lambda i: (i, 0, 0)),
            pl.BlockSpec((2, down.shape[1], 128), lambda i: (i, 0, 0)),
        ]
        + [ANY_SPEC] * len(filled),
        out_specs=[
            pl.BlockSpec((1, 3, 128, 128), lambda i: (layer, 0, 0, i)),
            pl.BlockSpec((1, 128, 128), lambda i: (layer, i, 0)),
            pl.BlockSpec((1, 128, 512), lambda i: (layer, 0, i)),
            pl.BlockSpec((1, 512, 128), lambda i: (layer, i, 0)),
            pl.BlockSpec((8, 128), lambda i: (0, 0)),
        ],
        out_shape=shapes,
        input_output_aliases={2 + n: n for n in range(len(filled))},
        name="spread_gradients",
    )(up, down, *filled)


def ring_total(core_ref, keep_ref, took_ref, moving_ref, got_ref):
    half = got_ref.shape[0]
    arrived = moving_ref[pl.ds(pl.multiple_of(core_ref[0] * half, half), half), :]
    return keep_ref[...].astype(f32) + took_ref[...].astype(f32) + arrived.astype(f32) + got_ref[...].astype(f32)


def centred_rows(state):
    centred = state - jnp.mean(state, axis=1, keepdims=True)
    return centred, lax.rsqrt(jnp.mean(centred * centred, axis=1, keepdims=True) + norm_epsilon)


def forward_end(last, core_ref, keep_ref, took_ref, moving_ref, got_ref, state_ref, after_ref, *rest):
    state = state_ref[...].astype(f32) + ring_total(core_ref, keep_ref, took_ref, moving_ref, got_ref) + after_ref[...]
    if last:
        rest[0][...] = state.astype(bf16)
        return
    gain_ref, shift_ref, state_out, normed_ref = rest
    state_out[...] = state
    centred, inverse = centred_rows(state)
    normed_ref[...] = (centred * inverse * gain_ref[...] + shift_ref[...]).astype(bf16)


def backward_end(core_ref, keep_ref, took_ref, moving_ref, got_ref, state_ref, grad_ref, gain_ref, *rest):
    grad_out, low_ref = rest[-2:]
    grad_normed = ring_total(core_ref, keep_ref, took_ref, moving_ref, got_ref)
    centred, inverse = centred_rows(state_ref[...].astype(f32))
    xhat = centred * inverse
    before = grad_ref[...].astype(f32)
    scaled = grad_normed * gain_ref[...]
    after = before + (
        scaled - jnp.mean(scaled, axis=1, keepdims=True) - xhat * jnp.mean(scaled * xhat, axis=1, keepdims=True)
    ) * inverse
    grad_out[...] = after
    low_ref[...] = after.astype(bf16)


def call_end(body, core, ring, extra, shapes, name):
    keep, took, moving, got, n_sum = ring
    _, half, width = got.shape

    def rows_of(array):
        n = array.shape[0] // half - 1
        return pl.BlockSpec((half, width), lambda i: (n, 0))

    def whole_of(array):
        return pl.BlockSpec(array.shape, lambda i: (0,) * len(array.shape))

    def one_of(array):
        return pl.BlockSpec((None,) + array.shape[1:], lambda i: (n_sum, 0, 0))

    return pl.pallas_call(
        body,
        grid=(1,),
        in_specs=[SMEM_SPEC, rows_of(keep), rows_of(took), one_of(moving), one_of(got)] + [whole_of(x) for x in extra],
        out_specs=[whole_of(x) for x in shapes],
        out_shape=shapes,
        name=name,
    )(core, keep, took, moving, got, *extra)


def per_device(
    n_dp,
    hidden_in,
    seq_lengths,
    seq_device,
    positions,
    norm_gain,
    norm_bias,
    qkv_weight,
    qkv_bias,
    out_weight,
    fc1_weight,
    fc1_bias,
    fc2_weight,
    output_bias,
    out_cotangent,
):
    block = hidden_in.shape[0]
    half = block // 2
    width = hidden_in.shape[1]
    piece = norm_gain.shape[1]
    hidden = fc1_weight.shape[2] // GROUP
    groups = n_dp // GROUP
    chips = GROUP // 2
    side = chips // 2 - 1

    if groups == 1:
        ring = [2 * a for a in range(chips // 2)] + [2 * a + 1 for a in reversed(range(chips // 2))]
    else:
        ring = list(range(chips // 2)) + list(reversed(range(chips // 2, chips)))
    ring_pairs = []
    for g in range(groups):
        for place in range(chips):
            for core, step in ((0, 1), (1, -1)):
                ring_pairs.append(
                    (
                        g * GROUP + ring[place] * 2 + core,
                        g * GROUP + ring[(place + step) % chips] * 2 + core,
                    )
                )
    core_pairs = [(i, i ^ 1) for i in range(n_dp)]
    inner = [[g * GROUP + i for i in range(GROUP)] for g in range(groups)]
    outer = [[g * GROUP + i for g in range(groups)] for i in range(GROUP)]
    if groups == 1:
        inner = None

    def along(x):
        return lax.ppermute(x, "dp", ring_pairs)

    def across(x):
        return lax.ppermute(x, "dp", core_pairs)

    def over(x):
        return lax.ppermute(x, "tensor", [(0, 1), (1, 0)])

    index = lax.axis_index("dp")
    group = index // GROUP
    chip = (index % GROUP) // 2
    core = index % 2
    tensor = lax.axis_index("tensor")
    is_first = core == 0
    at = core * half
    off = (1 - core) * half
    core_word = core.astype(jnp.int32).reshape(1)

    def my_half(x, start, axis=0):
        return lax.dynamic_slice_in_dim(x, start, half, axis)

    def in_order(own, other):
        return jnp.where(
            is_first, jnp.concatenate([own, other], 0), jnp.concatenate([other, own], 0)
        )

    def gather_rows(mine, needed={}):
        behind, ahead = [], []
        moving = mine
        for step in range(side):
            moving = along(after(moving, *needed.get(step, ())))
            behind.append(moving)
            ahead.append(across(moving))
        far = along(after(my_half(moving, at, moving.ndim - 2), *needed.get(side, ())))
        return [mine] + behind + ahead + [far, across(far)]

    rows = lax.broadcasted_iota(jnp.int32, (block, 1), 0)
    mine_rows = (rows < half) == is_first

    def ring_sum(*sets, needed={}):
        took_far = [across(give_far) for give_far, _, _ in sets]
        took = [across(give) for _, give, _ in sets]
        keep = [x for _, _, x in sets]
        far = [k[side * block : side * block + half].astype(f32) + t.astype(f32) for k, t in zip(keep, took_far)]
        moving = along(jnp.stack(far).astype(bf16))
        for step in reversed(range(side)):
            here = slice(step * block, (step + 1) * block)
            added = [k[here].astype(f32) + t[here].astype(f32) for k, t in zip(keep, took)]
            arrived = after(moving, *needed.get(step, ())).astype(f32)
            if step == side - 1:
                arrived = jnp.where(mine_rows, jnp.concatenate([arrived, arrived], 1), 0)
            moving = along((arrived + jnp.stack(added)).astype(bf16))
        got = across(my_half(moving, off, 1))
        return [(k, t, moving, got, n) for n, (k, t) in enumerate(zip(keep, took))]

    def spread(x):
        return lax.all_to_all(x, "dp", 0, 0, axis_index_groups=inner, tiled=True)

    small = jnp.concatenate(
        [
            norm_gain.reshape(-1),
            norm_bias.reshape(-1),
            output_bias.reshape(-1),
            (positions // 64).astype(bf16),
            (positions % 64).astype(bf16),
        ]
    )
    weights = []
    if groups == 1:
        qkv_turned = qkv_weight.transpose(0, 2, 1, 3)
        ups, downs = (qkv_turned, fc1_weight), (out_weight, fc2_weight)
        extra = jnp.concatenate([small, jnp.zeros_like(small)]).reshape(-1, 128)
        up = spread(call_pack(pack_first, 0, ups, (), (extra,)))
        small_all = up[:, UP_ROWS:].reshape(GROUP, -1)[:, : small.shape[0]]
        up_other = over(up)
        packed_down = call_pack(pack_down, 0, (), downs, ())
        down = spread(after(packed_down, up))
        down_other = over(down)
        weights.append(call_join(join_up, up, [up_other], True, False) + call_join(join_down, down, [down_other], False, True))
        packed_last = call_pack(pack_both, 1, ups, downs, ())
        firsts = (up, up_other, down)
    else:
        small_all = lax.all_gather(small, "dp", axis=0, tiled=False)
        for layer in range(LAYERS):
            up = jnp.concatenate(
                [
                    qkv_weight[layer].reshape(piece, 3, GROUP, HEAD_DIM).transpose(2, 0, 1, 3).reshape(GROUP, piece, -1),
                    fc1_weight[layer].reshape(piece, GROUP, hidden).transpose(1, 0, 2),
                ],
                axis=2,
            )
            up = lax.all_gather(spread(up), "dp", axis=0, axis_index_groups=outer, tiled=True)
            up = up.reshape(width // 128, 128, UP_ROWS)
            value = up[:, :, WIDE : WIDE + HEAD_DIM]
            first = WIDE + HEAD_DIM
            up = jnp.concatenate(
                [
                    up[:, :, :WIDE],
                    jnp.concatenate([value[:, :HEAD_DIM], value[:, HEAD_DIM:]], axis=2),
                    up[:, :, first : first + 128],
                    up[:, :, first + 128 :],
                ],
                axis=1,
            )
            down = jnp.concatenate(
                [out_weight[layer].reshape(GROUP, HEAD_DIM, piece), fc2_weight[layer].reshape(GROUP, hidden, piece)],
                axis=1,
            )
            down = lax.all_gather(spread(down), "dp", axis=0, axis_index_groups=outer, tiled=True)
            down = down.transpose(1, 0, 2).reshape(-1, width // 128, 128).transpose(1, 0, 2)
            weights.append(call_join(join_up, up, [over(up)], True, False) + call_join(join_down, down, [over(down)], False, True))
    if groups == 1:
        biases = jnp.concatenate([qkv_bias.reshape(LAYERS, 3 * HEAD_DIM), fc1_bias], axis=1)
    else:
        full_qkv = lax.all_gather(qkv_bias, "dp", axis=2, tiled=True)
        full_up = lax.all_gather(fc1_bias, "dp", axis=1, tiled=True)
        member = index % GROUP
        biases = jnp.concatenate(
            [
                lax.dynamic_slice_in_dim(full_qkv, member * HEAD_DIM, HEAD_DIM, 2).reshape(LAYERS, 3 * HEAD_DIM),
                lax.dynamic_slice_in_dim(full_up, member * hidden, hidden, 1),
            ],
            axis=1,
        )
    biases_other = over(biases)
    both_biases = jnp.stack([biases, biases_other], axis=1).astype(f32)
    bias_rows = jnp.concatenate(
        [
            both_biases[:, :, : 3 * HEAD_DIM].reshape(LAYERS, 2, 3, HEAD_DIM).transpose(0, 2, 1, 3).reshape(LAYERS, -1),
            both_biases[:, :, 3 * HEAD_DIM :].reshape(LAYERS, -1),
        ],
        axis=1,
    )
    vectors = small_all[:, : 6 * piece].reshape(n_dp, 3, LAYERS, piece).transpose(1, 2, 0, 3).reshape(3, LAYERS, 1, width).astype(f32)
    gains, shifts, added_bias = vectors[0], vectors[1], vectors[2]

    turned = jnp.where(is_first, 1, -1)
    place = jnp.sum(jnp.where(jnp.asarray(ring) == chip, jnp.arange(chips), 0))
    offsets = [0] + [-(s + 1) for s in range(side)] + [s + 1 for s in range(side)] + [chips // 2]
    places = (place + turned * jnp.asarray(offsets)) % chips
    chip_ids = jnp.sum(
        jnp.where(places[:, None] == jnp.arange(chips)[None, :], jnp.asarray(ring)[None, :], 0), axis=1
    )
    owners = group * GROUP + 2 * chip_ids + tensor
    labels = jax.vmap(lambda owner: sequence_labels(seq_lengths, seq_device, owner, block))(owners)
    rows_at = jnp.arange(block, dtype=jnp.int32)
    allowed = (
        (labels[:, :, None] == labels[:, None, :])
        & (labels[:, :, None] > 0)
        & (rows_at[None, None, :] <= rows_at[None, :, None])
    ) | (rows_at[None, None, :] == rows_at[None, :, None])
    allowed = allowed.astype(f32).reshape(chips * block, block)
    picked = (owners[:, None] == jnp.arange(n_dp)[None, :]).astype(f32)
    place_parts = jnp.dot(picked, small_all[:, 6 * piece :].astype(f32), precision=lax.Precision.HIGHEST)
    row_places = (place_parts[:, :block] * 64.0 + place_parts[:, block:]).reshape(chips * block)
    pair = ROT // 2
    frequency = 10000.0 ** (-2.0 * jnp.arange(pair, dtype=f32) / ROT)
    angles = row_places[:, None] * frequency[None, :]
    cosine, sine = jnp.cos(angles), jnp.sin(angles)
    nought = jnp.zeros_like(sine)
    rest = jnp.zeros((chips * block, HEAD_DIM - ROT), f32)
    tables = (
        jnp.concatenate([cosine, cosine, rest + 1.0] * 2, axis=1),
        jnp.concatenate([-sine, nought, rest] * 2, axis=1),
        jnp.concatenate([nought, sine, rest] * 2, axis=1),
    )

    both = jnp.stack([hidden_in, out_cotangent])
    both = jnp.where(tensor == core, both, across(both))
    keeps = jnp.stack([jnp.ones_like(labels[0]), (labels[0] > 0).astype(labels.dtype)]).astype(bf16)
    both = both * keeps[:, :, None]
    if groups == 1:
        inputs = gather_rows(
            after(both, packed_down, packed_last, firsts[0], firsts[2]),
            {1: (firsts[1], tables[0]), 2: (tables[1], tables[2], allowed), side: (down_other, weights[0][0])},
        )
        slab = spread(after(packed_last, inputs[-2]))
        others = tuple(over(slab[n * GROUP // 2 : (n + 1) * GROUP // 2]) for n in range(2))
        weights.append(call_join(join_halves, slab, others, True, True))
        slabs = (slab,)
    else:
        inputs = gather_rows(both)
        slabs, others = (), ()
    mine_inputs = my_half(both, at, 1)
    state, grad_state = mine_inputs[0], mine_inputs[1]

    normed, heads, hidden_pre, wide, *parts = call_pass(
        "first", core_word, weights[0], tables, allowed, [bias_rows[0:1], gains[0], shifts[0]], inputs
    )
    rows_shape = (half, width)
    next_state, normed_own = call_end(
        partial(forward_end, False),
        core_word,
        ring_sum((after(parts[0], *slabs), parts[1], parts[2]), needed={0: others[:1]})[0],
        [state, added_bias[0], gains[1], shifts[1]],
        [jax.ShapeDtypeStruct(rows_shape, f32), jax.ShapeDtypeStruct(rows_shape, bf16)],
        "forward_end",
    )
    normed_chunks = gather_rows(in_order(normed_own, across(normed_own)), {1: others[1:]})

    def handed_back(own_rows):
        filled = in_order(own_rows, across(own_rows))
        return jnp.where(tensor == core, filled, over(filled))

    def summed(own, other, *earlier):
        total = own.astype(f32) + other.astype(f32)
        if groups > 1:
            total = total.transpose(1, 0, 2).reshape(total.shape[1], width)
            total = lax.psum_scatter(total, "dp", scatter_dimension=1, axis_index_groups=outer, tiled=True)
            total = total.reshape(total.shape[0], GROUP, piece).transpose(1, 0, 2)
        return spread(after(total.astype(bf16), *earlier))

    down_own = [(0, HEAD_DIM), (WIDE, WIDE + hidden)]
    down_other = [(HEAD_DIM, WIDE), (WIDE + hidden, WIDE + 2 * hidden)]
    up_own = [(p * WIDE, p * WIDE + HEAD_DIM) for p in range(3)] + [(3 * WIDE, 3 * WIDE + hidden)]
    up_other = [(p * WIDE + HEAD_DIM, (p + 1) * WIDE) for p in range(3)] + [(3 * WIDE + hidden, 3 * WIDE + 2 * hidden)]

    def down_gradients(wide_rows, grad_rows):
        return call_gradients(core_word, wide_rows, grad_rows, down_own, down_other, [], "down_gradients")

    def up_gradients(slim_rows, normed_rows, sums):
        return call_gradients(core_word, slim_rows, [normed_rows], up_own, up_other, [sums], "up_gradients")

    def backward_finish(ring_end, state, grad_state, layer, *needed):
        return call_end(
            backward_end,
            core_word,
            ring_end,
            [state, grad_state, gains[layer], *needed],
            [jax.ShapeDtypeStruct(rows_shape, f32), jax.ShapeDtypeStruct(rows_shape, bf16)],
            "backward_end",
        )

    normed_last, grad_rows, wide_last, slim, sums, *parts = call_pass(
        "middle", core_word, weights[1], tables, allowed, [bias_rows[1:2]], normed_chunks + inputs
    )
    out_parts = parts[:3]
    down_pair = down_gradients(wide_last, [grad_rows])
    *up_pair, bias_last = up_gradients(slim, normed_last, sums)
    down_sent, up_sent = over(down_pair[1]), over(up_pair[1])
    grad_end, out_end = ring_sum(parts[3:], out_parts, needed={1: (down_pair[0],), 0: (up_pair[0],)})
    grad_state, grad_low = backward_finish(grad_end, next_state, grad_state, 1)
    (hidden_out,) = call_end(
        partial(forward_end, True),
        core_word,
        out_end,
        [next_state, added_bias[1]],
        [jax.ShapeDtypeStruct(rows_shape, bf16)],
        "forward_out",
    )
    hidden_out = handed_back(hidden_out)
    down_last = summed(down_pair[0], after(down_sent, grad_low))
    grad_chunks = gather_rows(in_order(grad_low, across(grad_low)), {0: (down_sent,), 2: (up_sent,), side: (down_last, hidden_out)})
    up_last = summed(up_pair[0], after(up_sent, grad_chunks[-2]), down_last)

    down_pair = down_gradients(wide, grad_chunks)
    down_sent = over(down_pair[1])
    grad_rows, slim, sums, *parts = call_pass(
        "last", core_word, weights[0], tables, allowed, [heads, after(hidden_pre, down_pair[0]), normed], grad_chunks
    )
    down_first = summed(down_pair[0], after(down_sent, slim), up_last)
    *up_pair, bias_first = up_gradients(slim, after(normed, up_last), sums)
    up_sent = over(up_pair[1])
    (grad_end,) = ring_sum((after(parts[0], up_pair[0]), parts[1], parts[2]), needed={1: (down_first,)})
    up_first = summed(up_pair[0], up_sent, down_first)
    sums = jnp.concatenate([bias_first, bias_last], axis=0)
    sums_qkv = sums[:, : 3 * WIDE].reshape(LAYERS, 3, 2, HEAD_DIM)
    sums_up = sums[:, 3 * WIDE :].reshape(LAYERS, 2, hidden)
    bias_own, bias_other = (
        jnp.concatenate([sums_qkv[:, :, n].reshape(LAYERS, -1), sums_up[:, n]], axis=1) for n in range(2)
    )
    bias_sent = over(bias_other)
    needed = [bias_sent]
    if groups == 1:
        *filled, mark = call_spread(up_last, down_last, 1, [])
        needed.append(mark)
    _, grad_low = backward_finish(grad_end, state, grad_state, 0, *needed)
    grad_hidden = handed_back(grad_low).astype(f32)

    ends = jnp.stack([jnp.sum(x[:, UP_ROWS : UP_ROWS + 3].astype(f32), axis=0) for x in (up_first, up_last)])
    shift_grads = ends[:, 0]
    gain_grads = (ends[:, 1] - norm_bias.astype(f32) * ends[:, 0]) / norm_gain.astype(f32)
    after_grads = ends[:, 2] / GROUP
    bias_sums = bias_own + bias_sent
    bias_qkv, bias_up = bias_sums[:, : 3 * HEAD_DIM].reshape(LAYERS, 3, HEAD_DIM), bias_sums[:, 3 * HEAD_DIM :]
    if groups == 1:
        grad_qkv, grad_out, grad_up, grad_down, _ = call_spread(up_first, down_first, 0, filled)
        grad_qkv = grad_qkv.transpose(0, 2, 1, 3)
    else:
        bias_qkv = lax.all_gather(lax.psum(bias_qkv, "dp", axis_index_groups=outer), "dp", axis=2, axis_index_groups=inner, tiled=True)
        bias_up = lax.all_gather(lax.psum(bias_up, "dp", axis_index_groups=outer), "dp", axis=1, axis_index_groups=inner, tiled=True)
        bias_qkv = lax.dynamic_slice_in_dim(bias_qkv, index * qkv_bias.shape[2], qkv_bias.shape[2], 2)
        bias_up = lax.dynamic_slice_in_dim(bias_up, index * fc1_bias.shape[1], fc1_bias.shape[1], 1)
        ups = jnp.stack([up_first, up_last]).astype(f32)
        downs = jnp.stack([down_first, down_last]).astype(f32)
        grad_qkv = ups[:, :, : 3 * HEAD_DIM].reshape(LAYERS, GROUP, 3, HEAD_DIM, piece).transpose(0, 4, 2, 1, 3).reshape(LAYERS, piece, 3, -1)
        grad_up = ups[:, :, 3 * HEAD_DIM : UP_ROWS].transpose(0, 3, 1, 2).reshape(LAYERS, piece, -1)
        grad_out = downs[:, :, :HEAD_DIM].reshape(LAYERS, -1, piece)
        grad_down = downs[:, :, HEAD_DIM:].reshape(LAYERS, -1, piece)
    return (
        hidden_out,
        grad_hidden,
        gain_grads,
        shift_grads,
        grad_qkv,
        bias_qkv,
        grad_out,
        grad_up,
        bias_up,
        grad_down,
        after_grads,
    )


def solution(mesh):
    placed = (
        P("dp", None),
        P(),
        P(),
        P("dp"),
        P(None, "dp"),
        P(None, "dp"),
        P(None, "dp", None, "tensor"),
        P(None, None, ("tensor", "dp")),
        P(None, "tensor", "dp"),
        P(None, "dp", "tensor"),
        P(None, ("tensor", "dp")),
        P(None, "tensor", "dp"),
        P(None, "dp"),
        P("dp", None),
    )
    return jax.shard_map(
        partial(per_device, mesh.shape["dp"]),
        mesh=mesh,
        in_specs=placed,
        out_specs=(
            P("dp", None),
            P("dp", None),
            P(None, "dp"),
            P(None, "dp"),
            P(None, "dp", None, "tensor"),
            P(None, None, ("tensor", "dp")),
            P(None, "tensor", "dp"),
            P(None, "dp", "tensor"),
            P(None, ("tensor", "dp")),
            P(None, "tensor", "dp"),
            P(None, "dp"),
        ),
        check_vma=False,
    )
```

```python
from functools import partial

import jax
import jax.numpy as jnp
from jax import lax
from jax.experimental import pallas as pl
from jax.experimental.pallas import tpu as pltpu
from jax.sharding import PartitionSpec as P

HEAD_DIM = 64
ROT = 32
LAYERS = 2
GROUP = 16

norm_epsilon = 1e-05
masked_score = -1e30
bf16 = jnp.bfloat16
f32 = jnp.float32

contract_last = (((1,), (1,)), ((), ()))
contract_first = (((0,), (0,)), ((), ()))


def dot(a, b, dims=(((1,), (0,)), ((), ()))):
    return lax.dot_general(a, b, dims, preferred_element_type=f32)


def turn(x, cosine, up, down):
    return x * cosine + pltpu.roll(x, x.shape[1] - ROT // 2, 1) * up + pltpu.roll(x, ROT // 2, 1) * down


def stacked_heads(x):
    lane = lax.broadcasted_iota(jnp.int32, x.shape, 1)
    zero = jnp.zeros_like(x)
    return jnp.concatenate(
        [jnp.where(lane < HEAD_DIM, x, zero), jnp.where(lane < HEAD_DIM, zero, x)], axis=0
    )


def merged_heads(x):
    rows = x.shape[0] // 2
    lane = lax.broadcasted_iota(jnp.int32, (rows, x.shape[1]), 1)
    return jnp.where(lane < HEAD_DIM, x[:rows], x[rows:])


def softmax_rows(queries, keys, allowed):
    scores = dot(stacked_heads(queries), keys, contract_last) * HEAD_DIM ** (-0.5)
    masked = jnp.where(jnp.concatenate([allowed, allowed], axis=0) > 0, scores, masked_score)
    weights = jnp.exp(masked - jnp.max(masked, axis=1, keepdims=True))
    return weights / jnp.sum(weights, axis=1, keepdims=True)


def sequence_labels(seq_lengths, seq_device, owner, count_rows):
    index = jnp.arange(seq_lengths.shape[0], dtype=jnp.int32)
    owned = jnp.where(seq_device == owner, seq_lengths, 0)
    earlier = index[None, :] < index[:, None]
    starts = jnp.sum(jnp.where(earlier, owned[None, :], 0), axis=1)
    places = jnp.arange(count_rows, dtype=jnp.int32)
    inside = (places[:, None] >= starts[None, :]) & (places[:, None] < (starts + owned)[None, :])
    return jnp.sum(jnp.where(inside, index[None, :] + 1, 0), axis=1)


def gelu_parts(v):
    c = (2.0 / jnp.pi) ** 0.5
    inner = jnp.tanh(c * (v + 0.044715 * v * v * v))
    value = 0.5 * v * (1.0 + inner)
    slope = 0.5 * (1.0 + inner) + 0.5 * v * (1.0 - inner * inner) * c * (1.0 + 3.0 * 0.044715 * v * v)
    return value, slope


VMEM_SPEC = pl.BlockSpec(memory_space=pltpu.VMEM)
ANY_SPEC = pl.BlockSpec(memory_space=pl.ANY)
SMEM_SPEC = pl.BlockSpec(memory_space=pltpu.SMEM)
WIDE = 2 * HEAD_DIM
UP_ROWS = 3 * HEAD_DIM + 256
DOWN_ROWS = HEAD_DIM + 256
SUM_ROWS = 16
MEMBERS = 4


def after(x, *others):
    if not others:
        return x
    return lax.optimization_barrier((x, *others))[0]


def left_lanes(x):
    return lax.broadcasted_iota(jnp.int32, x.shape, 1) < HEAD_DIM


def swapped(x):
    return pltpu.roll(x, HEAD_DIM, 1)


def zipped(a, b):
    left = left_lanes(a)
    return jnp.where(left, a, swapped(b)).astype(bf16), jnp.where(left, swapped(a), b).astype(bf16)


def pack_up(qkv_ref, fc1_ref, *rest):
    out_ref = rest[-1]
    for pair in range(MEMBERS // 2):
        lanes = slice(pair * 128, (pair + 1) * 128)
        q, k, v = (qkv_ref[0, p, :, lanes].astype(f32) for p in range(3))
        here, there = 2 * pair, 2 * pair + 1
        out_ref[here, :WIDE], out_ref[there, :WIDE] = zipped(q, k)
        rows = q.shape[0] // 2
        out_ref[here, WIDE : WIDE + rows], out_ref[there, WIDE : WIDE + rows] = zipped(v[:rows], v[rows:])
        base = WIDE + rows
        for d in (here, there):
            for h in range(2):
                out_ref[d, base + h * 128 : base + (h + 1) * 128] = fc1_ref[0, :, (2 * d + h) * 128 : (2 * d + h + 1) * 128]


def pack_first(qkv_ref, fc1_ref, small_ref, out_ref):
    pack_up(qkv_ref, fc1_ref, out_ref)
    for d in range(MEMBERS):
        out_ref[d, UP_ROWS:] = small_ref[...]


def pack_both(qkv_ref, fc1_ref, out_w_ref, fc2_ref, out_ref):
    pack_up(qkv_ref, fc1_ref, out_ref)
    pack_down(out_w_ref, fc2_ref, out_ref.at[:, UP_ROWS:])


def pack_down(out_w_ref, fc2_ref, out_ref):
    for d in range(MEMBERS):
        out_ref[d, :HEAD_DIM] = out_w_ref[0, d * HEAD_DIM : (d + 1) * HEAD_DIM]
        out_ref[d, HEAD_DIM:] = fc2_ref[0, d * 256 : (d + 1) * 256]


def call_pack(body, layer, ups, downs, small):
    rows, specs = 0, []
    if ups:
        rows += UP_ROWS
        specs += [
            pl.BlockSpec((1, 3, 128, MEMBERS * HEAD_DIM), lambda i: (layer, 0, 0, i)),
            pl.BlockSpec((1, 128, MEMBERS * 256), lambda i: (layer, 0, i)),
        ]
    if downs:
        rows += DOWN_ROWS
        specs += [
            pl.BlockSpec((1, MEMBERS * HEAD_DIM, 128), lambda i: (layer, i, 0)),
            pl.BlockSpec((1, MEMBERS * 256, 128), lambda i: (layer, i, 0)),
        ]
    if small:
        rows += small[0].shape[0]
        specs.append(pl.BlockSpec(small[0].shape, lambda i: (0, 0)))
    return pl.pallas_call(
        body,
        grid=(GROUP // MEMBERS,),
        in_specs=specs,
        out_specs=pl.BlockSpec((MEMBERS, rows, 128), lambda i: (i, 0, 0)),
        out_shape=jax.ShapeDtypeStruct((GROUP, rows, 128), bf16),
        cost_estimate=pl.CostEstimate(flops=0, bytes_accessed=GROUP * rows * 128 * 8, transcendentals=0),
        name=body.__name__,
    )(*ups, *downs, *small)


def join_up(own_ref, other_ref, out_ref):
    for e in range(MEMBERS):
        rows = slice(e * 128, (e + 1) * 128)
        a, b = own_ref[e, :WIDE].astype(f32), other_ref[e, :WIDE].astype(f32)
        out_ref[rows, :WIDE], out_ref[rows, WIDE : 2 * WIDE] = zipped(a, b)
        a, b = own_ref[e, WIDE : WIDE + 64].astype(f32), other_ref[e, WIDE : WIDE + 64].astype(f32)
        top, bottom = zipped(a, b)
        out_ref[e * 128 : e * 128 + 64, 2 * WIDE : 3 * WIDE] = top
        out_ref[e * 128 + 64 : (e + 1) * 128, 2 * WIDE : 3 * WIDE] = bottom
        for n, ref in enumerate((own_ref, other_ref)):
            for h in range(2):
                lanes = 3 * WIDE + n * 256 + h * 128
                out_ref[rows, lanes : lanes + 128] = ref[e, WIDE + 64 + h * 128 : WIDE + 64 + (h + 1) * 128]


def join_down(own_ref, other_ref, out_ref):
    base = own_ref.shape[1] - DOWN_ROWS
    for e in range(MEMBERS):
        lanes = slice(e * 128, (e + 1) * 128)
        for n, ref in enumerate((own_ref, other_ref)):
            out_ref[n * HEAD_DIM : (n + 1) * HEAD_DIM, lanes] = ref[e, base : base + HEAD_DIM]
            out_ref[WIDE + n * 256 : WIDE + (n + 1) * 256, lanes] = ref[e, base + HEAD_DIM :]


def join_both(own_ref, other_ref, up_ref, down_ref):
    join_up(own_ref, other_ref, up_ref)
    join_down(own_ref, other_ref, down_ref)


def join_halves(own_ref, lower_ref, upper_ref, up_ref, down_ref):
    lower = pl.program_id(0) < GROUP // MEMBERS // 2

    @pl.when(lower)
    def _():
        join_both(own_ref, lower_ref, up_ref, down_ref)

    @pl.when(jnp.logical_not(lower))
    def _():
        join_both(own_ref, upper_ref, up_ref, down_ref)


def call_join(body, own, others, ups, downs):
    rows = own.shape[1]
    steps = GROUP // MEMBERS
    spec = pl.BlockSpec((MEMBERS, rows, 128), lambda i: (i, 0, 0))
    other_specs = [spec]
    if len(others) == 2:
        other_specs = [
            pl.BlockSpec((MEMBERS, rows, 128), lambda i: (jnp.minimum(i, steps // 2 - 1), 0, 0)),
            pl.BlockSpec((MEMBERS, rows, 128), lambda i: (jnp.maximum(i - steps // 2, 0), 0, 0)),
        ]
    specs, shapes = [], []
    if ups:
        specs.append(pl.BlockSpec((MEMBERS * 128, 2 * UP_ROWS), lambda i: (i, 0)))
        shapes.append(jax.ShapeDtypeStruct((GROUP * 128, 2 * UP_ROWS), bf16))
    if downs:
        specs.append(pl.BlockSpec((2 * DOWN_ROWS, MEMBERS * 128), lambda i: (0, i)))
        shapes.append(jax.ShapeDtypeStruct((2 * DOWN_ROWS, GROUP * 128), bf16))
    return pl.pallas_call(
        body,
        grid=(GROUP // MEMBERS,),
        in_specs=[spec] + other_specs,
        out_specs=specs,
        out_shape=shapes,
        cost_estimate=pl.CostEstimate(flops=0, bytes_accessed=GROUP * rows * 128 * 12, transcendentals=0),
        name=body.__name__,
    )(own, *others)


def slot_copies(refs, which, target, core):
    block = target.shape[0] // 8
    half = block // 2
    pairs = []
    for slot in range(7):
        ref = refs[slot] if which is None else refs[slot].at[which]
        pairs.append((ref, target.at[pl.ds(slot * block, block)]))
    for n, at in ((7, core * half), (8, (1 - core) * half)):
        ref = refs[n] if which is None else refs[n].at[which]
        pairs.append((ref, target.at[pl.ds(pl.multiple_of(7 * block + at, half), half)]))
    return pairs


def split_copies(part, far_ref, give_ref, keep_ref, core):
    block = part.shape[0] // 8
    half = block // 2
    at, off = core * half, (1 - core) * half

    def rows(slot, start):
        return part.at[pl.ds(pl.multiple_of(slot * block + start, half), half)]

    return [
        (rows(7, off), far_ref),
        (part.at[pl.ds(block, 3 * block)], give_ref.at[pl.ds(0, 3 * block)]),
        (rows(0, off), give_ref.at[pl.ds(3 * block, half)]),
        (part.at[pl.ds(4 * block, 3 * block)], keep_ref.at[pl.ds(0, 3 * block)]),
        (rows(7, at), keep_ref.at[pl.ds(3 * block, half)]),
        (rows(0, at), keep_ref.at[pl.ds(3 * block + half, half)]),
    ]


def run_copies(pairs, sems, first):
    made = [pltpu.make_async_copy(a, b, sems.at[first + n]) for n, (a, b) in enumerate(pairs)]
    for copy in made:
        copy.start()
    return made


def heads_forward(chances, values):
    return merged_heads(dot(chances.astype(bf16), values)).astype(bf16)


def heads_backward(chances, queries, keys, values, grad, tables):
    grads = stacked_heads(grad)
    grad_chances = dot(grads, values, contract_last)
    grad_values = dot(chances.astype(bf16), grads, contract_first)
    centre = jnp.sum(grad_chances * chances, axis=1, keepdims=True)
    grad_scores = (chances * (grad_chances - centre)).astype(bf16)
    scale = HEAD_DIM ** (-0.5)
    grad_queries = merged_heads(dot(grad_scores, keys)) * scale
    grad_keys = dot(grad_scores, stacked_heads(queries), contract_first) * scale
    cosine, up, down = tables
    back = (cosine, -up, -down)
    return turn(grad_queries, *back).astype(bf16), turn(grad_keys, *back).astype(bf16), grad_values.astype(bf16)


def layer_pass(mode, *refs):
    refs = list(refs)

    def take(n):
        out = refs[:n]
        del refs[:n]
        return out

    forward, backward = mode != "last", mode != "first"
    core_ref, up_ref, down_ref, cos_ref, sin_up_ref, sin_down_ref, allowed_ref = take(7)
    core = core_ref[0]
    if mode == "first":
        bias_ref, gain_ref, shift_ref = take(3)
        rows_in = take(9)
    elif mode == "middle":
        (bias_ref,) = take(1)
        rows_in = take(9)
        grads_in = take(9)
    else:
        heads_ref, hidden_ref, normed_ref = take(3)
        grads_in = take(9)
    if mode == "first":
        normed_ref, heads_ref, hidden_ref, wide_ref = take(4)
        outs = take(3)
        raw, part, sems = take(3)
    elif mode == "middle":
        normed_ref, grad_rows_ref, wide_ref, slim_ref, sums_ref = take(5)
        outs = take(3)
        grad_outs = take(3)
        part, grad_part, sems = take(3)
    else:
        grad_rows_ref, slim_ref, sums_ref = take(3)
        grad_outs = take(3)
        grad_part, sems = take(2)

    pairs = []
    if mode == "first":
        pairs += slot_copies(rows_in, 0, raw, core)
    if mode == "middle":
        pairs += slot_copies(rows_in, None, normed_ref, core)
        pairs += slot_copies(grads_in, 1, grad_rows_ref, core)
    if mode == "last":
        pairs += slot_copies(grads_in, None, grad_rows_ref, core)
    for copy in run_copies(pairs, sems, 0):
        copy.wait()

    total = allowed_ref.shape[0]
    block = allowed_ref.shape[1]
    step = 2 * block

    if mode == "first":
        tile = 32

        def norm_tile(i, carry):
            at = pl.ds(pl.multiple_of(i * tile, tile), tile)
            x = raw[at, :].astype(f32)
            centred = x - jnp.mean(x, axis=1, keepdims=True)
            inverse = lax.rsqrt(jnp.mean(centred * centred, axis=1, keepdims=True) + norm_epsilon)
            normed_ref[at, :] = (centred * inverse * gain_ref[...] + shift_ref[...]).astype(bf16)
            return carry

        lax.fori_loop(0, total // tile, norm_tile, 0)

    if backward:
        sums_ref[...] = jnp.zeros_like(sums_ref)

    def one(p, carry):
        at = pl.ds(pl.multiple_of(p * step, step), step)
        if forward:
            before = dot(normed_ref[at, :], up_ref[...]) + bias_ref[...]
            hidden_pre = before[:, 3 * WIDE :]
        else:
            hidden_pre = hidden_ref[at, :]
        value, slope = gelu_parts(hidden_pre)
        if backward:
            grad_wide = dot(grad_rows_ref[at, :], down_ref[...], contract_last)
            slim_ref[at, 3 * WIDE :] = (grad_wide[:, WIDE:] * slope).astype(bf16)
        if forward:
            wide_ref[at, WIDE:] = value.astype(bf16)
        if mode == "first":
            hidden_ref[at, :] = hidden_pre
        for b in range(2):
            mine = slice(b * block, (b + 1) * block)
            own = pl.ds(pl.multiple_of(p * step + b * block, block), block)
            tables = (cos_ref[own, :], sin_up_ref[own, :], sin_down_ref[own, :])
            if forward:
                queries = turn(before[mine, :WIDE], *tables).astype(bf16)
                keys = turn(before[mine, WIDE : 2 * WIDE], *tables).astype(bf16)
                values = before[mine, 2 * WIDE : 3 * WIDE].astype(bf16)
            else:
                queries = heads_ref[own, :WIDE]
                keys = heads_ref[own, WIDE : 2 * WIDE]
                values = heads_ref[own, 2 * WIDE :]
            if mode == "first":
                heads_ref[own, :WIDE] = queries
                heads_ref[own, WIDE : 2 * WIDE] = keys
                heads_ref[own, 2 * WIDE :] = values
            chances = softmax_rows(queries, keys, allowed_ref[own, :])
            if forward:
                wide_ref[own, :WIDE] = heads_forward(chances, values)
            if backward:
                grads = heads_backward(
                    chances, queries, keys, values, grad_wide[mine, :WIDE].astype(bf16), tables
                )
                for n in range(3):
                    slim_ref[own, n * WIDE : (n + 1) * WIDE] = grads[n]
        if forward:
            part[at, :] = dot(wide_ref[at, :], down_ref[...]).astype(bf16)
        if backward:
            grad_normed = dot(slim_ref[at, :], up_ref[...], contract_last)
            grad_part[at, :] = grad_normed.astype(bf16)
            for n, rows in enumerate(
                (grad_normed, grad_normed * normed_ref[at, :].astype(f32), grad_rows_ref[at, :].astype(f32))
            ):
                sums_ref[n : n + 1] += jnp.sum(rows, axis=0, keepdims=True)
        return carry

    lax.fori_loop(0, total // step, one, 0)
    pairs = []
    if backward:
        pairs += split_copies(grad_part, *grad_outs, core)
    if forward:
        pairs += split_copies(part, *outs, core)
    for copy in run_copies(pairs, sems, 0):
        copy.wait()


def call_pass(mode, core, weights, tables, allowed, extra, chunks):
    total, block = allowed.shape
    half = block // 2
    width = weights[0].shape[0]
    slim = weights[0].shape[1]
    wide = weights[1].shape[0]
    parts = [
        jax.ShapeDtypeStruct((half, width), bf16),
        jax.ShapeDtypeStruct((3 * block + half, width), bf16),
        jax.ShapeDtypeStruct((4 * block, width), bf16),
    ]
    full = jax.ShapeDtypeStruct((total, width), bf16)
    sums = jax.ShapeDtypeStruct((SUM_ROWS, width), f32)
    slim_rows = jax.ShapeDtypeStruct((total, slim), bf16)
    wide_rows = jax.ShapeDtypeStruct((total, wide), bf16)
    if mode == "first":
        kept = [
            full,
            jax.ShapeDtypeStruct((total, 3 * WIDE), bf16),
            jax.ShapeDtypeStruct((total, slim - 3 * WIDE), f32),
            wide_rows,
        ]
        buffers = 2
    elif mode == "middle":
        kept = [full, full, wide_rows, slim_rows, sums]
        parts = parts * 2
        buffers = 2
    else:
        kept = [full, slim_rows, sums]
        buffers = 1
    passes = 2 if mode == "middle" else 1
    return pl.pallas_call(
        partial(layer_pass, mode),
        in_specs=[SMEM_SPEC] + [VMEM_SPEC] * (6 + len(extra)) + [ANY_SPEC] * len(chunks),
        out_specs=[VMEM_SPEC] * len(kept) + [ANY_SPEC] * len(parts),
        out_shape=kept + parts,
        scratch_shapes=[pltpu.VMEM((total, width), bf16)] * buffers + [pltpu.SemaphoreType.DMA((18,))],
        cost_estimate=pl.CostEstimate(
            flops=6 * total * width * (slim + wide) * passes,
            bytes_accessed=20_000_000 * passes,
            transcendentals=total * slim,
        ),
        name="pass_" + mode,
    )(core, *weights, *tables, allowed, *extra, *chunks)


def gradient_slabs(own_rows, other_rows, with_sums, pieces_in, core_ref, left_ref, *rest):
    right_refs, rest = rest[:pieces_in], rest[pieces_in:]
    if with_sums:
        sums_ref, *rest = rest
    own_ref, other_ref, *rest = rest
    turned_ref = rest[-1]
    if pieces_in == 1:
        right = right_refs[0][...]
    else:
        a, b = right_refs[-2][...], right_refs[-1][...]
        first = jnp.full(a.shape, core_ref[0]) == 0
        halves = [jnp.where(first, a, b), jnp.where(first, b, a)]
        right = jnp.concatenate([ref[...] for ref in right_refs[:-2]] + halves, axis=0)

    @pl.when(pl.program_id(0) == 0)
    def _():
        width = left_ref.shape[1]
        for n in range(width // 128):
            lanes = slice(n * 128, (n + 1) * 128)
            left = left_ref[:, lanes].astype(f32)
            if with_sums:
                rest[0][:, lanes] = jnp.sum(left, axis=0, keepdims=True)
            turned_ref[lanes, :] = left.T.astype(bf16)

    product = dot(turned_ref[...], right).astype(bf16)
    for ref, pieces in ((own_ref, own_rows), (other_ref, other_rows)):
        place = 0
        for first, last in pieces:
            for e in range(2):
                ref[e, place : place + last - first] = product[first:last, e * 128 : (e + 1) * 128]
            place += last - first
        if with_sums:
            for e in range(2):
                ref[e, place:] = sums_ref[:, e * 128 : (e + 1) * 128].astype(bf16)


def call_gradients(core, left, right, own_rows, other_rows, sums, name):
    total, height = left.shape
    width = right[0].shape[1]
    with_sums = len(sums) > 0
    rows = height // 2 + (SUM_ROWS if with_sums else 0)
    slab = pl.BlockSpec((2, rows, 128), lambda i: (i, 0, 0))
    shape = jax.ShapeDtypeStruct((width // 128, rows, 128), bf16)
    out_specs, out_shape = [slab, slab], [shape, shape]
    if with_sums:
        out_specs.append(pl.BlockSpec((1, height), lambda i: (0, 0)))
        out_shape.append(jax.ShapeDtypeStruct((1, height), f32))
    return pl.pallas_call(
        partial(gradient_slabs, own_rows, other_rows, with_sums, len(right)),
        grid=(width // 256,),
        in_specs=[SMEM_SPEC, pl.BlockSpec((total, height), lambda i: (0, 0))]
        + [pl.BlockSpec((x.shape[0], 256), lambda i: (0, i)) for x in (*right, *sums)],
        out_specs=out_specs,
        out_shape=out_shape,
        scratch_shapes=[pltpu.VMEM((height, total), bf16)],
        cost_estimate=pl.CostEstimate(
            flops=4 * total * height * width, bytes_accessed=2 * (total * (width + height) + 2 * height * width), transcendentals=0
        ),
        name=name,
    )(core, left, *right, *sums)


def spread_gradients(up_ref, down_ref, *rest):
    qkv_ref, out_w_ref, fc1_ref, fc2_ref, mark_ref = rest[-5:]
    mark_ref[...] = jnp.zeros_like(mark_ref)
    for p in range(3):
        rows = slice(p * HEAD_DIM, (p + 1) * HEAD_DIM)
        both = jnp.concatenate([up_ref[0, rows].astype(f32), up_ref[1, rows].astype(f32)], axis=0)
        qkv_ref[0, p] = both.T
    base = 3 * HEAD_DIM
    for d in range(2):
        for h in range(2):
            fc1_ref[0, :, (2 * d + h) * 128 : (2 * d + h + 1) * 128] = (
                up_ref[d, base + h * 128 : base + (h + 1) * 128].astype(f32).T
            )
        out_w_ref[0, d * HEAD_DIM : (d + 1) * HEAD_DIM] = down_ref[d, :HEAD_DIM].astype(f32)
        fc2_ref[0, d * 256 : (d + 1) * 256] = down_ref[d, HEAD_DIM:].astype(f32)


def call_spread(up, down, layer, filled):
    shapes = [
        jax.ShapeDtypeStruct((LAYERS, 3, 128, GROUP * HEAD_DIM), f32),
        jax.ShapeDtypeStruct((LAYERS, GROUP * HEAD_DIM, 128), f32),
        jax.ShapeDtypeStruct((LAYERS, 128, GROUP * 256), f32),
        jax.ShapeDtypeStruct((LAYERS, GROUP * 256, 128), f32),
        jax.ShapeDtypeStruct((8, 128), f32),
    ]
    return pl.pallas_call(
        spread_gradients,
        grid=(GROUP // 2,),
        in_specs=[
            pl.BlockSpec((2, up.shape[1], 128), lambda i: (i, 0, 0)),
            pl.BlockSpec((2, down.shape[1], 128), lambda i: (i, 0, 0)),
        ]
        + [ANY_SPEC] * len(filled),
        out_specs=[
            pl.BlockSpec((1, 3, 128, 128), lambda i: (layer, 0, 0, i)),
            pl.BlockSpec((1, 128, 128), lambda i: (layer, i, 0)),
            pl.BlockSpec((1, 128, 512), lambda i: (layer, 0, i)),
            pl.BlockSpec((1, 512, 128), lambda i: (layer, i, 0)),
            pl.BlockSpec((8, 128), lambda i: (0, 0)),
        ],
        out_shape=shapes,
        input_output_aliases={2 + n: n for n in range(len(filled))},
        name="spread_gradients",
    )(up, down, *filled)


def ring_total(core_ref, keep_ref, took_ref, moving_ref, got_ref):
    half = got_ref.shape[0]
    arrived = moving_ref[pl.ds(pl.multiple_of(core_ref[0] * half, half), half), :]
    return keep_ref[...].astype(f32) + took_ref[...].astype(f32) + arrived.astype(f32) + got_ref[...].astype(f32)


def centred_rows(state):
    centred = state - jnp.mean(state, axis=1, keepdims=True)
    return centred, lax.rsqrt(jnp.mean(centred * centred, axis=1, keepdims=True) + norm_epsilon)


def forward_end(last, core_ref, keep_ref, took_ref, moving_ref, got_ref, state_ref, after_ref, *rest):
    state = state_ref[...].astype(f32) + ring_total(core_ref, keep_ref, took_ref, moving_ref, got_ref) + after_ref[...]
    if last:
        rest[0][...] = state.astype(bf16)
        return
    gain_ref, shift_ref, state_out, normed_ref = rest
    state_out[...] = state
    centred, inverse = centred_rows(state)
    normed_ref[...] = (centred * inverse * gain_ref[...] + shift_ref[...]).astype(bf16)


def backward_end(core_ref, keep_ref, took_ref, moving_ref, got_ref, state_ref, grad_ref, gain_ref, *rest):
    grad_out, low_ref = rest[-2:]
    grad_normed = ring_total(core_ref, keep_ref, took_ref, moving_ref, got_ref)
    centred, inverse = centred_rows(state_ref[...].astype(f32))
    xhat = centred * inverse
    before = grad_ref[...].astype(f32)
    scaled = grad_normed * gain_ref[...]
    after = before + (
        scaled - jnp.mean(scaled, axis=1, keepdims=True) - xhat * jnp.mean(scaled * xhat, axis=1, keepdims=True)
    ) * inverse
    grad_out[...] = after
    low_ref[...] = after.astype(bf16)


def call_end(body, core, ring, extra, shapes, name):
    keep, took, moving, got, n_sum = ring
    _, half, width = got.shape

    def rows_of(array):
        n = array.shape[0] // half - 1
        return pl.BlockSpec((half, width), lambda i: (n, 0))

    def whole_of(array):
        return pl.BlockSpec(array.shape, lambda i: (0,) * len(array.shape))

    def one_of(array):
        return pl.BlockSpec((None,) + array.shape[1:], lambda i: (n_sum, 0, 0))

    return pl.pallas_call(
        body,
        grid=(1,),
        in_specs=[SMEM_SPEC, rows_of(keep), rows_of(took), one_of(moving), one_of(got)] + [whole_of(x) for x in extra],
        out_specs=[whole_of(x) for x in shapes],
        out_shape=shapes,
        name=name,
    )(core, keep, took, moving, got, *extra)


def per_device(
    n_dp,
    hidden_in,
    seq_lengths,
    seq_device,
    positions,
    norm_gain,
    norm_bias,
    qkv_weight,
    qkv_bias,
    out_weight,
    fc1_weight,
    fc1_bias,
    fc2_weight,
    output_bias,
    out_cotangent,
):
    block = hidden_in.shape[0]
    half = block // 2
    width = hidden_in.shape[1]
    piece = norm_gain.shape[1]
    hidden = fc1_weight.shape[2] // GROUP
    groups = n_dp // GROUP
    chips = GROUP // 2
    side = chips // 2 - 1

    if groups == 1:
        ring = [2 * a for a in range(chips // 2)] + [2 * a + 1 for a in reversed(range(chips // 2))]
    else:
        ring = list(range(chips // 2)) + list(reversed(range(chips // 2, chips)))
    ring_pairs = []
    for g in range(groups):
        for place in range(chips):
            for core, step in ((0, 1), (1, -1)):
                ring_pairs.append(
                    (
                        g * GROUP + ring[place] * 2 + core,
                        g * GROUP + ring[(place + step) % chips] * 2 + core,
                    )
                )
    core_pairs = [(i, i ^ 1) for i in range(n_dp)]
    inner = [[g * GROUP + i for i in range(GROUP)] for g in range(groups)]
    outer = [[g * GROUP + i for g in range(groups)] for i in range(GROUP)]
    if groups == 1:
        inner = None

    def along(x):
        return lax.ppermute(x, "dp", ring_pairs)

    def across(x):
        return lax.ppermute(x, "dp", core_pairs)

    def over(x):
        return lax.ppermute(x, "tensor", [(0, 1), (1, 0)])

    index = lax.axis_index("dp")
    group = index // GROUP
    chip = (index % GROUP) // 2
    core = index % 2
    tensor = lax.axis_index("tensor")
    is_first = core == 0
    at = core * half
    off = (1 - core) * half
    core_word = core.astype(jnp.int32).reshape(1)

    def my_half(x, start, axis=0):
        return lax.dynamic_slice_in_dim(x, start, half, axis)

    def in_order(own, other):
        return jnp.where(
            is_first, jnp.concatenate([own, other], 0), jnp.concatenate([other, own], 0)
        )

    def gather_rows(mine, needed={}):
        behind, ahead = [], []
        moving = mine
        for step in range(side):
            moving = along(after(moving, *needed.get(step, ())))
            behind.append(moving)
            ahead.append(across(moving))
        far = along(after(my_half(moving, at, moving.ndim - 2), *needed.get(side, ())))
        return [mine] + behind + ahead + [far, across(far)]

    rows = lax.broadcasted_iota(jnp.int32, (block, 1), 0)
    mine_rows = (rows < half) == is_first

    def ring_sum(*sets, needed={}):
        took_far = [across(give_far) for give_far, _, _ in sets]
        took = [across(give) for _, give, _ in sets]
        keep = [x for _, _, x in sets]
        far = [k[side * block : side * block + half].astype(f32) + t.astype(f32) for k, t in zip(keep, took_far)]
        moving = along(jnp.stack(far).astype(bf16))
        for step in reversed(range(side)):
            here = slice(step * block, (step + 1) * block)
            added = [k[here].astype(f32) + t[here].astype(f32) for k, t in zip(keep, took)]
            arrived = after(moving, *needed.get(step, ())).astype(f32)
            if step == side - 1:
                arrived = jnp.where(mine_rows, jnp.concatenate([arrived, arrived], 1), 0)
            moving = along((arrived + jnp.stack(added)).astype(bf16))
        got = across(my_half(moving, off, 1))
        return [(k, t, moving, got, n) for n, (k, t) in enumerate(zip(keep, took))]

    def spread(x):
        return lax.all_to_all(x, "dp", 0, 0, axis_index_groups=inner, tiled=True)

    small = jnp.concatenate(
        [
            norm_gain.reshape(-1),
            norm_bias.reshape(-1),
            output_bias.reshape(-1),
            (positions // 64).astype(bf16),
            (positions % 64).astype(bf16),
        ]
    )
    weights = []
    if groups == 1:
        qkv_turned = qkv_weight.transpose(0, 2, 1, 3)
        ups, downs = (qkv_turned, fc1_weight), (out_weight, fc2_weight)
        extra = jnp.concatenate([small, jnp.zeros_like(small)]).reshape(-1, 128)
        up = spread(call_pack(pack_first, 0, ups, (), (extra,)))
        small_all = up[:, UP_ROWS:].reshape(GROUP, -1)[:, : small.shape[0]]
        up_other = over(up)
        packed_down = call_pack(pack_down, 0, (), downs, ())
        down = spread(after(packed_down, up))
        down_other = over(down)
        weights.append(call_join(join_up, up, [up_other], True, False) + call_join(join_down, down, [down_other], False, True))
        packed_last = call_pack(pack_both, 1, ups, downs, ())
        firsts = (up, up_other, down)
    else:
        small_all = lax.all_gather(small, "dp", axis=0, tiled=False)
        for layer in range(LAYERS):
            up = jnp.concatenate(
                [
                    qkv_weight[layer].reshape(piece, 3, GROUP, HEAD_DIM).transpose(2, 0, 1, 3).reshape(GROUP, piece, -1),
                    fc1_weight[layer].reshape(piece, GROUP, hidden).transpose(1, 0, 2),
                ],
                axis=2,
            )
            up = lax.all_gather(spread(up), "dp", axis=0, axis_index_groups=outer, tiled=True)
            up = up.reshape(width // 128, 128, UP_ROWS)
            value = up[:, :, WIDE : WIDE + HEAD_DIM]
            first = WIDE + HEAD_DIM
            up = jnp.concatenate(
                [
                    up[:, :, :WIDE],
                    jnp.concatenate([value[:, :HEAD_DIM], value[:, HEAD_DIM:]], axis=2),
                    up[:, :, first : first + 128],
                    up[:, :, first + 128 :],
                ],
                axis=1,
            )
            down = jnp.concatenate(
                [out_weight[layer].reshape(GROUP, HEAD_DIM, piece), fc2_weight[layer].reshape(GROUP, hidden, piece)],
                axis=1,
            )
            down = lax.all_gather(spread(down), "dp", axis=0, axis_index_groups=outer, tiled=True)
            down = down.transpose(1, 0, 2).reshape(-1, width // 128, 128).transpose(1, 0, 2)
            weights.append(call_join(join_up, up, [over(up)], True, False) + call_join(join_down, down, [over(down)], False, True))
    if groups == 1:
        biases = jnp.concatenate([qkv_bias.reshape(LAYERS, 3 * HEAD_DIM), fc1_bias], axis=1)
    else:
        full_qkv = lax.all_gather(qkv_bias, "dp", axis=2, tiled=True)
        full_up = lax.all_gather(fc1_bias, "dp", axis=1, tiled=True)
        member = index % GROUP
        biases = jnp.concatenate(
            [
                lax.dynamic_slice_in_dim(full_qkv, member * HEAD_DIM, HEAD_DIM, 2).reshape(LAYERS, 3 * HEAD_DIM),
                lax.dynamic_slice_in_dim(full_up, member * hidden, hidden, 1),
            ],
            axis=1,
        )
    biases_other = over(biases)
    both_biases = jnp.stack([biases, biases_other], axis=1).astype(f32)
    bias_rows = jnp.concatenate(
        [
            both_biases[:, :, : 3 * HEAD_DIM].reshape(LAYERS, 2, 3, HEAD_DIM).transpose(0, 2, 1, 3).reshape(LAYERS, -1),
            both_biases[:, :, 3 * HEAD_DIM :].reshape(LAYERS, -1),
        ],
        axis=1,
    )
    vectors = small_all[:, : 6 * piece].reshape(n_dp, 3, LAYERS, piece).transpose(1, 2, 0, 3).reshape(3, LAYERS, 1, width).astype(f32)
    gains, shifts, added_bias = vectors[0], vectors[1], vectors[2]

    turned = jnp.where(is_first, 1, -1)
    place = jnp.sum(jnp.where(jnp.asarray(ring) == chip, jnp.arange(chips), 0))
    offsets = [0] + [-(s + 1) for s in range(side)] + [s + 1 for s in range(side)] + [chips // 2]
    places = (place + turned * jnp.asarray(offsets)) % chips
    chip_ids = jnp.sum(
        jnp.where(places[:, None] == jnp.arange(chips)[None, :], jnp.asarray(ring)[None, :], 0), axis=1
    )
    owners = group * GROUP + 2 * chip_ids + tensor
    labels = jax.vmap(lambda owner: sequence_labels(seq_lengths, seq_device, owner, block))(owners)
    rows_at = jnp.arange(block, dtype=jnp.int32)
    allowed = (
        (labels[:, :, None] == labels[:, None, :])
        & (labels[:, :, None] > 0)
        & (rows_at[None, None, :] <= rows_at[None, :, None])
    ) | (rows_at[None, None, :] == rows_at[None, :, None])
    allowed = allowed.astype(f32).reshape(chips * block, block)
    picked = (owners[:, None] == jnp.arange(n_dp)[None, :]).astype(f32)
    place_parts = jnp.dot(picked, small_all[:, 6 * piece :].astype(f32), precision=lax.Precision.HIGHEST)
    row_places = (place_parts[:, :block] * 64.0 + place_parts[:, block:]).reshape(chips * block)
    pair = ROT // 2
    frequency = 10000.0 ** (-2.0 * jnp.arange(pair, dtype=f32) / ROT)
    angles = row_places[:, None] * frequency[None, :]
    cosine, sine = jnp.cos(angles), jnp.sin(angles)
    nought = jnp.zeros_like(sine)
    rest = jnp.zeros((chips * block, HEAD_DIM - ROT), f32)
    tables = (
        jnp.concatenate([cosine, cosine, rest + 1.0] * 2, axis=1),
        jnp.concatenate([-sine, nought, rest] * 2, axis=1),
        jnp.concatenate([nought, sine, rest] * 2, axis=1),
    )

    both = jnp.stack([hidden_in, out_cotangent])
    both = jnp.where(tensor == core, both, across(both))
    keeps = jnp.stack([jnp.ones_like(labels[0]), (labels[0] > 0).astype(labels.dtype)]).astype(bf16)
    both = both * keeps[:, :, None]
    if groups == 1:
        inputs = gather_rows(
            after(both, packed_down, packed_last, firsts[0], firsts[2]),
            {1: (firsts[1], tables[0]), 2: (tables[1], tables[2], allowed), side: (down_other, weights[0][0])},
        )
        slab = spread(after(packed_last, inputs[-2]))
        others = tuple(over(slab[n * GROUP // 2 : (n + 1) * GROUP // 2]) for n in range(2))
        weights.append(call_join(join_halves, slab, others, True, True))
        slabs = (slab,)
    else:
        inputs = gather_rows(both)
        slabs, others = (), ()
    mine_inputs = my_half(both, at, 1)
    state, grad_state = mine_inputs[0], mine_inputs[1]

    normed, heads, hidden_pre, wide, *parts = call_pass(
        "first", core_word, weights[0], tables, allowed, [bias_rows[0:1], gains[0], shifts[0]], inputs
    )
    rows_shape = (half, width)
    next_state, normed_own = call_end(
        partial(forward_end, False),
        core_word,
        ring_sum((after(parts[0], *slabs), parts[1], parts[2]), needed={0: others[:1]})[0],
        [state, added_bias[0], gains[1], shifts[1]],
        [jax.ShapeDtypeStruct(rows_shape, f32), jax.ShapeDtypeStruct(rows_shape, bf16)],
        "forward_end",
    )
    normed_chunks = gather_rows(in_order(normed_own, across(normed_own)), {1: others[1:]})

    def handed_back(own_rows):
        filled = in_order(own_rows, across(own_rows))
        return jnp.where(tensor == core, filled, over(filled))

    def summed(own, other, *earlier):
        total = own.astype(f32) + other.astype(f32)
        if groups > 1:
            total = total.transpose(1, 0, 2).reshape(total.shape[1], width)
            total = lax.psum_scatter(total, "dp", scatter_dimension=1, axis_index_groups=outer, tiled=True)
            total = total.reshape(total.shape[0], GROUP, piece).transpose(1, 0, 2)
        return spread(after(total.astype(bf16), *earlier))

    down_own = [(0, HEAD_DIM), (WIDE, WIDE + hidden)]
    down_other = [(HEAD_DIM, WIDE), (WIDE + hidden, WIDE + 2 * hidden)]
    up_own = [(p * WIDE, p * WIDE + HEAD_DIM) for p in range(3)] + [(3 * WIDE, 3 * WIDE + hidden)]
    up_other = [(p * WIDE + HEAD_DIM, (p + 1) * WIDE) for p in range(3)] + [(3 * WIDE + hidden, 3 * WIDE + 2 * hidden)]

    def down_gradients(wide_rows, grad_rows):
        return call_gradients(core_word, wide_rows, grad_rows, down_own, down_other, [], "down_gradients")

    def up_gradients(slim_rows, normed_rows, sums):
        return call_gradients(core_word, slim_rows, [normed_rows], up_own, up_other, [sums], "up_gradients")

    def backward_finish(ring_end, state, grad_state, layer, *needed):
        return call_end(
            backward_end,
            core_word,
            ring_end,
            [state, grad_state, gains[layer], *needed],
            [jax.ShapeDtypeStruct(rows_shape, f32), jax.ShapeDtypeStruct(rows_shape, bf16)],
            "backward_end",
        )

    normed_last, grad_rows, wide_last, slim, sums, *parts = call_pass(
        "middle", core_word, weights[1], tables, allowed, [bias_rows[1:2]], normed_chunks + inputs
    )
    out_parts = parts[:3]
    down_pair = down_gradients(wide_last, [grad_rows])
    *up_pair, bias_last = up_gradients(slim, normed_last, sums)
    down_sent, up_sent = over(down_pair[1]), over(up_pair[1])
    grad_end, out_end = ring_sum(parts[3:], out_parts, needed={1: (down_pair[0],), 0: (up_pair[0],)})
    grad_state, grad_low = backward_finish(grad_end, next_state, grad_state, 1)
    (hidden_out,) = call_end(
        partial(forward_end, True),
        core_word,
        out_end,
        [next_state, added_bias[1]],
        [jax.ShapeDtypeStruct(rows_shape, bf16)],
        "forward_out",
    )
    hidden_out = handed_back(hidden_out)
    down_last = summed(down_pair[0], after(down_sent, grad_low))
    grad_chunks = gather_rows(in_order(grad_low, across(grad_low)), {0: (down_sent,), 2: (up_sent,), side: (down_last, hidden_out)})
    up_last = summed(up_pair[0], after(up_sent, grad_chunks[-2]), down_last)

    down_pair = down_gradients(wide, grad_chunks)
    down_sent = over(down_pair[1])
    grad_rows, slim, sums, *parts = call_pass(
        "last", core_word, weights[0], tables, allowed, [heads, after(hidden_pre, down_pair[0]), normed], grad_chunks
    )
    down_first = summed(down_pair[0], after(down_sent, slim), up_last)
    *up_pair, bias_first = up_gradients(slim, after(normed, up_last), sums)
    up_sent = over(up_pair[1])
    (grad_end,) = ring_sum((after(parts[0], up_pair[0]), parts[1], parts[2]), needed={1: (down_first,)})
    up_first = summed(up_pair[0], up_sent, down_first, grad_end[2])
    sums = jnp.concatenate([bias_first, bias_last], axis=0)
    sums_qkv = sums[:, : 3 * WIDE].reshape(LAYERS, 3, 2, HEAD_DIM)
    sums_up = sums[:, 3 * WIDE :].reshape(LAYERS, 2, hidden)
    bias_own, bias_other = (
        jnp.concatenate([sums_qkv[:, :, n].reshape(LAYERS, -1), sums_up[:, n]], axis=1) for n in range(2)
    )
    bias_sent = over(bias_other)
    needed = [bias_sent]
    if groups == 1:
        *filled, mark = call_spread(up_last, down_last, 1, [])
        needed.append(mark)
    _, grad_low = backward_finish(grad_end, state, grad_state, 0, *needed)
    grad_hidden = handed_back(grad_low).astype(f32)

    ends = jnp.stack([jnp.sum(x[:, UP_ROWS : UP_ROWS + 3].astype(f32), axis=0) for x in (up_first, up_last)])
    shift_grads = ends[:, 0]
    gain_grads = (ends[:, 1] - norm_bias.astype(f32) * ends[:, 0]) / norm_gain.astype(f32)
    after_grads = ends[:, 2] / GROUP
    bias_sums = bias_own + bias_sent
    bias_qkv, bias_up = bias_sums[:, : 3 * HEAD_DIM].reshape(LAYERS, 3, HEAD_DIM), bias_sums[:, 3 * HEAD_DIM :]
    if groups == 1:
        grad_qkv, grad_out, grad_up, grad_down, _ = call_spread(up_first, down_first, 0, filled)
        grad_qkv = grad_qkv.transpose(0, 2, 1, 3)
    else:
        bias_qkv = lax.all_gather(lax.psum(bias_qkv, "dp", axis_index_groups=outer), "dp", axis=2, axis_index_groups=inner, tiled=True)
        bias_up = lax.all_gather(lax.psum(bias_up, "dp", axis_index_groups=outer), "dp", axis=1, axis_index_groups=inner, tiled=True)
        bias_qkv = lax.dynamic_slice_in_dim(bias_qkv, index * qkv_bias.shape[2], qkv_bias.shape[2], 2)
        bias_up = lax.dynamic_slice_in_dim(bias_up, index * fc1_bias.shape[1], fc1_bias.shape[1], 1)
        ups = jnp.stack([up_first, up_last]).astype(f32)
        downs = jnp.stack([down_first, down_last]).astype(f32)
        grad_qkv = ups[:, :, : 3 * HEAD_DIM].reshape(LAYERS, GROUP, 3, HEAD_DIM, piece).transpose(0, 4, 2, 1, 3).reshape(LAYERS, piece, 3, -1)
        grad_up = ups[:, :, 3 * HEAD_DIM : UP_ROWS].transpose(0, 3, 1, 2).reshape(LAYERS, piece, -1)
        grad_out = downs[:, :, :HEAD_DIM].reshape(LAYERS, -1, piece)
        grad_down = downs[:, :, HEAD_DIM:].reshape(LAYERS, -1, piece)
    return (
        hidden_out,
        grad_hidden,
        gain_grads,
        shift_grads,
        grad_qkv,
        bias_qkv,
        grad_out,
        grad_up,
        bias_up,
        grad_down,
        after_grads,
    )


def solution(mesh):
    placed = (
        P("dp", None),
        P(),
        P(),
        P("dp"),
        P(None, "dp"),
        P(None, "dp"),
        P(None, "dp", None, "tensor"),
        P(None, None, ("tensor", "dp")),
        P(None, "tensor", "dp"),
        P(None, "dp", "tensor"),
        P(None, ("tensor", "dp")),
        P(None, "tensor", "dp"),
        P(None, "dp"),
        P("dp", None),
    )
    return jax.shard_map(
        partial(per_device, mesh.shape["dp"]),
        mesh=mesh,
        in_specs=placed,
        out_specs=(
            P("dp", None),
            P("dp", None),
            P(None, "dp"),
            P(None, "dp"),
            P(None, "dp", None, "tensor"),
            P(None, None, ("tensor", "dp")),
            P(None, "tensor", "dp"),
            P(None, "dp", "tensor"),
            P(None, ("tensor", "dp")),
            P(None, "tensor", "dp"),
            P(None, "dp"),
        ),
        check_vma=False,
    )
```

```python
from functools import partial

import jax
import jax.numpy as jnp
from jax import lax
from jax.experimental import pallas as pl
from jax.experimental.pallas import tpu as pltpu
from jax.sharding import PartitionSpec as P

HEAD_DIM = 64
ROT = 32
LAYERS = 2
GROUP = 16

norm_epsilon = 1e-05
masked_score = -1e30
bf16 = jnp.bfloat16
f32 = jnp.float32

contract_last = (((1,), (1,)), ((), ()))
contract_first = (((0,), (0,)), ((), ()))


def dot(a, b, dims=(((1,), (0,)), ((), ()))):
    return lax.dot_general(a, b, dims, preferred_element_type=f32)


def turn(x, cosine, up, down):
    return x * cosine + pltpu.roll(x, x.shape[1] - ROT // 2, 1) * up + pltpu.roll(x, ROT // 2, 1) * down


def stacked_heads(x):
    lane = lax.broadcasted_iota(jnp.int32, x.shape, 1)
    zero = jnp.zeros_like(x)
    return jnp.concatenate(
        [jnp.where(lane < HEAD_DIM, x, zero), jnp.where(lane < HEAD_DIM, zero, x)], axis=0
    )


def merged_heads(x):
    rows = x.shape[0] // 2
    lane = lax.broadcasted_iota(jnp.int32, (rows, x.shape[1]), 1)
    return jnp.where(lane < HEAD_DIM, x[:rows], x[rows:])


def softmax_rows(queries, keys, allowed):
    scores = dot(stacked_heads(queries), keys, contract_last) * HEAD_DIM ** (-0.5)
    masked = jnp.where(jnp.concatenate([allowed, allowed], axis=0) > 0, scores, masked_score)
    weights = jnp.exp(masked - jnp.max(masked, axis=1, keepdims=True))
    return weights / jnp.sum(weights, axis=1, keepdims=True)


def sequence_labels(seq_lengths, seq_device, owner, count_rows):
    index = jnp.arange(seq_lengths.shape[0], dtype=jnp.int32)
    owned = jnp.where(seq_device == owner, seq_lengths, 0)
    earlier = index[None, :] < index[:, None]
    starts = jnp.sum(jnp.where(earlier, owned[None, :], 0), axis=1)
    places = jnp.arange(count_rows, dtype=jnp.int32)
    inside = (places[:, None] >= starts[None, :]) & (places[:, None] < (starts + owned)[None, :])
    return jnp.sum(jnp.where(inside, index[None, :] + 1, 0), axis=1)


def gelu_parts(v):
    c = (2.0 / jnp.pi) ** 0.5
    inner = jnp.tanh(c * (v + 0.044715 * v * v * v))
    value = 0.5 * v * (1.0 + inner)
    slope = 0.5 * (1.0 + inner) + 0.5 * v * (1.0 - inner * inner) * c * (1.0 + 3.0 * 0.044715 * v * v)
    return value, slope


VMEM_SPEC = pl.BlockSpec(memory_space=pltpu.VMEM)
ANY_SPEC = pl.BlockSpec(memory_space=pl.ANY)
SMEM_SPEC = pl.BlockSpec(memory_space=pltpu.SMEM)
WIDE = 2 * HEAD_DIM
UP_ROWS = 3 * HEAD_DIM + 256
DOWN_ROWS = HEAD_DIM + 256
SUM_ROWS = 16
MEMBERS = 4


def after(x, *others):
    if not others:
        return x
    return lax.optimization_barrier((x, *others))[0]


def left_lanes(x):
    return lax.broadcasted_iota(jnp.int32, x.shape, 1) < HEAD_DIM


def swapped(x):
    return pltpu.roll(x, HEAD_DIM, 1)


def zipped(a, b):
    left = left_lanes(a)
    return jnp.where(left, a, swapped(b)).astype(bf16), jnp.where(left, swapped(a), b).astype(bf16)


def pack_up(qkv_ref, fc1_ref, *rest):
    out_ref = rest[-1]
    for pair in range(MEMBERS // 2):
        lanes = slice(pair * 128, (pair + 1) * 128)
        q, k, v = (qkv_ref[0, p, :, lanes].astype(f32) for p in range(3))
        here, there = 2 * pair, 2 * pair + 1
        out_ref[here, :WIDE], out_ref[there, :WIDE] = zipped(q, k)
        rows = q.shape[0] // 2
        out_ref[here, WIDE : WIDE + rows], out_ref[there, WIDE : WIDE + rows] = zipped(v[:rows], v[rows:])
        base = WIDE + rows
        for d in (here, there):
            for h in range(2):
                out_ref[d, base + h * 128 : base + (h + 1) * 128] = fc1_ref[0, :, (2 * d + h) * 128 : (2 * d + h + 1) * 128]


def pack_first(qkv_ref, fc1_ref, small_ref, out_ref):
    pack_up(qkv_ref, fc1_ref, out_ref)
    for d in range(MEMBERS):
        out_ref[d, UP_ROWS:] = small_ref[...]


def pack_both(qkv_ref, fc1_ref, out_w_ref, fc2_ref, out_ref):
    pack_up(qkv_ref, fc1_ref, out_ref)
    pack_down(out_w_ref, fc2_ref, out_ref.at[:, UP_ROWS:])


def pack_down(out_w_ref, fc2_ref, out_ref):
    for d in range(MEMBERS):
        out_ref[d, :HEAD_DIM] = out_w_ref[0, d * HEAD_DIM : (d + 1) * HEAD_DIM]
        out_ref[d, HEAD_DIM:] = fc2_ref[0, d * 256 : (d + 1) * 256]


def call_pack(body, layer, ups, downs, small):
    rows, specs = 0, []
    if ups:
        rows += UP_ROWS
        specs += [
            pl.BlockSpec((1, 3, 128, MEMBERS * HEAD_DIM), lambda i: (layer, 0, 0, i)),
            pl.BlockSpec((1, 128, MEMBERS * 256), lambda i: (layer, 0, i)),
        ]
    if downs:
        rows += DOWN_ROWS
        specs += [
            pl.BlockSpec((1, MEMBERS * HEAD_DIM, 128), lambda i: (layer, i, 0)),
            pl.BlockSpec((1, MEMBERS * 256, 128), lambda i: (layer, i, 0)),
        ]
    if small:
        rows += small[0].shape[0]
        specs.append(pl.BlockSpec(small[0].shape, lambda i: (0, 0)))
    return pl.pallas_call(
        body,
        grid=(GROUP // MEMBERS,),
        in_specs=specs,
        out_specs=pl.BlockSpec((MEMBERS, rows, 128), lambda i: (i, 0, 0)),
        out_shape=jax.ShapeDtypeStruct((GROUP, rows, 128), bf16),
        cost_estimate=pl.CostEstimate(flops=0, bytes_accessed=GROUP * rows * 128 * 8, transcendentals=0),
        name=body.__name__,
    )(*ups, *downs, *small)


def join_up(own_ref, other_ref, out_ref):
    for e in range(MEMBERS):
        rows = slice(e * 128, (e + 1) * 128)
        a, b = own_ref[e, :WIDE].astype(f32), other_ref[e, :WIDE].astype(f32)
        out_ref[rows, :WIDE], out_ref[rows, WIDE : 2 * WIDE] = zipped(a, b)
        a, b = own_ref[e, WIDE : WIDE + 64].astype(f32), other_ref[e, WIDE : WIDE + 64].astype(f32)
        top, bottom = zipped(a, b)
        out_ref[e * 128 : e * 128 + 64, 2 * WIDE : 3 * WIDE] = top
        out_ref[e * 128 + 64 : (e + 1) * 128, 2 * WIDE : 3 * WIDE] = bottom
        for n, ref in enumerate((own_ref, other_ref)):
            for h in range(2):
                lanes = 3 * WIDE + n * 256 + h * 128
                out_ref[rows, lanes : lanes + 128] = ref[e, WIDE + 64 + h * 128 : WIDE + 64 + (h + 1) * 128]


def join_down(own_ref, other_ref, out_ref):
    base = own_ref.shape[1] - DOWN_ROWS
    for e in range(MEMBERS):
        lanes = slice(e * 128, (e + 1) * 128)
        for n, ref in enumerate((own_ref, other_ref)):
            out_ref[n * HEAD_DIM : (n + 1) * HEAD_DIM, lanes] = ref[e, base : base + HEAD_DIM]
            out_ref[WIDE + n * 256 : WIDE + (n + 1) * 256, lanes] = ref[e, base + HEAD_DIM :]


def join_both(own_ref, other_ref, up_ref, down_ref):
    join_up(own_ref, other_ref, up_ref)
    join_down(own_ref, other_ref, down_ref)


def join_halves(own_ref, lower_ref, upper_ref, up_ref, down_ref):
    lower = pl.program_id(0) < GROUP // MEMBERS // 2

    @pl.when(lower)
    def _():
        join_both(own_ref, lower_ref, up_ref, down_ref)

    @pl.when(jnp.logical_not(lower))
    def _():
        join_both(own_ref, upper_ref, up_ref, down_ref)


def call_join(body, own, others, ups, downs):
    rows = own.shape[1]
    steps = GROUP // MEMBERS
    spec = pl.BlockSpec((MEMBERS, rows, 128), lambda i: (i, 0, 0))
    other_specs = [spec]
    if len(others) == 2:
        other_specs = [
            pl.BlockSpec((MEMBERS, rows, 128), lambda i: (jnp.minimum(i, steps // 2 - 1), 0, 0)),
            pl.BlockSpec((MEMBERS, rows, 128), lambda i: (jnp.maximum(i - steps // 2, 0), 0, 0)),
        ]
    specs, shapes = [], []
    if ups:
        specs.append(pl.BlockSpec((MEMBERS * 128, 2 * UP_ROWS), lambda i: (i, 0)))
        shapes.append(jax.ShapeDtypeStruct((GROUP * 128, 2 * UP_ROWS), bf16))
    if downs:
        specs.append(pl.BlockSpec((2 * DOWN_ROWS, MEMBERS * 128), lambda i: (0, i)))
        shapes.append(jax.ShapeDtypeStruct((2 * DOWN_ROWS, GROUP * 128), bf16))
    return pl.pallas_call(
        body,
        grid=(GROUP // MEMBERS,),
        in_specs=[spec] + other_specs,
        out_specs=specs,
        out_shape=shapes,
        cost_estimate=pl.CostEstimate(flops=0, bytes_accessed=GROUP * rows * 128 * 12, transcendentals=0),
        name=body.__name__,
    )(own, *others)


def slot_copies(refs, which, target, core):
    block = target.shape[0] // 8
    half = block // 2
    pairs = []
    for slot in range(7):
        ref = refs[slot] if which is None else refs[slot].at[which]
        pairs.append((ref, target.at[pl.ds(slot * block, block)]))
    for n, at in ((7, core * half), (8, (1 - core) * half)):
        ref = refs[n] if which is None else refs[n].at[which]
        pairs.append((ref, target.at[pl.ds(pl.multiple_of(7 * block + at, half), half)]))
    return pairs


def split_copies(part, far_ref, give_ref, keep_ref, core):
    block = part.shape[0] // 8
    half = block // 2
    at, off = core * half, (1 - core) * half

    def rows(slot, start):
        return part.at[pl.ds(pl.multiple_of(slot * block + start, half), half)]

    return [
        (rows(7, off), far_ref),
        (part.at[pl.ds(block, 3 * block)], give_ref.at[pl.ds(0, 3 * block)]),
        (rows(0, off), give_ref.at[pl.ds(3 * block, half)]),
        (part.at[pl.ds(4 * block, 3 * block)], keep_ref.at[pl.ds(0, 3 * block)]),
        (rows(7, at), keep_ref.at[pl.ds(3 * block, half)]),
        (rows(0, at), keep_ref.at[pl.ds(3 * block + half, half)]),
    ]


def run_copies(pairs, sems, first):
    made = [pltpu.make_async_copy(a, b, sems.at[first + n]) for n, (a, b) in enumerate(pairs)]
    for copy in made:
        copy.start()
    return made


def heads_forward(chances, values):
    return merged_heads(dot(chances.astype(bf16), values)).astype(bf16)


def heads_backward(chances, queries, keys, values, grad, tables):
    grads = stacked_heads(grad)
    grad_chances = dot(grads, values, contract_last)
    grad_values = dot(chances.astype(bf16), grads, contract_first)
    centre = jnp.sum(grad_chances * chances, axis=1, keepdims=True)
    grad_scores = (chances * (grad_chances - centre)).astype(bf16)
    scale = HEAD_DIM ** (-0.5)
    grad_queries = merged_heads(dot(grad_scores, keys)) * scale
    grad_keys = dot(grad_scores, stacked_heads(queries), contract_first) * scale
    cosine, up, down = tables
    back = (cosine, -up, -down)
    return turn(grad_queries, *back).astype(bf16), turn(grad_keys, *back).astype(bf16), grad_values.astype(bf16)


def layer_pass(mode, *refs):
    refs = list(refs)

    def take(n):
        out = refs[:n]
        del refs[:n]
        return out

    forward, backward = mode != "last", mode != "first"
    core_ref, up_ref, down_ref, cos_ref, sin_up_ref, sin_down_ref, allowed_ref = take(7)
    core = core_ref[0]
    if mode == "first":
        bias_ref, gain_ref, shift_ref = take(3)
        rows_in = take(9)
    elif mode == "middle":
        (bias_ref,) = take(1)
        rows_in = take(9)
        grads_in = take(9)
    else:
        heads_ref, hidden_ref, normed_ref = take(3)
        grads_in = take(9)
    if mode == "first":
        normed_ref, heads_ref, hidden_ref, wide_ref = take(4)
        outs = take(3)
        raw, part, sems = take(3)
    elif mode == "middle":
        normed_ref, grad_rows_ref, wide_ref, slim_ref, sums_ref = take(5)
        outs = take(3)
        grad_outs = take(3)
        part, grad_part, sems = take(3)
    else:
        grad_rows_ref, slim_ref, sums_ref = take(3)
        grad_outs = take(3)
        grad_part, sems = take(2)

    pairs = []
    if mode == "first":
        pairs += slot_copies(rows_in, 0, raw, core)
    if mode == "middle":
        pairs += slot_copies(rows_in, None, normed_ref, core)
        pairs += slot_copies(grads_in, 1, grad_rows_ref, core)
    if mode == "last":
        pairs += slot_copies(grads_in, None, grad_rows_ref, core)
    for copy in run_copies(pairs, sems, 0):
        copy.wait()

    total = allowed_ref.shape[0]
    block = allowed_ref.shape[1]
    step = 2 * block

    if mode == "first":
        tile = 32

        def norm_tile(i, carry):
            at = pl.ds(pl.multiple_of(i * tile, tile), tile)
            x = raw[at, :].astype(f32)
            centred = x - jnp.mean(x, axis=1, keepdims=True)
            inverse = lax.rsqrt(jnp.mean(centred * centred, axis=1, keepdims=True) + norm_epsilon)
            normed_ref[at, :] = (centred * inverse * gain_ref[...] + shift_ref[...]).astype(bf16)
            return carry

        lax.fori_loop(0, total // tile, norm_tile, 0)

    if backward:
        sums_ref[...] = jnp.zeros_like(sums_ref)

    def one(p, carry):
        at = pl.ds(pl.multiple_of(p * step, step), step)
        if forward:
            before = dot(normed_ref[at, :], up_ref[...]) + bias_ref[...]
            hidden_pre = before[:, 3 * WIDE :]
        else:
            hidden_pre = hidden_ref[at, :]
        value, slope = gelu_parts(hidden_pre)
        if backward:
            grad_wide = dot(grad_rows_ref[at, :], down_ref[...], contract_last)
            slim_ref[at, 3 * WIDE :] = (grad_wide[:, WIDE:] * slope).astype(bf16)
        if forward:
            wide_ref[at, WIDE:] = value.astype(bf16)
        if mode == "first":
            hidden_ref[at, :] = hidden_pre
        for b in range(2):
            mine = slice(b * block, (b + 1) * block)
            own = pl.ds(pl.multiple_of(p * step + b * block, block), block)
            tables = (cos_ref[own, :], sin_up_ref[own, :], sin_down_ref[own, :])
            if forward:
                queries = turn(before[mine, :WIDE], *tables).astype(bf16)
                keys = turn(before[mine, WIDE : 2 * WIDE], *tables).astype(bf16)
                values = before[mine, 2 * WIDE : 3 * WIDE].astype(bf16)
            else:
                queries = heads_ref[own, :WIDE]
                keys = heads_ref[own, WIDE : 2 * WIDE]
                values = heads_ref[own, 2 * WIDE :]
            if mode == "first":
                heads_ref[own, :WIDE] = queries
                heads_ref[own, WIDE : 2 * WIDE] = keys
                heads_ref[own, 2 * WIDE :] = values
            chances = softmax_rows(queries, keys, allowed_ref[own, :])
            if forward:
                wide_ref[own, :WIDE] = heads_forward(chances, values)
            if backward:
                grads = heads_backward(
                    chances, queries, keys, values, grad_wide[mine, :WIDE].astype(bf16), tables
                )
                for n in range(3):
                    slim_ref[own, n * WIDE : (n + 1) * WIDE] = grads[n]
        if forward:
            part[at, :] = dot(wide_ref[at, :], down_ref[...]).astype(bf16)
        if backward:
            grad_normed = dot(slim_ref[at, :], up_ref[...], contract_last)
            grad_part[at, :] = grad_normed.astype(bf16)
            for n, rows in enumerate(
                (grad_normed, grad_normed * normed_ref[at, :].astype(f32), grad_rows_ref[at, :].astype(f32))
            ):
                sums_ref[n : n + 1] += jnp.sum(rows, axis=0, keepdims=True)
        return carry

    lax.fori_loop(0, total // step, one, 0)
    pairs = []
    if backward:
        pairs += split_copies(grad_part, *grad_outs, core)
    if forward:
        pairs += split_copies(part, *outs, core)
    for copy in run_copies(pairs, sems, 0):
        copy.wait()


def call_pass(mode, core, weights, tables, allowed, extra, chunks):
    total, block = allowed.shape
    half = block // 2
    width = weights[0].shape[0]
    slim = weights[0].shape[1]
    wide = weights[1].shape[0]
    parts = [
        jax.ShapeDtypeStruct((half, width), bf16),
        jax.ShapeDtypeStruct((3 * block + half, width), bf16),
        jax.ShapeDtypeStruct((4 * block, width), bf16),
    ]
    full = jax.ShapeDtypeStruct((total, width), bf16)
    sums = jax.ShapeDtypeStruct((SUM_ROWS, width), f32)
    slim_rows = jax.ShapeDtypeStruct((total, slim), bf16)
    wide_rows = jax.ShapeDtypeStruct((total, wide), bf16)
    if mode == "first":
        kept = [
            full,
            jax.ShapeDtypeStruct((total, 3 * WIDE), bf16),
            jax.ShapeDtypeStruct((total, slim - 3 * WIDE), f32),
            wide_rows,
        ]
        buffers = 2
    elif mode == "middle":
        kept = [full, full, wide_rows, slim_rows, sums]
        parts = parts * 2
        buffers = 2
    else:
        kept = [full, slim_rows, sums]
        buffers = 1
    passes = 2 if mode == "middle" else 1
    return pl.pallas_call(
        partial(layer_pass, mode),
        in_specs=[SMEM_SPEC] + [VMEM_SPEC] * (6 + len(extra)) + [ANY_SPEC] * len(chunks),
        out_specs=[VMEM_SPEC] * len(kept) + [ANY_SPEC] * len(parts),
        out_shape=kept + parts,
        scratch_shapes=[pltpu.VMEM((total, width), bf16)] * buffers + [pltpu.SemaphoreType.DMA((18,))],
        cost_estimate=pl.CostEstimate(
            flops=6 * total * width * (slim + wide) * passes,
            bytes_accessed=20_000_000 * passes,
            transcendentals=total * slim,
        ),
        name="pass_" + mode,
    )(core, *weights, *tables, allowed, *extra, *chunks)


def gradient_slabs(own_rows, other_rows, with_sums, pieces_in, core_ref, left_ref, *rest):
    right_refs, rest = rest[:pieces_in], rest[pieces_in:]
    if with_sums:
        sums_ref, *rest = rest
    own_ref, other_ref, *rest = rest
    turned_ref = rest[-1]
    if pieces_in == 1:
        right = right_refs[0][...]
    else:
        a, b = right_refs[-2][...], right_refs[-1][...]
        first = jnp.full(a.shape, core_ref[0]) == 0
        halves = [jnp.where(first, a, b), jnp.where(first, b, a)]
        right = jnp.concatenate([ref[...] for ref in right_refs[:-2]] + halves, axis=0)

    @pl.when(pl.program_id(0) == 0)
    def _():
        width = left_ref.shape[1]
        for n in range(width // 128):
            lanes = slice(n * 128, (n + 1) * 128)
            left = left_ref[:, lanes].astype(f32)
            if with_sums:
                rest[0][:, lanes] = jnp.sum(left, axis=0, keepdims=True)
            turned_ref[lanes, :] = left.T.astype(bf16)

    product = dot(turned_ref[...], right).astype(bf16)
    for ref, pieces in ((own_ref, own_rows), (other_ref, other_rows)):
        place = 0
        for first, last in pieces:
            for e in range(2):
                ref[e, place : place + last - first] = product[first:last, e * 128 : (e + 1) * 128]
            place += last - first
        if with_sums:
            for e in range(2):
                ref[e, place:] = sums_ref[:, e * 128 : (e + 1) * 128].astype(bf16)


def call_gradients(core, left, right, own_rows, other_rows, sums, name):
    total, height = left.shape
    width = right[0].shape[1]
    with_sums = len(sums) > 0
    rows = height // 2 + (SUM_ROWS if with_sums else 0)
    slab = pl.BlockSpec((2, rows, 128), lambda i: (i, 0, 0))
    shape = jax.ShapeDtypeStruct((width // 128, rows, 128), bf16)
    out_specs, out_shape = [slab, slab], [shape, shape]
    if with_sums:
        out_specs.append(pl.BlockSpec((1, height), lambda i: (0, 0)))
        out_shape.append(jax.ShapeDtypeStruct((1, height), f32))
    return pl.pallas_call(
        partial(gradient_slabs, own_rows, other_rows, with_sums, len(right)),
        grid=(width // 256,),
        in_specs=[SMEM_SPEC, pl.BlockSpec((total, height), lambda i: (0, 0))]
        + [pl.BlockSpec((x.shape[0], 256), lambda i: (0, i)) for x in (*right, *sums)],
        out_specs=out_specs,
        out_shape=out_shape,
        scratch_shapes=[pltpu.VMEM((height, total), bf16)],
        cost_estimate=pl.CostEstimate(
            flops=4 * total * height * width, bytes_accessed=2 * (total * (width + height) + 2 * height * width), transcendentals=0
        ),
        name=name,
    )(core, left, *right, *sums)


def spread_gradients(up_ref, down_ref, *rest):
    qkv_ref, out_w_ref, fc1_ref, fc2_ref, mark_ref = rest[-5:]
    mark_ref[...] = jnp.zeros_like(mark_ref)
    for p in range(3):
        rows = slice(p * HEAD_DIM, (p + 1) * HEAD_DIM)
        both = jnp.concatenate([up_ref[0, rows].astype(f32), up_ref[1, rows].astype(f32)], axis=0)
        qkv_ref[0, p] = both.T
    base = 3 * HEAD_DIM
    for d in range(2):
        for h in range(2):
            fc1_ref[0, :, (2 * d + h) * 128 : (2 * d + h + 1) * 128] = (
                up_ref[d, base + h * 128 : base + (h + 1) * 128].astype(f32).T
            )
        out_w_ref[0, d * HEAD_DIM : (d + 1) * HEAD_DIM] = down_ref[d, :HEAD_DIM].astype(f32)
        fc2_ref[0, d * 256 : (d + 1) * 256] = down_ref[d, HEAD_DIM:].astype(f32)


def call_spread(up, down, layer, filled):
    shapes = [
        jax.ShapeDtypeStruct((LAYERS, 3, 128, GROUP * HEAD_DIM), f32),
        jax.ShapeDtypeStruct((LAYERS, GROUP * HEAD_DIM, 128), f32),
        jax.ShapeDtypeStruct((LAYERS, 128, GROUP * 256), f32),
        jax.ShapeDtypeStruct((LAYERS, GROUP * 256, 128), f32),
        jax.ShapeDtypeStruct((8, 128), f32),
    ]
    return pl.pallas_call(
        spread_gradients,
        grid=(GROUP // 2,),
        in_specs=[
            pl.BlockSpec((2, up.shape[1], 128), lambda i: (i, 0, 0)),
            pl.BlockSpec((2, down.shape[1], 128), lambda i: (i, 0, 0)),
        ]
        + [ANY_SPEC] * len(filled),
        out_specs=[
            pl.BlockSpec((1, 3, 128, 128), lambda i: (layer, 0, 0, i)),
            pl.BlockSpec((1, 128, 128), lambda i: (layer, i, 0)),
            pl.BlockSpec((1, 128, 512), lambda i: (layer, 0, i)),
            pl.BlockSpec((1, 512, 128), lambda i: (layer, i, 0)),
            pl.BlockSpec((8, 128), lambda i: (0, 0)),
        ],
        out_shape=shapes,
        input_output_aliases={2 + n: n for n in range(len(filled))},
        name="spread_gradients",
    )(up, down, *filled)


def ring_total(core_ref, keep_ref, took_ref, moving_ref, got_ref):
    half = got_ref.shape[0]
    arrived = moving_ref[pl.ds(pl.multiple_of(core_ref[0] * half, half), half), :]
    return keep_ref[...].astype(f32) + took_ref[...].astype(f32) + arrived.astype(f32) + got_ref[...].astype(f32)


def centred_rows(state):
    centred = state - jnp.mean(state, axis=1, keepdims=True)
    return centred, lax.rsqrt(jnp.mean(centred * centred, axis=1, keepdims=True) + norm_epsilon)


def forward_end(last, core_ref, keep_ref, took_ref, moving_ref, got_ref, state_ref, after_ref, *rest):
    state = state_ref[...].astype(f32) + ring_total(core_ref, keep_ref, took_ref, moving_ref, got_ref) + after_ref[...]
    if last:
        rest[0][...] = state.astype(bf16)
        return
    gain_ref, shift_ref, state_out, normed_ref = rest
    state_out[...] = state
    centred, inverse = centred_rows(state)
    normed_ref[...] = (centred * inverse * gain_ref[...] + shift_ref[...]).astype(bf16)


def backward_end(core_ref, keep_ref, took_ref, moving_ref, got_ref, state_ref, grad_ref, gain_ref, *rest):
    grad_out, low_ref = rest[-2:]
    grad_normed = ring_total(core_ref, keep_ref, took_ref, moving_ref, got_ref)
    centred, inverse = centred_rows(state_ref[...].astype(f32))
    xhat = centred * inverse
    before = grad_ref[...].astype(f32)
    scaled = grad_normed * gain_ref[...]
    after = before + (
        scaled - jnp.mean(scaled, axis=1, keepdims=True) - xhat * jnp.mean(scaled * xhat, axis=1, keepdims=True)
    ) * inverse
    grad_out[...] = after
    low_ref[...] = after.astype(bf16)


def call_end(body, core, ring, extra, shapes, name):
    keep, took, moving, got, n_sum = ring
    _, half, width = got.shape

    def rows_of(array):
        n = array.shape[0] // half - 1
        return pl.BlockSpec((half, width), lambda i: (n, 0))

    def whole_of(array):
        return pl.BlockSpec(array.shape, lambda i: (0,) * len(array.shape))

    def one_of(array):
        return pl.BlockSpec((None,) + array.shape[1:], lambda i: (n_sum, 0, 0))

    return pl.pallas_call(
        body,
        grid=(1,),
        in_specs=[SMEM_SPEC, rows_of(keep), rows_of(took), one_of(moving), one_of(got)] + [whole_of(x) for x in extra],
        out_specs=[whole_of(x) for x in shapes],
        out_shape=shapes,
        name=name,
    )(core, keep, took, moving, got, *extra)


def per_device(
    n_dp,
    hidden_in,
    seq_lengths,
    seq_device,
    positions,
    norm_gain,
    norm_bias,
    qkv_weight,
    qkv_bias,
    out_weight,
    fc1_weight,
    fc1_bias,
    fc2_weight,
    output_bias,
    out_cotangent,
):
    block = hidden_in.shape[0]
    half = block // 2
    width = hidden_in.shape[1]
    piece = norm_gain.shape[1]
    hidden = fc1_weight.shape[2] // GROUP
    groups = n_dp // GROUP
    chips = GROUP // 2
    side = chips // 2 - 1

    if groups == 1:
        ring = [2 * a for a in range(chips // 2)] + [2 * a + 1 for a in reversed(range(chips // 2))]
    else:
        ring = list(range(chips // 2)) + list(reversed(range(chips // 2, chips)))
    ring_pairs = []
    for g in range(groups):
        for place in range(chips):
            for core, step in ((0, 1), (1, -1)):
                ring_pairs.append(
                    (
                        g * GROUP + ring[place] * 2 + core,
                        g * GROUP + ring[(place + step) % chips] * 2 + core,
                    )
                )
    core_pairs = [(i, i ^ 1) for i in range(n_dp)]
    inner = [[g * GROUP + i for i in range(GROUP)] for g in range(groups)]
    outer = [[g * GROUP + i for g in range(groups)] for i in range(GROUP)]
    if groups == 1:
        inner = None

    def along(x):
        return lax.ppermute(x, "dp", ring_pairs)

    def across(x):
        return lax.ppermute(x, "dp", core_pairs)

    def over(x):
        return lax.ppermute(x, "tensor", [(0, 1), (1, 0)])

    index = lax.axis_index("dp")
    group = index // GROUP
    chip = (index % GROUP) // 2
    core = index % 2
    tensor = lax.axis_index("tensor")
    is_first = core == 0
    at = core * half
    off = (1 - core) * half
    core_word = core.astype(jnp.int32).reshape(1)

    def my_half(x, start, axis=0):
        return lax.dynamic_slice_in_dim(x, start, half, axis)

    def in_order(own, other):
        return jnp.where(
            is_first, jnp.concatenate([own, other], 0), jnp.concatenate([other, own], 0)
        )

    def gather_rows(mine, needed={}):
        behind, ahead = [], []
        moving = mine
        for step in range(side):
            moving = along(after(moving, *needed.get(step, ())))
            behind.append(moving)
            ahead.append(across(moving))
        far = along(after(my_half(moving, at, moving.ndim - 2), *needed.get(side, ())))
        return [mine] + behind + ahead + [far, across(far)]

    rows = lax.broadcasted_iota(jnp.int32, (block, 1), 0)
    mine_rows = (rows < half) == is_first

    def ring_sum(*sets, needed={}):
        took_far = [across(give_far) for give_far, _, _ in sets]
        took = [across(give) for _, give, _ in sets]
        keep = [x for _, _, x in sets]
        far = [k[side * block : side * block + half].astype(f32) + t.astype(f32) for k, t in zip(keep, took_far)]
        moving = along(jnp.stack(far).astype(bf16))
        for step in reversed(range(side)):
            here = slice(step * block, (step + 1) * block)
            added = [k[here].astype(f32) + t[here].astype(f32) for k, t in zip(keep, took)]
            arrived = after(moving, *needed.get(step, ())).astype(f32)
            if step == side - 1:
                arrived = jnp.where(mine_rows, jnp.concatenate([arrived, arrived], 1), 0)
            moving = along((arrived + jnp.stack(added)).astype(bf16))
        got = across(my_half(moving, off, 1))
        return [(k, t, moving, got, n) for n, (k, t) in enumerate(zip(keep, took))]

    def spread(x):
        return lax.all_to_all(x, "dp", 0, 0, axis_index_groups=inner, tiled=True)

    small = jnp.concatenate(
        [
            norm_gain.reshape(-1),
            norm_bias.reshape(-1),
            output_bias.reshape(-1),
            (positions // 64).astype(bf16),
            (positions % 64).astype(bf16),
        ]
    )
    weights = []
    if groups == 1:
        qkv_turned = qkv_weight.transpose(0, 2, 1, 3)
        ups, downs = (qkv_turned, fc1_weight), (out_weight, fc2_weight)
        extra = jnp.concatenate([small, jnp.zeros_like(small)]).reshape(-1, 128)
        up = spread(call_pack(pack_first, 0, ups, (), (extra,)))
        small_all = up[:, UP_ROWS:].reshape(GROUP, -1)[:, : small.shape[0]]
        up_other = over(up)
        packed_down = call_pack(pack_down, 0, (), downs, ())
        down = spread(after(packed_down, up))
        down_other = over(down)
        weights.append(call_join(join_up, up, [up_other], True, False) + call_join(join_down, down, [down_other], False, True))
        packed_last = call_pack(pack_both, 1, ups, downs, ())
        firsts = (up, up_other, down)
    else:
        small_all = lax.all_gather(small, "dp", axis=0, tiled=False)
        for layer in range(LAYERS):
            up = jnp.concatenate(
                [
                    qkv_weight[layer].reshape(piece, 3, GROUP, HEAD_DIM).transpose(2, 0, 1, 3).reshape(GROUP, piece, -1),
                    fc1_weight[layer].reshape(piece, GROUP, hidden).transpose(1, 0, 2),
                ],
                axis=2,
            )
            up = lax.all_gather(spread(up), "dp", axis=0, axis_index_groups=outer, tiled=True)
            up = up.reshape(width // 128, 128, UP_ROWS)
            value = up[:, :, WIDE : WIDE + HEAD_DIM]
            first = WIDE + HEAD_DIM
            up = jnp.concatenate(
                [
                    up[:, :, :WIDE],
                    jnp.concatenate([value[:, :HEAD_DIM], value[:, HEAD_DIM:]], axis=2),
                    up[:, :, first : first + 128],
                    up[:, :, first + 128 :],
                ],
                axis=1,
            )
            down = jnp.concatenate(
                [out_weight[layer].reshape(GROUP, HEAD_DIM, piece), fc2_weight[layer].reshape(GROUP, hidden, piece)],
                axis=1,
            )
            down = lax.all_gather(spread(down), "dp", axis=0, axis_index_groups=outer, tiled=True)
            down = down.transpose(1, 0, 2).reshape(-1, width // 128, 128).transpose(1, 0, 2)
            weights.append(call_join(join_up, up, [over(up)], True, False) + call_join(join_down, down, [over(down)], False, True))
    if groups == 1:
        biases = jnp.concatenate([qkv_bias.reshape(LAYERS, 3 * HEAD_DIM), fc1_bias], axis=1)
    else:
        full_qkv = lax.all_gather(qkv_bias, "dp", axis=2, tiled=True)
        full_up = lax.all_gather(fc1_bias, "dp", axis=1, tiled=True)
        member = index % GROUP
        biases = jnp.concatenate(
            [
                lax.dynamic_slice_in_dim(full_qkv, member * HEAD_DIM, HEAD_DIM, 2).reshape(LAYERS, 3 * HEAD_DIM),
                lax.dynamic_slice_in_dim(full_up, member * hidden, hidden, 1),
            ],
            axis=1,
        )
    biases_other = over(biases)
    both_biases = jnp.stack([biases, biases_other], axis=1).astype(f32)
    bias_rows = jnp.concatenate(
        [
            both_biases[:, :, : 3 * HEAD_DIM].reshape(LAYERS, 2, 3, HEAD_DIM).transpose(0, 2, 1, 3).reshape(LAYERS, -1),
            both_biases[:, :, 3 * HEAD_DIM :].reshape(LAYERS, -1),
        ],
        axis=1,
    )
    vectors = small_all[:, : 6 * piece].reshape(n_dp, 3, LAYERS, piece).transpose(1, 2, 0, 3).reshape(3, LAYERS, 1, width).astype(f32)
    gains, shifts, added_bias = vectors[0], vectors[1], vectors[2]

    turned = jnp.where(is_first, 1, -1)
    place = jnp.sum(jnp.where(jnp.asarray(ring) == chip, jnp.arange(chips), 0))
    offsets = [0] + [-(s + 1) for s in range(side)] + [s + 1 for s in range(side)] + [chips // 2]
    places = (place + turned * jnp.asarray(offsets)) % chips
    chip_ids = jnp.sum(
        jnp.where(places[:, None] == jnp.arange(chips)[None, :], jnp.asarray(ring)[None, :], 0), axis=1
    )
    owners = group * GROUP + 2 * chip_ids + tensor
    labels = jax.vmap(lambda owner: sequence_labels(seq_lengths, seq_device, owner, block))(owners)
    rows_at = jnp.arange(block, dtype=jnp.int32)
    allowed = (
        (labels[:, :, None] == labels[:, None, :])
        & (labels[:, :, None] > 0)
        & (rows_at[None, None, :] <= rows_at[None, :, None])
    ) | (rows_at[None, None, :] == rows_at[None, :, None])
    allowed = allowed.astype(f32).reshape(chips * block, block)
    picked = (owners[:, None] == jnp.arange(n_dp)[None, :]).astype(f32)
    place_parts = jnp.dot(picked, small_all[:, 6 * piece :].astype(f32), precision=lax.Precision.HIGHEST)
    row_places = (place_parts[:, :block] * 64.0 + place_parts[:, block:]).reshape(chips * block)
    pair = ROT // 2
    frequency = 10000.0 ** (-2.0 * jnp.arange(pair, dtype=f32) / ROT)
    angles = row_places[:, None] * frequency[None, :]
    cosine, sine = jnp.cos(angles), jnp.sin(angles)
    nought = jnp.zeros_like(sine)
    rest = jnp.zeros((chips * block, HEAD_DIM - ROT), f32)
    tables = (
        jnp.concatenate([cosine, cosine, rest + 1.0] * 2, axis=1),
        jnp.concatenate([-sine, nought, rest] * 2, axis=1),
        jnp.concatenate([nought, sine, rest] * 2, axis=1),
    )

    both = jnp.stack([hidden_in, out_cotangent])
    both = jnp.where(tensor == core, both, across(both))
    keeps = jnp.stack([jnp.ones_like(labels[0]), (labels[0] > 0).astype(labels.dtype)]).astype(bf16)
    both = both * keeps[:, :, None]
    if groups == 1:
        inputs = gather_rows(
            after(both, packed_down, packed_last, firsts[0], firsts[2]),
            {1: (firsts[1], tables[0]), 2: (tables[1], tables[2], allowed), side: (down_other, weights[0][0])},
        )
        slab = spread(after(packed_last, inputs[-2]))
        others = tuple(over(slab[n * GROUP // 2 : (n + 1) * GROUP // 2]) for n in range(2))
        weights.append(call_join(join_halves, slab, others, True, True))
        slabs = (slab,)
    else:
        inputs = gather_rows(both)
        slabs, others = (), ()
    mine_inputs = my_half(both, at, 1)
    state, grad_state = mine_inputs[0], mine_inputs[1]

    normed, heads, hidden_pre, wide, *parts = call_pass(
        "first", core_word, weights[0], tables, allowed, [bias_rows[0:1], gains[0], shifts[0]], inputs
    )
    rows_shape = (half, width)
    next_state, normed_own = call_end(
        partial(forward_end, False),
        core_word,
        ring_sum((after(parts[0], *slabs), parts[1], parts[2]), needed={0: others[:1]})[0],
        [state, added_bias[0], gains[1], shifts[1]],
        [jax.ShapeDtypeStruct(rows_shape, f32), jax.ShapeDtypeStruct(rows_shape, bf16)],
        "forward_end",
    )
    normed_chunks = gather_rows(in_order(normed_own, across(normed_own)), {1: others[1:]})

    def handed_back(own_rows):
        filled = in_order(own_rows, across(own_rows))
        return jnp.where(tensor == core, filled, over(filled))

    def summed(own, other, *earlier):
        total = own.astype(f32) + other.astype(f32)
        if groups > 1:
            total = total.transpose(1, 0, 2).reshape(total.shape[1], width)
            total = lax.psum_scatter(total, "dp", scatter_dimension=1, axis_index_groups=outer, tiled=True)
            total = total.reshape(total.shape[0], GROUP, piece).transpose(1, 0, 2)
        return spread(after(total.astype(bf16), *earlier))

    down_own = [(0, HEAD_DIM), (WIDE, WIDE + hidden)]
    down_other = [(HEAD_DIM, WIDE), (WIDE + hidden, WIDE + 2 * hidden)]
    up_own = [(p * WIDE, p * WIDE + HEAD_DIM) for p in range(3)] + [(3 * WIDE, 3 * WIDE + hidden)]
    up_other = [(p * WIDE + HEAD_DIM, (p + 1) * WIDE) for p in range(3)] + [(3 * WIDE + hidden, 3 * WIDE + 2 * hidden)]

    def down_gradients(wide_rows, grad_rows):
        return call_gradients(core_word, wide_rows, grad_rows, down_own, down_other, [], "down_gradients")

    def up_gradients(slim_rows, normed_rows, sums):
        return call_gradients(core_word, slim_rows, [normed_rows], up_own, up_other, [sums], "up_gradients")

    def backward_finish(ring_end, state, grad_state, layer, *needed):
        return call_end(
            backward_end,
            core_word,
            ring_end,
            [state, grad_state, gains[layer], *needed],
            [jax.ShapeDtypeStruct(rows_shape, f32), jax.ShapeDtypeStruct(rows_shape, bf16)],
            "backward_end",
        )

    normed_last, grad_rows, wide_last, slim, sums, *parts = call_pass(
        "middle", core_word, weights[1], tables, allowed, [bias_rows[1:2]], normed_chunks + inputs
    )
    out_parts = parts[:3]
    down_pair = down_gradients(wide_last, [grad_rows])
    *up_pair, bias_last = up_gradients(slim, normed_last, sums)
    down_sent, up_sent = over(down_pair[1]), over(up_pair[1])
    grad_end, out_end = ring_sum(parts[3:], out_parts, needed={1: (down_pair[0],), 0: (up_pair[0],)})
    grad_state, grad_low = backward_finish(grad_end, next_state, grad_state, 1)
    (hidden_out,) = call_end(
        partial(forward_end, True),
        core_word,
        out_end,
        [next_state, added_bias[1]],
        [jax.ShapeDtypeStruct(rows_shape, bf16)],
        "forward_out",
    )
    hidden_out = handed_back(hidden_out)
    down_last = summed(down_pair[0], after(down_sent, grad_low))
    grad_chunks = gather_rows(in_order(grad_low, across(grad_low)), {0: (down_sent,), 2: (up_sent,), side: (down_last, hidden_out)})
    up_last = summed(up_pair[0], after(up_sent, grad_chunks[-2]), down_last)

    down_pair = down_gradients(wide, grad_chunks)
    down_sent = over(down_pair[1])
    grad_rows, slim, sums, *parts = call_pass(
        "last", core_word, weights[0], tables, allowed, [heads, after(hidden_pre, down_pair[0]), normed], grad_chunks
    )
    down_first = summed(down_pair[0], after(down_sent, slim), up_last)
    *up_pair, bias_first = up_gradients(slim, after(normed, up_last), sums)
    up_sent = over(up_pair[1])
    (grad_end,) = ring_sum((after(parts[0], up_pair[0]), parts[1], parts[2]), needed={1: (down_first,), 0: (up_sent,)})
    up_first = summed(up_pair[0], up_sent, down_first, grad_end[2])
    sums = jnp.concatenate([bias_first, bias_last], axis=0)
    sums_qkv = sums[:, : 3 * WIDE].reshape(LAYERS, 3, 2, HEAD_DIM)
    sums_up = sums[:, 3 * WIDE :].reshape(LAYERS, 2, hidden)
    bias_own, bias_other = (
        jnp.concatenate([sums_qkv[:, :, n].reshape(LAYERS, -1), sums_up[:, n]], axis=1) for n in range(2)
    )
    bias_sent = over(bias_other)
    needed = [bias_sent]
    if groups == 1:
        *filled, mark = call_spread(up_last, down_last, 1, [])
        needed.append(mark)
    _, grad_low = backward_finish(grad_end, state, grad_state, 0, *needed)
    grad_hidden = handed_back(grad_low).astype(f32)

    ends = jnp.stack([jnp.sum(x[:, UP_ROWS : UP_ROWS + 3].astype(f32), axis=0) for x in (up_first, up_last)])
    shift_grads = ends[:, 0]
    gain_grads = (ends[:, 1] - norm_bias.astype(f32) * ends[:, 0]) / norm_gain.astype(f32)
    after_grads = ends[:, 2] / GROUP
    bias_sums = bias_own + bias_sent
    bias_qkv, bias_up = bias_sums[:, : 3 * HEAD_DIM].reshape(LAYERS, 3, HEAD_DIM), bias_sums[:, 3 * HEAD_DIM :]
    if groups == 1:
        grad_qkv, grad_out, grad_up, grad_down, _ = call_spread(up_first, down_first, 0, filled)
        grad_qkv = grad_qkv.transpose(0, 2, 1, 3)
    else:
        bias_qkv = lax.all_gather(lax.psum(bias_qkv, "dp", axis_index_groups=outer), "dp", axis=2, axis_index_groups=inner, tiled=True)
        bias_up = lax.all_gather(lax.psum(bias_up, "dp", axis_index_groups=outer), "dp", axis=1, axis_index_groups=inner, tiled=True)
        bias_qkv = lax.dynamic_slice_in_dim(bias_qkv, index * qkv_bias.shape[2], qkv_bias.shape[2], 2)
        bias_up = lax.dynamic_slice_in_dim(bias_up, index * fc1_bias.shape[1], fc1_bias.shape[1], 1)
        ups = jnp.stack([up_first, up_last]).astype(f32)
        downs = jnp.stack([down_first, down_last]).astype(f32)
        grad_qkv = ups[:, :, : 3 * HEAD_DIM].reshape(LAYERS, GROUP, 3, HEAD_DIM, piece).transpose(0, 4, 2, 1, 3).reshape(LAYERS, piece, 3, -1)
        grad_up = ups[:, :, 3 * HEAD_DIM : UP_ROWS].transpose(0, 3, 1, 2).reshape(LAYERS, piece, -1)
        grad_out = downs[:, :, :HEAD_DIM].reshape(LAYERS, -1, piece)
        grad_down = downs[:, :, HEAD_DIM:].reshape(LAYERS, -1, piece)
    return (
        hidden_out,
        grad_hidden,
        gain_grads,
        shift_grads,
        grad_qkv,
        bias_qkv,
        grad_out,
        grad_up,
        bias_up,
        grad_down,
        after_grads,
    )


def solution(mesh):
    placed = (
        P("dp", None),
        P(),
        P(),
        P("dp"),
        P(None, "dp"),
        P(None, "dp"),
        P(None, "dp", None, "tensor"),
        P(None, None, ("tensor", "dp")),
        P(None, "tensor", "dp"),
        P(None, "dp", "tensor"),
        P(None, ("tensor", "dp")),
        P(None, "tensor", "dp"),
        P(None, "dp"),
        P("dp", None),
    )
    return jax.shard_map(
        partial(per_device, mesh.shape["dp"]),
        mesh=mesh,
        in_specs=placed,
        out_specs=(
            P("dp", None),
            P("dp", None),
            P(None, "dp"),
            P(None, "dp"),
            P(None, "dp", None, "tensor"),
            P(None, None, ("tensor", "dp")),
            P(None, "tensor", "dp"),
            P(None, "dp", "tensor"),
            P(None, ("tensor", "dp")),
            P(None, "tensor", "dp"),
            P(None, "dp"),
        ),
        check_vma=False,
    )
```

```python
from functools import partial

import jax
import jax.numpy as jnp
from jax import lax
from jax.experimental import pallas as pl
from jax.experimental.pallas import tpu as pltpu
from jax.sharding import PartitionSpec as P

HEAD_DIM = 64
ROT = 32
LAYERS = 2
GROUP = 16

norm_epsilon = 1e-05
masked_score = -1e30
bf16 = jnp.bfloat16
f32 = jnp.float32

contract_last = (((1,), (1,)), ((), ()))
contract_first = (((0,), (0,)), ((), ()))


def dot(a, b, dims=(((1,), (0,)), ((), ()))):
    return lax.dot_general(a, b, dims, preferred_element_type=f32)


def turn(x, cosine, up, down):
    return x * cosine + pltpu.roll(x, x.shape[1] - ROT // 2, 1) * up + pltpu.roll(x, ROT // 2, 1) * down


def stacked_heads(x):
    lane = lax.broadcasted_iota(jnp.int32, x.shape, 1)
    zero = jnp.zeros_like(x)
    return jnp.concatenate(
        [jnp.where(lane < HEAD_DIM, x, zero), jnp.where(lane < HEAD_DIM, zero, x)], axis=0
    )


def merged_heads(x):
    rows = x.shape[0] // 2
    lane = lax.broadcasted_iota(jnp.int32, (rows, x.shape[1]), 1)
    return jnp.where(lane < HEAD_DIM, x[:rows], x[rows:])


def softmax_rows(queries, keys, allowed):
    scores = dot(stacked_heads(queries), keys, contract_last) * HEAD_DIM ** (-0.5)
    masked = jnp.where(jnp.concatenate([allowed, allowed], axis=0) > 0, scores, masked_score)
    weights = jnp.exp(masked - jnp.max(masked, axis=1, keepdims=True))
    return weights / jnp.sum(weights, axis=1, keepdims=True)


def sequence_labels(seq_lengths, seq_device, owner, count_rows):
    index = jnp.arange(seq_lengths.shape[0], dtype=jnp.int32)
    owned = jnp.where(seq_device == owner, seq_lengths, 0)
    earlier = index[None, :] < index[:, None]
    starts = jnp.sum(jnp.where(earlier, owned[None, :], 0), axis=1)
    places = jnp.arange(count_rows, dtype=jnp.int32)
    inside = (places[:, None] >= starts[None, :]) & (places[:, None] < (starts + owned)[None, :])
    return jnp.sum(jnp.where(inside, index[None, :] + 1, 0), axis=1)


def gelu_parts(v):
    c = (2.0 / jnp.pi) ** 0.5
    inner = jnp.tanh(c * (v + 0.044715 * v * v * v))
    value = 0.5 * v * (1.0 + inner)
    slope = 0.5 * (1.0 + inner) + 0.5 * v * (1.0 - inner * inner) * c * (1.0 + 3.0 * 0.044715 * v * v)
    return value, slope


VMEM_SPEC = pl.BlockSpec(memory_space=pltpu.VMEM)
ANY_SPEC = pl.BlockSpec(memory_space=pl.ANY)
SMEM_SPEC = pl.BlockSpec(memory_space=pltpu.SMEM)
WIDE = 2 * HEAD_DIM
UP_ROWS = 3 * HEAD_DIM + 256
DOWN_ROWS = HEAD_DIM + 256
SUM_ROWS = 16
MEMBERS = 4


def after(x, *others):
    if not others:
        return x
    return lax.optimization_barrier((x, *others))[0]


def left_lanes(x):
    return lax.broadcasted_iota(jnp.int32, x.shape, 1) < HEAD_DIM


def swapped(x):
    return pltpu.roll(x, HEAD_DIM, 1)


def zipped(a, b):
    left = left_lanes(a)
    return jnp.where(left, a, swapped(b)).astype(bf16), jnp.where(left, swapped(a), b).astype(bf16)


def pack_up(qkv_ref, fc1_ref, *rest):
    out_ref = rest[-1]
    for pair in range(MEMBERS // 2):
        lanes = slice(pair * 128, (pair + 1) * 128)
        q, k, v = (qkv_ref[0, p, :, lanes].astype(f32) for p in range(3))
        here, there = 2 * pair, 2 * pair + 1
        out_ref[here, :WIDE], out_ref[there, :WIDE] = zipped(q, k)
        rows = q.shape[0] // 2
        out_ref[here, WIDE : WIDE + rows], out_ref[there, WIDE : WIDE + rows] = zipped(v[:rows], v[rows:])
        base = WIDE + rows
        for d in (here, there):
            for h in range(2):
                out_ref[d, base + h * 128 : base + (h + 1) * 128] = fc1_ref[0, :, (2 * d + h) * 128 : (2 * d + h + 1) * 128]


def pack_first(qkv_ref, fc1_ref, small_ref, out_ref):
    pack_up(qkv_ref, fc1_ref, out_ref)
    for d in range(MEMBERS):
        out_ref[d, UP_ROWS:] = small_ref[...]


def pack_both(qkv_ref, fc1_ref, out_w_ref, fc2_ref, out_ref):
    pack_up(qkv_ref, fc1_ref, out_ref)
    pack_down(out_w_ref, fc2_ref, out_ref.at[:, UP_ROWS:])


def pack_down(out_w_ref, fc2_ref, out_ref):
    for d in range(MEMBERS):
        out_ref[d, :HEAD_DIM] = out_w_ref[0, d * HEAD_DIM : (d + 1) * HEAD_DIM]
        out_ref[d, HEAD_DIM:] = fc2_ref[0, d * 256 : (d + 1) * 256]


def call_pack(body, layer, ups, downs, small):
    rows, specs = 0, []
    if ups:
        rows += UP_ROWS
        specs += [
            pl.BlockSpec((1, 3, 128, MEMBERS * HEAD_DIM), lambda i: (layer, 0, 0, i)),
            pl.BlockSpec((1, 128, MEMBERS * 256), lambda i: (layer, 0, i)),
        ]
    if downs:
        rows += DOWN_ROWS
        specs += [
            pl.BlockSpec((1, MEMBERS * HEAD_DIM, 128), lambda i: (layer, i, 0)),
            pl.BlockSpec((1, MEMBERS * 256, 128), lambda i: (layer, i, 0)),
        ]
    if small:
        rows += small[0].shape[0]
        specs.append(pl.BlockSpec(small[0].shape, lambda i: (0, 0)))
    return pl.pallas_call(
        body,
        grid=(GROUP // MEMBERS,),
        in_specs=specs,
        out_specs=pl.BlockSpec((MEMBERS, rows, 128), lambda i: (i, 0, 0)),
        out_shape=jax.ShapeDtypeStruct((GROUP, rows, 128), bf16),
        cost_estimate=pl.CostEstimate(flops=0, bytes_accessed=GROUP * rows * 128 * 8, transcendentals=0),
        name=body.__name__,
    )(*ups, *downs, *small)


def join_up(own_ref, other_ref, out_ref):
    for e in range(MEMBERS):
        rows = slice(e * 128, (e + 1) * 128)
        a, b = own_ref[e, :WIDE].astype(f32), other_ref[e, :WIDE].astype(f32)
        out_ref[rows, :WIDE], out_ref[rows, WIDE : 2 * WIDE] = zipped(a, b)
        a, b = own_ref[e, WIDE : WIDE + 64].astype(f32), other_ref[e, WIDE : WIDE + 64].astype(f32)
        top, bottom = zipped(a, b)
        out_ref[e * 128 : e * 128 + 64, 2 * WIDE : 3 * WIDE] = top
        out_ref[e * 128 + 64 : (e + 1) * 128, 2 * WIDE : 3 * WIDE] = bottom
        for n, ref in enumerate((own_ref, other_ref)):
            for h in range(2):
                lanes = 3 * WIDE + n * 256 + h * 128
                out_ref[rows, lanes : lanes + 128] = ref[e, WIDE + 64 + h * 128 : WIDE + 64 + (h + 1) * 128]


def join_down(own_ref, other_ref, out_ref):
    base = own_ref.shape[1] - DOWN_ROWS
    for e in range(MEMBERS):
        lanes = slice(e * 128, (e + 1) * 128)
        for n, ref in enumerate((own_ref, other_ref)):
            out_ref[n * HEAD_DIM : (n + 1) * HEAD_DIM, lanes] = ref[e, base : base + HEAD_DIM]
            out_ref[WIDE + n * 256 : WIDE + (n + 1) * 256, lanes] = ref[e, base + HEAD_DIM :]


def join_both(own_ref, other_ref, up_ref, down_ref):
    join_up(own_ref, other_ref, up_ref)
    join_down(own_ref, other_ref, down_ref)


def join_halves(own_ref, lower_ref, upper_ref, up_ref, down_ref):
    lower = pl.program_id(0) < GROUP // MEMBERS // 2

    @pl.when(lower)
    def _():
        join_both(own_ref, lower_ref, up_ref, down_ref)

    @pl.when(jnp.logical_not(lower))
    def _():
        join_both(own_ref, upper_ref, up_ref, down_ref)


def call_join(body, own, others, ups, downs):
    rows = own.shape[1]
    steps = GROUP // MEMBERS
    spec = pl.BlockSpec((MEMBERS, rows, 128), lambda i: (i, 0, 0))
    other_specs = [spec]
    if len(others) == 2:
        other_specs = [
            pl.BlockSpec((MEMBERS, rows, 128), lambda i: (jnp.minimum(i, steps // 2 - 1), 0, 0)),
            pl.BlockSpec((MEMBERS, rows, 128), lambda i: (jnp.maximum(i - steps // 2, 0), 0, 0)),
        ]
    specs, shapes = [], []
    if ups:
        specs.append(pl.BlockSpec((MEMBERS * 128, 2 * UP_ROWS), lambda i: (i, 0)))
        shapes.append(jax.ShapeDtypeStruct((GROUP * 128, 2 * UP_ROWS), bf16))
    if downs:
        specs.append(pl.BlockSpec((2 * DOWN_ROWS, MEMBERS * 128), lambda i: (0, i)))
        shapes.append(jax.ShapeDtypeStruct((2 * DOWN_ROWS, GROUP * 128), bf16))
    return pl.pallas_call(
        body,
        grid=(GROUP // MEMBERS,),
        in_specs=[spec] + other_specs,
        out_specs=specs,
        out_shape=shapes,
        cost_estimate=pl.CostEstimate(flops=0, bytes_accessed=GROUP * rows * 128 * 12, transcendentals=0),
        name=body.__name__,
    )(own, *others)


def slot_copies(refs, which, target, core):
    block = target.shape[0] // 8
    half = block // 2
    pairs = []
    for slot in range(7):
        ref = refs[slot] if which is None else refs[slot].at[which]
        pairs.append((ref, target.at[pl.ds(slot * block, block)]))
    for n, at in ((7, core * half), (8, (1 - core) * half)):
        ref = refs[n] if which is None else refs[n].at[which]
        pairs.append((ref, target.at[pl.ds(pl.multiple_of(7 * block + at, half), half)]))
    return pairs


def split_copies(part, far_ref, give_ref, keep_ref, core):
    block = part.shape[0] // 8
    half = block // 2
    at, off = core * half, (1 - core) * half

    def rows(slot, start):
        return part.at[pl.ds(pl.multiple_of(slot * block + start, half), half)]

    return [
        (rows(7, off), far_ref),
        (part.at[pl.ds(block, 3 * block)], give_ref.at[pl.ds(0, 3 * block)]),
        (rows(0, off), give_ref.at[pl.ds(3 * block, half)]),
        (part.at[pl.ds(4 * block, 3 * block)], keep_ref.at[pl.ds(0, 3 * block)]),
        (rows(7, at), keep_ref.at[pl.ds(3 * block, half)]),
        (rows(0, at), keep_ref.at[pl.ds(3 * block + half, half)]),
    ]


def run_copies(pairs, sems, first):
    made = [pltpu.make_async_copy(a, b, sems.at[first + n]) for n, (a, b) in enumerate(pairs)]
    for copy in made:
        copy.start()
    return made


def heads_forward(chances, values):
    return merged_heads(dot(chances.astype(bf16), values)).astype(bf16)


def heads_backward(chances, queries, keys, values, grad, tables):
    grads = stacked_heads(grad)
    grad_chances = dot(grads, values, contract_last)
    grad_values = dot(chances.astype(bf16), grads, contract_first)
    centre = jnp.sum(grad_chances * chances, axis=1, keepdims=True)
    grad_scores = (chances * (grad_chances - centre)).astype(bf16)
    scale = HEAD_DIM ** (-0.5)
    grad_queries = merged_heads(dot(grad_scores, keys)) * scale
    grad_keys = dot(grad_scores, stacked_heads(queries), contract_first) * scale
    cosine, up, down = tables
    back = (cosine, -up, -down)
    return turn(grad_queries, *back).astype(bf16), turn(grad_keys, *back).astype(bf16), grad_values.astype(bf16)


def layer_pass(mode, *refs):
    refs = list(refs)

    def take(n):
        out = refs[:n]
        del refs[:n]
        return out

    forward, backward = mode != "last", mode != "first"
    core_ref, up_ref, down_ref, cos_ref, sin_up_ref, sin_down_ref, allowed_ref = take(7)
    core = core_ref[0]
    if mode == "first":
        bias_ref, gain_ref, shift_ref = take(3)
        rows_in = take(9)
    elif mode == "middle":
        (bias_ref,) = take(1)
        rows_in = take(9)
        grads_in = take(9)
    else:
        heads_ref, hidden_ref, normed_ref = take(3)
        grads_in = take(9)
    if mode == "first":
        normed_ref, heads_ref, hidden_ref, wide_ref = take(4)
        outs = take(3)
        raw, part, sems = take(3)
    elif mode == "middle":
        normed_ref, grad_rows_ref, wide_ref, slim_ref, sums_ref = take(5)
        outs = take(3)
        grad_outs = take(3)
        part, grad_part, sems = take(3)
    else:
        grad_rows_ref, slim_ref, sums_ref = take(3)
        grad_outs = take(3)
        grad_part, sems = take(2)

    pairs = []
    if mode == "first":
        pairs += slot_copies(rows_in, 0, raw, core)
    if mode == "middle":
        pairs += slot_copies(rows_in, None, normed_ref, core)
        pairs += slot_copies(grads_in, 1, grad_rows_ref, core)
    if mode == "last":
        pairs += slot_copies(grads_in, None, grad_rows_ref, core)
    for copy in run_copies(pairs, sems, 0):
        copy.wait()

    total = allowed_ref.shape[0]
    block = allowed_ref.shape[1]
    step = 2 * block

    if mode == "first":
        tile = 32

        def norm_tile(i, carry):
            at = pl.ds(pl.multiple_of(i * tile, tile), tile)
            x = raw[at, :].astype(f32)
            centred = x - jnp.mean(x, axis=1, keepdims=True)
            inverse = lax.rsqrt(jnp.mean(centred * centred, axis=1, keepdims=True) + norm_epsilon)
            normed_ref[at, :] = (centred * inverse * gain_ref[...] + shift_ref[...]).astype(bf16)
            return carry

        lax.fori_loop(0, total // tile, norm_tile, 0)

    if backward:
        sums_ref[...] = jnp.zeros_like(sums_ref)

    def one(p, carry):
        at = pl.ds(pl.multiple_of(p * step, step), step)
        if forward:
            before = dot(normed_ref[at, :], up_ref[...]) + bias_ref[...]
            hidden_pre = before[:, 3 * WIDE :]
        else:
            hidden_pre = hidden_ref[at, :]
        value, slope = gelu_parts(hidden_pre)
        if backward:
            grad_wide = dot(grad_rows_ref[at, :], down_ref[...], contract_last)
            slim_ref[at, 3 * WIDE :] = (grad_wide[:, WIDE:] * slope).astype(bf16)
        if forward:
            wide_ref[at, WIDE:] = value.astype(bf16)
        if mode == "first":
            hidden_ref[at, :] = hidden_pre
        for b in range(2):
            mine = slice(b * block, (b + 1) * block)
            own = pl.ds(pl.multiple_of(p * step + b * block, block), block)
            tables = (cos_ref[own, :], sin_up_ref[own, :], sin_down_ref[own, :])
            if forward:
                queries = turn(before[mine, :WIDE], *tables).astype(bf16)
                keys = turn(before[mine, WIDE : 2 * WIDE], *tables).astype(bf16)
                values = before[mine, 2 * WIDE : 3 * WIDE].astype(bf16)
            else:
                queries = heads_ref[own, :WIDE]
                keys = heads_ref[own, WIDE : 2 * WIDE]
                values = heads_ref[own, 2 * WIDE :]
            if mode == "first":
                heads_ref[own, :WIDE] = queries
                heads_ref[own, WIDE : 2 * WIDE] = keys
                heads_ref[own, 2 * WIDE :] = values
            chances = softmax_rows(queries, keys, allowed_ref[own, :])
            if forward:
                wide_ref[own, :WIDE] = heads_forward(chances, values)
            if backward:
                grads = heads_backward(
                    chances, queries, keys, values, grad_wide[mine, :WIDE].astype(bf16), tables
                )
                for n in range(3):
                    slim_ref[own, n * WIDE : (n + 1) * WIDE] = grads[n]
        if forward:
            part[at, :] = dot(wide_ref[at, :], down_ref[...]).astype(bf16)
        if backward:
            grad_normed = dot(slim_ref[at, :], up_ref[...], contract_last)
            grad_part[at, :] = grad_normed.astype(bf16)
            for n, rows in enumerate(
                (grad_normed, grad_normed * normed_ref[at, :].astype(f32), grad_rows_ref[at, :].astype(f32))
            ):
                sums_ref[n : n + 1] += jnp.sum(rows, axis=0, keepdims=True)
        return carry

    lax.fori_loop(0, total // step, one, 0)
    pairs = []
    if backward:
        pairs += split_copies(grad_part, *grad_outs, core)
    if forward:
        pairs += split_copies(part, *outs, core)
    for copy in run_copies(pairs, sems, 0):
        copy.wait()


def call_pass(mode, core, weights, tables, allowed, extra, chunks):
    total, block = allowed.shape
    half = block // 2
    width = weights[0].shape[0]
    slim = weights[0].shape[1]
    wide = weights[1].shape[0]
    parts = [
        jax.ShapeDtypeStruct((half, width), bf16),
        jax.ShapeDtypeStruct((3 * block + half, width), bf16),
        jax.ShapeDtypeStruct((4 * block, width), bf16),
    ]
    full = jax.ShapeDtypeStruct((total, width), bf16)
    sums = jax.ShapeDtypeStruct((SUM_ROWS, width), f32)
    slim_rows = jax.ShapeDtypeStruct((total, slim), bf16)
    wide_rows = jax.ShapeDtypeStruct((total, wide), bf16)
    if mode == "first":
        kept = [
            full,
            jax.ShapeDtypeStruct((total, 3 * WIDE), bf16),
            jax.ShapeDtypeStruct((total, slim - 3 * WIDE), f32),
            wide_rows,
        ]
        buffers = 2
    elif mode == "middle":
        kept = [full, full, wide_rows, slim_rows, sums]
        parts = parts * 2
        buffers = 2
    else:
        kept = [full, slim_rows, sums]
        buffers = 1
    passes = 2 if mode == "middle" else 1
    return pl.pallas_call(
        partial(layer_pass, mode),
        in_specs=[SMEM_SPEC] + [VMEM_SPEC] * (6 + len(extra)) + [ANY_SPEC] * len(chunks),
        out_specs=[VMEM_SPEC] * len(kept) + [ANY_SPEC] * len(parts),
        out_shape=kept + parts,
        scratch_shapes=[pltpu.VMEM((total, width), bf16)] * buffers + [pltpu.SemaphoreType.DMA((18,))],
        cost_estimate=pl.CostEstimate(
            flops=6 * total * width * (slim + wide) * passes,
            bytes_accessed=20_000_000 * passes,
            transcendentals=total * slim,
        ),
        name="pass_" + mode,
    )(core, *weights, *tables, allowed, *extra, *chunks)


def gradient_slabs(own_rows, other_rows, with_sums, pieces_in, core_ref, left_ref, *rest):
    right_refs, rest = rest[:pieces_in], rest[pieces_in:]
    if with_sums:
        sums_ref, *rest = rest
    own_ref, other_ref, *rest = rest
    turned_ref = rest[-1]
    if pieces_in == 1:
        right = right_refs[0][...]
    else:
        a, b = right_refs[-2][...], right_refs[-1][...]
        first = jnp.full(a.shape, core_ref[0]) == 0
        halves = [jnp.where(first, a, b), jnp.where(first, b, a)]
        right = jnp.concatenate([ref[...] for ref in right_refs[:-2]] + halves, axis=0)

    @pl.when(pl.program_id(0) == 0)
    def _():
        width = left_ref.shape[1]
        for n in range(width // 128):
            lanes = slice(n * 128, (n + 1) * 128)
            left = left_ref[:, lanes].astype(f32)
            if with_sums:
                rest[0][:, lanes] = jnp.sum(left, axis=0, keepdims=True)
            turned_ref[lanes, :] = left.T.astype(bf16)

    product = dot(turned_ref[...], right).astype(bf16)
    for ref, pieces in ((own_ref, own_rows), (other_ref, other_rows)):
        place = 0
        for first, last in pieces:
            for e in range(2):
                ref[e, place : place + last - first] = product[first:last, e * 128 : (e + 1) * 128]
            place += last - first
        if with_sums:
            for e in range(2):
                ref[e, place:] = sums_ref[:, e * 128 : (e + 1) * 128].astype(bf16)


def call_gradients(core, left, right, own_rows, other_rows, sums, name):
    total, height = left.shape
    width = right[0].shape[1]
    with_sums = len(sums) > 0
    rows = height // 2 + (SUM_ROWS if with_sums else 0)
    slab = pl.BlockSpec((2, rows, 128), lambda i: (i, 0, 0))
    shape = jax.ShapeDtypeStruct((width // 128, rows, 128), bf16)
    out_specs, out_shape = [slab, slab], [shape, shape]
    if with_sums:
        out_specs.append(pl.BlockSpec((1, height), lambda i: (0, 0)))
        out_shape.append(jax.ShapeDtypeStruct((1, height), f32))
    return pl.pallas_call(
        partial(gradient_slabs, own_rows, other_rows, with_sums, len(right)),
        grid=(width // 256,),
        in_specs=[SMEM_SPEC, pl.BlockSpec((total, height), lambda i: (0, 0))]
        + [pl.BlockSpec((x.shape[0], 256), lambda i: (0, i)) for x in (*right, *sums)],
        out_specs=out_specs,
        out_shape=out_shape,
        scratch_shapes=[pltpu.VMEM((height, total), bf16)],
        cost_estimate=pl.CostEstimate(
            flops=4 * total * height * width, bytes_accessed=2 * (total * (width + height) + 2 * height * width), transcendentals=0
        ),
        name=name,
    )(core, left, *right, *sums)


def spread_gradients(up_ref, down_ref, *rest):
    qkv_ref, out_w_ref, fc1_ref, fc2_ref, mark_ref = rest[-5:]
    mark_ref[...] = jnp.zeros_like(mark_ref)
    for p in range(3):
        rows = slice(p * HEAD_DIM, (p + 1) * HEAD_DIM)
        both = jnp.concatenate([up_ref[0, rows].astype(f32), up_ref[1, rows].astype(f32)], axis=0)
        qkv_ref[0, p] = both.T
    base = 3 * HEAD_DIM
    for d in range(2):
        for h in range(2):
            fc1_ref[0, :, (2 * d + h) * 128 : (2 * d + h + 1) * 128] = (
                up_ref[d, base + h * 128 : base + (h + 1) * 128].astype(f32).T
            )
        out_w_ref[0, d * HEAD_DIM : (d + 1) * HEAD_DIM] = down_ref[d, :HEAD_DIM].astype(f32)
        fc2_ref[0, d * 256 : (d + 1) * 256] = down_ref[d, HEAD_DIM:].astype(f32)


def call_spread(up, down, layer, filled):
    shapes = [
        jax.ShapeDtypeStruct((LAYERS, 3, 128, GROUP * HEAD_DIM), f32),
        jax.ShapeDtypeStruct((LAYERS, GROUP * HEAD_DIM, 128), f32),
        jax.ShapeDtypeStruct((LAYERS, 128, GROUP * 256), f32),
        jax.ShapeDtypeStruct((LAYERS, GROUP * 256, 128), f32),
        jax.ShapeDtypeStruct((8, 128), f32),
    ]
    return pl.pallas_call(
        spread_gradients,
        grid=(GROUP // 2,),
        in_specs=[
            pl.BlockSpec((2, up.shape[1], 128), lambda i: (i, 0, 0)),
            pl.BlockSpec((2, down.shape[1], 128), lambda i: (i, 0, 0)),
        ]
        + [ANY_SPEC] * len(filled),
        out_specs=[
            pl.BlockSpec((1, 3, 128, 128), lambda i: (layer, 0, 0, i)),
            pl.BlockSpec((1, 128, 128), lambda i: (layer, i, 0)),
            pl.BlockSpec((1, 128, 512), lambda i: (layer, 0, i)),
            pl.BlockSpec((1, 512, 128), lambda i: (layer, i, 0)),
            pl.BlockSpec((8, 128), lambda i: (0, 0)),
        ],
        out_shape=shapes,
        input_output_aliases={2 + n: n for n in range(len(filled))},
        name="spread_gradients",
    )(up, down, *filled)


def ring_total(core_ref, keep_ref, took_ref, moving_ref, got_ref):
    half = got_ref.shape[0]
    arrived = moving_ref[pl.ds(pl.multiple_of(core_ref[0] * half, half), half), :]
    return keep_ref[...].astype(f32) + took_ref[...].astype(f32) + arrived.astype(f32) + got_ref[...].astype(f32)


def centred_rows(state):
    centred = state - jnp.mean(state, axis=1, keepdims=True)
    return centred, lax.rsqrt(jnp.mean(centred * centred, axis=1, keepdims=True) + norm_epsilon)


def forward_end(last, core_ref, keep_ref, took_ref, moving_ref, got_ref, state_ref, after_ref, *rest):
    state = state_ref[...].astype(f32) + ring_total(core_ref, keep_ref, took_ref, moving_ref, got_ref) + after_ref[...]
    if last:
        rest[0][...] = state.astype(bf16)
        return
    gain_ref, shift_ref, state_out, normed_ref = rest
    state_out[...] = state
    centred, inverse = centred_rows(state)
    normed_ref[...] = (centred * inverse * gain_ref[...] + shift_ref[...]).astype(bf16)


def backward_end(core_ref, keep_ref, took_ref, moving_ref, got_ref, state_ref, grad_ref, gain_ref, *rest):
    grad_out, low_ref = rest[-2:]
    grad_normed = ring_total(core_ref, keep_ref, took_ref, moving_ref, got_ref)
    centred, inverse = centred_rows(state_ref[...].astype(f32))
    xhat = centred * inverse
    before = grad_ref[...].astype(f32)
    scaled = grad_normed * gain_ref[...]
    after = before + (
        scaled - jnp.mean(scaled, axis=1, keepdims=True) - xhat * jnp.mean(scaled * xhat, axis=1, keepdims=True)
    ) * inverse
    grad_out[...] = after
    low_ref[...] = after.astype(bf16)


def call_end(body, core, ring, extra, shapes, name):
    keep, took, moving, got, n_sum = ring
    _, half, width = got.shape

    def rows_of(array):
        n = array.shape[0] // half - 1
        return pl.BlockSpec((half, width), lambda i: (n, 0))

    def whole_of(array):
        return pl.BlockSpec(array.shape, lambda i: (0,) * len(array.shape))

    def one_of(array):
        return pl.BlockSpec((None,) + array.shape[1:], lambda i: (n_sum, 0, 0))

    return pl.pallas_call(
        body,
        grid=(1,),
        in_specs=[SMEM_SPEC, rows_of(keep), rows_of(took), one_of(moving), one_of(got)] + [whole_of(x) for x in extra],
        out_specs=[whole_of(x) for x in shapes],
        out_shape=shapes,
        name=name,
    )(core, keep, took, moving, got, *extra)


def per_device(
    n_dp,
    hidden_in,
    seq_lengths,
    seq_device,
    positions,
    norm_gain,
    norm_bias,
    qkv_weight,
    qkv_bias,
    out_weight,
    fc1_weight,
    fc1_bias,
    fc2_weight,
    output_bias,
    out_cotangent,
):
    block = hidden_in.shape[0]
    half = block // 2
    width = hidden_in.shape[1]
    piece = norm_gain.shape[1]
    hidden = fc1_weight.shape[2] // GROUP
    groups = n_dp // GROUP
    chips = GROUP // 2
    side = chips // 2 - 1

    if groups == 1:
        ring = [2 * a for a in range(chips // 2)] + [2 * a + 1 for a in reversed(range(chips // 2))]
    else:
        ring = list(range(chips // 2)) + list(reversed(range(chips // 2, chips)))
    ring_pairs = []
    for g in range(groups):
        for place in range(chips):
            for core, step in ((0, 1), (1, -1)):
                ring_pairs.append(
                    (
                        g * GROUP + ring[place] * 2 + core,
                        g * GROUP + ring[(place + step) % chips] * 2 + core,
                    )
                )
    core_pairs = [(i, i ^ 1) for i in range(n_dp)]
    inner = [[g * GROUP + i for i in range(GROUP)] for g in range(groups)]
    outer = [[g * GROUP + i for g in range(groups)] for i in range(GROUP)]
    if groups == 1:
        inner = None

    def along(x):
        return lax.ppermute(x, "dp", ring_pairs)

    def across(x):
        return lax.ppermute(x, "dp", core_pairs)

    def over(x):
        return lax.ppermute(x, "tensor", [(0, 1), (1, 0)])

    index = lax.axis_index("dp")
    group = index // GROUP
    chip = (index % GROUP) // 2
    core = index % 2
    tensor = lax.axis_index("tensor")
    is_first = core == 0
    at = core * half
    off = (1 - core) * half
    core_word = core.astype(jnp.int32).reshape(1)

    def my_half(x, start, axis=0):
        return lax.dynamic_slice_in_dim(x, start, half, axis)

    def in_order(own, other):
        return jnp.where(
            is_first, jnp.concatenate([own, other], 0), jnp.concatenate([other, own], 0)
        )

    def gather_rows(mine, needed={}):
        behind, ahead = [], []
        moving = mine
        for step in range(side):
            moving = along(after(moving, *needed.get(step, ())))
            behind.append(moving)
            ahead.append(across(moving))
        far = along(after(my_half(moving, at, moving.ndim - 2), *needed.get(side, ())))
        return [mine] + behind + ahead + [far, across(far)]

    rows = lax.broadcasted_iota(jnp.int32, (block, 1), 0)
    mine_rows = (rows < half) == is_first

    def ring_sum(*sets, needed={}):
        took_far = [across(give_far) for give_far, _, _ in sets]
        took = [across(give) for _, give, _ in sets]
        keep = [x for _, _, x in sets]
        far = [k[side * block : side * block + half].astype(f32) + t.astype(f32) for k, t in zip(keep, took_far)]
        moving = along(jnp.stack(far).astype(bf16))
        for step in reversed(range(side)):
            here = slice(step * block, (step + 1) * block)
            added = [k[here].astype(f32) + t[here].astype(f32) for k, t in zip(keep, took)]
            arrived = after(moving, *needed.get(step, ())).astype(f32)
            if step == side - 1:
                arrived = jnp.where(mine_rows, jnp.concatenate([arrived, arrived], 1), 0)
            moving = along((arrived + jnp.stack(added)).astype(bf16))
        got = across(my_half(moving, off, 1))
        return [(k, t, moving, got, n) for n, (k, t) in enumerate(zip(keep, took))]

    def spread(x):
        return lax.all_to_all(x, "dp", 0, 0, axis_index_groups=inner, tiled=True)

    small = jnp.concatenate(
        [
            norm_gain.reshape(-1),
            norm_bias.reshape(-1),
            output_bias.reshape(-1),
            (positions // 64).astype(bf16),
            (positions % 64).astype(bf16),
        ]
    )
    weights = []
    if groups == 1:
        qkv_turned = qkv_weight.transpose(0, 2, 1, 3)
        ups, downs = (qkv_turned, fc1_weight), (out_weight, fc2_weight)
        extra = jnp.concatenate([small, jnp.zeros_like(small)]).reshape(-1, 128)
        up = spread(call_pack(pack_first, 0, ups, (), (extra,)))
        small_all = up[:, UP_ROWS:].reshape(GROUP, -1)[:, : small.shape[0]]
        up_other = over(up)
        packed_down = call_pack(pack_down, 0, (), downs, ())
        down = spread(after(packed_down, up))
        down_other = over(down)
        weights.append(call_join(join_up, up, [up_other], True, False) + call_join(join_down, down, [down_other], False, True))
        packed_last = call_pack(pack_both, 1, ups, downs, ())
        firsts = (up, up_other, down)
    else:
        small_all = lax.all_gather(small, "dp", axis=0, tiled=False)
        for layer in range(LAYERS):
            up = jnp.concatenate(
                [
                    qkv_weight[layer].reshape(piece, 3, GROUP, HEAD_DIM).transpose(2, 0, 1, 3).reshape(GROUP, piece, -1),
                    fc1_weight[layer].reshape(piece, GROUP, hidden).transpose(1, 0, 2),
                ],
                axis=2,
            )
            up = lax.all_gather(spread(up), "dp", axis=0, axis_index_groups=outer, tiled=True)
            up = up.reshape(width // 128, 128, UP_ROWS)
            value = up[:, :, WIDE : WIDE + HEAD_DIM]
            first = WIDE + HEAD_DIM
            up = jnp.concatenate(
                [
                    up[:, :, :WIDE],
                    jnp.concatenate([value[:, :HEAD_DIM], value[:, HEAD_DIM:]], axis=2),
                    up[:, :, first : first + 128],
                    up[:, :, first + 128 :],
                ],
                axis=1,
            )
            down = jnp.concatenate(
                [out_weight[layer].reshape(GROUP, HEAD_DIM, piece), fc2_weight[layer].reshape(GROUP, hidden, piece)],
                axis=1,
            )
            down = lax.all_gather(spread(down), "dp", axis=0, axis_index_groups=outer, tiled=True)
            down = down.transpose(1, 0, 2).reshape(-1, width // 128, 128).transpose(1, 0, 2)
            weights.append(call_join(join_up, up, [over(up)], True, False) + call_join(join_down, down, [over(down)], False, True))
    if groups == 1:
        biases = jnp.concatenate([qkv_bias.reshape(LAYERS, 3 * HEAD_DIM), fc1_bias], axis=1)
    else:
        full_qkv = lax.all_gather(qkv_bias, "dp", axis=2, tiled=True)
        full_up = lax.all_gather(fc1_bias, "dp", axis=1, tiled=True)
        member = index % GROUP
        biases = jnp.concatenate(
            [
                lax.dynamic_slice_in_dim(full_qkv, member * HEAD_DIM, HEAD_DIM, 2).reshape(LAYERS, 3 * HEAD_DIM),
                lax.dynamic_slice_in_dim(full_up, member * hidden, hidden, 1),
            ],
            axis=1,
        )
    biases_other = over(biases)
    both_biases = jnp.stack([biases, biases_other], axis=1).astype(f32)
    bias_rows = jnp.concatenate(
        [
            both_biases[:, :, : 3 * HEAD_DIM].reshape(LAYERS, 2, 3, HEAD_DIM).transpose(0, 2, 1, 3).reshape(LAYERS, -1),
            both_biases[:, :, 3 * HEAD_DIM :].reshape(LAYERS, -1),
        ],
        axis=1,
    )
    vectors = small_all[:, : 6 * piece].reshape(n_dp, 3, LAYERS, piece).transpose(1, 2, 0, 3).reshape(3, LAYERS, 1, width).astype(f32)
    gains, shifts, added_bias = vectors[0], vectors[1], vectors[2]

    turned = jnp.where(is_first, 1, -1)
    place = jnp.sum(jnp.where(jnp.asarray(ring) == chip, jnp.arange(chips), 0))
    offsets = [0] + [-(s + 1) for s in range(side)] + [s + 1 for s in range(side)] + [chips // 2]
    places = (place + turned * jnp.asarray(offsets)) % chips
    chip_ids = jnp.sum(
        jnp.where(places[:, None] == jnp.arange(chips)[None, :], jnp.asarray(ring)[None, :], 0), axis=1
    )
    owners = group * GROUP + 2 * chip_ids + tensor
    labels = jax.vmap(lambda owner: sequence_labels(seq_lengths, seq_device, owner, block))(owners)
    rows_at = jnp.arange(block, dtype=jnp.int32)
    allowed = (
        (labels[:, :, None] == labels[:, None, :])
        & (labels[:, :, None] > 0)
        & (rows_at[None, None, :] <= rows_at[None, :, None])
    ) | (rows_at[None, None, :] == rows_at[None, :, None])
    allowed = allowed.astype(f32).reshape(chips * block, block)
    picked = (owners[:, None] == jnp.arange(n_dp)[None, :]).astype(f32)
    place_parts = jnp.dot(picked, small_all[:, 6 * piece :].astype(f32), precision=lax.Precision.HIGHEST)
    row_places = (place_parts[:, :block] * 64.0 + place_parts[:, block:]).reshape(chips * block)
    pair = ROT // 2
    frequency = 10000.0 ** (-2.0 * jnp.arange(pair, dtype=f32) / ROT)
    angles = row_places[:, None] * frequency[None, :]
    cosine, sine = jnp.cos(angles), jnp.sin(angles)
    nought = jnp.zeros_like(sine)
    rest = jnp.zeros((chips * block, HEAD_DIM - ROT), f32)
    tables = (
        jnp.concatenate([cosine, cosine, rest + 1.0] * 2, axis=1),
        jnp.concatenate([-sine, nought, rest] * 2, axis=1),
        jnp.concatenate([nought, sine, rest] * 2, axis=1),
    )

    both = jnp.stack([hidden_in, out_cotangent])
    both = jnp.where(tensor == core, both, across(both))
    keeps = jnp.stack([jnp.ones_like(labels[0]), (labels[0] > 0).astype(labels.dtype)]).astype(bf16)
    both = both * keeps[:, :, None]
    if groups == 1:
        inputs = gather_rows(
            after(both, packed_down, packed_last, firsts[0], firsts[2]),
            {1: (firsts[1], tables[0]), 2: (tables[1], tables[2], allowed), side: (down_other, weights[0][0])},
        )
        slab = spread(after(packed_last, inputs[-2]))
        others = tuple(over(slab[n * GROUP // 2 : (n + 1) * GROUP // 2]) for n in range(2))
        weights.append(call_join(join_halves, slab, others, True, True))
        slabs = (slab,)
    else:
        inputs = gather_rows(both)
        slabs, others = (), ()
    mine_inputs = my_half(both, at, 1)
    state, grad_state = mine_inputs[0], mine_inputs[1]

    normed, heads, hidden_pre, wide, *parts = call_pass(
        "first", core_word, weights[0], tables, allowed, [bias_rows[0:1], gains[0], shifts[0]], inputs
    )
    rows_shape = (half, width)
    next_state, normed_own = call_end(
        partial(forward_end, False),
        core_word,
        ring_sum((after(parts[0], *slabs), parts[1], parts[2]), needed={1: others[:1]})[0],
        [state, added_bias[0], gains[1], shifts[1]],
        [jax.ShapeDtypeStruct(rows_shape, f32), jax.ShapeDtypeStruct(rows_shape, bf16)],
        "forward_end",
    )
    normed_chunks = gather_rows(in_order(normed_own, across(normed_own)), {1: others[1:]})

    def handed_back(own_rows):
        filled = in_order(own_rows, across(own_rows))
        return jnp.where(tensor == core, filled, over(filled))

    def summed(own, other, *earlier):
        total = own.astype(f32) + other.astype(f32)
        if groups > 1:
            total = total.transpose(1, 0, 2).reshape(total.shape[1], width)
            total = lax.psum_scatter(total, "dp", scatter_dimension=1, axis_index_groups=outer, tiled=True)
            total = total.reshape(total.shape[0], GROUP, piece).transpose(1, 0, 2)
        return spread(after(total.astype(bf16), *earlier))

    down_own = [(0, HEAD_DIM), (WIDE, WIDE + hidden)]
    down_other = [(HEAD_DIM, WIDE), (WIDE + hidden, WIDE + 2 * hidden)]
    up_own = [(p * WIDE, p * WIDE + HEAD_DIM) for p in range(3)] + [(3 * WIDE, 3 * WIDE + hidden)]
    up_other = [(p * WIDE + HEAD_DIM, (p + 1) * WIDE) for p in range(3)] + [(3 * WIDE + hidden, 3 * WIDE + 2 * hidden)]

    def down_gradients(wide_rows, grad_rows):
        return call_gradients(core_word, wide_rows, grad_rows, down_own, down_other, [], "down_gradients")

    def up_gradients(slim_rows, normed_rows, sums):
        return call_gradients(core_word, slim_rows, [normed_rows], up_own, up_other, [sums], "up_gradients")

    def backward_finish(ring_end, state, grad_state, layer, *needed):
        return call_end(
            backward_end,
            core_word,
            ring_end,
            [state, grad_state, gains[layer], *needed],
            [jax.ShapeDtypeStruct(rows_shape, f32), jax.ShapeDtypeStruct(rows_shape, bf16)],
            "backward_end",
        )

    normed_last, grad_rows, wide_last, slim, sums, *parts = call_pass(
        "middle", core_word, weights[1], tables, allowed, [bias_rows[1:2]], normed_chunks + inputs
    )
    out_parts = parts[:3]
    down_pair = down_gradients(wide_last, [grad_rows])
    *up_pair, bias_last = up_gradients(slim, normed_last, sums)
    down_sent, up_sent = over(down_pair[1]), over(up_pair[1])
    grad_end, out_end = ring_sum(parts[3:], out_parts, needed={1: (down_pair[0],), 0: (up_pair[0],)})
    grad_state, grad_low = backward_finish(grad_end, next_state, grad_state, 1)
    (hidden_out,) = call_end(
        partial(forward_end, True),
        core_word,
        out_end,
        [next_state, added_bias[1]],
        [jax.ShapeDtypeStruct(rows_shape, bf16)],
        "forward_out",
    )
    hidden_out = handed_back(hidden_out)
    down_last = summed(down_pair[0], after(down_sent, grad_low))
    grad_chunks = gather_rows(in_order(grad_low, across(grad_low)), {0: (down_sent,), 2: (up_sent,), side: (down_last, hidden_out)})
    up_last = summed(up_pair[0], after(up_sent, grad_chunks[-2]), down_last)

    down_pair = down_gradients(wide, grad_chunks)
    down_sent = over(down_pair[1])
    grad_rows, slim, sums, *parts = call_pass(
        "last", core_word, weights[0], tables, allowed, [heads, after(hidden_pre, down_pair[0]), normed], grad_chunks
    )
    down_first = summed(down_pair[0], after(down_sent, slim), up_last)
    *up_pair, bias_first = up_gradients(slim, after(normed, up_last), sums)
    up_sent = over(up_pair[1])
    (grad_end,) = ring_sum((after(parts[0], up_pair[0]), parts[1], parts[2]), needed={1: (down_first,), 0: (up_sent,)})
    up_first = summed(up_pair[0], up_sent, down_first, grad_end[2])
    sums = jnp.concatenate([bias_first, bias_last], axis=0)
    sums_qkv = sums[:, : 3 * WIDE].reshape(LAYERS, 3, 2, HEAD_DIM)
    sums_up = sums[:, 3 * WIDE :].reshape(LAYERS, 2, hidden)
    bias_own, bias_other = (
        jnp.concatenate([sums_qkv[:, :, n].reshape(LAYERS, -1), sums_up[:, n]], axis=1) for n in range(2)
    )
    bias_sent = over(bias_other)
    needed = [bias_sent]
    if groups == 1:
        *filled, mark = call_spread(up_last, down_last, 1, [])
        needed.append(mark)
    _, grad_low = backward_finish(grad_end, state, grad_state, 0, *needed)
    grad_hidden = handed_back(grad_low).astype(f32)

    ends = jnp.stack([jnp.sum(x[:, UP_ROWS : UP_ROWS + 3].astype(f32), axis=0) for x in (up_first, up_last)])
    shift_grads = ends[:, 0]
    gain_grads = (ends[:, 1] - norm_bias.astype(f32) * ends[:, 0]) / norm_gain.astype(f32)
    after_grads = ends[:, 2] / GROUP
    bias_sums = bias_own + bias_sent
    bias_qkv, bias_up = bias_sums[:, : 3 * HEAD_DIM].reshape(LAYERS, 3, HEAD_DIM), bias_sums[:, 3 * HEAD_DIM :]
    if groups == 1:
        grad_qkv, grad_out, grad_up, grad_down, _ = call_spread(up_first, down_first, 0, filled)
        grad_qkv = grad_qkv.transpose(0, 2, 1, 3)
    else:
        bias_qkv = lax.all_gather(lax.psum(bias_qkv, "dp", axis_index_groups=outer), "dp", axis=2, axis_index_groups=inner, tiled=True)
        bias_up = lax.all_gather(lax.psum(bias_up, "dp", axis_index_groups=outer), "dp", axis=1, axis_index_groups=inner, tiled=True)
        bias_qkv = lax.dynamic_slice_in_dim(bias_qkv, index * qkv_bias.shape[2], qkv_bias.shape[2], 2)
        bias_up = lax.dynamic_slice_in_dim(bias_up, index * fc1_bias.shape[1], fc1_bias.shape[1], 1)
        ups = jnp.stack([up_first, up_last]).astype(f32)
        downs = jnp.stack([down_first, down_last]).astype(f32)
        grad_qkv = ups[:, :, : 3 * HEAD_DIM].reshape(LAYERS, GROUP, 3, HEAD_DIM, piece).transpose(0, 4, 2, 1, 3).reshape(LAYERS, piece, 3, -1)
        grad_up = ups[:, :, 3 * HEAD_DIM : UP_ROWS].transpose(0, 3, 1, 2).reshape(LAYERS, piece, -1)
        grad_out = downs[:, :, :HEAD_DIM].reshape(LAYERS, -1, piece)
        grad_down = downs[:, :, HEAD_DIM:].reshape(LAYERS, -1, piece)
    return (
        hidden_out,
        grad_hidden,
        gain_grads,
        shift_grads,
        grad_qkv,
        bias_qkv,
        grad_out,
        grad_up,
        bias_up,
        grad_down,
        after_grads,
    )


def solution(mesh):
    placed = (
        P("dp", None),
        P(),
        P(),
        P("dp"),
        P(None, "dp"),
        P(None, "dp"),
        P(None, "dp", None, "tensor"),
        P(None, None, ("tensor", "dp")),
        P(None, "tensor", "dp"),
        P(None, "dp", "tensor"),
        P(None, ("tensor", "dp")),
        P(None, "tensor", "dp"),
        P(None, "dp"),
        P("dp", None),
    )
    return jax.shard_map(
        partial(per_device, mesh.shape["dp"]),
        mesh=mesh,
        in_specs=placed,
        out_specs=(
            P("dp", None),
            P("dp", None),
            P(None, "dp"),
            P(None, "dp"),
            P(None, "dp", None, "tensor"),
            P(None, None, ("tensor", "dp")),
            P(None, "tensor", "dp"),
            P(None, "dp", "tensor"),
            P(None, ("tensor", "dp")),
            P(None, "tensor", "dp"),
            P(None, "dp"),
        ),
        check_vma=False,
    )
```

```python
from functools import partial

import jax
import jax.numpy as jnp
from jax import lax
from jax.experimental import pallas as pl
from jax.experimental.pallas import tpu as pltpu
from jax.sharding import PartitionSpec as P

HEAD_DIM = 64
ROT = 32
LAYERS = 2
GROUP = 16

norm_epsilon = 1e-05
masked_score = -1e30
bf16 = jnp.bfloat16
f32 = jnp.float32

contract_last = (((1,), (1,)), ((), ()))
contract_first = (((0,), (0,)), ((), ()))


def dot(a, b, dims=(((1,), (0,)), ((), ()))):
    return lax.dot_general(a, b, dims, preferred_element_type=f32)


def turn(x, cosine, up, down):
    return x * cosine + pltpu.roll(x, x.shape[1] - ROT // 2, 1) * up + pltpu.roll(x, ROT // 2, 1) * down


def stacked_heads(x):
    lane = lax.broadcasted_iota(jnp.int32, x.shape, 1)
    zero = jnp.zeros_like(x)
    return jnp.concatenate(
        [jnp.where(lane < HEAD_DIM, x, zero), jnp.where(lane < HEAD_DIM, zero, x)], axis=0
    )


def merged_heads(x):
    rows = x.shape[0] // 2
    lane = lax.broadcasted_iota(jnp.int32, (rows, x.shape[1]), 1)
    return jnp.where(lane < HEAD_DIM, x[:rows], x[rows:])


def softmax_rows(queries, keys, allowed):
    scores = dot(stacked_heads(queries), keys, contract_last) * HEAD_DIM ** (-0.5)
    masked = jnp.where(jnp.concatenate([allowed, allowed], axis=0) > 0, scores, masked_score)
    weights = jnp.exp(masked - jnp.max(masked, axis=1, keepdims=True))
    return weights / jnp.sum(weights, axis=1, keepdims=True)


def sequence_labels(seq_lengths, seq_device, owner, count_rows):
    index = jnp.arange(seq_lengths.shape[0], dtype=jnp.int32)
    owned = jnp.where(seq_device == owner, seq_lengths, 0)
    earlier = index[None, :] < index[:, None]
    starts = jnp.sum(jnp.where(earlier, owned[None, :], 0), axis=1)
    places = jnp.arange(count_rows, dtype=jnp.int32)
    inside = (places[:, None] >= starts[None, :]) & (places[:, None] < (starts + owned)[None, :])
    return jnp.sum(jnp.where(inside, index[None, :] + 1, 0), axis=1)


def gelu_parts(v):
    c = (2.0 / jnp.pi) ** 0.5
    inner = jnp.tanh(c * (v + 0.044715 * v * v * v))
    value = 0.5 * v * (1.0 + inner)
    slope = 0.5 * (1.0 + inner) + 0.5 * v * (1.0 - inner * inner) * c * (1.0 + 3.0 * 0.044715 * v * v)
    return value, slope


VMEM_SPEC = pl.BlockSpec(memory_space=pltpu.VMEM)
ANY_SPEC = pl.BlockSpec(memory_space=pl.ANY)
SMEM_SPEC = pl.BlockSpec(memory_space=pltpu.SMEM)
WIDE = 2 * HEAD_DIM
UP_ROWS = 3 * HEAD_DIM + 256
DOWN_ROWS = HEAD_DIM + 256
SUM_ROWS = 16
MEMBERS = 4


def after(x, *others):
    if not others:
        return x
    return lax.optimization_barrier((x, *others))[0]


def left_lanes(x):
    return lax.broadcasted_iota(jnp.int32, x.shape, 1) < HEAD_DIM


def swapped(x):
    return pltpu.roll(x, HEAD_DIM, 1)


def zipped(a, b):
    left = left_lanes(a)
    return jnp.where(left, a, swapped(b)).astype(bf16), jnp.where(left, swapped(a), b).astype(bf16)


def pack_up(qkv_ref, fc1_ref, *rest):
    out_ref = rest[-1]
    for pair in range(MEMBERS // 2):
        lanes = slice(pair * 128, (pair + 1) * 128)
        q, k, v = (qkv_ref[0, p, :, lanes].astype(f32) for p in range(3))
        here, there = 2 * pair, 2 * pair + 1
        out_ref[here, :WIDE], out_ref[there, :WIDE] = zipped(q, k)
        rows = q.shape[0] // 2
        out_ref[here, WIDE : WIDE + rows], out_ref[there, WIDE : WIDE + rows] = zipped(v[:rows], v[rows:])
        base = WIDE + rows
        for d in (here, there):
            for h in range(2):
                out_ref[d, base + h * 128 : base + (h + 1) * 128] = fc1_ref[0, :, (2 * d + h) * 128 : (2 * d + h + 1) * 128]


def pack_first(qkv_ref, fc1_ref, small_ref, out_ref):
    pack_up(qkv_ref, fc1_ref, out_ref)
    for d in range(MEMBERS):
        out_ref[d, UP_ROWS:] = small_ref[...]


def pack_down(out_w_ref, fc2_ref, out_ref):
    for d in range(MEMBERS):
        out_ref[d, :HEAD_DIM] = out_w_ref[0, d * HEAD_DIM : (d + 1) * HEAD_DIM]
        out_ref[d, HEAD_DIM:] = fc2_ref[0, d * 256 : (d + 1) * 256]


def call_pack(body, layer, ups, downs, small):
    rows, specs = 0, []
    if ups:
        rows += UP_ROWS
        specs += [
            pl.BlockSpec((1, 3, 128, MEMBERS * HEAD_DIM), lambda i: (layer, 0, 0, i)),
            pl.BlockSpec((1, 128, MEMBERS * 256), lambda i: (layer, 0, i)),
        ]
    if downs:
        rows += DOWN_ROWS
        specs += [
            pl.BlockSpec((1, MEMBERS * HEAD_DIM, 128), lambda i: (layer, i, 0)),
            pl.BlockSpec((1, MEMBERS * 256, 128), lambda i: (layer, i, 0)),
        ]
    if small:
        rows += small[0].shape[0]
        specs.append(pl.BlockSpec(small[0].shape, lambda i: (0, 0)))
    return pl.pallas_call(
        body,
        grid=(GROUP // MEMBERS,),
        in_specs=specs,
        out_specs=pl.BlockSpec((MEMBERS, rows, 128), lambda i: (i, 0, 0)),
        out_shape=jax.ShapeDtypeStruct((GROUP, rows, 128), bf16),
        cost_estimate=pl.CostEstimate(flops=0, bytes_accessed=GROUP * rows * 128 * 8, transcendentals=0),
        name=body.__name__,
    )(*ups, *downs, *small)


def join_up(own_ref, other_ref, out_ref):
    for e in range(MEMBERS):
        rows = slice(e * 128, (e + 1) * 128)
        a, b = own_ref[e, :WIDE].astype(f32), other_ref[e, :WIDE].astype(f32)
        out_ref[rows, :WIDE], out_ref[rows, WIDE : 2 * WIDE] = zipped(a, b)
        a, b = own_ref[e, WIDE : WIDE + 64].astype(f32), other_ref[e, WIDE : WIDE + 64].astype(f32)
        top, bottom = zipped(a, b)
        out_ref[e * 128 : e * 128 + 64, 2 * WIDE : 3 * WIDE] = top
        out_ref[e * 128 + 64 : (e + 1) * 128, 2 * WIDE : 3 * WIDE] = bottom
        for n, ref in enumerate((own_ref, other_ref)):
            for h in range(2):
                lanes = 3 * WIDE + n * 256 + h * 128
                out_ref[rows, lanes : lanes + 128] = ref[e, WIDE + 64 + h * 128 : WIDE + 64 + (h + 1) * 128]


def join_down(own_ref, other_ref, out_ref):
    base = own_ref.shape[1] - DOWN_ROWS
    for e in range(MEMBERS):
        lanes = slice(e * 128, (e + 1) * 128)
        for n, ref in enumerate((own_ref, other_ref)):
            out_ref[n * HEAD_DIM : (n + 1) * HEAD_DIM, lanes] = ref[e, base : base + HEAD_DIM]
            out_ref[WIDE + n * 256 : WIDE + (n + 1) * 256, lanes] = ref[e, base + HEAD_DIM :]


def call_join(body, own, others, ups, downs):
    rows = own.shape[1]
    spec = pl.BlockSpec((MEMBERS, rows, 128), lambda i: (i, 0, 0))
    specs, shapes = [], []
    if ups:
        specs.append(pl.BlockSpec((MEMBERS * 128, 2 * UP_ROWS), lambda i: (i, 0)))
        shapes.append(jax.ShapeDtypeStruct((GROUP * 128, 2 * UP_ROWS), bf16))
    if downs:
        specs.append(pl.BlockSpec((2 * DOWN_ROWS, MEMBERS * 128), lambda i: (0, i)))
        shapes.append(jax.ShapeDtypeStruct((2 * DOWN_ROWS, GROUP * 128), bf16))
    return pl.pallas_call(
        body,
        grid=(GROUP // MEMBERS,),
        in_specs=[spec] * (1 + len(others)),
        out_specs=specs,
        out_shape=shapes,
        cost_estimate=pl.CostEstimate(flops=0, bytes_accessed=GROUP * rows * 128 * 12, transcendentals=0),
        name=body.__name__,
    )(own, *others)


def slot_copies(refs, which, target, core):
    block = target.shape[0] // 8
    half = block // 2
    pairs = []
    for slot in range(7):
        ref = refs[slot] if which is None else refs[slot].at[which]
        pairs.append((ref, target.at[pl.ds(slot * block, block)]))
    for n, at in ((7, core * half), (8, (1 - core) * half)):
        ref = refs[n] if which is None else refs[n].at[which]
        pairs.append((ref, target.at[pl.ds(pl.multiple_of(7 * block + at, half), half)]))
    return pairs


def split_copies(part, far_ref, give_ref, keep_ref, core):
    block = part.shape[0] // 8
    half = block // 2
    at, off = core * half, (1 - core) * half

    def rows(slot, start):
        return part.at[pl.ds(pl.multiple_of(slot * block + start, half), half)]

    return [
        (rows(7, off), far_ref),
        (part.at[pl.ds(block, 3 * block)], give_ref.at[pl.ds(0, 3 * block)]),
        (rows(0, off), give_ref.at[pl.ds(3 * block, half)]),
        (part.at[pl.ds(4 * block, 3 * block)], keep_ref.at[pl.ds(0, 3 * block)]),
        (rows(7, at), keep_ref.at[pl.ds(3 * block, half)]),
        (rows(0, at), keep_ref.at[pl.ds(3 * block + half, half)]),
    ]


def run_copies(pairs, sems, first):
    made = [pltpu.make_async_copy(a, b, sems.at[first + n]) for n, (a, b) in enumerate(pairs)]
    for copy in made:
        copy.start()
    return made


def heads_forward(chances, values):
    return merged_heads(dot(chances.astype(bf16), values)).astype(bf16)


def heads_backward(chances, queries, keys, values, grad, tables):
    grads = stacked_heads(grad)
    grad_chances = dot(grads, values, contract_last)
    grad_values = dot(chances.astype(bf16), grads, contract_first)
    centre = jnp.sum(grad_chances * chances, axis=1, keepdims=True)
    grad_scores = (chances * (grad_chances - centre)).astype(bf16)
    scale = HEAD_DIM ** (-0.5)
    grad_queries = merged_heads(dot(grad_scores, keys)) * scale
    grad_keys = dot(grad_scores, stacked_heads(queries), contract_first) * scale
    cosine, up, down = tables
    back = (cosine, -up, -down)
    return turn(grad_queries, *back).astype(bf16), turn(grad_keys, *back).astype(bf16), grad_values.astype(bf16)


def layer_pass(mode, *refs):
    refs = list(refs)

    def take(n):
        out = refs[:n]
        del refs[:n]
        return out

    forward, backward = mode != "last", mode != "first"
    core_ref, up_ref, down_ref, cos_ref, sin_up_ref, sin_down_ref, allowed_ref = take(7)
    core = core_ref[0]
    if mode == "first":
        bias_ref, gain_ref, shift_ref = take(3)
        rows_in = take(9)
    elif mode == "middle":
        (bias_ref,) = take(1)
        rows_in = take(9)
        grads_in = take(9)
    else:
        heads_ref, hidden_ref, normed_ref = take(3)
        grads_in = take(9)
    if mode == "first":
        normed_ref, heads_ref, hidden_ref, wide_ref = take(4)
        outs = take(3)
        raw, part, sems = take(3)
    elif mode == "middle":
        normed_ref, grad_rows_ref, wide_ref, slim_ref, sums_ref = take(5)
        outs = take(3)
        grad_outs = take(3)
        part, grad_part, sems = take(3)
    else:
        grad_rows_ref, slim_ref, sums_ref = take(3)
        grad_outs = take(3)
        grad_part, sems = take(2)

    pairs = []
    if mode == "first":
        pairs += slot_copies(rows_in, 0, raw, core)
    if mode == "middle":
        pairs += slot_copies(rows_in, None, normed_ref, core)
        pairs += slot_copies(grads_in, 1, grad_rows_ref, core)
    if mode == "last":
        pairs += slot_copies(grads_in, None, grad_rows_ref, core)
    for copy in run_copies(pairs, sems, 0):
        copy.wait()

    total = allowed_ref.shape[0]
    block = allowed_ref.shape[1]
    step = 2 * block

    if mode == "first":
        tile = 32

        def norm_tile(i, carry):
            at = pl.ds(pl.multiple_of(i * tile, tile), tile)
            x = raw[at, :].astype(f32)
            centred = x - jnp.mean(x, axis=1, keepdims=True)
            inverse = lax.rsqrt(jnp.mean(centred * centred, axis=1, keepdims=True) + norm_epsilon)
            normed_ref[at, :] = (centred * inverse * gain_ref[...] + shift_ref[...]).astype(bf16)
            return carry

        lax.fori_loop(0, total // tile, norm_tile, 0)

    if backward:
        sums_ref[...] = jnp.zeros_like(sums_ref)

    def one(p, carry):
        at = pl.ds(pl.multiple_of(p * step, step), step)
        if forward:
            before = dot(normed_ref[at, :], up_ref[...]) + bias_ref[...]
            hidden_pre = before[:, 3 * WIDE :]
        else:
            hidden_pre = hidden_ref[at, :]
        value, slope = gelu_parts(hidden_pre)
        if backward:
            grad_wide = dot(grad_rows_ref[at, :], down_ref[...], contract_last)
            slim_ref[at, 3 * WIDE :] = (grad_wide[:, WIDE:] * slope).astype(bf16)
        if forward:
            wide_ref[at, WIDE:] = value.astype(bf16)
        if mode == "first":
            hidden_ref[at, :] = hidden_pre
        for b in range(2):
            mine = slice(b * block, (b + 1) * block)
            own = pl.ds(pl.multiple_of(p * step + b * block, block), block)
            tables = (cos_ref[own, :], sin_up_ref[own, :], sin_down_ref[own, :])
            if forward:
                queries = turn(before[mine, :WIDE], *tables).astype(bf16)
                keys = turn(before[mine, WIDE : 2 * WIDE], *tables).astype(bf16)
                values = before[mine, 2 * WIDE : 3 * WIDE].astype(bf16)
            else:
                queries = heads_ref[own, :WIDE]
                keys = heads_ref[own, WIDE : 2 * WIDE]
                values = heads_ref[own, 2 * WIDE :]
            if mode == "first":
                heads_ref[own, :WIDE] = queries
                heads_ref[own, WIDE : 2 * WIDE] = keys
                heads_ref[own, 2 * WIDE :] = values
            chances = softmax_rows(queries, keys, allowed_ref[own, :])
            if forward:
                wide_ref[own, :WIDE] = heads_forward(chances, values)
            if backward:
                grads = heads_backward(
                    chances, queries, keys, values, grad_wide[mine, :WIDE].astype(bf16), tables
                )
                for n in range(3):
                    slim_ref[own, n * WIDE : (n + 1) * WIDE] = grads[n]
        if forward:
            part[at, :] = dot(wide_ref[at, :], down_ref[...]).astype(bf16)
        if backward:
            grad_normed = dot(slim_ref[at, :], up_ref[...], contract_last)
            grad_part[at, :] = grad_normed.astype(bf16)
            for n, rows in enumerate(
                (grad_normed, grad_normed * normed_ref[at, :].astype(f32), grad_rows_ref[at, :].astype(f32))
            ):
                sums_ref[n : n + 1] += jnp.sum(rows, axis=0, keepdims=True)
        return carry

    lax.fori_loop(0, total // step, one, 0)
    pairs = []
    if backward:
        pairs += split_copies(grad_part, *grad_outs, core)
    if forward:
        pairs += split_copies(part, *outs, core)
    for copy in run_copies(pairs, sems, 0):
        copy.wait()


def call_pass(mode, core, weights, tables, allowed, extra, chunks):
    total, block = allowed.shape
    half = block // 2
    width = weights[0].shape[0]
    slim = weights[0].shape[1]
    wide = weights[1].shape[0]
    parts = [
        jax.ShapeDtypeStruct((half, width), bf16),
        jax.ShapeDtypeStruct((3 * block + half, width), bf16),
        jax.ShapeDtypeStruct((4 * block, width), bf16),
    ]
    full = jax.ShapeDtypeStruct((total, width), bf16)
    sums = jax.ShapeDtypeStruct((SUM_ROWS, width), f32)
    slim_rows = jax.ShapeDtypeStruct((total, slim), bf16)
    wide_rows = jax.ShapeDtypeStruct((total, wide), bf16)
    if mode == "first":
        kept = [
            full,
            jax.ShapeDtypeStruct((total, 3 * WIDE), bf16),
            jax.ShapeDtypeStruct((total, slim - 3 * WIDE), f32),
            wide_rows,
        ]
        buffers = 2
    elif mode == "middle":
        kept = [full, full, wide_rows, slim_rows, sums]
        parts = parts * 2
        buffers = 2
    else:
        kept = [full, slim_rows, sums]
        buffers = 1
    passes = 2 if mode == "middle" else 1
    return pl.pallas_call(
        partial(layer_pass, mode),
        in_specs=[SMEM_SPEC] + [VMEM_SPEC] * (6 + len(extra)) + [ANY_SPEC] * len(chunks),
        out_specs=[VMEM_SPEC] * len(kept) + [ANY_SPEC] * len(parts),
        out_shape=kept + parts,
        scratch_shapes=[pltpu.VMEM((total, width), bf16)] * buffers + [pltpu.SemaphoreType.DMA((18,))],
        cost_estimate=pl.CostEstimate(
            flops=6 * total * width * (slim + wide) * passes,
            bytes_accessed=20_000_000 * passes,
            transcendentals=total * slim,
        ),
        name="pass_" + mode,
    )(core, *weights, *tables, allowed, *extra, *chunks)


def gradient_slabs(own_rows, other_rows, with_sums, pieces_in, core_ref, left_ref, *rest):
    right_refs, rest = rest[:pieces_in], rest[pieces_in:]
    if with_sums:
        sums_ref, *rest = rest
    own_ref, other_ref, *rest = rest
    turned_ref = rest[-1]
    if pieces_in == 1:
        right = right_refs[0][...]
    else:
        a, b = right_refs[-2][...], right_refs[-1][...]
        first = jnp.full(a.shape, core_ref[0]) == 0
        halves = [jnp.where(first, a, b), jnp.where(first, b, a)]
        right = jnp.concatenate([ref[...] for ref in right_refs[:-2]] + halves, axis=0)

    @pl.when(pl.program_id(0) == 0)
    def _():
        width = left_ref.shape[1]
        for n in range(width // 128):
            lanes = slice(n * 128, (n + 1) * 128)
            left = left_ref[:, lanes].astype(f32)
            if with_sums:
                rest[0][:, lanes] = jnp.sum(left, axis=0, keepdims=True)
            turned_ref[lanes, :] = left.T.astype(bf16)

    product = dot(turned_ref[...], right).astype(bf16)
    for ref, pieces in ((own_ref, own_rows), (other_ref, other_rows)):
        place = 0
        for first, last in pieces:
            for e in range(2):
                ref[e, place : place + last - first] = product[first:last, e * 128 : (e + 1) * 128]
            place += last - first
        if with_sums:
            for e in range(2):
                ref[e, place:] = sums_ref[:, e * 128 : (e + 1) * 128].astype(bf16)


def call_gradients(core, left, right, own_rows, other_rows, sums, name):
    total, height = left.shape
    width = right[0].shape[1]
    with_sums = len(sums) > 0
    rows = height // 2 + (SUM_ROWS if with_sums else 0)
    slab = pl.BlockSpec((2, rows, 128), lambda i: (i, 0, 0))
    shape = jax.ShapeDtypeStruct((width // 128, rows, 128), bf16)
    out_specs, out_shape = [slab, slab], [shape, shape]
    if with_sums:
        out_specs.append(pl.BlockSpec((1, height), lambda i: (0, 0)))
        out_shape.append(jax.ShapeDtypeStruct((1, height), f32))
    return pl.pallas_call(
        partial(gradient_slabs, own_rows, other_rows, with_sums, len(right)),
        grid=(width // 256,),
        in_specs=[SMEM_SPEC, pl.BlockSpec((total, height), lambda i: (0, 0))]
        + [pl.BlockSpec((x.shape[0], 256), lambda i: (0, i)) for x in (*right, *sums)],
        out_specs=out_specs,
        out_shape=out_shape,
        scratch_shapes=[pltpu.VMEM((height, total), bf16)],
        cost_estimate=pl.CostEstimate(
            flops=4 * total * height * width, bytes_accessed=2 * (total * (width + height) + 2 * height * width), transcendentals=0
        ),
        name=name,
    )(core, left, *right, *sums)


def spread_gradients(up_ref, down_ref, *rest):
    qkv_ref, out_w_ref, fc1_ref, fc2_ref, mark_ref = rest[-5:]
    mark_ref[...] = jnp.zeros_like(mark_ref)
    for p in range(3):
        rows = slice(p * HEAD_DIM, (p + 1) * HEAD_DIM)
        both = jnp.concatenate([up_ref[0, rows].astype(f32), up_ref[1, rows].astype(f32)], axis=0)
        qkv_ref[0, p] = both.T
    base = 3 * HEAD_DIM
    for d in range(2):
        for h in range(2):
            fc1_ref[0, :, (2 * d + h) * 128 : (2 * d + h + 1) * 128] = (
                up_ref[d, base + h * 128 : base + (h + 1) * 128].astype(f32).T
            )
        out_w_ref[0, d * HEAD_DIM : (d + 1) * HEAD_DIM] = down_ref[d, :HEAD_DIM].astype(f32)
        fc2_ref[0, d * 256 : (d + 1) * 256] = down_ref[d, HEAD_DIM:].astype(f32)


def call_spread(up, down, layer, filled):
    shapes = [
        jax.ShapeDtypeStruct((LAYERS, 3, 128, GROUP * HEAD_DIM), f32),
        jax.ShapeDtypeStruct((LAYERS, GROUP * HEAD_DIM, 128), f32),
        jax.ShapeDtypeStruct((LAYERS, 128, GROUP * 256), f32),
        jax.ShapeDtypeStruct((LAYERS, GROUP * 256, 128), f32),
        jax.ShapeDtypeStruct((8, 128), f32),
    ]
    return pl.pallas_call(
        spread_gradients,
        grid=(GROUP // 2,),
        in_specs=[
            pl.BlockSpec((2, up.shape[1], 128), lambda i: (i, 0, 0)),
            pl.BlockSpec((2, down.shape[1], 128), lambda i: (i, 0, 0)),
        ]
        + [ANY_SPEC] * len(filled),
        out_specs=[
            pl.BlockSpec((1, 3, 128, 128), lambda i: (layer, 0, 0, i)),
            pl.BlockSpec((1, 128, 128), lambda i: (layer, i, 0)),
            pl.BlockSpec((1, 128, 512), lambda i: (layer, 0, i)),
            pl.BlockSpec((1, 512, 128), lambda i: (layer, i, 0)),
            pl.BlockSpec((8, 128), lambda i: (0, 0)),
        ],
        out_shape=shapes,
        input_output_aliases={2 + n: n for n in range(len(filled))},
        name="spread_gradients",
    )(up, down, *filled)


def ring_total(core_ref, keep_ref, took_ref, moving_ref, got_ref):
    half = got_ref.shape[0]
    arrived = moving_ref[pl.ds(pl.multiple_of(core_ref[0] * half, half), half), :]
    return keep_ref[...].astype(f32) + took_ref[...].astype(f32) + arrived.astype(f32) + got_ref[...].astype(f32)


def centred_rows(state):
    centred = state - jnp.mean(state, axis=1, keepdims=True)
    return centred, lax.rsqrt(jnp.mean(centred * centred, axis=1, keepdims=True) + norm_epsilon)


def forward_end(last, core_ref, keep_ref, took_ref, moving_ref, got_ref, state_ref, after_ref, *rest):
    state = state_ref[...].astype(f32) + ring_total(core_ref, keep_ref, took_ref, moving_ref, got_ref) + after_ref[...]
    if last:
        rest[0][...] = state.astype(bf16)
        return
    gain_ref, shift_ref, state_out, normed_ref = rest
    state_out[...] = state
    centred, inverse = centred_rows(state)
    normed_ref[...] = (centred * inverse * gain_ref[...] + shift_ref[...]).astype(bf16)


def backward_end(core_ref, keep_ref, took_ref, moving_ref, got_ref, state_ref, grad_ref, gain_ref, *rest):
    grad_out, low_ref = rest[-2:]
    grad_normed = ring_total(core_ref, keep_ref, took_ref, moving_ref, got_ref)
    centred, inverse = centred_rows(state_ref[...].astype(f32))
    xhat = centred * inverse
    before = grad_ref[...].astype(f32)
    scaled = grad_normed * gain_ref[...]
    after = before + (
        scaled - jnp.mean(scaled, axis=1, keepdims=True) - xhat * jnp.mean(scaled * xhat, axis=1, keepdims=True)
    ) * inverse
    grad_out[...] = after
    low_ref[...] = after.astype(bf16)


def call_end(body, core, ring, extra, shapes, name):
    keep, took, moving, got, n_sum = ring
    _, half, width = got.shape

    def rows_of(array):
        n = array.shape[0] // half - 1
        return pl.BlockSpec((half, width), lambda i: (n, 0))

    def whole_of(array):
        return pl.BlockSpec(array.shape, lambda i: (0,) * len(array.shape))

    def one_of(array):
        return pl.BlockSpec((None,) + array.shape[1:], lambda i: (n_sum, 0, 0))

    return pl.pallas_call(
        body,
        grid=(1,),
        in_specs=[SMEM_SPEC, rows_of(keep), rows_of(took), one_of(moving), one_of(got)] + [whole_of(x) for x in extra],
        out_specs=[whole_of(x) for x in shapes],
        out_shape=shapes,
        name=name,
    )(core, keep, took, moving, got, *extra)


def per_device(
    n_dp,
    hidden_in,
    seq_lengths,
    seq_device,
    positions,
    norm_gain,
    norm_bias,
    qkv_weight,
    qkv_bias,
    out_weight,
    fc1_weight,
    fc1_bias,
    fc2_weight,
    output_bias,
    out_cotangent,
):
    block = hidden_in.shape[0]
    half = block // 2
    width = hidden_in.shape[1]
    piece = norm_gain.shape[1]
    hidden = fc1_weight.shape[2] // GROUP
    groups = n_dp // GROUP
    chips = GROUP // 2
    side = chips // 2 - 1

    if groups == 1:
        ring = [2 * a for a in range(chips // 2)] + [2 * a + 1 for a in reversed(range(chips // 2))]
    else:
        ring = list(range(chips // 2)) + list(reversed(range(chips // 2, chips)))
    ring_pairs = []
    for g in range(groups):
        for place in range(chips):
            for core, step in ((0, 1), (1, -1)):
                ring_pairs.append(
                    (
                        g * GROUP + ring[place] * 2 + core,
                        g * GROUP + ring[(place + step) % chips] * 2 + core,
                    )
                )
    core_pairs = [(i, i ^ 1) for i in range(n_dp)]
    inner = [[g * GROUP + i for i in range(GROUP)] for g in range(groups)]
    outer = [[g * GROUP + i for g in range(groups)] for i in range(GROUP)]
    if groups == 1:
        inner = None

    def along(x):
        return lax.ppermute(x, "dp", ring_pairs)

    def across(x):
        return lax.ppermute(x, "dp", core_pairs)

    def over(x):
        return lax.ppermute(x, "tensor", [(0, 1), (1, 0)])

    index = lax.axis_index("dp")
    group = index // GROUP
    chip = (index % GROUP) // 2
    core = index % 2
    tensor = lax.axis_index("tensor")
    is_first = core == 0
    at = core * half
    off = (1 - core) * half
    core_word = core.astype(jnp.int32).reshape(1)

    def my_half(x, start, axis=0):
        return lax.dynamic_slice_in_dim(x, start, half, axis)

    def in_order(own, other):
        return jnp.where(
            is_first, jnp.concatenate([own, other], 0), jnp.concatenate([other, own], 0)
        )

    def gather_rows(mine, needed={}):
        behind, ahead = [], []
        moving = mine
        for step in range(side):
            moving = along(after(moving, *needed.get(step, ())))
            behind.append(moving)
            ahead.append(across(moving))
        far = along(after(my_half(moving, at, moving.ndim - 2), *needed.get(side, ())))
        return [mine] + behind + ahead + [far, across(far)]

    rows = lax.broadcasted_iota(jnp.int32, (block, 1), 0)
    mine_rows = (rows < half) == is_first

    def ring_sum(*sets, needed={}):
        took_far = [across(give_far) for give_far, _, _ in sets]
        took = [across(give) for _, give, _ in sets]
        keep = [x for _, _, x in sets]
        far = [k[side * block : side * block + half].astype(f32) + t.astype(f32) for k, t in zip(keep, took_far)]
        moving = along(jnp.stack(far).astype(bf16))
        for step in reversed(range(side)):
            here = slice(step * block, (step + 1) * block)
            added = [k[here].astype(f32) + t[here].astype(f32) for k, t in zip(keep, took)]
            arrived = after(moving, *needed.get(step, ())).astype(f32)
            if step == side - 1:
                arrived = jnp.where(mine_rows, jnp.concatenate([arrived, arrived], 1), 0)
            moving = along((arrived + jnp.stack(added)).astype(bf16))
        got = across(my_half(moving, off, 1))
        return [(k, t, moving, got, n) for n, (k, t) in enumerate(zip(keep, took))]

    def spread(x):
        return lax.all_to_all(x, "dp", 0, 0, axis_index_groups=inner, tiled=True)

    small = jnp.concatenate(
        [
            norm_gain.reshape(-1),
            norm_bias.reshape(-1),
            output_bias.reshape(-1),
            (positions // 64).astype(bf16),
            (positions % 64).astype(bf16),
        ]
    )
    weights = []
    if groups == 1:
        qkv_turned = qkv_weight.transpose(0, 2, 1, 3)
        ups, downs = (qkv_turned, fc1_weight), (out_weight, fc2_weight)
        extra = jnp.concatenate([small, jnp.zeros_like(small)]).reshape(-1, 128)
        up = spread(call_pack(pack_first, 0, ups, (), (extra,)))
        small_all = up[:, UP_ROWS:].reshape(GROUP, -1)[:, : small.shape[0]]
        up_other = over(up)
        packed_down = call_pack(pack_down, 0, (), downs, ())
        down = spread(after(packed_down, up))
        down_other = over(down)
        weights.append(call_join(join_up, up, [up_other], True, False) + call_join(join_down, down, [down_other], False, True))
        packed_last = (call_pack(pack_up, 1, ups, (), ()), call_pack(pack_down, 1, (), downs, ()))
        firsts = (up, up_other, down)
    else:
        small_all = lax.all_gather(small, "dp", axis=0, tiled=False)
        for layer in range(LAYERS):
            up = jnp.concatenate(
                [
                    qkv_weight[layer].reshape(piece, 3, GROUP, HEAD_DIM).transpose(2, 0, 1, 3).reshape(GROUP, piece, -1),
                    fc1_weight[layer].reshape(piece, GROUP, hidden).transpose(1, 0, 2),
                ],
                axis=2,
            )
            up = lax.all_gather(spread(up), "dp", axis=0, axis_index_groups=outer, tiled=True)
            up = up.reshape(width // 128, 128, UP_ROWS)
            value = up[:, :, WIDE : WIDE + HEAD_DIM]
            first = WIDE + HEAD_DIM
            up = jnp.concatenate(
                [
                    up[:, :, :WIDE],
                    jnp.concatenate([value[:, :HEAD_DIM], value[:, HEAD_DIM:]], axis=2),
                    up[:, :, first : first + 128],
                    up[:, :, first + 128 :],
                ],
                axis=1,
            )
            down = jnp.concatenate(
                [out_weight[layer].reshape(GROUP, HEAD_DIM, piece), fc2_weight[layer].reshape(GROUP, hidden, piece)],
                axis=1,
            )
            down = lax.all_gather(spread(down), "dp", axis=0, axis_index_groups=outer, tiled=True)
            down = down.transpose(1, 0, 2).reshape(-1, width // 128, 128).transpose(1, 0, 2)
            weights.append(call_join(join_up, up, [over(up)], True, False) + call_join(join_down, down, [over(down)], False, True))
    if groups == 1:
        biases = jnp.concatenate([qkv_bias.reshape(LAYERS, 3 * HEAD_DIM), fc1_bias], axis=1)
    else:
        full_qkv = lax.all_gather(qkv_bias, "dp", axis=2, tiled=True)
        full_up = lax.all_gather(fc1_bias, "dp", axis=1, tiled=True)
        member = index % GROUP
        biases = jnp.concatenate(
            [
                lax.dynamic_slice_in_dim(full_qkv, member * HEAD_DIM, HEAD_DIM, 2).reshape(LAYERS, 3 * HEAD_DIM),
                lax.dynamic_slice_in_dim(full_up, member * hidden, hidden, 1),
            ],
            axis=1,
        )
    biases_other = over(biases)
    both_biases = jnp.stack([biases, biases_other], axis=1).astype(f32)
    bias_rows = jnp.concatenate(
        [
            both_biases[:, :, : 3 * HEAD_DIM].reshape(LAYERS, 2, 3, HEAD_DIM).transpose(0, 2, 1, 3).reshape(LAYERS, -1),
            both_biases[:, :, 3 * HEAD_DIM :].reshape(LAYERS, -1),
        ],
        axis=1,
    )
    vectors = small_all[:, : 6 * piece].reshape(n_dp, 3, LAYERS, piece).transpose(1, 2, 0, 3).reshape(3, LAYERS, 1, width).astype(f32)
    gains, shifts, added_bias = vectors[0], vectors[1], vectors[2]

    turned = jnp.where(is_first, 1, -1)
    place = jnp.sum(jnp.where(jnp.asarray(ring) == chip, jnp.arange(chips), 0))
    offsets = [0] + [-(s + 1) for s in range(side)] + [s + 1 for s in range(side)] + [chips // 2]
    places = (place + turned * jnp.asarray(offsets)) % chips
    chip_ids = jnp.sum(
        jnp.where(places[:, None] == jnp.arange(chips)[None, :], jnp.asarray(ring)[None, :], 0), axis=1
    )
    owners = group * GROUP + 2 * chip_ids + tensor
    labels = jax.vmap(lambda owner: sequence_labels(seq_lengths, seq_device, owner, block))(owners)
    rows_at = jnp.arange(block, dtype=jnp.int32)
    allowed = (
        (labels[:, :, None] == labels[:, None, :])
        & (labels[:, :, None] > 0)
        & (rows_at[None, None, :] <= rows_at[None, :, None])
    ) | (rows_at[None, None, :] == rows_at[None, :, None])
    allowed = allowed.astype(f32).reshape(chips * block, block)
    picked = (owners[:, None] == jnp.arange(n_dp)[None, :]).astype(f32)
    place_parts = jnp.dot(picked, small_all[:, 6 * piece :].astype(f32), precision=lax.Precision.HIGHEST)
    row_places = (place_parts[:, :block] * 64.0 + place_parts[:, block:]).reshape(chips * block)
    pair = ROT // 2
    frequency = 10000.0 ** (-2.0 * jnp.arange(pair, dtype=f32) / ROT)
    angles = row_places[:, None] * frequency[None, :]
    cosine, sine = jnp.cos(angles), jnp.sin(angles)
    nought = jnp.zeros_like(sine)
    rest = jnp.zeros((chips * block, HEAD_DIM - ROT), f32)
    tables = (
        jnp.concatenate([cosine, cosine, rest + 1.0] * 2, axis=1),
        jnp.concatenate([-sine, nought, rest] * 2, axis=1),
        jnp.concatenate([nought, sine, rest] * 2, axis=1),
    )

    both = jnp.stack([hidden_in, out_cotangent])
    both = jnp.where(tensor == core, both, across(both))
    keeps = jnp.stack([jnp.ones_like(labels[0]), (labels[0] > 0).astype(labels.dtype)]).astype(bf16)
    both = both * keeps[:, :, None]
    if groups == 1:
        inputs = gather_rows(
            after(both, packed_down, *packed_last, firsts[0], firsts[2]),
            {1: (firsts[1], tables[0]), 2: (tables[1], tables[2], allowed), side: (down_other, weights[0][0])},
        )
        up = spread(after(packed_last[0], inputs[-2]))
        up_other = over(up)
    else:
        inputs = gather_rows(both)
    mine_inputs = my_half(both, at, 1)
    state, grad_state = mine_inputs[0], mine_inputs[1]

    normed, heads, hidden_pre, wide, *parts = call_pass(
        "first", core_word, weights[0], tables, allowed, [bias_rows[0:1], gains[0], shifts[0]], inputs
    )
    slabs, others = (), ()
    if groups == 1:
        down = spread(after(packed_last[1], up, parts[0]))
        down_other = over(down)
        weights.append(call_join(join_up, up, [up_other], True, False) + call_join(join_down, down, [down_other], False, True))
        slabs, others = (down,), (up_other, down_other)
    rows_shape = (half, width)
    next_state, normed_own = call_end(
        partial(forward_end, False),
        core_word,
        ring_sum((after(parts[0], *slabs), parts[1], parts[2]), needed={2: others[:1]})[0],
        [state, added_bias[0], gains[1], shifts[1]],
        [jax.ShapeDtypeStruct(rows_shape, f32), jax.ShapeDtypeStruct(rows_shape, bf16)],
        "forward_end",
    )
    normed_chunks = gather_rows(in_order(normed_own, across(normed_own)), {1: others[1:]})

    def handed_back(own_rows):
        filled = in_order(own_rows, across(own_rows))
        return jnp.where(tensor == core, filled, over(filled))

    def summed(own, other, *earlier):
        total = own.astype(f32) + other.astype(f32)
        if groups > 1:
            total = total.transpose(1, 0, 2).reshape(total.shape[1], width)
            total = lax.psum_scatter(total, "dp", scatter_dimension=1, axis_index_groups=outer, tiled=True)
            total = total.reshape(total.shape[0], GROUP, piece).transpose(1, 0, 2)
        return spread(after(total.astype(bf16), *earlier))

    down_own = [(0, HEAD_DIM), (WIDE, WIDE + hidden)]
    down_other = [(HEAD_DIM, WIDE), (WIDE + hidden, WIDE + 2 * hidden)]
    up_own = [(p * WIDE, p * WIDE + HEAD_DIM) for p in range(3)] + [(3 * WIDE, 3 * WIDE + hidden)]
    up_other = [(p * WIDE + HEAD_DIM, (p + 1) * WIDE) for p in range(3)] + [(3 * WIDE + hidden, 3 * WIDE + 2 * hidden)]

    def down_gradients(wide_rows, grad_rows):
        return call_gradients(core_word, wide_rows, grad_rows, down_own, down_other, [], "down_gradients")

    def up_gradients(slim_rows, normed_rows, sums):
        return call_gradients(core_word, slim_rows, [normed_rows], up_own, up_other, [sums], "up_gradients")

    def backward_finish(ring_end, state, grad_state, layer, *needed):
        return call_end(
            backward_end,
            core_word,
            ring_end,
            [state, grad_state, gains[layer], *needed],
            [jax.ShapeDtypeStruct(rows_shape, f32), jax.ShapeDtypeStruct(rows_shape, bf16)],
            "backward_end",
        )

    normed_last, grad_rows, wide_last, slim, sums, *parts = call_pass(
        "middle", core_word, weights[1], tables, allowed, [bias_rows[1:2]], normed_chunks + inputs
    )
    out_parts = parts[:3]
    down_pair = down_gradients(wide_last, [grad_rows])
    *up_pair, bias_last = up_gradients(slim, normed_last, sums)
    down_sent, up_sent = over(down_pair[1]), over(up_pair[1])
    grad_end, out_end = ring_sum(parts[3:], out_parts, needed={1: (down_pair[0],), 0: (up_pair[0],)})
    grad_state, grad_low = backward_finish(grad_end, next_state, grad_state, 1)
    (hidden_out,) = call_end(
        partial(forward_end, True),
        core_word,
        out_end,
        [next_state, added_bias[1]],
        [jax.ShapeDtypeStruct(rows_shape, bf16)],
        "forward_out",
    )
    hidden_out = handed_back(hidden_out)
    down_last = summed(down_pair[0], after(down_sent, grad_low))
    grad_chunks = gather_rows(in_order(grad_low, across(grad_low)), {0: (down_sent,), 2: (up_sent,), side: (down_last, hidden_out)})
    up_last = summed(up_pair[0], after(up_sent, grad_chunks[-2]), down_last)

    down_pair = down_gradients(wide, grad_chunks)
    down_sent = over(down_pair[1])
    grad_rows, slim, sums, *parts = call_pass(
        "last", core_word, weights[0], tables, allowed, [heads, after(hidden_pre, down_pair[0]), normed], grad_chunks
    )
    down_first = summed(down_pair[0], after(down_sent, slim), up_last)
    *up_pair, bias_first = up_gradients(slim, after(normed, up_last), sums)
    up_sent = over(up_pair[1])
    (grad_end,) = ring_sum((after(parts[0], up_pair[0]), parts[1], parts[2]), needed={1: (down_first,), 0: (up_sent,)})
    up_first = summed(up_pair[0], up_sent, down_first, grad_end[2])
    sums = jnp.concatenate([bias_first, bias_last], axis=0)
    sums_qkv = sums[:, : 3 * WIDE].reshape(LAYERS, 3, 2, HEAD_DIM)
    sums_up = sums[:, 3 * WIDE :].reshape(LAYERS, 2, hidden)
    bias_own, bias_other = (
        jnp.concatenate([sums_qkv[:, :, n].reshape(LAYERS, -1), sums_up[:, n]], axis=1) for n in range(2)
    )
    bias_sent = over(bias_other)
    needed = [bias_sent]
    if groups == 1:
        *filled, mark = call_spread(up_last, down_last, 1, [])
        needed.append(mark)
    _, grad_low = backward_finish(grad_end, state, grad_state, 0, *needed)
    grad_hidden = handed_back(grad_low).astype(f32)

    ends = jnp.stack([jnp.sum(x[:, UP_ROWS : UP_ROWS + 3].astype(f32), axis=0) for x in (up_first, up_last)])
    shift_grads = ends[:, 0]
    gain_grads = (ends[:, 1] - norm_bias.astype(f32) * ends[:, 0]) / norm_gain.astype(f32)
    after_grads = ends[:, 2] / GROUP
    bias_sums = bias_own + bias_sent
    bias_qkv, bias_up = bias_sums[:, : 3 * HEAD_DIM].reshape(LAYERS, 3, HEAD_DIM), bias_sums[:, 3 * HEAD_DIM :]
    if groups == 1:
        grad_qkv, grad_out, grad_up, grad_down, _ = call_spread(up_first, down_first, 0, filled)
        grad_qkv = grad_qkv.transpose(0, 2, 1, 3)
    else:
        bias_qkv = lax.all_gather(lax.psum(bias_qkv, "dp", axis_index_groups=outer), "dp", axis=2, axis_index_groups=inner, tiled=True)
        bias_up = lax.all_gather(lax.psum(bias_up, "dp", axis_index_groups=outer), "dp", axis=1, axis_index_groups=inner, tiled=True)
        bias_qkv = lax.dynamic_slice_in_dim(bias_qkv, index * qkv_bias.shape[2], qkv_bias.shape[2], 2)
        bias_up = lax.dynamic_slice_in_dim(bias_up, index * fc1_bias.shape[1], fc1_bias.shape[1], 1)
        ups = jnp.stack([up_first, up_last]).astype(f32)
        downs = jnp.stack([down_first, down_last]).astype(f32)
        grad_qkv = ups[:, :, : 3 * HEAD_DIM].reshape(LAYERS, GROUP, 3, HEAD_DIM, piece).transpose(0, 4, 2, 1, 3).reshape(LAYERS, piece, 3, -1)
        grad_up = ups[:, :, 3 * HEAD_DIM : UP_ROWS].transpose(0, 3, 1, 2).reshape(LAYERS, piece, -1)
        grad_out = downs[:, :, :HEAD_DIM].reshape(LAYERS, -1, piece)
        grad_down = downs[:, :, HEAD_DIM:].reshape(LAYERS, -1, piece)
    return (
        hidden_out,
        grad_hidden,
        gain_grads,
        shift_grads,
        grad_qkv,
        bias_qkv,
        grad_out,
        grad_up,
        bias_up,
        grad_down,
        after_grads,
    )


def solution(mesh):
    placed = (
        P("dp", None),
        P(),
        P(),
        P("dp"),
        P(None, "dp"),
        P(None, "dp"),
        P(None, "dp", None, "tensor"),
        P(None, None, ("tensor", "dp")),
        P(None, "tensor", "dp"),
        P(None, "dp", "tensor"),
        P(None, ("tensor", "dp")),
        P(None, "tensor", "dp"),
        P(None, "dp"),
        P("dp", None),
    )
    return jax.shard_map(
        partial(per_device, mesh.shape["dp"]),
        mesh=mesh,
        in_specs=placed,
        out_specs=(
            P("dp", None),
            P("dp", None),
            P(None, "dp"),
            P(None, "dp"),
            P(None, "dp", None, "tensor"),
            P(None, None, ("tensor", "dp")),
            P(None, "tensor", "dp"),
            P(None, "dp", "tensor"),
            P(None, ("tensor", "dp")),
            P(None, "tensor", "dp"),
            P(None, "dp"),
        ),
        check_vma=False,
    )
```

```python
from functools import partial

import jax
import jax.numpy as jnp
from jax import lax
from jax.experimental import pallas as pl
from jax.experimental.pallas import tpu as pltpu
from jax.sharding import PartitionSpec as P

HEAD_DIM = 64
ROT = 32
LAYERS = 2
GROUP = 16

norm_epsilon = 1e-05
masked_score = -1e30
bf16 = jnp.bfloat16
f32 = jnp.float32

contract_last = (((1,), (1,)), ((), ()))
contract_first = (((0,), (0,)), ((), ()))


def dot(a, b, dims=(((1,), (0,)), ((), ()))):
    return lax.dot_general(a, b, dims, preferred_element_type=f32)


def turn(x, cosine, up, down):
    return x * cosine + pltpu.roll(x, x.shape[1] - ROT // 2, 1) * up + pltpu.roll(x, ROT // 2, 1) * down


def stacked_heads(x):
    lane = lax.broadcasted_iota(jnp.int32, x.shape, 1)
    zero = jnp.zeros_like(x)
    return jnp.concatenate(
        [jnp.where(lane < HEAD_DIM, x, zero), jnp.where(lane < HEAD_DIM, zero, x)], axis=0
    )


def merged_heads(x):
    rows = x.shape[0] // 2
    lane = lax.broadcasted_iota(jnp.int32, (rows, x.shape[1]), 1)
    return jnp.where(lane < HEAD_DIM, x[:rows], x[rows:])


def softmax_rows(queries, keys, allowed):
    scores = dot(stacked_heads(queries), keys, contract_last) * HEAD_DIM ** (-0.5)
    masked = jnp.where(jnp.concatenate([allowed, allowed], axis=0) > 0, scores, masked_score)
    weights = jnp.exp(masked - jnp.max(masked, axis=1, keepdims=True))
    return weights / jnp.sum(weights, axis=1, keepdims=True)


def sequence_labels(seq_lengths, seq_device, owner, count_rows):
    index = jnp.arange(seq_lengths.shape[0], dtype=jnp.int32)
    owned = jnp.where(seq_device == owner, seq_lengths, 0)
    earlier = index[None, :] < index[:, None]
    starts = jnp.sum(jnp.where(earlier, owned[None, :], 0), axis=1)
    places = jnp.arange(count_rows, dtype=jnp.int32)
    inside = (places[:, None] >= starts[None, :]) & (places[:, None] < (starts + owned)[None, :])
    return jnp.sum(jnp.where(inside, index[None, :] + 1, 0), axis=1)


def gelu_parts(v):
    c = (2.0 / jnp.pi) ** 0.5
    inner = jnp.tanh(c * (v + 0.044715 * v * v * v))
    value = 0.5 * v * (1.0 + inner)
    slope = 0.5 * (1.0 + inner) + 0.5 * v * (1.0 - inner * inner) * c * (1.0 + 3.0 * 0.044715 * v * v)
    return value, slope


VMEM_SPEC = pl.BlockSpec(memory_space=pltpu.VMEM)
ANY_SPEC = pl.BlockSpec(memory_space=pl.ANY)
SMEM_SPEC = pl.BlockSpec(memory_space=pltpu.SMEM)
WIDE = 2 * HEAD_DIM
UP_ROWS = 3 * HEAD_DIM + 256
DOWN_ROWS = HEAD_DIM + 256
SUM_ROWS = 16
MEMBERS = 4


def after(x, *others):
    if not others:
        return x
    return lax.optimization_barrier((x, *others))[0]


def left_lanes(x):
    return lax.broadcasted_iota(jnp.int32, x.shape, 1) < HEAD_DIM


def swapped(x):
    return pltpu.roll(x, HEAD_DIM, 1)


def zipped(a, b):
    left = left_lanes(a)
    return jnp.where(left, a, swapped(b)).astype(bf16), jnp.where(left, swapped(a), b).astype(bf16)


def pack_up(qkv_ref, fc1_ref, *rest):
    out_ref = rest[-1]
    for pair in range(MEMBERS // 2):
        lanes = slice(pair * 128, (pair + 1) * 128)
        q, k, v = (qkv_ref[0, p, :, lanes].astype(f32) for p in range(3))
        here, there = 2 * pair, 2 * pair + 1
        out_ref[here, :WIDE], out_ref[there, :WIDE] = zipped(q, k)
        rows = q.shape[0] // 2
        out_ref[here, WIDE : WIDE + rows], out_ref[there, WIDE : WIDE + rows] = zipped(v[:rows], v[rows:])
        base = WIDE + rows
        for d in (here, there):
            for h in range(2):
                out_ref[d, base + h * 128 : base + (h + 1) * 128] = fc1_ref[0, :, (2 * d + h) * 128 : (2 * d + h + 1) * 128]


def pack_first(qkv_ref, fc1_ref, small_ref, out_ref):
    pack_up(qkv_ref, fc1_ref, out_ref)
    for d in range(MEMBERS):
        out_ref[d, UP_ROWS:] = small_ref[...]


def pack_down(out_w_ref, fc2_ref, out_ref):
    for d in range(MEMBERS):
        out_ref[d, :HEAD_DIM] = out_w_ref[0, d * HEAD_DIM : (d + 1) * HEAD_DIM]
        out_ref[d, HEAD_DIM:] = fc2_ref[0, d * 256 : (d + 1) * 256]


def call_pack(body, layer, ups, downs, small):
    rows, specs = 0, []
    if ups:
        rows += UP_ROWS
        specs += [
            pl.BlockSpec((1, 3, 128, MEMBERS * HEAD_DIM), lambda i: (layer, 0, 0, i)),
            pl.BlockSpec((1, 128, MEMBERS * 256), lambda i: (layer, 0, i)),
        ]
    if downs:
        rows += DOWN_ROWS
        specs += [
            pl.BlockSpec((1, MEMBERS * HEAD_DIM, 128), lambda i: (layer, i, 0)),
            pl.BlockSpec((1, MEMBERS * 256, 128), lambda i: (layer, i, 0)),
        ]
    if small:
        rows += small[0].shape[0]
        specs.append(pl.BlockSpec(small[0].shape, lambda i: (0, 0)))
    return pl.pallas_call(
        body,
        grid=(GROUP // MEMBERS,),
        in_specs=specs,
        out_specs=pl.BlockSpec((MEMBERS, rows, 128), lambda i: (i, 0, 0)),
        out_shape=jax.ShapeDtypeStruct((GROUP, rows, 128), bf16),
        cost_estimate=pl.CostEstimate(flops=0, bytes_accessed=GROUP * rows * 128 * 8, transcendentals=0),
        name=body.__name__,
    )(*ups, *downs, *small)


def join_up(own_ref, other_ref, out_ref):
    for e in range(MEMBERS):
        rows = slice(e * 128, (e + 1) * 128)
        a, b = own_ref[e, :WIDE].astype(f32), other_ref[e, :WIDE].astype(f32)
        out_ref[rows, :WIDE], out_ref[rows, WIDE : 2 * WIDE] = zipped(a, b)
        a, b = own_ref[e, WIDE : WIDE + 64].astype(f32), other_ref[e, WIDE : WIDE + 64].astype(f32)
        top, bottom = zipped(a, b)
        out_ref[e * 128 : e * 128 + 64, 2 * WIDE : 3 * WIDE] = top
        out_ref[e * 128 + 64 : (e + 1) * 128, 2 * WIDE : 3 * WIDE] = bottom
        for n, ref in enumerate((own_ref, other_ref)):
            for h in range(2):
                lanes = 3 * WIDE + n * 256 + h * 128
                out_ref[rows, lanes : lanes + 128] = ref[e, WIDE + 64 + h * 128 : WIDE + 64 + (h + 1) * 128]


def join_down(own_ref, other_ref, out_ref):
    base = own_ref.shape[1] - DOWN_ROWS
    for e in range(MEMBERS):
        lanes = slice(e * 128, (e + 1) * 128)
        for n, ref in enumerate((own_ref, other_ref)):
            out_ref[n * HEAD_DIM : (n + 1) * HEAD_DIM, lanes] = ref[e, base : base + HEAD_DIM]
            out_ref[WIDE + n * 256 : WIDE + (n + 1) * 256, lanes] = ref[e, base + HEAD_DIM :]


def call_join(body, own, others, ups, downs):
    rows = own.shape[1]
    spec = pl.BlockSpec((MEMBERS, rows, 128), lambda i: (i, 0, 0))
    specs, shapes = [], []
    if ups:
        specs.append(pl.BlockSpec((MEMBERS * 128, 2 * UP_ROWS), lambda i: (i, 0)))
        shapes.append(jax.ShapeDtypeStruct((GROUP * 128, 2 * UP_ROWS), bf16))
    if downs:
        specs.append(pl.BlockSpec((2 * DOWN_ROWS, MEMBERS * 128), lambda i: (0, i)))
        shapes.append(jax.ShapeDtypeStruct((2 * DOWN_ROWS, GROUP * 128), bf16))
    return pl.pallas_call(
        body,
        grid=(GROUP // MEMBERS,),
        in_specs=[spec] * (1 + len(others)),
        out_specs=specs,
        out_shape=shapes,
        cost_estimate=pl.CostEstimate(flops=0, bytes_accessed=GROUP * rows * 128 * 12, transcendentals=0),
        name=body.__name__,
    )(own, *others)


def slot_copies(refs, which, target, core):
    block = target.shape[0] // 8
    half = block // 2
    pairs = []
    for slot in range(7):
        ref = refs[slot] if which is None else refs[slot].at[which]
        pairs.append((ref, target.at[pl.ds(slot * block, block)]))
    for n, at in ((7, core * half), (8, (1 - core) * half)):
        ref = refs[n] if which is None else refs[n].at[which]
        pairs.append((ref, target.at[pl.ds(pl.multiple_of(7 * block + at, half), half)]))
    return pairs


def split_copies(part, far_ref, give_ref, keep_ref, core):
    block = part.shape[0] // 8
    half = block // 2
    at, off = core * half, (1 - core) * half

    def rows(slot, start):
        return part.at[pl.ds(pl.multiple_of(slot * block + start, half), half)]

    return [
        (rows(7, off), far_ref),
        (part.at[pl.ds(block, 3 * block)], give_ref.at[pl.ds(0, 3 * block)]),
        (rows(0, off), give_ref.at[pl.ds(3 * block, half)]),
        (part.at[pl.ds(4 * block, 3 * block)], keep_ref.at[pl.ds(0, 3 * block)]),
        (rows(7, at), keep_ref.at[pl.ds(3 * block, half)]),
        (rows(0, at), keep_ref.at[pl.ds(3 * block + half, half)]),
    ]


def run_copies(pairs, sems, first):
    made = [pltpu.make_async_copy(a, b, sems.at[first + n]) for n, (a, b) in enumerate(pairs)]
    for copy in made:
        copy.start()
    return made


def heads_forward(chances, values):
    return merged_heads(dot(chances.astype(bf16), values)).astype(bf16)


def heads_backward(chances, queries, keys, values, grad, tables):
    grads = stacked_heads(grad)
    grad_chances = dot(grads, values, contract_last)
    grad_values = dot(chances.astype(bf16), grads, contract_first)
    centre = jnp.sum(grad_chances * chances, axis=1, keepdims=True)
    grad_scores = (chances * (grad_chances - centre)).astype(bf16)
    scale = HEAD_DIM ** (-0.5)
    grad_queries = merged_heads(dot(grad_scores, keys)) * scale
    grad_keys = dot(grad_scores, stacked_heads(queries), contract_first) * scale
    cosine, up, down = tables
    back = (cosine, -up, -down)
    return turn(grad_queries, *back).astype(bf16), turn(grad_keys, *back).astype(bf16), grad_values.astype(bf16)


def layer_pass(mode, *refs):
    refs = list(refs)

    def take(n):
        out = refs[:n]
        del refs[:n]
        return out

    forward, backward = mode != "last", mode != "first"
    core_ref, up_ref, down_ref, cos_ref, sin_up_ref, sin_down_ref, allowed_ref = take(7)
    core = core_ref[0]
    if mode == "first":
        bias_ref, gain_ref, shift_ref = take(3)
        rows_in = take(9)
    elif mode == "middle":
        (bias_ref,) = take(1)
        rows_in = take(9)
        grads_in = take(9)
    else:
        heads_ref, hidden_ref, normed_ref = take(3)
        grads_in = take(9)
    if mode == "first":
        normed_ref, heads_ref, hidden_ref, wide_ref = take(4)
        outs = take(3)
        raw, part, sems = take(3)
    elif mode == "middle":
        normed_ref, grad_rows_ref, wide_ref, slim_ref, sums_ref = take(5)
        outs = take(3)
        grad_outs = take(3)
        part, grad_part, sems = take(3)
    else:
        grad_rows_ref, slim_ref, sums_ref = take(3)
        grad_outs = take(3)
        grad_part, sems = take(2)

    pairs = []
    if mode == "first":
        pairs += slot_copies(rows_in, 0, raw, core)
    if mode == "middle":
        pairs += slot_copies(rows_in, None, normed_ref, core)
        pairs += slot_copies(grads_in, 1, grad_rows_ref, core)
    if mode == "last":
        pairs += slot_copies(grads_in, None, grad_rows_ref, core)
    for copy in run_copies(pairs, sems, 0):
        copy.wait()

    total = allowed_ref.shape[0]
    block = allowed_ref.shape[1]
    step = 2 * block

    if mode == "first":
        tile = 32

        def norm_tile(i, carry):
            at = pl.ds(pl.multiple_of(i * tile, tile), tile)
            x = raw[at, :].astype(f32)
            centred = x - jnp.mean(x, axis=1, keepdims=True)
            inverse = lax.rsqrt(jnp.mean(centred * centred, axis=1, keepdims=True) + norm_epsilon)
            normed_ref[at, :] = (centred * inverse * gain_ref[...] + shift_ref[...]).astype(bf16)
            return carry

        lax.fori_loop(0, total // tile, norm_tile, 0)

    if backward:
        sums_ref[...] = jnp.zeros_like(sums_ref)

    def one(p, carry):
        at = pl.ds(pl.multiple_of(p * step, step), step)
        if forward:
            before = dot(normed_ref[at, :], up_ref[...]) + bias_ref[...]
            hidden_pre = before[:, 3 * WIDE :]
        else:
            hidden_pre = hidden_ref[at, :]
        value, slope = gelu_parts(hidden_pre)
        if backward:
            grad_wide = dot(grad_rows_ref[at, :], down_ref[...], contract_last)
            slim_ref[at, 3 * WIDE :] = (grad_wide[:, WIDE:] * slope).astype(bf16)
        if forward:
            wide_ref[at, WIDE:] = value.astype(bf16)
        if mode == "first":
            hidden_ref[at, :] = hidden_pre
        for b in range(2):
            mine = slice(b * block, (b + 1) * block)
            own = pl.ds(pl.multiple_of(p * step + b * block, block), block)
            tables = (cos_ref[own, :], sin_up_ref[own, :], sin_down_ref[own, :])
            if forward:
                queries = turn(before[mine, :WIDE], *tables).astype(bf16)
                keys = turn(before[mine, WIDE : 2 * WIDE], *tables).astype(bf16)
                values = before[mine, 2 * WIDE : 3 * WIDE].astype(bf16)
            else:
                queries = heads_ref[own, :WIDE]
                keys = heads_ref[own, WIDE : 2 * WIDE]
                values = heads_ref[own, 2 * WIDE :]
            if mode == "first":
                heads_ref[own, :WIDE] = queries
                heads_ref[own, WIDE : 2 * WIDE] = keys
                heads_ref[own, 2 * WIDE :] = values
            chances = softmax_rows(queries, keys, allowed_ref[own, :])
            if forward:
                wide_ref[own, :WIDE] = heads_forward(chances, values)
            if backward:
                grads = heads_backward(
                    chances, queries, keys, values, grad_wide[mine, :WIDE].astype(bf16), tables
                )
                for n in range(3):
                    slim_ref[own, n * WIDE : (n + 1) * WIDE] = grads[n]
        if forward:
            part[at, :] = dot(wide_ref[at, :], down_ref[...]).astype(bf16)
        if backward:
            grad_normed = dot(slim_ref[at, :], up_ref[...], contract_last)
            grad_part[at, :] = grad_normed.astype(bf16)
            for n, rows in enumerate(
                (grad_normed, grad_normed * normed_ref[at, :].astype(f32), grad_rows_ref[at, :].astype(f32))
            ):
                sums_ref[n : n + 1] += jnp.sum(rows, axis=0, keepdims=True)
        return carry

    lax.fori_loop(0, total // step, one, 0)
    pairs = []
    if backward:
        pairs += split_copies(grad_part, *grad_outs, core)
    if forward:
        pairs += split_copies(part, *outs, core)
    for copy in run_copies(pairs, sems, 0):
        copy.wait()


def call_pass(mode, core, weights, tables, allowed, extra, chunks):
    total, block = allowed.shape
    half = block // 2
    width = weights[0].shape[0]
    slim = weights[0].shape[1]
    wide = weights[1].shape[0]
    parts = [
        jax.ShapeDtypeStruct((half, width), bf16),
        jax.ShapeDtypeStruct((3 * block + half, width), bf16),
        jax.ShapeDtypeStruct((4 * block, width), bf16),
    ]
    full = jax.ShapeDtypeStruct((total, width), bf16)
    sums = jax.ShapeDtypeStruct((SUM_ROWS, width), f32)
    slim_rows = jax.ShapeDtypeStruct((total, slim), bf16)
    wide_rows = jax.ShapeDtypeStruct((total, wide), bf16)
    if mode == "first":
        kept = [
            full,
            jax.ShapeDtypeStruct((total, 3 * WIDE), bf16),
            jax.ShapeDtypeStruct((total, slim - 3 * WIDE), f32),
            wide_rows,
        ]
        buffers = 2
    elif mode == "middle":
        kept = [full, full, wide_rows, slim_rows, sums]
        parts = parts * 2
        buffers = 2
    else:
        kept = [full, slim_rows, sums]
        buffers = 1
    passes = 2 if mode == "middle" else 1
    return pl.pallas_call(
        partial(layer_pass, mode),
        in_specs=[SMEM_SPEC] + [VMEM_SPEC] * (6 + len(extra)) + [ANY_SPEC] * len(chunks),
        out_specs=[VMEM_SPEC] * len(kept) + [ANY_SPEC] * len(parts),
        out_shape=kept + parts,
        scratch_shapes=[pltpu.VMEM((total, width), bf16)] * buffers + [pltpu.SemaphoreType.DMA((18,))],
        cost_estimate=pl.CostEstimate(
            flops=6 * total * width * (slim + wide) * passes,
            bytes_accessed=20_000_000 * passes,
            transcendentals=total * slim,
        ),
        name="pass_" + mode,
    )(core, *weights, *tables, allowed, *extra, *chunks)


def gradient_slabs(own_rows, other_rows, with_sums, pieces_in, core_ref, left_ref, *rest):
    right_refs, rest = rest[:pieces_in], rest[pieces_in:]
    if with_sums:
        sums_ref, *rest = rest
    own_ref, other_ref, *rest = rest
    turned_ref = rest[-1]
    if pieces_in == 1:
        right = right_refs[0][...]
    else:
        a, b = right_refs[-2][...], right_refs[-1][...]
        first = jnp.full(a.shape, core_ref[0]) == 0
        halves = [jnp.where(first, a, b), jnp.where(first, b, a)]
        right = jnp.concatenate([ref[...] for ref in right_refs[:-2]] + halves, axis=0)

    @pl.when(pl.program_id(0) == 0)
    def _():
        width = left_ref.shape[1]
        for n in range(width // 128):
            lanes = slice(n * 128, (n + 1) * 128)
            left = left_ref[:, lanes].astype(f32)
            if with_sums:
                rest[0][:, lanes] = jnp.sum(left, axis=0, keepdims=True)
            turned_ref[lanes, :] = left.T.astype(bf16)

    product = dot(turned_ref[...], right).astype(bf16)
    for ref, pieces in ((own_ref, own_rows), (other_ref, other_rows)):
        place = 0
        for first, last in pieces:
            for e in range(2):
                ref[e, place : place + last - first] = product[first:last, e * 128 : (e + 1) * 128]
            place += last - first
        if with_sums:
            for e in range(2):
                ref[e, place:] = sums_ref[:, e * 128 : (e + 1) * 128].astype(bf16)


def call_gradients(core, left, right, own_rows, other_rows, sums, name):
    total, height = left.shape
    width = right[0].shape[1]
    with_sums = len(sums) > 0
    rows = height // 2 + (SUM_ROWS if with_sums else 0)
    slab = pl.BlockSpec((2, rows, 128), lambda i: (i, 0, 0))
    shape = jax.ShapeDtypeStruct((width // 128, rows, 128), bf16)
    out_specs, out_shape = [slab, slab], [shape, shape]
    if with_sums:
        out_specs.append(pl.BlockSpec((1, height), lambda i: (0, 0)))
        out_shape.append(jax.ShapeDtypeStruct((1, height), f32))
    return pl.pallas_call(
        partial(gradient_slabs, own_rows, other_rows, with_sums, len(right)),
        grid=(width // 256,),
        in_specs=[SMEM_SPEC, pl.BlockSpec((total, height), lambda i: (0, 0))]
        + [pl.BlockSpec((x.shape[0], 256), lambda i: (0, i)) for x in (*right, *sums)],
        out_specs=out_specs,
        out_shape=out_shape,
        scratch_shapes=[pltpu.VMEM((height, total), bf16)],
        cost_estimate=pl.CostEstimate(
            flops=4 * total * height * width, bytes_accessed=2 * (total * (width + height) + 2 * height * width), transcendentals=0
        ),
        name=name,
    )(core, left, *right, *sums)


def spread_gradients(up_ref, down_ref, *rest):
    qkv_ref, out_w_ref, fc1_ref, fc2_ref, mark_ref = rest[-5:]
    mark_ref[...] = jnp.zeros_like(mark_ref)
    for p in range(3):
        rows = slice(p * HEAD_DIM, (p + 1) * HEAD_DIM)
        both = jnp.concatenate([up_ref[0, rows].astype(f32), up_ref[1, rows].astype(f32)], axis=0)
        qkv_ref[0, p] = both.T
    base = 3 * HEAD_DIM
    for d in range(2):
        for h in range(2):
            fc1_ref[0, :, (2 * d + h) * 128 : (2 * d + h + 1) * 128] = (
                up_ref[d, base + h * 128 : base + (h + 1) * 128].astype(f32).T
            )
        out_w_ref[0, d * HEAD_DIM : (d + 1) * HEAD_DIM] = down_ref[d, :HEAD_DIM].astype(f32)
        fc2_ref[0, d * 256 : (d + 1) * 256] = down_ref[d, HEAD_DIM:].astype(f32)


def call_spread(up, down, layer, filled):
    shapes = [
        jax.ShapeDtypeStruct((LAYERS, 3, 128, GROUP * HEAD_DIM), f32),
        jax.ShapeDtypeStruct((LAYERS, GROUP * HEAD_DIM, 128), f32),
        jax.ShapeDtypeStruct((LAYERS, 128, GROUP * 256), f32),
        jax.ShapeDtypeStruct((LAYERS, GROUP * 256, 128), f32),
        jax.ShapeDtypeStruct((8, 128), f32),
    ]
    return pl.pallas_call(
        spread_gradients,
        grid=(GROUP // 2,),
        in_specs=[
            pl.BlockSpec((2, up.shape[1], 128), lambda i: (i, 0, 0)),
            pl.BlockSpec((2, down.shape[1], 128), lambda i: (i, 0, 0)),
        ]
        + [ANY_SPEC] * len(filled),
        out_specs=[
            pl.BlockSpec((1, 3, 128, 128), lambda i: (layer, 0, 0, i)),
            pl.BlockSpec((1, 128, 128), lambda i: (layer, i, 0)),
            pl.BlockSpec((1, 128, 512), lambda i: (layer, 0, i)),
            pl.BlockSpec((1, 512, 128), lambda i: (layer, i, 0)),
            pl.BlockSpec((8, 128), lambda i: (0, 0)),
        ],
        out_shape=shapes,
        input_output_aliases={2 + n: n for n in range(len(filled))},
        name="spread_gradients",
    )(up, down, *filled)


def ring_total(core_ref, keep_ref, took_ref, moving_ref, got_ref):
    half = got_ref.shape[0]
    arrived = moving_ref[pl.ds(pl.multiple_of(core_ref[0] * half, half), half), :]
    return keep_ref[...].astype(f32) + took_ref[...].astype(f32) + arrived.astype(f32) + got_ref[...].astype(f32)


def centred_rows(state):
    centred = state - jnp.mean(state, axis=1, keepdims=True)
    return centred, lax.rsqrt(jnp.mean(centred * centred, axis=1, keepdims=True) + norm_epsilon)


def forward_end(last, core_ref, keep_ref, took_ref, moving_ref, got_ref, state_ref, after_ref, *rest):
    state = state_ref[...].astype(f32) + ring_total(core_ref, keep_ref, took_ref, moving_ref, got_ref) + after_ref[...]
    if last:
        rest[0][...] = state.astype(bf16)
        return
    gain_ref, shift_ref, state_out, normed_ref = rest
    state_out[...] = state
    centred, inverse = centred_rows(state)
    normed_ref[...] = (centred * inverse * gain_ref[...] + shift_ref[...]).astype(bf16)


def backward_end(core_ref, keep_ref, took_ref, moving_ref, got_ref, state_ref, grad_ref, gain_ref, *rest):
    grad_out, low_ref = rest[-2:]
    grad_normed = ring_total(core_ref, keep_ref, took_ref, moving_ref, got_ref)
    centred, inverse = centred_rows(state_ref[...].astype(f32))
    xhat = centred * inverse
    before = grad_ref[...].astype(f32)
    scaled = grad_normed * gain_ref[...]
    after = before + (
        scaled - jnp.mean(scaled, axis=1, keepdims=True) - xhat * jnp.mean(scaled * xhat, axis=1, keepdims=True)
    ) * inverse
    grad_out[...] = after
    low_ref[...] = after.astype(bf16)


def call_end(body, core, ring, extra, shapes, name):
    keep, took, moving, got, n_sum = ring
    _, half, width = got.shape

    def rows_of(array):
        n = array.shape[0] // half - 1
        return pl.BlockSpec((half, width), lambda i: (n, 0))

    def whole_of(array):
        return pl.BlockSpec(array.shape, lambda i: (0,) * len(array.shape))

    def one_of(array):
        return pl.BlockSpec((None,) + array.shape[1:], lambda i: (n_sum, 0, 0))

    return pl.pallas_call(
        body,
        grid=(1,),
        in_specs=[SMEM_SPEC, rows_of(keep), rows_of(took), one_of(moving), one_of(got)] + [whole_of(x) for x in extra],
        out_specs=[whole_of(x) for x in shapes],
        out_shape=shapes,
        name=name,
    )(core, keep, took, moving, got, *extra)


def per_device(
    n_dp,
    hidden_in,
    seq_lengths,
    seq_device,
    positions,
    norm_gain,
    norm_bias,
    qkv_weight,
    qkv_bias,
    out_weight,
    fc1_weight,
    fc1_bias,
    fc2_weight,
    output_bias,
    out_cotangent,
):
    block = hidden_in.shape[0]
    half = block // 2
    width = hidden_in.shape[1]
    piece = norm_gain.shape[1]
    hidden = fc1_weight.shape[2] // GROUP
    groups = n_dp // GROUP
    chips = GROUP // 2
    side = chips // 2 - 1

    if groups == 1:
        ring = [2 * a for a in range(chips // 2)] + [2 * a + 1 for a in reversed(range(chips // 2))]
    else:
        ring = list(range(chips // 2)) + list(reversed(range(chips // 2, chips)))
    ring_pairs = []
    for g in range(groups):
        for place in range(chips):
            for core, step in ((0, 1), (1, -1)):
                ring_pairs.append(
                    (
                        g * GROUP + ring[place] * 2 + core,
                        g * GROUP + ring[(place + step) % chips] * 2 + core,
                    )
                )
    core_pairs = [(i, i ^ 1) for i in range(n_dp)]
    inner = [[g * GROUP + i for i in range(GROUP)] for g in range(groups)]
    outer = [[g * GROUP + i for g in range(groups)] for i in range(GROUP)]
    if groups == 1:
        inner = None

    def along(x):
        return lax.ppermute(x, "dp", ring_pairs)

    def across(x):
        return lax.ppermute(x, "dp", core_pairs)

    def over(x):
        return lax.ppermute(x, "tensor", [(0, 1), (1, 0)])

    index = lax.axis_index("dp")
    group = index // GROUP
    chip = (index % GROUP) // 2
    core = index % 2
    tensor = lax.axis_index("tensor")
    is_first = core == 0
    at = core * half
    off = (1 - core) * half
    core_word = core.astype(jnp.int32).reshape(1)

    def my_half(x, start, axis=0):
        return lax.dynamic_slice_in_dim(x, start, half, axis)

    def in_order(own, other):
        return jnp.where(
            is_first, jnp.concatenate([own, other], 0), jnp.concatenate([other, own], 0)
        )

    def gather_rows(mine, needed={}):
        behind, ahead = [], []
        moving = mine
        for step in range(side):
            moving = along(after(moving, *needed.get(step, ())))
            behind.append(moving)
            ahead.append(across(moving))
        far = along(after(my_half(moving, at, moving.ndim - 2), *needed.get(side, ())))
        return [mine] + behind + ahead + [far, across(far)]

    rows = lax.broadcasted_iota(jnp.int32, (block, 1), 0)
    mine_rows = (rows < half) == is_first

    def ring_sum(*sets, needed={}):
        took_far = [across(give_far) for give_far, _, _ in sets]
        took = [across(give) for _, give, _ in sets]
        keep = [x for _, _, x in sets]
        far = [k[side * block : side * block + half].astype(f32) + t.astype(f32) for k, t in zip(keep, took_far)]
        moving = along(jnp.stack(far).astype(bf16))
        for step in reversed(range(side)):
            here = slice(step * block, (step + 1) * block)
            added = [k[here].astype(f32) + t[here].astype(f32) for k, t in zip(keep, took)]
            arrived = after(moving, *needed.get(step, ())).astype(f32)
            if step == side - 1:
                arrived = jnp.where(mine_rows, jnp.concatenate([arrived, arrived], 1), 0)
            moving = along((arrived + jnp.stack(added)).astype(bf16))
        got = across(my_half(moving, off, 1))
        return [(k, t, moving, got, n) for n, (k, t) in enumerate(zip(keep, took))]

    def spread(x):
        return lax.all_to_all(x, "dp", 0, 0, axis_index_groups=inner, tiled=True)

    small = jnp.concatenate(
        [
            norm_gain.reshape(-1),
            norm_bias.reshape(-1),
            output_bias.reshape(-1),
            (positions // 64).astype(bf16),
            (positions % 64).astype(bf16),
        ]
    )
    weights = []
    if groups == 1:
        qkv_turned = qkv_weight.transpose(0, 2, 1, 3)
        ups, downs = (qkv_turned, fc1_weight), (out_weight, fc2_weight)
        extra = jnp.concatenate([small, jnp.zeros_like(small)]).reshape(-1, 128)
        up = spread(call_pack(pack_first, 0, ups, (), (extra,)))
        small_all = up[:, UP_ROWS:].reshape(GROUP, -1)[:, : small.shape[0]]
        up_other = over(up)
        packed_down = call_pack(pack_down, 0, (), downs, ())
        down = spread(after(packed_down, up))
        down_other = over(down)
        weights.append(call_join(join_up, up, [up_other], True, False) + call_join(join_down, down, [down_other], False, True))
        packed_last = (call_pack(pack_up, 1, ups, (), ()), call_pack(pack_down, 1, (), downs, ()))
        firsts = (up, up_other, down)
    else:
        small_all = lax.all_gather(small, "dp", axis=0, tiled=False)
        for layer in range(LAYERS):
            up = jnp.concatenate(
                [
                    qkv_weight[layer].reshape(piece, 3, GROUP, HEAD_DIM).transpose(2, 0, 1, 3).reshape(GROUP, piece, -1),
                    fc1_weight[layer].reshape(piece, GROUP, hidden).transpose(1, 0, 2),
                ],
                axis=2,
            )
            up = lax.all_gather(spread(up), "dp", axis=0, axis_index_groups=outer, tiled=True)
            up = up.reshape(width // 128, 128, UP_ROWS)
            value = up[:, :, WIDE : WIDE + HEAD_DIM]
            first = WIDE + HEAD_DIM
            up = jnp.concatenate(
                [
                    up[:, :, :WIDE],
                    jnp.concatenate([value[:, :HEAD_DIM], value[:, HEAD_DIM:]], axis=2),
                    up[:, :, first : first + 128],
                    up[:, :, first + 128 :],
                ],
                axis=1,
            )
            down = jnp.concatenate(
                [out_weight[layer].reshape(GROUP, HEAD_DIM, piece), fc2_weight[layer].reshape(GROUP, hidden, piece)],
                axis=1,
            )
            down = lax.all_gather(spread(down), "dp", axis=0, axis_index_groups=outer, tiled=True)
            down = down.transpose(1, 0, 2).reshape(-1, width // 128, 128).transpose(1, 0, 2)
            weights.append(call_join(join_up, up, [over(up)], True, False) + call_join(join_down, down, [over(down)], False, True))
    if groups == 1:
        biases = jnp.concatenate([qkv_bias.reshape(LAYERS, 3 * HEAD_DIM), fc1_bias], axis=1)
    else:
        full_qkv = lax.all_gather(qkv_bias, "dp", axis=2, tiled=True)
        full_up = lax.all_gather(fc1_bias, "dp", axis=1, tiled=True)
        member = index % GROUP
        biases = jnp.concatenate(
            [
                lax.dynamic_slice_in_dim(full_qkv, member * HEAD_DIM, HEAD_DIM, 2).reshape(LAYERS, 3 * HEAD_DIM),
                lax.dynamic_slice_in_dim(full_up, member * hidden, hidden, 1),
            ],
            axis=1,
        )
    biases_other = over(biases)
    both_biases = jnp.stack([biases, biases_other], axis=1).astype(f32)
    bias_rows = jnp.concatenate(
        [
            both_biases[:, :, : 3 * HEAD_DIM].reshape(LAYERS, 2, 3, HEAD_DIM).transpose(0, 2, 1, 3).reshape(LAYERS, -1),
            both_biases[:, :, 3 * HEAD_DIM :].reshape(LAYERS, -1),
        ],
        axis=1,
    )
    vectors = small_all[:, : 6 * piece].reshape(n_dp, 3, LAYERS, piece).transpose(1, 2, 0, 3).reshape(3, LAYERS, 1, width).astype(f32)
    gains, shifts, added_bias = vectors[0], vectors[1], vectors[2]

    turned = jnp.where(is_first, 1, -1)
    place = jnp.sum(jnp.where(jnp.asarray(ring) == chip, jnp.arange(chips), 0))
    offsets = [0] + [-(s + 1) for s in range(side)] + [s + 1 for s in range(side)] + [chips // 2]
    places = (place + turned * jnp.asarray(offsets)) % chips
    chip_ids = jnp.sum(
        jnp.where(places[:, None] == jnp.arange(chips)[None, :], jnp.asarray(ring)[None, :], 0), axis=1
    )
    owners = group * GROUP + 2 * chip_ids + tensor
    labels = jax.vmap(lambda owner: sequence_labels(seq_lengths, seq_device, owner, block))(owners)
    rows_at = jnp.arange(block, dtype=jnp.int32)
    allowed = (
        (labels[:, :, None] == labels[:, None, :])
        & (labels[:, :, None] > 0)
        & (rows_at[None, None, :] <= rows_at[None, :, None])
    ) | (rows_at[None, None, :] == rows_at[None, :, None])
    allowed = allowed.astype(f32).reshape(chips * block, block)
    picked = (owners[:, None] == jnp.arange(n_dp)[None, :]).astype(f32)
    place_parts = jnp.dot(picked, small_all[:, 6 * piece :].astype(f32), precision=lax.Precision.HIGHEST)
    row_places = (place_parts[:, :block] * 64.0 + place_parts[:, block:]).reshape(chips * block)
    pair = ROT // 2
    frequency = 10000.0 ** (-2.0 * jnp.arange(pair, dtype=f32) / ROT)
    angles = row_places[:, None] * frequency[None, :]
    cosine, sine = jnp.cos(angles), jnp.sin(angles)
    nought = jnp.zeros_like(sine)
    rest = jnp.zeros((chips * block, HEAD_DIM - ROT), f32)
    tables = (
        jnp.concatenate([cosine, cosine, rest + 1.0] * 2, axis=1),
        jnp.concatenate([-sine, nought, rest] * 2, axis=1),
        jnp.concatenate([nought, sine, rest] * 2, axis=1),
    )

    both = jnp.stack([hidden_in, out_cotangent])
    both = jnp.where(tensor == core, both, across(both))
    keeps = jnp.stack([jnp.ones_like(labels[0]), (labels[0] > 0).astype(labels.dtype)]).astype(bf16)
    both = both * keeps[:, :, None]
    if groups == 1:
        inputs = gather_rows(
            after(both, packed_down, *packed_last, firsts[0], firsts[2]),
            {1: (firsts[1], tables[0]), 2: (tables[1], tables[2], allowed), side: (down_other, weights[0][0])},
        )
        up = spread(after(packed_last[0], inputs[-2]))
        up_other = over(up)
    else:
        inputs = gather_rows(both)
    mine_inputs = my_half(both, at, 1)
    state, grad_state = mine_inputs[0], mine_inputs[1]

    normed, heads, hidden_pre, wide, *parts = call_pass(
        "first", core_word, weights[0], tables, allowed, [bias_rows[0:1], gains[0], shifts[0]], inputs
    )
    slabs, others = (), ()
    if groups == 1:
        down = spread(after(packed_last[1], up, parts[0]))
        down_other = over(down)
        weights.append(call_join(join_up, up, [up_other], True, False) + call_join(join_down, down, [down_other], False, True))
        slabs, others = (down,), (up_other, down_other)
    rows_shape = (half, width)
    next_state, normed_own = call_end(
        partial(forward_end, False),
        core_word,
        ring_sum((after(parts[0], *slabs), parts[1], parts[2]), needed={2: others[:1]})[0],
        [state, added_bias[0], gains[1], shifts[1]],
        [jax.ShapeDtypeStruct(rows_shape, f32), jax.ShapeDtypeStruct(rows_shape, bf16)],
        "forward_end",
    )
    normed_chunks = gather_rows(in_order(normed_own, across(normed_own)), {0: others[1:]})

    def handed_back(own_rows):
        filled = in_order(own_rows, across(own_rows))
        return jnp.where(tensor == core, filled, over(filled))

    def summed(own, other, *earlier):
        total = own.astype(f32) + other.astype(f32)
        if groups > 1:
            total = total.transpose(1, 0, 2).reshape(total.shape[1], width)
            total = lax.psum_scatter(total, "dp", scatter_dimension=1, axis_index_groups=outer, tiled=True)
            total = total.reshape(total.shape[0], GROUP, piece).transpose(1, 0, 2)
        return spread(after(total.astype(bf16), *earlier))

    down_own = [(0, HEAD_DIM), (WIDE, WIDE + hidden)]
    down_other = [(HEAD_DIM, WIDE), (WIDE + hidden, WIDE + 2 * hidden)]
    up_own = [(p * WIDE, p * WIDE + HEAD_DIM) for p in range(3)] + [(3 * WIDE, 3 * WIDE + hidden)]
    up_other = [(p * WIDE + HEAD_DIM, (p + 1) * WIDE) for p in range(3)] + [(3 * WIDE + hidden, 3 * WIDE + 2 * hidden)]

    def down_gradients(wide_rows, grad_rows):
        return call_gradients(core_word, wide_rows, grad_rows, down_own, down_other, [], "down_gradients")

    def up_gradients(slim_rows, normed_rows, sums):
        return call_gradients(core_word, slim_rows, [normed_rows], up_own, up_other, [sums], "up_gradients")

    def backward_finish(ring_end, state, grad_state, layer, *needed):
        return call_end(
            backward_end,
            core_word,
            ring_end,
            [state, grad_state, gains[layer], *needed],
            [jax.ShapeDtypeStruct(rows_shape, f32), jax.ShapeDtypeStruct(rows_shape, bf16)],
            "backward_end",
        )

    normed_last, grad_rows, wide_last, slim, sums, *parts = call_pass(
        "middle", core_word, weights[1], tables, allowed, [bias_rows[1:2]], normed_chunks + inputs
    )
    out_parts = parts[:3]
    down_pair = down_gradients(wide_last, [grad_rows])
    *up_pair, bias_last = up_gradients(slim, normed_last, sums)
    down_sent, up_sent = over(down_pair[1]), over(up_pair[1])
    grad_end, out_end = ring_sum(parts[3:], out_parts, needed={1: (down_pair[0],), 0: (up_pair[0],)})
    grad_state, grad_low = backward_finish(grad_end, next_state, grad_state, 1)
    (hidden_out,) = call_end(
        partial(forward_end, True),
        core_word,
        out_end,
        [next_state, added_bias[1]],
        [jax.ShapeDtypeStruct(rows_shape, bf16)],
        "forward_out",
    )
    hidden_out = handed_back(hidden_out)
    down_last = summed(down_pair[0], after(down_sent, grad_low))
    grad_chunks = gather_rows(in_order(grad_low, across(grad_low)), {0: (down_sent,), 2: (up_sent,), side: (down_last, hidden_out)})
    up_last = summed(up_pair[0], after(up_sent, grad_chunks[-2]), down_last)

    down_pair = down_gradients(wide, grad_chunks)
    down_sent = over(down_pair[1])
    grad_rows, slim, sums, *parts = call_pass(
        "last", core_word, weights[0], tables, allowed, [heads, after(hidden_pre, down_pair[0]), normed], grad_chunks
    )
    down_first = summed(down_pair[0], after(down_sent, slim), up_last)
    *up_pair, bias_first = up_gradients(slim, after(normed, up_last), sums)
    up_sent = over(up_pair[1])
    (grad_end,) = ring_sum((after(parts[0], up_pair[0]), parts[1], parts[2]), needed={1: (down_first,), 0: (up_sent,)})
    up_first = summed(up_pair[0], up_sent, down_first, grad_end[2])
    sums = jnp.concatenate([bias_first, bias_last], axis=0)
    sums_qkv = sums[:, : 3 * WIDE].reshape(LAYERS, 3, 2, HEAD_DIM)
    sums_up = sums[:, 3 * WIDE :].reshape(LAYERS, 2, hidden)
    bias_own, bias_other = (
        jnp.concatenate([sums_qkv[:, :, n].reshape(LAYERS, -1), sums_up[:, n]], axis=1) for n in range(2)
    )
    bias_sent = over(bias_other)
    needed = [bias_sent]
    if groups == 1:
        *filled, mark = call_spread(up_last, down_last, 1, [])
        needed.append(mark)
    _, grad_low = backward_finish(grad_end, state, grad_state, 0, *needed)
    grad_hidden = handed_back(grad_low).astype(f32)

    ends = jnp.stack([jnp.sum(x[:, UP_ROWS : UP_ROWS + 3].astype(f32), axis=0) for x in (up_first, up_last)])
    shift_grads = ends[:, 0]
    gain_grads = (ends[:, 1] - norm_bias.astype(f32) * ends[:, 0]) / norm_gain.astype(f32)
    after_grads = ends[:, 2] / GROUP
    bias_sums = bias_own + bias_sent
    bias_qkv, bias_up = bias_sums[:, : 3 * HEAD_DIM].reshape(LAYERS, 3, HEAD_DIM), bias_sums[:, 3 * HEAD_DIM :]
    if groups == 1:
        grad_qkv, grad_out, grad_up, grad_down, _ = call_spread(up_first, down_first, 0, filled)
        grad_qkv = grad_qkv.transpose(0, 2, 1, 3)
    else:
        bias_qkv = lax.all_gather(lax.psum(bias_qkv, "dp", axis_index_groups=outer), "dp", axis=2, axis_index_groups=inner, tiled=True)
        bias_up = lax.all_gather(lax.psum(bias_up, "dp", axis_index_groups=outer), "dp", axis=1, axis_index_groups=inner, tiled=True)
        bias_qkv = lax.dynamic_slice_in_dim(bias_qkv, index * qkv_bias.shape[2], qkv_bias.shape[2], 2)
        bias_up = lax.dynamic_slice_in_dim(bias_up, index * fc1_bias.shape[1], fc1_bias.shape[1], 1)
        ups = jnp.stack([up_first, up_last]).astype(f32)
        downs = jnp.stack([down_first, down_last]).astype(f32)
        grad_qkv = ups[:, :, : 3 * HEAD_DIM].reshape(LAYERS, GROUP, 3, HEAD_DIM, piece).transpose(0, 4, 2, 1, 3).reshape(LAYERS, piece, 3, -1)
        grad_up = ups[:, :, 3 * HEAD_DIM : UP_ROWS].transpose(0, 3, 1, 2).reshape(LAYERS, piece, -1)
        grad_out = downs[:, :, :HEAD_DIM].reshape(LAYERS, -1, piece)
        grad_down = downs[:, :, HEAD_DIM:].reshape(LAYERS, -1, piece)
    return (
        hidden_out,
        grad_hidden,
        gain_grads,
        shift_grads,
        grad_qkv,
        bias_qkv,
        grad_out,
        grad_up,
        bias_up,
        grad_down,
        after_grads,
    )


def solution(mesh):
    placed = (
        P("dp", None),
        P(),
        P(),
        P("dp"),
        P(None, "dp"),
        P(None, "dp"),
        P(None, "dp", None, "tensor"),
        P(None, None, ("tensor", "dp")),
        P(None, "tensor", "dp"),
        P(None, "dp", "tensor"),
        P(None, ("tensor", "dp")),
        P(None, "tensor", "dp"),
        P(None, "dp"),
        P("dp", None),
    )
    return jax.shard_map(
        partial(per_device, mesh.shape["dp"]),
        mesh=mesh,
        in_specs=placed,
        out_specs=(
            P("dp", None),
            P("dp", None),
            P(None, "dp"),
            P(None, "dp"),
            P(None, "dp", None, "tensor"),
            P(None, None, ("tensor", "dp")),
            P(None, "tensor", "dp"),
            P(None, "dp", "tensor"),
            P(None, ("tensor", "dp")),
            P(None, "tensor", "dp"),
            P(None, "dp"),
        ),
        check_vma=False,
    )
```
